32 devices in a mesh: stream: 4 (over x, core), frames: 8 (over z, y).
Axes of the slice: x: 2, y: 2, z: 4, core: 2. Of those that a mesh axis runs over, the one named last changes fastest.
Arguments:
- inputs: bfloat16 [4096, 4, 1024], P('frames', 'stream'), may hold values from -6 to 6
- context: bfloat16 [4096, 4096], P('frames'), may hold values from -6 to 6
- cotangent: float32 [4096, 4, 1024], P('frames', 'stream'), may hold values from -6 to 6
- live_frames: int32 [32], P('frames'), may hold values from 0 to 128, as said below
- ctx_weight: bfloat16 [4096, 1024], P(None, 'frames'), may hold values from -0.09375 to 0.09375
- norm_gains: float32 [2, 1024], replicated, may hold values from 0.5 to 1.5
- qkv_weight: bfloat16 [4, 2, 1024, 1536], P('stream', None, 'frames'), may hold values from -0.1875 to 0.1875
- out_weight: bfloat16 [4, 2, 1024, 512], P('stream', None, 'frames'), may hold values from -0.25 to 0.25
- gate_up_weight: bfloat16 [4, 2, 1024, 2816], P('stream', None, 'frames'), may hold values from -0.1875 to 0.1875
- down_weight: bfloat16 [4, 2, 1024, 1408], P('stream', None, 'frames'), may hold values from -0.109375 to 0.109375
Outputs:
- result: float32 [4096, 4, 1024], P('frames', 'stream')
- grad_input: float32 [4096, 4, 1024], P('frames', 'stream')
- grad_context: float32 [4096, 4096], P('frames', 'stream')
- grad_ctx_weight: float32 [4096, 1024], P(None, ('stream', 'frames'))
- grad_norm_gains: float32 [2, 1024], P(None, ('stream', 'frames'))
- grad_qkv_weight: float32 [4, 2, 1024, 1536], P('stream', None, 'frames')
- grad_out_weight: float32 [4, 2, 1024, 512], P('stream', None, 'frames')
- grad_gate_up_weight: float32 [4, 2, 1024, 2816], P('stream', None, 'frames')
- grad_down_weight: float32 [4, 2, 1024, 1408], P('stream', None, 'frames')
The draws below stay inside these ranges and needn't reach their ends.
Inputs may be any that keep to these rules, and one draw needn't show every extreme that they name: `live_frames`: slots form buckets of 24 consecutive slots; each bucket holds one item that fills its first frames, so padding lies only at the end of a bucket (the last slot of all is always padding). Slot 0 is full.
All inputs are finite; a program needn't handle non-finite values.
Results may differ from the reference program's by a relative error of at most 0.015.
Values may be sent and summed in bfloat16 or wider, within the bound.
A program may use at most 256 MiB of HBM per device.

```python
import jax
import jax.numpy as jnp
from jax import lax

D = 1024
HEADS = 16
HD = 64
FF = 2816
CTX = 4096
SIDES = 2
HALVES = 2
POS = 2
SLOT = 128
F_DEV = 512
FRAMES = 4096
SLOTS = 32


def draw_live_frames(key, part):
    bucket_frames = 24 * SLOT
    least = bucket_frames * 500 // 3072
    bucket_count = (SLOTS + 23) // 24
    item_lengths = jax.random.randint(key, (bucket_count,), least, bucket_frames + 1)
    slot_ids = jnp.arange(SLOTS, dtype=jnp.int32)
    within = slot_ids % 24
    counts = jnp.clip(item_lengths[slot_ids // 24] - within * SLOT, 0, SLOT)
    counts = counts.at[0].set(SLOT)
    counts = counts.at[SLOTS - 1].set(0)
    return counts.astype(jnp.int32)


def steps_of(rng, extent, cuts, smallest, largest):
    loudness = 1.0
    for axis_at, blocks in cuts:
        draws = jax.random.uniform(jax.random.fold_in(jax.random.fold_in(rng, 6), axis_at), (blocks,), jnp.float32, smallest / len(cuts), largest / len(cuts))
        loudness = loudness * jnp.repeat(jnp.exp(draws), extent[axis_at] // blocks).reshape((-1,) + (1,) * (len(extent) - 1 - axis_at))
    return loudness


def gaussian(rng, extent, deviation, reach, cuts=(), held_as=jnp.bfloat16):
    entries = jax.random.normal(rng, extent, jnp.float32) * deviation
    if len(cuts) > 0:
        entries = steps_of(rng, extent, cuts, -0.22, 0.18) * entries
    return jnp.clip(entries, min=-reach, max=reach).astype(held_as)


def setup_inputs(seed: int = 0) -> dict:
    key_of = jax.random.split(jax.random.key(seed), 11)
    return {
        "inputs": gaussian(key_of[0], (FRAMES, SIDES * POS, D), 1.0, 6.0, ((0, 8), (1, 4))),
        "context": gaussian(key_of[1], (FRAMES, CTX), 1.0, 6.0, ((0, 8),)),
        "cotangent": gaussian(key_of[2], (FRAMES, SIDES * POS, D), 1.0, 6.0, ((0, 8), (1, 4)), jnp.float32),
        "live_frames": draw_live_frames(jax.random.fold_in(key_of[10], 71), 0),
        "ctx_weight": gaussian(key_of[4], (CTX, D), CTX ** -0.5, 0.09375, ((1, 8),)),
        "norm_gains": jnp.clip(1.0 + 0.1 * jax.random.normal(key_of[5], (2, D), jnp.float32), 0.5, 1.5),
        "qkv_weight": gaussian(key_of[6], (SIDES * HALVES, POS, D, 3 * HEADS * HD // HALVES), D ** -0.5, 0.1875, ((0, 4), (2, 8))),
        "out_weight": gaussian(key_of[7], (SIDES * HALVES, POS, D, HEADS * HD // HALVES), (HEADS * HD // 2) ** -0.5, 0.25, ((0, 4), (2, 8))),
        "gate_up_weight": gaussian(key_of[8], (SIDES * HALVES, POS, D, 2 * FF // HALVES), D ** -0.5, 0.1875, ((0, 4), (2, 8))),
        "down_weight": gaussian(key_of[9], (SIDES * HALVES, POS, D, FF // HALVES), FF ** -0.5, 0.109375, ((0, 4), (2, 8))),
    }


@jax.custom_vjp
def low(v):
    return lax.optimization_barrier(v.astype(jnp.bfloat16)).astype(jnp.float32)

@jax.custom_vjp
def low_back(v):
    return v

def low_keep(v):
    return (low(v), None)

def low_pass(kept, grad):
    return (grad,)

def back_keep(v):
    return (v, None)

def back_low(kept, grad):
    return (low(grad),)
low.defvjp(low_keep, low_pass)
low_back.defvjp(back_keep, back_low)
norm_eps = 1e-05

def precise(form, left, right):
    return jnp.einsum(form, left, right, precision=lax.Precision.HIGHEST)

def arrange(weight, parts):
    col_width = weight.shape[3] // parts
    shaped = weight.reshape(SIDES, HALVES, POS, D, parts, col_width)
    return shaped.transpose(0, 2, 3, 4, 1, 5).reshape(SIDES * POS, D, parts * HALVES * col_width)

def restore(grad, parts):
    col_width = grad.shape[2] // (parts * HALVES)
    shaped = grad.reshape(SIDES, POS, D, parts, HALVES, col_width)
    return shaped.transpose(0, 4, 1, 2, 3, 5).reshape(SIDES * HALVES, POS, D, parts * col_width)

def rms_norm(values, gain):
    return values * lax.rsqrt(lax.optimization_barrier(jnp.mean(values * values, axis=-1, keepdims=True)) + norm_eps) * gain

def frame_block(params, pieces):
    ctx_full, gains, qkv_full, out_full, gate_up_full, down_full = params
    hidden_in, context_in, valid_mask = pieces
    frame_count = hidden_in.shape[0]
    npos_all = SIDES * POS
    model_width = HEADS * HD
    projected = precise('fc,cd->fd', context_in, ctx_full)
    resid_in = hidden_in + low_back(jnp.broadcast_to(projected[:, None, :], hidden_in.shape))
    normed_one = low(rms_norm(resid_in, gains[0]))
    qkv_all = low_back(low(precise('fpd,pdc->fpc', normed_one, qkv_full)))
    query = qkv_all[..., :model_width].reshape(frame_count, npos_all, HEADS, HD)
    keys = qkv_all[..., model_width:2 * model_width].reshape(frame_count, npos_all, HEADS, HD)
    values = qkv_all[..., 2 * model_width:].reshape(frame_count, npos_all, HEADS, HD)
    raw_scores = low_back(precise('fqhd,fkhd->fhqk', query, keys) * HD ** (-0.5))
    rows = lax.broadcasted_iota(jnp.int32, (npos_all, npos_all), 0)
    cols = lax.broadcasted_iota(jnp.int32, (npos_all, npos_all), 1)
    scores = jnp.where(cols <= rows, raw_scores, -1e+30)
    attn_probs = jax.nn.softmax(scores, axis=-1)
    mixed = low_back(low(precise('fhqk,fkhd->fqhd', low(attn_probs), values)))
    mixed = mixed.reshape(frame_count, npos_all, model_width)
    attn_sum = low_back(precise('fpc,pdc->fpd', mixed, out_full))
    resid_mid = resid_in + attn_sum
    normed_two = low(rms_norm(resid_mid, gains[1]))
    gate_up = low_back(precise('fpd,pdc->fpc', normed_two, gate_up_full))
    gate_part = gate_up[..., :FF]
    up_part = gate_up[..., FF:]
    hidden = low(jax.nn.silu(gate_part) * up_part)
    ffn_sum = low_back(precise('fpc,pdc->fpd', hidden, down_full))
    return (resid_mid + ffn_sum) * valid_mask[:, None, None]

def reference(inputs, context, cotangent, live_frames, ctx_weight, norm_gains, qkv_weight, out_weight, gate_up_weight, down_weight):
    frames_all = inputs.shape[0]
    block_count = frames_all // F_DEV
    offsets = lax.broadcasted_iota(jnp.int32, (frames_all,), 0)
    valid_mask = (offsets % SLOT < jnp.repeat(live_frames, SLOT)).astype(jnp.float32)
    params = (ctx_weight.astype(jnp.float32), norm_gains.astype(jnp.float32), arrange(qkv_weight.astype(jnp.float32), 3), arrange(out_weight.astype(jnp.float32), 1), arrange(gate_up_weight.astype(jnp.float32), 2), arrange(down_weight.astype(jnp.float32), 1))

    def forward(params_in, hidden_all, context_all):

        def one_block(pieces):
            return jax.checkpoint(frame_block)(params_in, pieces)
        stacked = (hidden_all.reshape(block_count, F_DEV, SIDES * POS, D), context_all.reshape(block_count, F_DEV, CTX), valid_mask.reshape(block_count, F_DEV))
        return lax.map(one_block, stacked).reshape(frames_all, SIDES * POS, D)
    result, pullback = jax.vjp(forward, params, inputs.astype(jnp.float32), context.astype(jnp.float32))
    grad_params, grad_input, grad_context = pullback(cotangent.astype(jnp.float32))
    grad_ctx, grad_gains, grad_qkv, grad_out, grad_gate_up, grad_down = grad_params
    return (result, grad_input, grad_context, grad_ctx, grad_gains, restore(grad_qkv, 3), restore(grad_out, 1), restore(grad_gate_up, 2), restore(grad_down, 1))
```

```python
import functools

import jax
import jax.numpy as jnp
from jax import lax
from jax.experimental import pallas as pl
from jax.experimental.pallas import tpu as pltpu
from jax.sharding import PartitionSpec as P

HD = 64
SLOT = 128
LANES = 128
norm_eps = 1e-05
f32 = jnp.float32
bf16 = jnp.bfloat16

PAIRS = [(q, k) for q in range(4) for k in range(q + 1)]


def swap_frames(value, mask):
    n = lax.axis_size("frames")
    return lax.ppermute(value, "frames", [(d, d ^ mask) for d in range(n)])


def swap_stream(value, mask):
    n = lax.axis_size("stream")
    return lax.ppermute(value, "stream", [(d, d ^ mask) for d in range(n)])


def joint(value, target):
    streams, n = lax.axis_size("stream"), lax.axis_size("frames")
    pairs = []
    for s in range(streams):
        for f in range(n):
            to_s, to_f = target(s, f)
            pairs.append((s * n + f, to_s * n + to_f))
    return lax.ppermute(value, ("stream", "frames"), pairs)


def transposed(value):
    def target(s, f):
        core, place = s % 2, (f // 2) % 2
        return s - core + place, f - 2 * place + 2 * core

    return joint(value, target)


def peer(value, mask):
    return joint(value, lambda s, f: (s ^ (mask & 2), f ^ (2 * (mask & 1))))


def norm_scale(values):
    return lax.rsqrt(jnp.mean(values * values, axis=-1, keepdims=True) + norm_eps)


def norm_back(values, scale, gain, grad):
    weighted = grad * gain
    inner_mean = jnp.mean(weighted * values, axis=-1, keepdims=True)
    grad_values = scale * weighted - values * (scale * scale * scale) * inner_mean
    grad_gain = jnp.sum(grad * values * scale, axis=0)
    return (grad_values, grad_gain)


def exchange_rows(qkv, position):
    rows, width = qkv.shape
    quarter = rows // 4
    parts = qkv.reshape(4, quarter, width)
    out = jnp.zeros((4, quarter, width), qkv.dtype)
    own = lax.dynamic_index_in_dim(parts, position, 0, keepdims=False)
    out = lax.dynamic_update_index_in_dim(out, own, position, 0)
    for mask in (2, 1, 3):
        there = position ^ mask
        got = peer(lax.dynamic_index_in_dim(parts, there, 0, keepdims=False), mask)
        out = lax.dynamic_update_index_in_dim(out, got, there, 0)
    return out


def heads_sum(product, fold):
    high = product.astype(bf16)
    low = (product - high.astype(f32)).astype(bf16)
    return jnp.dot(high, fold, preferred_element_type=f32) + jnp.dot(
        low, fold, preferred_element_type=f32
    )


def attention_forward_body(qkv_ref, fold_ref, spread_ref, probs_ref, out_ref):
    width = out_ref.shape[2]
    fold, spread = fold_ref[...], spread_ref[...]
    for q in range(4):
        query = qkv_ref[q, :, :width].astype(f32)
        scores = []
        for k in range(q + 1):
            key = qkv_ref[k, :, width : 2 * width].astype(f32)
            scores.append(heads_sum(query * key, fold) * HD ** (-0.5))
        top = functools.reduce(jnp.maximum, scores)
        expo = [jnp.exp(s - top) for s in scores]
        total = functools.reduce(jnp.add, expo)
        mixed = None
        for k in range(q + 1):
            prob = expo[k] / total
            probs_ref[PAIRS.index((q, k))] = prob
            wide = jnp.dot(prob.astype(bf16), spread, preferred_element_type=f32)
            term = wide * qkv_ref[k, :, 2 * width :].astype(f32)
            mixed = term if mixed is None else mixed + term
        out_ref[q] = mixed.astype(bf16)


def attention_backward_body(qkv_ref, probs_ref, grad_ref, fold_ref, spread_ref, out_ref):
    width = grad_ref.shape[2]
    fold, spread = fold_ref[...], spread_ref[...]
    grad_keys, grad_values = [None] * 4, [None] * 4
    for q in range(4):
        grad = grad_ref[q].astype(f32)
        query = qkv_ref[q, :, :width].astype(f32)
        probs = [probs_ref[PAIRS.index((q, k))] for k in range(q + 1)]
        grad_probs = [
            heads_sum(grad * qkv_ref[k, :, 2 * width :].astype(f32), fold) for k in range(q + 1)
        ]
        total = functools.reduce(jnp.add, [p * g for p, g in zip(probs, grad_probs)])
        grad_query = None
        for k in range(q + 1):
            wide = jnp.dot(probs[k].astype(bf16), spread, preferred_element_type=f32)
            term = wide * grad
            grad_values[k] = term if grad_values[k] is None else grad_values[k] + term
            grad_score = (probs[k] * (grad_probs[k] - total)).astype(bf16)
            wide = jnp.dot(grad_score, spread, preferred_element_type=f32)
            term = wide * qkv_ref[k, :, width : 2 * width].astype(f32)
            grad_query = term if grad_query is None else grad_query + term
            term = wide * query
            grad_keys[k] = term if grad_keys[k] is None else grad_keys[k] + term
        out_ref[q, :, :width] = (grad_query * HD ** (-0.5)).astype(bf16)
    for k in range(4):
        out_ref[k, :, width : 2 * width] = (grad_keys[k] * HD ** (-0.5)).astype(bf16)
        out_ref[k, :, 2 * width :] = grad_values[k].astype(bf16)


def fold_matrices(width):
    feature = lax.broadcasted_iota(jnp.int32, (width, LANES), 0) // HD
    head = lax.broadcasted_iota(jnp.int32, (width, LANES), 1)
    fold = (feature == head).astype(bf16)
    return fold, fold.T


def attention_forward(qkv, step=64):
    _, rows, triple = qkv.shape
    width = triple // 3
    fold, spread = fold_matrices(width)
    return pl.pallas_call(
        attention_forward_body,
        grid=(rows // step,),
        in_specs=[
            pl.BlockSpec((4, step, triple), lambda r: (0, r, 0)),
            pl.BlockSpec((width, LANES), lambda r: (0, 0)),
            pl.BlockSpec((LANES, width), lambda r: (0, 0)),
        ],
        out_specs=[
            pl.BlockSpec((len(PAIRS), step, LANES), lambda r: (0, r, 0)),
            pl.BlockSpec((4, step, width), lambda r: (0, r, 0)),
        ],
        out_shape=[
            jax.ShapeDtypeStruct((len(PAIRS), rows, LANES), f32),
            jax.ShapeDtypeStruct((4, rows, width), bf16),
        ],
        name="attention_forward",
    )(qkv, fold, spread)


def attention_backward(qkv, probs, grad, step=64):
    _, rows, triple = qkv.shape
    width = triple // 3
    fold, spread = fold_matrices(width)
    return pl.pallas_call(
        attention_backward_body,
        grid=(rows // step,),
        in_specs=[
            pl.BlockSpec((4, step, triple), lambda r: (0, r, 0)),
            pl.BlockSpec((len(PAIRS), step, LANES), lambda r: (0, r, 0)),
            pl.BlockSpec((4, step, width), lambda r: (0, r, 0)),
            pl.BlockSpec((width, LANES), lambda r: (0, 0)),
            pl.BlockSpec((LANES, width), lambda r: (0, 0)),
        ],
        out_specs=pl.BlockSpec((4, step, triple), lambda r: (0, r, 0)),
        out_shape=jax.ShapeDtypeStruct((4, rows, triple), bf16),
        name="attention_backward",
    )(qkv, probs, grad, fold, spread)


def gathered(weight, frame_index, place):
    n = lax.axis_size("frames")
    own = lax.dynamic_index_in_dim(weight, place, 0, keepdims=False)
    other = lax.dynamic_index_in_dim(weight, 1 - place, 0, keepdims=False)
    block, width = own.shape
    full = jnp.zeros((n, block, width), own.dtype)
    for mask in range(0, n, 2):
        got = own if mask == 0 else swap_frames(other if mask & 2 else own, mask)
        near = swap_frames(got, 1)
        full = lax.dynamic_update_index_in_dim(full, got, frame_index ^ mask, 0)
        full = lax.dynamic_update_index_in_dim(full, near, frame_index ^ mask ^ 1, 0)
    return full.reshape(n * block, width)


def scattered(left, right, frame_index, place):
    n = lax.axis_size("frames")
    rows, depth = left.shape
    block = depth // n
    near = frame_index % 2
    shaped = left.reshape(rows, n // 2, 2, block)

    def product(which):
        part = lax.dynamic_index_in_dim(shaped, which, 2, keepdims=False).reshape(rows, depth // 2)
        return lax.dot_general(
            part, right, (((0,), (0,)), ((), ())), preferred_element_type=f32
        ).astype(bf16)

    arrived = swap_frames(product(1 - near), 1)
    half_sum = (product(near).astype(f32) + arrived.astype(f32)).astype(bf16)
    half_sum = half_sum.reshape(n // 2, block, -1)
    at = frame_index // 2
    own = lax.dynamic_index_in_dim(half_sum, at, 0, keepdims=False).astype(f32)
    other = None
    for mask in range(2, n, 2):
        got = swap_frames(
            lax.dynamic_index_in_dim(half_sum, at ^ (mask // 2), 0, keepdims=False), mask
        ).astype(f32)
        if mask & 2:
            other = got if other is None else other + got
        else:
            own = own + got
    first = jnp.where(place == 0, own, other)
    second = jnp.where(place == 0, other, own)
    return jnp.stack([first, second], axis=0)


def shards(
    inputs,
    context,
    cotangent,
    live_frames,
    ctx_weight,
    norm_gains,
    qkv_weight,
    out_weight,
    gate_up_weight,
    down_weight,
):
    n = lax.axis_size("frames")
    stream_index = lax.axis_index("stream")
    frame_index = lax.axis_index("frames")
    half_index = stream_index % 2
    place = (frame_index // 2) % 2
    position = (stream_index // 2) * 2 + place
    frame_count = inputs.shape[0]
    width_model = inputs.shape[2]
    offsets = lax.broadcasted_iota(jnp.int32, (frame_count,), 0)
    valid_mask = (offsets % SLOT < jnp.repeat(live_frames, SLOT)).astype(f32)[:, None]
    gain_one = norm_gains[0]
    gain_two = norm_gains[1]

    ctx_rows = ctx_weight.shape[0] // 4
    piece = lax.dynamic_slice_in_dim(ctx_weight, stream_index * ctx_rows, ctx_rows, 0)
    block = piece.shape[1]
    held = piece[None]
    order = [0]
    for bit in reversed(range(1, n.bit_length() - 1)):
        got = swap_frames(held, 1 << bit)
        held = jnp.concatenate([held, got], axis=0)
        order = order + [o ^ (1 << bit) for o in order]
    got = swap_frames(held, 1)
    held = jnp.concatenate([held, got], axis=0)
    order = order + [o ^ 1 for o in order]
    ctx_full = jnp.zeros((ctx_rows, n, block), bf16)
    for at, o in enumerate(order):
        ctx_full = lax.dynamic_update_index_in_dim(ctx_full, held[at], frame_index ^ o, 1)
    ctx_full = ctx_full.reshape(ctx_rows, width_model)
    context_part = lax.dynamic_slice_in_dim(context, stream_index * ctx_rows, ctx_rows, 1)
    projected = jnp.dot(context_part, ctx_full, preferred_element_type=f32)

    def summed(value):
        value = value.astype(f32) + swap_stream(value.astype(bf16), 1).astype(f32)
        half = value.shape[0] // 2
        mine = lax.dynamic_slice_in_dim(value, half_index * half, half, 0)
        mine = (mine + swap_stream(mine.astype(bf16), 2).astype(f32)).astype(bf16)
        far = swap_stream(mine, 1)
        first = jnp.where(half_index == 0, mine, far)
        second = jnp.where(half_index == 0, far, mine)
        return jnp.concatenate([first, second], axis=0)

    resid_home = inputs[:, 0].astype(f32) + summed(projected).astype(f32)
    resid_in = transposed(resid_home.astype(bf16)).astype(f32)
    grad_res = transposed((cotangent[:, 0] * valid_mask).astype(bf16))

    qkv_full = gathered(qkv_weight[0], frame_index, place)
    out_full = gathered(out_weight[0], frame_index, place)
    gate_up_full = gathered(gate_up_weight[0], frame_index, place)
    down_full = gathered(down_weight[0], frame_index, place)

    def paired(mine):
        return jnp.concatenate([mine, swap_stream(mine, 1)], axis=0)

    def own_sum(partial_value):
        return partial_value[:frame_count] + swap_stream(
            partial_value[frame_count:].astype(bf16), 1
        ).astype(f32)

    def rows_times(left, right):
        return jnp.dot(left, right, preferred_element_type=f32)

    def rows_back(left, right):
        return lax.dot_general(left, right, (((1,), (1,)), ((), ())), preferred_element_type=f32)

    scale_one = norm_scale(resid_in)
    paired_one = paired((resid_in * scale_one * gain_one).astype(bf16))
    qkv_rows = rows_times(paired_one, qkv_full).astype(bf16)
    qkv_mixed = exchange_rows(qkv_rows, position)
    probs, mixed_quarter = attention_forward(qkv_mixed)

    def returned(value):
        _, quarter, width = value.shape
        out = jnp.zeros((4, quarter, width), value.dtype)
        own = lax.dynamic_index_in_dim(value, position, 0, keepdims=False)
        out = lax.dynamic_update_index_in_dim(out, own, position, 0)
        for mask in (2, 1, 3):
            there = position ^ mask
            got = peer(lax.dynamic_index_in_dim(value, there, 0, keepdims=False), mask)
            out = lax.dynamic_update_index_in_dim(out, got, there, 0)
        return out.reshape(4 * quarter, width)

    mixed = returned(mixed_quarter)
    resid_mid = resid_in + own_sum(rows_back(mixed, out_full))
    scale_two = norm_scale(resid_mid)
    paired_two = paired((resid_mid * scale_two * gain_two).astype(bf16))
    gate_up = rows_times(paired_two, gate_up_full)
    ffn_half = down_full.shape[1]
    gate_part = gate_up[:, :ffn_half]
    up_part = gate_up[:, ffn_half:]
    sigmoid_gate = jax.nn.sigmoid(gate_part)
    activated = gate_part * sigmoid_gate
    hidden = (activated * up_part).astype(bf16)

    paired_grad_ffn = paired(grad_res)
    sum_down = scattered(paired_grad_ffn, hidden, frame_index, place)
    grad_hidden = rows_times(paired_grad_ffn, down_full)
    grad_gate = grad_hidden * up_part * (sigmoid_gate * (1.0 + gate_part * (1.0 - sigmoid_gate)))
    grad_up = grad_hidden * activated
    grad_gu_low = jnp.concatenate([grad_gate, grad_up], axis=-1).astype(bf16)
    grad_normed_two = own_sum(rows_back(grad_gu_low, gate_up_full))
    sum_gate_up = scattered(paired_two, grad_gu_low, frame_index, place)
    back_two, grad_gain_two = norm_back(resid_mid, scale_two, gain_two, grad_normed_two)
    grad_mid = grad_res.astype(f32) + back_two
    paired_grad_attn = paired(grad_mid.astype(bf16))
    grad_mixed = rows_times(paired_grad_attn, out_full).astype(bf16)
    sum_out = scattered(paired_grad_attn, mixed, frame_index, place)
    grad_qkv_mixed = attention_backward(qkv_mixed, probs, exchange_rows(grad_mixed, position))
    grad_qkv_low = returned(grad_qkv_mixed)
    grad_normed_one = own_sum(rows_back(grad_qkv_low, qkv_full))
    sum_qkv = scattered(paired_one, grad_qkv_low, frame_index, place)
    back_one, grad_gain_one = norm_back(resid_in, scale_one, gain_one, grad_normed_one)
    gain_rows = jnp.pad(jnp.stack([grad_gain_one, grad_gain_two]), ((0, 14), (0, 0)))
    carried = jnp.concatenate([grad_mid + back_one, gain_rows], axis=0).astype(bf16)
    grad_home = transposed(carried)

    ffn_sum = own_sum(rows_back(hidden, down_full))
    result = transposed((resid_mid + ffn_sum).astype(bf16)).astype(f32) * valid_mask

    grad_sum = summed(grad_home)
    grad_ctx_low = grad_sum[:frame_count]
    sum_context = rows_back(grad_ctx_low, ctx_full)
    share = width_model // 4
    grad_share = lax.dynamic_slice_in_dim(grad_sum, stream_index * share, share, 1)
    ctx_term = lax.dot_general(
        grad_share[:frame_count], context, (((0,), (0,)), ((), ())), preferred_element_type=f32
    ).astype(bf16)
    gain_term = jnp.pad(grad_share[frame_count : frame_count + 2].T, ((0, 0), (0, LANES - 2)))
    total = jnp.concatenate([ctx_term, gain_term], axis=1).reshape(n, share // n, -1)
    for bit in range(n.bit_length() - 1):
        shaped = total.reshape((-1, 2) + total.shape[1:])
        at = (frame_index >> bit) % 2
        keep = lax.dynamic_index_in_dim(shaped, at, 1, keepdims=False)
        send = lax.dynamic_index_in_dim(shaped, 1 - at, 1, keepdims=False)
        total = keep.astype(f32) + swap_frames(send.astype(bf16), 1 << bit).astype(f32)
    total = total.reshape(share // n, -1).T
    sum_ctx = total[: ctx_weight.shape[0]]
    sum_gains = total[ctx_weight.shape[0] : ctx_weight.shape[0] + 2]

    return (
        result[:, None],
        grad_home[:frame_count].astype(f32)[:, None],
        sum_context,
        sum_ctx,
        sum_gains,
        sum_qkv[None],
        sum_out[None],
        sum_gate_up[None],
        sum_down[None],
    )


def solution(mesh):
    placed = (
        P("frames", "stream", None),
        P("frames", None),
        P("frames", "stream", None),
        P("frames"),
        P(None, "frames"),
        P(),
        P("stream", None, "frames", None),
        P("stream", None, "frames", None),
        P("stream", None, "frames", None),
        P("stream", None, "frames", None),
    )
    return jax.shard_map(
        shards,
        mesh=mesh,
        in_specs=placed,
        out_specs=(
            P("frames", "stream", None),
            P("frames", "stream", None),
            P("frames", "stream"),
            P(None, ("stream", "frames")),
            P(None, ("stream", "frames")),
            P("stream", None, "frames", None),
            P("stream", None, "frames", None),
            P("stream", None, "frames", None),
            P("stream", None, "frames", None),
        ),
        check_vma=False,
    )
```

```python
import functools

import jax
import jax.numpy as jnp
from jax import lax
from jax.experimental import pallas as pl
from jax.experimental.pallas import tpu as pltpu
from jax.sharding import PartitionSpec as P

HD = 64
SLOT = 128
LANES = 128
norm_eps = 1e-05
f32 = jnp.float32
bf16 = jnp.bfloat16

PAIRS = [(q, k) for q in range(4) for k in range(q + 1)]


ANY = pl.BlockSpec(memory_space=pl.ANY)
VMEM = pl.BlockSpec(memory_space=pltpu.VMEM)
EXTRA = 32


def flip(value, mask):
    bit = 1
    while bit <= mask:
        if mask & bit:
            value = value + bit - 2 * bit * ((value // bit) % 2)
        bit *= 2
    return value


class Where:
    def __init__(self, n):
        self.n = n
        self.stream = lax.axis_index("stream")
        self.frame = lax.axis_index("frames")
        self.core = self.stream % 2
        self.place = (self.frame // 2) % 2
        self.position = (self.stream // 2) * 2 + self.place
        self.near = self.frame % 2
        self.at = self.frame // 2
        self.far_masks = [m for m in range(2, n, 2) if not m & 2]
        self.both_masks = [m for m in range(2, n, 2) if m & 2 and m > 2]
        self.masks = self.far_masks + self.both_masks + [2]

    def along_stream(self, mask):
        return (flip(self.stream, mask), self.frame)

    def along_frames(self, mask):
        return (self.stream, flip(self.frame, mask))

    def with_position(self, mask):
        return (flip(self.stream, mask & 2), flip(self.frame, 2 * (mask & 1)))

    def across(self):
        return (flip(self.stream, 1), flip(self.frame, 2))


class Wire:
    def __init__(self, send, recv):
        self.send, self.recv, self.count, self.started = send, recv, 0, []

    def make(self, src, dst, device):
        k = self.count
        self.count += 1
        return pltpu.make_async_remote_copy(
            src_ref=src,
            dst_ref=dst,
            send_sem=self.send.at[k],
            recv_sem=self.recv.at[k],
            device_id=device,
            device_id_type=pl.DeviceIdType.MESH,
        )

    def start(self, src, dst, device):
        copy = self.make(src, dst, device)
        copy.start()
        self.started.append(copy)
        return copy

    def finish(self):
        for copy in self.started:
            copy.wait_send()


class Local:
    def __init__(self, sems):
        self.sems, self.count = sems, 0

    def start(self, src, dst):
        copy = pltpu.make_async_copy(src, dst, self.sems.at[self.count])
        self.count += 1
        copy.start()
        return copy


def greet(devices):
    barrier = pltpu.get_barrier_semaphore()
    for device in devices:
        pl.semaphore_signal(
            barrier, inc=1, device_id=device, device_id_type=pl.DeviceIdType.MESH
        )
    pl.semaphore_wait(barrier, len(devices))


def dot_rows(left, right):
    return lax.dot_general(left, right, (((0,), (0,)), ((), ())), preferred_element_type=f32)


def dot_columns(left, right):
    return lax.dot_general(left, right, (((1,), (1,)), ((), ())), preferred_element_type=f32)


class Reduction:
    def __init__(self, w, wire, send, keep, arrived, sums, landed, out):
        self.w, self.wire = w, wire
        self.send, self.keep, self.arrived = send, keep, arrived
        self.sums, self.landed, self.out = sums, landed, out
        self.first, self.second = {}, {}
        self.order = w.masks + [0]

    def begin(self, mask):
        block = flip(self.w.at, mask // 2)
        self.first[mask] = self.wire.start(
            self.send.at[block], self.arrived.at[block], self.w.along_frames(1)
        )

    def forward(self, mask):
        block = flip(self.w.at, mask // 2)
        self.first[mask].wait_recv()
        total = self.keep[block].astype(f32) + self.arrived[block].astype(f32)
        self.sums[block] = total.astype(bf16)
        if mask:
            self.second[mask] = self.wire.start(
                self.sums.at[block], self.landed.at[mask // 2], self.w.along_frames(mask)
            )

    def close(self):
        own, other = self.sums[self.w.at].astype(f32), None
        for mask in self.w.masks:
            self.second[mask].wait_recv()
            got = self.landed[mask // 2].astype(f32)
            if mask & 2:
                other = got if other is None else other + got
            else:
                own = own + got
        self.out[self.w.place] = own
        self.out[1 - self.w.place] = other


def tail_body(
    n, part_send, part_own, resid, mid, gains, gain_two, result_rows,
    gq_send, gq_keep, go_send, go_keep, context, ctx_full,
    out_q, out_o, out_grad, out_result, out_context, out_ctx,
    part_got, low, home, partner_half, half_sum, far_half, whole, kept_q, kept_o,
    arrived_q, arrived_o, sums_q, sums_o, landed_q, landed_o,
    context_held, ctx_held, term, term_got, term_sum, term_landed, gain_sum,
    send_sem, recv_sem, local_sem,
):
    w = Where(n)
    wire, local = Wire(send_sem, recv_sem), Local(local_sem)
    rows, depth = resid.shape
    crossing = w.core != w.place
    load_q = local.start(gq_keep, kept_q)
    load_o = local.start(go_keep, kept_o)
    load_context = local.start(context, context_held)
    load_ctx = local.start(ctx_full, ctx_held)
    greet(
        [w.along_stream(1), w.along_stream(2), w.along_frames(1)]
        + [w.along_frames(m) for m in w.masks]
        + [w.across()]
    )
    part = wire.start(part_send, part_got, w.along_stream(1))
    red_o = Reduction(w, wire, go_send, kept_o, arrived_o, sums_o, landed_o, out_o)
    red_q = Reduction(w, wire, gq_send, kept_q, arrived_q, sums_q, landed_q, out_q)
    for mask in red_o.order:
        red_o.begin(mask)
    for mask in red_q.order:
        red_q.begin(mask)

    part.wait_recv()
    gain = gains[0:1, :]
    gain_sum[...] = jnp.zeros_like(gain_sum)
    step = 64

    @pl.loop(0, rows // step)
    def _(t):
        at = pl.ds(pl.multiple_of(t * step, step), step)
        grad = part_own[at, :].astype(f32) + part_got[at, :].astype(f32)
        values = resid[at, :].astype(f32)
        scale = lax.rsqrt(jnp.mean(values * values, axis=-1, keepdims=True) + norm_eps)
        weighted = grad * gain
        inner = jnp.mean(weighted * values, axis=-1, keepdims=True)
        back = scale * weighted - values * (scale * scale * scale * inner)
        low[at, :] = (mid[at, :] + back).astype(bf16)
        gain_sum[...] += jnp.sum(grad * values * scale, axis=0, keepdims=True)

    row = lax.broadcasted_iota(jnp.int32, (EXTRA, depth), 0)
    low[rows:, :] = jnp.where(
        row == 0, gain_sum[...], jnp.where(row == 1, gain_two[...], 0.0)
    ).astype(bf16)

    cross = wire.make(low, home, w.across())
    cross_result = wire.make(result_rows, out_result, w.across())

    @pl.when(crossing)
    def _():
        cross.start()

    load_o.wait()
    load_q.wait()
    for mask in red_o.order:
        red_o.forward(mask)

    @pl.when(crossing)
    def _():
        cross_result.start()
        cross.wait_recv()

    stay = pltpu.make_async_copy(low, home, local.sems.at[4])
    stay_result = pltpu.make_async_copy(result_rows, out_result, local.sems.at[5])

    @pl.when(jnp.logical_not(crossing))
    def _():
        stay.start()
        stay_result.start()
        stay.wait()

    half = (rows + EXTRA) // 2
    mine = pl.ds(pl.multiple_of(w.core * half, 16), half)
    theirs = pl.ds(pl.multiple_of((1 - w.core) * half, 16), half)
    first = wire.start(home.at[theirs, :], partner_half, w.along_stream(1))
    out_grad[...] = home[:rows, :].astype(f32)
    first.wait_recv()
    half_sum[...] = (home[mine, :].astype(f32) + partner_half[...].astype(f32)).astype(bf16)
    second = wire.start(half_sum, far_half, w.along_stream(2))
    red_q.forward(red_q.order[0])
    red_q.forward(red_q.order[1])
    second.wait_recv()
    whole[mine, :] = (half_sum[...].astype(f32) + far_half[...].astype(f32)).astype(bf16)
    third = wire.start(whole.at[mine, :], whole.at[mine, :], w.along_stream(1))
    load_context.wait()
    third.wait_recv()

    share = depth // 4
    columns = pl.ds(pl.multiple_of(w.stream * share, LANES), share)
    block = share // n
    wide = context_held.shape[1]
    pieces = 2
    grad_share = whole[:rows, columns]
    firsts, seconds = [], []
    row = lax.broadcasted_iota(jnp.int32, (EXTRA, LANES), 0)
    select = (row == lax.broadcasted_iota(jnp.int32, (EXTRA, LANES), 1)).astype(bf16)
    edges = [wide * p // pieces for p in range(pieces)] + [wide + LANES]
    for p in range(pieces):
        lo, hi = edges[p], edges[p + 1]
        for at in range(lo, min(hi, wide), 1024):
            to = min(at + 1024, wide)
            value = dot_rows(grad_share, context_held[:, at:to]).astype(bf16)
            for k in range(n):
                term[k // 2, k % 2, :, at:to] = value[k * block : (k + 1) * block]
        if hi > wide:
            value = dot_rows(whole[rows:, columns], select).astype(bf16)
            for k in range(n):
                term[k // 2, k % 2, :, wide:hi] = value[k * block : (k + 1) * block]
        firsts.append(
            wire.start(
                term.at[:, 1 - w.near, :, lo:hi], term_got.at[:, :, lo:hi], w.along_frames(1)
            )
        )
    for mask in red_q.order[2:]:
        red_q.forward(mask)
    load_ctx.wait()

    def context_rows(t):
        at = pl.ds(pl.multiple_of(t * LANES, LANES), LANES)
        out_context[at, :] = dot_columns(whole[at, :], ctx_held[...])

    @pl.loop(0, rows // LANES)
    def _(t):
        context_rows(t)

    for p in range(pieces):
        lo, hi = edges[p], edges[p + 1]
        firsts[p].wait_recv()
        for mask in w.masks + [0]:
            to = flip(w.at, mask // 2)
            total = term[to, w.near, :, lo:hi].astype(f32) + term_got[to, :, lo:hi].astype(f32)
            term_sum[to, :, lo:hi] = total.astype(bf16)
            if mask:
                seconds.append(
                    wire.start(
                        term_sum.at[to, :, lo:hi],
                        term_landed.at[mask // 2, :, lo:hi],
                        w.along_frames(mask),
                    )
                )
    red_o.close()
    red_q.close()

    @pl.when(crossing)
    def _():
        cross_result.wait_recv()
        cross.wait_send()
        cross_result.wait_send()

    @pl.when(jnp.logical_not(crossing))
    def _():
        stay_result.wait()

    for copy in seconds:
        copy.wait_recv()
    total = term_sum[w.at].astype(f32)
    for mask in w.masks:
        total = total + term_landed[mask // 2].astype(f32)
    out_ctx[...] = total
    wire.finish()


def tail(
    n, part_send, part_own, resid, mid, gains, gain_two, result_rows,
    gq_send, gq_keep, go_send, go_keep, context, ctx_full,
):
    rows, depth = resid.shape
    halfn, block, wide_q = gq_send.shape
    wide_o = go_send.shape[2]
    share = depth // 4 // n
    wide = context.shape[1] + LANES
    half = (rows + EXTRA) // 2
    count = 64 + 2 * n
    scratch = [
        pltpu.VMEM((rows, depth), bf16),
        pltpu.VMEM((rows + EXTRA, depth), bf16),
        pltpu.VMEM((rows + EXTRA, depth), bf16),
        pltpu.VMEM((half, depth), bf16),
        pltpu.VMEM((half, depth), bf16),
        pltpu.VMEM((half, depth), bf16),
        pltpu.VMEM((rows + EXTRA, depth), bf16),
        pltpu.VMEM((halfn, block, wide_q), bf16),
        pltpu.VMEM((halfn, block, wide_o), bf16),
        pltpu.VMEM((halfn, block, wide_q), bf16),
        pltpu.VMEM((halfn, block, wide_o), bf16),
        pltpu.VMEM((halfn, block, wide_q), bf16),
        pltpu.VMEM((halfn, block, wide_o), bf16),
        pltpu.VMEM((halfn, block, wide_q), bf16),
        pltpu.VMEM((halfn, block, wide_o), bf16),
        pltpu.VMEM(context.shape, bf16),
        pltpu.VMEM(ctx_full.shape, bf16),
        pltpu.VMEM((halfn, 2, share, wide), bf16),
        pltpu.VMEM((halfn, share, wide), bf16),
        pltpu.VMEM((halfn, share, wide), bf16),
        pltpu.VMEM((halfn, share, wide), bf16),
        pltpu.VMEM((1, depth), f32),
        pltpu.SemaphoreType.DMA((count,)),
        pltpu.SemaphoreType.DMA((count,)),
        pltpu.SemaphoreType.DMA((6,)),
    ]
    return pl.pallas_call(
        functools.partial(tail_body, n),
        in_specs=[ANY, VMEM, VMEM, VMEM, VMEM, VMEM, VMEM, ANY, ANY, ANY, ANY, ANY, ANY],
        out_specs=[VMEM, VMEM, VMEM, VMEM, VMEM, VMEM],
        out_shape=[
            jax.ShapeDtypeStruct((2, block, wide_q), f32),
            jax.ShapeDtypeStruct((2, block, wide_o), f32),
            jax.ShapeDtypeStruct((rows, depth), f32),
            jax.ShapeDtypeStruct((rows, depth), bf16),
            jax.ShapeDtypeStruct((rows, ctx_full.shape[0]), f32),
            jax.ShapeDtypeStruct((share, wide), f32),
        ],
        scratch_shapes=scratch,
        compiler_params=pltpu.CompilerParams(
            collective_id=5, has_side_effects=True, vmem_limit_bytes=60 << 20
        ),
        name="tail",
    )(
        part_send, part_own, resid, mid, gains, gain_two, result_rows,
        gq_send, gq_keep, go_send, go_keep, context, ctx_full,
    )


def swap_frames(value, mask):
    n = lax.axis_size("frames")
    return lax.ppermute(value, "frames", [(d, d ^ mask) for d in range(n)])


def swap_stream(value, mask):
    n = lax.axis_size("stream")
    return lax.ppermute(value, "stream", [(d, d ^ mask) for d in range(n)])


def joint(value, target):
    streams, n = lax.axis_size("stream"), lax.axis_size("frames")
    pairs = []
    for s in range(streams):
        for f in range(n):
            to_s, to_f = target(s, f)
            pairs.append((s * n + f, to_s * n + to_f))
    return lax.ppermute(value, ("stream", "frames"), pairs)


def transposed(value):
    def target(s, f):
        core, place = s % 2, (f // 2) % 2
        return s - core + place, f - 2 * place + 2 * core

    return joint(value, target)


def peer(value, mask):
    return joint(value, lambda s, f: (s ^ (mask & 2), f ^ (2 * (mask & 1))))


def norm_scale(values):
    return lax.rsqrt(jnp.mean(values * values, axis=-1, keepdims=True) + norm_eps)


def norm_back(values, scale, gain, grad):
    weighted = grad * gain
    inner_mean = jnp.mean(weighted * values, axis=-1, keepdims=True)
    grad_values = scale * weighted - values * (scale * scale * scale) * inner_mean
    grad_gain = jnp.sum(grad * values * scale, axis=0)
    return (grad_values, grad_gain)


def exchange_rows(qkv, position):
    rows, width = qkv.shape
    quarter = rows // 4
    parts = qkv.reshape(4, quarter, width)
    out = jnp.zeros((4, quarter, width), qkv.dtype)
    own = lax.dynamic_index_in_dim(parts, position, 0, keepdims=False)
    out = lax.dynamic_update_index_in_dim(out, own, position, 0)
    for mask in (2, 1, 3):
        there = position ^ mask
        got = peer(lax.dynamic_index_in_dim(parts, there, 0, keepdims=False), mask)
        out = lax.dynamic_update_index_in_dim(out, got, there, 0)
    return out


def heads_sum(product, fold):
    high = product.astype(bf16)
    low = (product - high.astype(f32)).astype(bf16)
    return jnp.dot(high, fold, preferred_element_type=f32) + jnp.dot(
        low, fold, preferred_element_type=f32
    )


def attention_forward_body(qkv_ref, fold_ref, spread_ref, probs_ref, out_ref):
    width = out_ref.shape[2]
    fold, spread = fold_ref[...], spread_ref[...]
    for q in range(4):
        query = qkv_ref[q, :, :width].astype(f32)
        scores = []
        for k in range(q + 1):
            key = qkv_ref[k, :, width : 2 * width].astype(f32)
            scores.append(heads_sum(query * key, fold) * HD ** (-0.5))
        top = functools.reduce(jnp.maximum, scores)
        expo = [jnp.exp(s - top) for s in scores]
        total = functools.reduce(jnp.add, expo)
        mixed = None
        for k in range(q + 1):
            prob = expo[k] / total
            probs_ref[PAIRS.index((q, k))] = prob
            wide = jnp.dot(prob.astype(bf16), spread, preferred_element_type=f32)
            term = wide * qkv_ref[k, :, 2 * width :].astype(f32)
            mixed = term if mixed is None else mixed + term
        out_ref[q] = mixed.astype(bf16)


def attention_backward_body(qkv_ref, probs_ref, grad_ref, fold_ref, spread_ref, out_ref):
    width = grad_ref.shape[2]
    fold, spread = fold_ref[...], spread_ref[...]
    grad_keys, grad_values = [None] * 4, [None] * 4
    for q in range(4):
        grad = grad_ref[q].astype(f32)
        query = qkv_ref[q, :, :width].astype(f32)
        probs = [probs_ref[PAIRS.index((q, k))] for k in range(q + 1)]
        grad_probs = [
            heads_sum(grad * qkv_ref[k, :, 2 * width :].astype(f32), fold) for k in range(q + 1)
        ]
        total = functools.reduce(jnp.add, [p * g for p, g in zip(probs, grad_probs)])
        grad_query = None
        for k in range(q + 1):
            wide = jnp.dot(probs[k].astype(bf16), spread, preferred_element_type=f32)
            term = wide * grad
            grad_values[k] = term if grad_values[k] is None else grad_values[k] + term
            grad_score = (probs[k] * (grad_probs[k] - total)).astype(bf16)
            wide = jnp.dot(grad_score, spread, preferred_element_type=f32)
            term = wide * qkv_ref[k, :, width : 2 * width].astype(f32)
            grad_query = term if grad_query is None else grad_query + term
            term = wide * query
            grad_keys[k] = term if grad_keys[k] is None else grad_keys[k] + term
        out_ref[q, :, :width] = (grad_query * HD ** (-0.5)).astype(bf16)
    for k in range(4):
        out_ref[k, :, width : 2 * width] = (grad_keys[k] * HD ** (-0.5)).astype(bf16)
        out_ref[k, :, 2 * width :] = grad_values[k].astype(bf16)


def fold_matrices(width):
    feature = lax.broadcasted_iota(jnp.int32, (width, LANES), 0) // HD
    head = lax.broadcasted_iota(jnp.int32, (width, LANES), 1)
    fold = (feature == head).astype(bf16)
    return fold, fold.T


def attention_forward(qkv, step=64):
    _, rows, triple = qkv.shape
    width = triple // 3
    fold, spread = fold_matrices(width)
    return pl.pallas_call(
        attention_forward_body,
        grid=(rows // step,),
        in_specs=[
            pl.BlockSpec((4, step, triple), lambda r: (0, r, 0)),
            pl.BlockSpec((width, LANES), lambda r: (0, 0)),
            pl.BlockSpec((LANES, width), lambda r: (0, 0)),
        ],
        out_specs=[
            pl.BlockSpec((len(PAIRS), step, LANES), lambda r: (0, r, 0)),
            pl.BlockSpec((4, step, width), lambda r: (0, r, 0)),
        ],
        out_shape=[
            jax.ShapeDtypeStruct((len(PAIRS), rows, LANES), f32),
            jax.ShapeDtypeStruct((4, rows, width), bf16),
        ],
        name="attention_forward",
    )(qkv, fold, spread)


def attention_backward(qkv, probs, grad, step=64):
    _, rows, triple = qkv.shape
    width = triple // 3
    fold, spread = fold_matrices(width)
    return pl.pallas_call(
        attention_backward_body,
        grid=(rows // step,),
        in_specs=[
            pl.BlockSpec((4, step, triple), lambda r: (0, r, 0)),
            pl.BlockSpec((len(PAIRS), step, LANES), lambda r: (0, r, 0)),
            pl.BlockSpec((4, step, width), lambda r: (0, r, 0)),
            pl.BlockSpec((width, LANES), lambda r: (0, 0)),
            pl.BlockSpec((LANES, width), lambda r: (0, 0)),
        ],
        out_specs=pl.BlockSpec((4, step, triple), lambda r: (0, r, 0)),
        out_shape=jax.ShapeDtypeStruct((4, rows, triple), bf16),
        name="attention_backward",
    )(qkv, probs, grad, fold, spread)


def after(value, *others):
    return lax.optimization_barrier((value,) + others)[0]


def taken(weights, place):
    own = [lax.dynamic_index_in_dim(w, place, 0, keepdims=False) for w in weights]
    other = [lax.dynamic_index_in_dim(w, 1 - place, 0, keepdims=False) for w in weights]
    if len(weights) == 1:
        return own[0], other[0]
    return jnp.concatenate(own, axis=1), jnp.concatenate(other, axis=1)


def placed_rows(pieces, frame_index, start, width):
    n = lax.axis_size("frames")
    block = pieces[0].shape[0]
    full = jnp.zeros((n, block, width), pieces[0].dtype)
    for mask in range(n):
        part = pieces[mask][:, start : start + width]
        full = lax.dynamic_update_index_in_dim(full, part, frame_index ^ mask, 0)
    return full.reshape(n * block, width)


def halves(left, near):
    n = lax.axis_size("frames")
    rows, depth = left.shape
    block = depth // n
    even = jnp.concatenate([left[:, k * block : (k + 1) * block] for k in range(0, n, 2)], axis=1)
    odd = jnp.concatenate([left[:, k * block : (k + 1) * block] for k in range(1, n, 2)], axis=1)
    return jnp.where(near == 0, odd, even), jnp.where(near == 0, even, odd)


def scattered(left_halves, right, frame_index, place):
    n = lax.axis_size("frames")

    def product(part):
        return lax.dot_general(
            part, right, (((0,), (0,)), ((), ())), preferred_element_type=f32
        ).astype(bf16)

    arrived = swap_frames(product(left_halves[0]), 1)
    half_sum = (product(left_halves[1]).astype(f32) + arrived.astype(f32)).astype(bf16)
    half_sum = half_sum.reshape(n // 2, -1, right.shape[1])
    at = frame_index // 2
    own = lax.dynamic_index_in_dim(half_sum, at, 0, keepdims=False).astype(f32)
    other = None
    for mask in range(2, n, 2):
        got = swap_frames(
            lax.dynamic_index_in_dim(half_sum, at ^ (mask // 2), 0, keepdims=False), mask
        ).astype(f32)
        if mask & 2:
            other = got if other is None else other + got
        else:
            own = own + got
    first = jnp.where(place == 0, own, other)
    second = jnp.where(place == 0, other, own)
    return jnp.stack([first, second], axis=0)


def shards(
    inputs,
    context,
    cotangent,
    live_frames,
    ctx_weight,
    norm_gains,
    qkv_weight,
    out_weight,
    gate_up_weight,
    down_weight,
):
    n = lax.axis_size("frames")
    stream_index = lax.axis_index("stream")
    frame_index = lax.axis_index("frames")
    half_index = stream_index % 2
    place = (frame_index // 2) % 2
    position = (stream_index // 2) * 2 + place
    frame_count = inputs.shape[0]
    width_model = inputs.shape[2]
    offsets = lax.broadcasted_iota(jnp.int32, (frame_count,), 0)
    valid_mask = (offsets % SLOT < jnp.repeat(live_frames, SLOT)).astype(f32)[:, None]
    gain_one = norm_gains[0]
    gain_two = norm_gains[1]

    ctx_rows = ctx_weight.shape[0] // 4
    piece = lax.dynamic_slice_in_dim(ctx_weight, stream_index * ctx_rows, ctx_rows, 0)
    block = piece.shape[1]
    held = piece[None]
    order = [0]
    near_pieces = []
    attn_own, attn_other = taken((qkv_weight[0], out_weight[0]), place)
    near_first = {}
    near_first["attn"] = swap_frames(attn_own, 1)
    far_context = None
    for bit in reversed(range(1, n.bit_length() - 1)):
        got = swap_frames(held, 1 << bit)
        if far_context is None:
            far_context = got
            near_pieces.append(swap_frames(jnp.concatenate([held, got], axis=0), 1))
        else:
            near_pieces.append(swap_frames(got, 1))
        held = jnp.concatenate([held, got], axis=0)
        order = order + [o ^ (1 << bit) for o in order]
    held = jnp.concatenate([held] + near_pieces, axis=0)
    order = order + [o ^ 1 for o in order]
    ctx_full = jnp.zeros((ctx_rows, n, block), bf16)
    for at, o in enumerate(order):
        ctx_full = lax.dynamic_update_index_in_dim(ctx_full, held[at], frame_index ^ o, 1)
    ctx_full = ctx_full.reshape(ctx_rows, width_model)
    context_part = lax.dynamic_slice_in_dim(context, stream_index * ctx_rows, ctx_rows, 1)
    projected = jnp.dot(context_part, ctx_full, preferred_element_type=f32)

    def summed(value):
        value = value.astype(f32) + swap_stream(value.astype(bf16), 1).astype(f32)
        half = value.shape[0] // 2
        mine = lax.dynamic_slice_in_dim(value, half_index * half, half, 0)
        mine = (mine + swap_stream(mine.astype(bf16), 2).astype(f32)).astype(bf16)
        far = swap_stream(mine, 1)
        first = jnp.where(half_index == 0, mine, far)
        second = jnp.where(half_index == 0, far, mine)
        return jnp.concatenate([first, second], axis=0)

    def sent(own, other, masks, *others):
        pieces = {}
        for mask in masks:
            got = swap_frames(after(other if mask & 2 else own, *others), mask)
            pieces[mask] = got
            pieces[mask + 1] = swap_frames(got, 1)
        return pieces

    far_masks = [m for m in range(2, n, 2) if not m & 2]
    both_masks = [m for m in range(2, n, 2) if m & 2 and m > 2]
    near_masks = [2]
    attn_pieces = {0: attn_own, 1: near_first["attn"]}
    attn_pieces.update(sent(attn_own, attn_other, far_masks + both_masks + near_masks, far_context))
    head_width = out_weight.shape[3]
    qkv_full = placed_rows(attn_pieces, frame_index, 0, 3 * head_width)
    out_full = placed_rows(attn_pieces, frame_index, 3 * head_width, head_width)

    home_sum = summed(projected).astype(f32)
    resid_home = (inputs[:, 0].astype(f32) + home_sum).astype(bf16)
    resid_in = transposed(resid_home).astype(f32)
    gu_own, gu_other = taken((gate_up_weight[0],), place)
    down_own, down_other = taken((down_weight[0],), place)
    gu_pieces = {0: gu_own, 1: swap_frames(after(gu_own, near_pieces[-1]), 1)}
    gu_pieces.update(sent(gu_own, gu_other, far_masks, resid_home))

    def paired(mine):
        return jnp.concatenate([mine, swap_stream(mine, 1)], axis=0)

    def own_sum(partial_value):
        return partial_value[:frame_count] + swap_stream(
            partial_value[frame_count:].astype(bf16), 1
        ).astype(f32)

    def rows_times(left, right):
        return jnp.dot(left, right, preferred_element_type=f32)

    def rows_back(left, right):
        return lax.dot_general(left, right, (((1,), (1,)), ((), ())), preferred_element_type=f32)

    scale_one = norm_scale(resid_in)
    paired_one = paired((resid_in * scale_one * gain_one).astype(bf16))
    qkv_rows = rows_times(paired_one, qkv_full).astype(bf16)
    qkv_mixed = exchange_rows(qkv_rows, position)
    gu_pieces.update(sent(gu_own, gu_other, both_masks, qkv_rows))
    down_pieces = {0: down_own, 1: swap_frames(after(down_own, qkv_rows), 1)}
    probs, mixed_quarter = attention_forward(qkv_mixed)

    def returned(value):
        _, quarter, width = value.shape
        out = jnp.zeros((4, quarter, width), value.dtype)
        own = lax.dynamic_index_in_dim(value, position, 0, keepdims=False)
        out = lax.dynamic_update_index_in_dim(out, own, position, 0)
        for mask in (2, 1, 3):
            there = position ^ mask
            got = peer(lax.dynamic_index_in_dim(value, there, 0, keepdims=False), mask)
            out = lax.dynamic_update_index_in_dim(out, got, there, 0)
        return out.reshape(4 * quarter, width)

    mixed = returned(mixed_quarter)
    gu_pieces.update(sent(gu_own, gu_other, near_masks, mixed_quarter))
    gate_up_full = placed_rows(gu_pieces, frame_index, 0, gate_up_weight.shape[3])
    down_pieces.update(
        sent(down_own, down_other, far_masks + both_masks + near_masks, mixed_quarter)
    )
    down_full = placed_rows(down_pieces, frame_index, 0, down_weight.shape[3])
    grad_home_rows = (cotangent[:, 0] * valid_mask).astype(bf16)
    grad_res = transposed(after(grad_home_rows, mixed_quarter))
    near = frame_index % 2
    resid_mid = resid_in + own_sum(rows_back(mixed, out_full))
    scale_two = norm_scale(resid_mid)
    paired_two = paired((resid_mid * scale_two * gain_two).astype(bf16))
    gate_up = rows_times(paired_two, gate_up_full)
    ffn_half = down_full.shape[1]
    gate_part = gate_up[:, :ffn_half]
    up_part = gate_up[:, ffn_half:]
    sigmoid_gate = jax.nn.sigmoid(gate_part)
    activated = gate_part * sigmoid_gate
    hidden = (activated * up_part).astype(bf16)

    paired_grad_ffn = paired(grad_res)
    sum_down = scattered(halves(paired_grad_ffn, near), hidden, frame_index, place)
    grad_hidden = rows_times(paired_grad_ffn, down_full)
    grad_gate = grad_hidden * up_part * (sigmoid_gate * (1.0 + gate_part * (1.0 - sigmoid_gate)))
    grad_up = grad_hidden * activated
    grad_gu_low = jnp.concatenate([grad_gate, grad_up], axis=-1).astype(bf16)
    grad_normed_two = own_sum(rows_back(grad_gu_low, gate_up_full))
    sum_gate_up = scattered(halves(paired_two, near), grad_gu_low, frame_index, place)
    back_two, grad_gain_two = norm_back(resid_mid, scale_two, gain_two, grad_normed_two)
    grad_mid = grad_res.astype(f32) + back_two
    paired_grad_attn = paired(grad_mid.astype(bf16))
    grad_mixed = rows_times(paired_grad_attn, out_full).astype(bf16)
    grad_qkv_mixed = attention_backward(qkv_mixed, probs, exchange_rows(grad_mixed, position))
    grad_qkv_low = returned(grad_qkv_mixed)
    def parts(left, right):
        away, stay = halves(left, near)
        block = width_model // n
        return [
            dot_rows(part, right).astype(bf16).reshape(n // 2, block, right.shape[1])
            for part in (away, stay)
        ]

    part_away = rows_back(grad_qkv_low[frame_count:], qkv_full).astype(bf16)
    part_stay = rows_back(grad_qkv_low[:frame_count], qkv_full)
    result_rows = (resid_mid + own_sum(rows_back(hidden, down_full))).astype(bf16)
    sum_qkv, sum_out, grad_home, result, sum_context, ctx_total = tail(
        n,
        part_away,
        part_stay,
        resid_in.astype(bf16),
        grad_mid,
        norm_gains,
        grad_gain_two[None],
        result_rows,
        *parts(paired_one, grad_qkv_low),
        *parts(paired_grad_attn, mixed),
        context,
        ctx_full,
    )
    result = result.astype(f32) * valid_mask
    ctx_total = ctx_total.T
    sum_ctx = ctx_total[: ctx_weight.shape[0]]
    sum_gains = ctx_total[ctx_weight.shape[0] : ctx_weight.shape[0] + 2]

    return (
        result[:, None],
        grad_home[:, None],
        sum_context,
        sum_ctx,
        sum_gains,
        sum_qkv[None],
        sum_out[None],
        sum_gate_up[None],
        sum_down[None],
    )


def solution(mesh):
    placed = (
        P("frames", "stream", None),
        P("frames", None),
        P("frames", "stream", None),
        P("frames"),
        P(None, "frames"),
        P(),
        P("stream", None, "frames", None),
        P("stream", None, "frames", None),
        P("stream", None, "frames", None),
        P("stream", None, "frames", None),
    )
    return jax.shard_map(
        shards,
        mesh=mesh,
        in_specs=placed,
        out_specs=(
            P("frames", "stream", None),
            P("frames", "stream", None),
            P("frames", "stream"),
            P(None, ("stream", "frames")),
            P(None, ("stream", "frames")),
            P("stream", None, "frames", None),
            P("stream", None, "frames", None),
            P("stream", None, "frames", None),
            P("stream", None, "frames", None),
        ),
        check_vma=False,
    )
```

```python
import functools

import jax
import jax.numpy as jnp
from jax import lax
from jax.experimental import pallas as pl
from jax.experimental.pallas import tpu as pltpu
from jax.sharding import PartitionSpec as P

HD = 64
SLOT = 128
LANES = 128
norm_eps = 1e-05
f32 = jnp.float32
bf16 = jnp.bfloat16

PAIRS = [(q, k) for q in range(4) for k in range(q + 1)]


ANY = pl.BlockSpec(memory_space=pl.ANY)
VMEM = pl.BlockSpec(memory_space=pltpu.VMEM)
EXTRA = 32


def flip(value, mask):
    bit = 1
    while bit <= mask:
        if mask & bit:
            value = value + bit - 2 * bit * ((value // bit) % 2)
        bit *= 2
    return value


class Where:
    def __init__(self, n):
        self.n = n
        self.stream = lax.axis_index("stream")
        self.frame = lax.axis_index("frames")
        self.core = self.stream % 2
        self.place = (self.frame // 2) % 2
        self.position = (self.stream // 2) * 2 + self.place
        self.near = self.frame % 2
        self.at = self.frame // 2
        self.far_masks = [m for m in range(2, n, 2) if not m & 2]
        self.both_masks = [m for m in range(2, n, 2) if m & 2 and m > 2]
        self.masks = self.far_masks + self.both_masks + [2]

    def along_stream(self, mask):
        return (flip(self.stream, mask), self.frame)

    def along_frames(self, mask):
        return (self.stream, flip(self.frame, mask))

    def with_position(self, mask):
        return (flip(self.stream, mask & 2), flip(self.frame, 2 * (mask & 1)))

    def across(self):
        return (flip(self.stream, 1), flip(self.frame, 2))


class Wire:
    def __init__(self, send, recv):
        self.send, self.recv, self.count, self.started = send, recv, 0, []

    def make(self, src, dst, device):
        k = self.count
        self.count += 1
        return pltpu.make_async_remote_copy(
            src_ref=src,
            dst_ref=dst,
            send_sem=self.send.at[k],
            recv_sem=self.recv.at[k],
            device_id=device,
            device_id_type=pl.DeviceIdType.MESH,
        )

    def start(self, src, dst, device):
        copy = self.make(src, dst, device)
        copy.start()
        self.started.append(copy)
        return copy

    def sent(self, copy):
        self.started = [c for c in self.started if c is not copy]
        copy.wait_send()

    def finish(self):
        for copy in self.started:
            copy.wait_send()


class Local:
    def __init__(self, sems):
        self.sems, self.count = sems, 0

    def start(self, src, dst):
        copy = pltpu.make_async_copy(src, dst, self.sems.at[self.count])
        self.count += 1
        copy.start()
        return copy


def greet(devices):
    barrier = pltpu.get_barrier_semaphore()
    for device in devices:
        pl.semaphore_signal(
            barrier, inc=1, device_id=device, device_id_type=pl.DeviceIdType.MESH
        )
    pl.semaphore_wait(barrier, len(devices))


def dot_rows(left, right):
    return lax.dot_general(left, right, (((0,), (0,)), ((), ())), preferred_element_type=f32)


def dot_columns(left, right):
    return lax.dot_general(left, right, (((1,), (1,)), ((), ())), preferred_element_type=f32)


class Reduction:
    def __init__(self, w, wire, send, keep, arrived, sums, landed, out):
        self.w, self.wire = w, wire
        self.send, self.keep, self.arrived = send, keep, arrived
        self.sums, self.landed, self.out = sums, landed, out
        self.first, self.second = {}, {}
        self.order = w.masks + [0]

    def begin(self, mask):
        block = flip(self.w.at, mask // 2)
        self.first[mask] = self.wire.start(
            self.send.at[block], self.arrived.at[block], self.w.along_frames(1)
        )

    def forward(self, mask):
        block = flip(self.w.at, mask // 2)
        self.first[mask].wait_recv()
        total = self.keep[block].astype(f32) + self.arrived[block].astype(f32)
        self.sums[block] = total.astype(bf16)
        if mask:
            self.second[mask] = self.wire.start(
                self.sums.at[block], self.landed.at[mask // 2], self.w.along_frames(mask)
            )

    def close(self):
        own, other = self.sums[self.w.at].astype(f32), None
        for mask in self.w.masks:
            self.second[mask].wait_recv()
            got = self.landed[mask // 2].astype(f32)
            if mask & 2:
                other = got if other is None else other + got
            else:
                own = own + got
        self.out[self.w.place] = own
        self.out[1 - self.w.place] = other


def tail_body(
    n, part_send, part_own, resid, mid, gains, gain_two, result_rows,
    gq_send, gq_keep, go_send, go_keep, context, ctx_full,
    out_q, out_o, out_grad, out_result, out_context, out_ctx,
    part_got, low, home, partner_half, half_sum, far_half, whole, kept_q, kept_o,
    arrived_q, arrived_o, sums_q, sums_o, landed_q, landed_o,
    context_held, ctx_held, term, term_got, term_sum, term_landed, gain_sum,
    send_sem, recv_sem, local_sem,
):
    w = Where(n)
    wire, local = Wire(send_sem, recv_sem), Local(local_sem)
    rows, depth = resid.shape
    crossing = w.core != w.place
    load_q = local.start(gq_keep, kept_q)
    load_o = local.start(go_keep, kept_o)
    load_context = local.start(context, context_held)
    load_ctx = local.start(ctx_full, ctx_held)
    greet(
        [w.along_stream(1), w.along_stream(2), w.along_frames(1)]
        + [w.along_frames(m) for m in w.masks]
        + [w.across()]
    )
    part = wire.start(part_send, part_got, w.along_stream(1))
    red_o = Reduction(w, wire, go_send, kept_o, arrived_o, sums_o, landed_o, out_o)
    red_q = Reduction(w, wire, gq_send, kept_q, arrived_q, sums_q, landed_q, out_q)
    for mask in red_o.order:
        red_o.begin(mask)
    for mask in red_q.order:
        red_q.begin(mask)

    part.wait_recv()
    gain = gains[0:1, :]
    gain_sum[...] = jnp.zeros_like(gain_sum)
    step = 64

    @pl.loop(0, rows // step)
    def _(t):
        at = pl.ds(pl.multiple_of(t * step, step), step)
        grad = part_own[at, :].astype(f32) + part_got[at, :].astype(f32)
        values = resid[at, :].astype(f32)
        scale = lax.rsqrt(jnp.mean(values * values, axis=-1, keepdims=True) + norm_eps)
        weighted = grad * gain
        inner = jnp.mean(weighted * values, axis=-1, keepdims=True)
        back = scale * weighted - values * (scale * scale * scale * inner)
        low[at, :] = (mid[at, :] + back).astype(bf16)
        gain_sum[...] += jnp.sum(grad * values * scale, axis=0, keepdims=True)

    row = lax.broadcasted_iota(jnp.int32, (EXTRA, depth), 0)
    low[rows:, :] = jnp.where(
        row == 0, gain_sum[...], jnp.where(row == 1, gain_two[...], 0.0)
    ).astype(bf16)

    cross = wire.make(low, home, w.across())
    cross_result = wire.make(result_rows, out_result, w.across())

    @pl.when(crossing)
    def _():
        cross.start()

    load_o.wait()
    load_q.wait()
    for mask in red_o.order:
        red_o.forward(mask)

    @pl.when(crossing)
    def _():
        cross_result.start()
        cross.wait_recv()

    stay = pltpu.make_async_copy(low, home, local.sems.at[4])
    stay_result = pltpu.make_async_copy(result_rows, out_result, local.sems.at[5])

    @pl.when(jnp.logical_not(crossing))
    def _():
        stay.start()
        stay_result.start()
        stay.wait()

    half = (rows + EXTRA) // 2
    mine = pl.ds(pl.multiple_of(w.core * half, 16), half)
    theirs = pl.ds(pl.multiple_of((1 - w.core) * half, 16), half)
    first = wire.start(home.at[theirs, :], partner_half, w.along_stream(1))
    out_grad[...] = home[:rows, :].astype(f32)
    first.wait_recv()
    half_sum[...] = (home[mine, :].astype(f32) + partner_half[...].astype(f32)).astype(bf16)
    second = wire.start(half_sum, far_half, w.along_stream(2))
    red_q.forward(red_q.order[0])
    red_q.forward(red_q.order[1])
    second.wait_recv()
    whole[mine, :] = (half_sum[...].astype(f32) + far_half[...].astype(f32)).astype(bf16)
    third = wire.start(whole.at[mine, :], whole.at[mine, :], w.along_stream(1))
    load_context.wait()
    third.wait_recv()

    share = depth // 4
    columns = pl.ds(pl.multiple_of(w.stream * share, LANES), share)
    block = share // n
    wide = context_held.shape[1]
    pieces = 2
    grad_share = whole[:rows, columns]
    firsts, seconds = [], []
    row = lax.broadcasted_iota(jnp.int32, (EXTRA, LANES), 0)
    select = (row == lax.broadcasted_iota(jnp.int32, (EXTRA, LANES), 1)).astype(bf16)
    edges = [wide * p // pieces for p in range(pieces)] + [wide + LANES]
    for p in range(pieces):
        lo, hi = edges[p], edges[p + 1]
        for at in range(lo, min(hi, wide), 1024):
            to = min(at + 1024, wide)
            value = dot_rows(grad_share, context_held[:, at:to]).astype(bf16)
            for k in range(n):
                term[k // 2, k % 2, :, at:to] = value[k * block : (k + 1) * block]
        if hi > wide:
            value = dot_rows(whole[rows:, columns], select).astype(bf16)
            for k in range(n):
                term[k // 2, k % 2, :, wide:hi] = value[k * block : (k + 1) * block]
        firsts.append(
            wire.start(
                term.at[:, 1 - w.near, :, lo:hi], term_got.at[:, :, lo:hi], w.along_frames(1)
            )
        )
    for mask in red_q.order[2:]:
        red_q.forward(mask)
    load_ctx.wait()

    def context_rows(t):
        at = pl.ds(pl.multiple_of(t * LANES, LANES), LANES)
        out_context[at, :] = dot_columns(whole[at, :], ctx_held[...])

    @pl.loop(0, rows // LANES)
    def _(t):
        context_rows(t)

    for p in range(pieces):
        lo, hi = edges[p], edges[p + 1]
        firsts[p].wait_recv()
        for mask in w.masks + [0]:
            to = flip(w.at, mask // 2)
            total = term[to, w.near, :, lo:hi].astype(f32) + term_got[to, :, lo:hi].astype(f32)
            term_sum[to, :, lo:hi] = total.astype(bf16)
            if mask:
                seconds.append(
                    wire.start(
                        term_sum.at[to, :, lo:hi],
                        term_landed.at[mask // 2, :, lo:hi],
                        w.along_frames(mask),
                    )
                )
    red_o.close()
    red_q.close()

    @pl.when(crossing)
    def _():
        cross_result.wait_recv()
        cross.wait_send()
        cross_result.wait_send()

    @pl.when(jnp.logical_not(crossing))
    def _():
        stay_result.wait()

    for copy in seconds:
        copy.wait_recv()
    total = term_sum[w.at].astype(f32)
    for mask in w.masks:
        total = total + term_landed[mask // 2].astype(f32)
    out_ctx[...] = total
    wire.finish()


def tail(
    n, part_send, part_own, resid, mid, gains, gain_two, result_rows,
    gq_send, gq_keep, go_send, go_keep, context, ctx_full,
):
    rows, depth = resid.shape
    halfn, block, wide_q = gq_send.shape
    wide_o = go_send.shape[2]
    share = depth // 4 // n
    wide = context.shape[1] + LANES
    half = (rows + EXTRA) // 2
    count = 64 + 2 * n
    scratch = [
        pltpu.VMEM((rows, depth), bf16),
        pltpu.VMEM((rows + EXTRA, depth), bf16),
        pltpu.VMEM((rows + EXTRA, depth), bf16),
        pltpu.VMEM((half, depth), bf16),
        pltpu.VMEM((half, depth), bf16),
        pltpu.VMEM((half, depth), bf16),
        pltpu.VMEM((rows + EXTRA, depth), bf16),
        pltpu.VMEM((halfn, block, wide_q), bf16),
        pltpu.VMEM((halfn, block, wide_o), bf16),
        pltpu.VMEM((halfn, block, wide_q), bf16),
        pltpu.VMEM((halfn, block, wide_o), bf16),
        pltpu.VMEM((halfn, block, wide_q), bf16),
        pltpu.VMEM((halfn, block, wide_o), bf16),
        pltpu.VMEM((halfn, block, wide_q), bf16),
        pltpu.VMEM((halfn, block, wide_o), bf16),
        pltpu.VMEM(context.shape, bf16),
        pltpu.VMEM(ctx_full.shape, bf16),
        pltpu.VMEM((halfn, 2, share, wide), bf16),
        pltpu.VMEM((halfn, share, wide), bf16),
        pltpu.VMEM((halfn, share, wide), bf16),
        pltpu.VMEM((halfn, share, wide), bf16),
        pltpu.VMEM((1, depth), f32),
        pltpu.SemaphoreType.DMA((count,)),
        pltpu.SemaphoreType.DMA((count,)),
        pltpu.SemaphoreType.DMA((6,)),
    ]
    return pl.pallas_call(
        functools.partial(tail_body, n),
        in_specs=[ANY, VMEM, VMEM, VMEM, VMEM, VMEM, VMEM, ANY, ANY, ANY, ANY, ANY, ANY],
        out_specs=[VMEM, VMEM, VMEM, VMEM, VMEM, VMEM],
        out_shape=[
            jax.ShapeDtypeStruct((2, block, wide_q), f32),
            jax.ShapeDtypeStruct((2, block, wide_o), f32),
            jax.ShapeDtypeStruct((rows, depth), f32),
            jax.ShapeDtypeStruct((rows, depth), bf16),
            jax.ShapeDtypeStruct((rows, ctx_full.shape[0]), f32),
            jax.ShapeDtypeStruct((share, wide), f32),
        ],
        scratch_shapes=scratch,
        compiler_params=pltpu.CompilerParams(
            collective_id=5, has_side_effects=True, vmem_limit_bytes=60 << 20
        ),
        name="tail",
    )(
        part_send, part_own, resid, mid, gains, gain_two, result_rows,
        gq_send, gq_keep, go_send, go_keep, context, ctx_full,
    )


def swap_frames(value, mask):
    n = lax.axis_size("frames")
    return lax.ppermute(value, "frames", [(d, d ^ mask) for d in range(n)])


def swap_stream(value, mask):
    n = lax.axis_size("stream")
    return lax.ppermute(value, "stream", [(d, d ^ mask) for d in range(n)])


def joint(value, target):
    streams, n = lax.axis_size("stream"), lax.axis_size("frames")
    pairs = []
    for s in range(streams):
        for f in range(n):
            to_s, to_f = target(s, f)
            pairs.append((s * n + f, to_s * n + to_f))
    return lax.ppermute(value, ("stream", "frames"), pairs)


def transposed(value):
    def target(s, f):
        core, place = s % 2, (f // 2) % 2
        return s - core + place, f - 2 * place + 2 * core

    return joint(value, target)


def peer(value, mask):
    return joint(value, lambda s, f: (s ^ (mask & 2), f ^ (2 * (mask & 1))))


def norm_scale(values):
    return lax.rsqrt(jnp.mean(values * values, axis=-1, keepdims=True) + norm_eps)


def norm_back(values, scale, gain, grad):
    weighted = grad * gain
    inner_mean = jnp.mean(weighted * values, axis=-1, keepdims=True)
    grad_values = scale * weighted - values * (scale * scale * scale) * inner_mean
    grad_gain = jnp.sum(grad * values * scale, axis=0)
    return (grad_values, grad_gain)


def exchange_rows(qkv, position):
    rows, width = qkv.shape
    quarter = rows // 4
    parts = qkv.reshape(4, quarter, width)
    out = jnp.zeros((4, quarter, width), qkv.dtype)
    own = lax.dynamic_index_in_dim(parts, position, 0, keepdims=False)
    out = lax.dynamic_update_index_in_dim(out, own, position, 0)
    for mask in (2, 1, 3):
        there = position ^ mask
        got = peer(lax.dynamic_index_in_dim(parts, there, 0, keepdims=False), mask)
        out = lax.dynamic_update_index_in_dim(out, got, there, 0)
    return out


def heads_sum(product, fold):
    high = product.astype(bf16)
    low = (product - high.astype(f32)).astype(bf16)
    return jnp.dot(high, fold, preferred_element_type=f32) + jnp.dot(
        low, fold, preferred_element_type=f32
    )


def attention_forward_rows(at, qkv_ref, fold, spread, probs_ref, out_ref):
    width = out_ref.shape[2]
    for q in range(4):
        query = qkv_ref[q, at, :width].astype(f32)
        scores = []
        for k in range(q + 1):
            key = qkv_ref[k, at, width : 2 * width].astype(f32)
            scores.append(heads_sum(query * key, fold) * HD ** (-0.5))
        top = functools.reduce(jnp.maximum, scores)
        expo = [jnp.exp(s - top) for s in scores]
        total = functools.reduce(jnp.add, expo)
        mixed = None
        for k in range(q + 1):
            prob = expo[k] / total
            probs_ref[PAIRS.index((q, k)), at, :] = prob
            wide = jnp.dot(prob.astype(bf16), spread, preferred_element_type=f32)
            term = wide * qkv_ref[k, at, 2 * width :].astype(f32)
            mixed = term if mixed is None else mixed + term
        out_ref[q, at, :] = mixed.astype(bf16)


def attention_backward_body(qkv_ref, probs_ref, grad_ref, fold_ref, spread_ref, out_ref):
    width = grad_ref.shape[2]
    fold, spread = fold_ref[...], spread_ref[...]
    grad_keys, grad_values = [None] * 4, [None] * 4
    for q in range(4):
        grad = grad_ref[q].astype(f32)
        query = qkv_ref[q, :, :width].astype(f32)
        probs = [probs_ref[PAIRS.index((q, k))] for k in range(q + 1)]
        grad_probs = [
            heads_sum(grad * qkv_ref[k, :, 2 * width :].astype(f32), fold) for k in range(q + 1)
        ]
        total = functools.reduce(jnp.add, [p * g for p, g in zip(probs, grad_probs)])
        grad_query = None
        for k in range(q + 1):
            wide = jnp.dot(probs[k].astype(bf16), spread, preferred_element_type=f32)
            term = wide * grad
            grad_values[k] = term if grad_values[k] is None else grad_values[k] + term
            grad_score = (probs[k] * (grad_probs[k] - total)).astype(bf16)
            wide = jnp.dot(grad_score, spread, preferred_element_type=f32)
            term = wide * qkv_ref[k, :, width : 2 * width].astype(f32)
            grad_query = term if grad_query is None else grad_query + term
            term = wide * query
            grad_keys[k] = term if grad_keys[k] is None else grad_keys[k] + term
        out_ref[q, :, :width] = (grad_query * HD ** (-0.5)).astype(bf16)
    for k in range(4):
        out_ref[k, :, width : 2 * width] = (grad_keys[k] * HD ** (-0.5)).astype(bf16)
        out_ref[k, :, 2 * width :] = grad_values[k].astype(bf16)


def fold_matrices(width):
    feature = lax.broadcasted_iota(jnp.int32, (width, LANES), 0) // HD
    head = lax.broadcasted_iota(jnp.int32, (width, LANES), 1)
    fold = (feature == head).astype(bf16)
    return fold, fold.T


def attention_backward(qkv, probs, grad, step=64):
    _, rows, triple = qkv.shape
    width = triple // 3
    fold, spread = fold_matrices(width)
    return pl.pallas_call(
        attention_backward_body,
        grid=(rows // step,),
        in_specs=[
            pl.BlockSpec((4, step, triple), lambda r: (0, r, 0)),
            pl.BlockSpec((len(PAIRS), step, LANES), lambda r: (0, r, 0)),
            pl.BlockSpec((4, step, width), lambda r: (0, r, 0)),
            pl.BlockSpec((width, LANES), lambda r: (0, 0)),
            pl.BlockSpec((LANES, width), lambda r: (0, 0)),
        ],
        out_specs=pl.BlockSpec((4, step, triple), lambda r: (0, r, 0)),
        out_shape=jax.ShapeDtypeStruct((4, rows, triple), bf16),
        name="attention_backward",
    )(qkv, probs, grad, fold, spread)


def after(value, *others):
    return lax.optimization_barrier((value,) + others)[0]


def taken(weights, place):
    own = [lax.dynamic_index_in_dim(w, place, 0, keepdims=False) for w in weights]
    other = [lax.dynamic_index_in_dim(w, 1 - place, 0, keepdims=False) for w in weights]
    if len(weights) == 1:
        return own[0], other[0]
    return jnp.concatenate(own, axis=1), jnp.concatenate(other, axis=1)


def placed_rows(pieces, frame_index, start, width):
    n = lax.axis_size("frames")
    block = pieces[0].shape[0]
    full = jnp.zeros((n, block, width), pieces[0].dtype)
    for mask in range(n):
        part = pieces[mask][:, start : start + width]
        full = lax.dynamic_update_index_in_dim(full, part, frame_index ^ mask, 0)
    return full.reshape(n * block, width)


def halves(left, near):
    n = lax.axis_size("frames")
    rows, depth = left.shape
    block = depth // n
    even = jnp.concatenate([left[:, k * block : (k + 1) * block] for k in range(0, n, 2)], axis=1)
    odd = jnp.concatenate([left[:, k * block : (k + 1) * block] for k in range(1, n, 2)], axis=1)
    return jnp.where(near == 0, odd, even), jnp.where(near == 0, even, odd)


def scattered(left_halves, right, frame_index, place):
    n = lax.axis_size("frames")

    def product(part):
        return lax.dot_general(
            part, right, (((0,), (0,)), ((), ())), preferred_element_type=f32
        ).astype(bf16)

    arrived = swap_frames(product(left_halves[0]), 1)
    half_sum = (product(left_halves[1]).astype(f32) + arrived.astype(f32)).astype(bf16)
    half_sum = half_sum.reshape(n // 2, -1, right.shape[1])
    at = frame_index // 2
    own = lax.dynamic_index_in_dim(half_sum, at, 0, keepdims=False).astype(f32)
    other = None
    for mask in range(2, n, 2):
        got = swap_frames(
            lax.dynamic_index_in_dim(half_sum, at ^ (mask // 2), 0, keepdims=False), mask
        ).astype(f32)
        if mask & 2:
            other = got if other is None else other + got
        else:
            own = own + got
    first = jnp.where(place == 0, own, other)
    second = jnp.where(place == 0, other, own)
    return jnp.stack([first, second], axis=0)


class Spread:
    def __init__(self, w, wire, weight, full):
        self.w, self.wire, self.weight, self.full = w, wire, weight, full
        self.block = full.shape[0] // w.n
        self.far, self.near = {}, {}

    def rows(self, frame):
        return self.full.at[pl.ds(pl.multiple_of(frame * self.block, self.block), self.block), :]

    def own(self, local):
        return local.start(self.weight.at[self.w.place], self.rows(self.w.frame))

    def own_near(self):
        w = self.w
        self.near[0] = self.wire.start(
            self.weight.at[w.place], self.rows(w.frame), w.along_frames(1)
        )

    def send(self, mask):
        w = self.w
        which = 1 - w.place if mask & 2 else w.place
        self.far[mask] = self.wire.start(
            self.weight.at[which], self.rows(w.frame), w.along_frames(mask)
        )

    def relay(self, mask):
        self.far[mask].wait_recv()
        rows = self.rows(flip(self.w.frame, mask))
        self.near[mask] = self.wire.start(rows, rows, self.w.along_frames(1))

    def close(self):
        for copy in self.near.values():
            copy.wait_recv()


def front_body(
    n, context, ctx_weight, inputs, grad_rows, gains, fold, spread,
    qkv_weight, out_weight, gu_weight, down_weight,
    out_qkv, out_out, out_gu, out_down, out_ctx, out_resid, out_mid, out_one, out_two, out_grad,
    out_qkv_mixed, out_probs, out_mixed,
    ctx_held, context_held, total, partner_half, half_sum, far_half, whole, home, resid, pair,
    qkv_full, out_full, qkv_rows, qkv_mixed, probs, mixed_quarter, mixed, away, got, grad_pair,
    send_sem, recv_sem, local_sem,
):
    w = Where(n)
    wire, local = Wire(send_sem, recv_sem), Local(local_sem)
    rows, depth = inputs.shape
    count = ctx_weight.shape[0] // 4
    piece = depth // n
    crossing = w.core != w.place
    half = rows // 2
    step = 64
    quarter_of_context = pl.ds(pl.multiple_of(w.stream * count, LANES), count)
    load_context = local.start(context.at[:, quarter_of_context], context_held)
    load_ctx = local.start(ctx_weight.at[quarter_of_context, :], ctx_held.at[w.frame])
    qkv = Spread(w, wire, qkv_weight, qkv_full)
    out = Spread(w, wire, out_weight, out_full)
    gu = Spread(w, wire, gu_weight, out_gu)
    down = Spread(w, wire, down_weight, out_down)
    owns = [qkv.own(local), out.own(local)]
    greet(
        [w.along_stream(1), w.along_stream(2), w.along_frames(1)]
        + [w.along_frames(m) for m in w.masks]
        + [w.across(), w.with_position(3)]
    )

    load_ctx.wait()
    held, near = [0], {}

    def ctx_near(o):
        at = flip(w.frame, o)
        near[o] = wire.start(ctx_held.at[at], ctx_held.at[at], w.along_frames(1))

    ready = []
    for bit in reversed(range(1, n.bit_length() - 1)):
        copies = []
        for o in held:
            at = flip(w.frame, o)
            copies.append(
                (o, wire.start(ctx_held.at[at], ctx_held.at[at], w.along_frames(1 << bit)))
            )
        if bit == n.bit_length() - 2:
            ctx_near(0)
            qkv.own_near()
            out.own_near()
        if bit == 1:
            for mask in w.masks:
                qkv.send(mask)
                out.send(mask)
        for o, copy in copies:
            copy.wait_recv()
            ctx_near(o ^ (1 << bit))
            held.append(o ^ (1 << bit))

    load_context.wait()

    def project(o):
        at = flip(w.frame, o)
        columns = pl.ds(pl.multiple_of(at * piece, piece), piece)
        value = jnp.dot(context_held[...], ctx_held[at], preferred_element_type=f32)
        total[:, columns] = value

    if piece % LANES == 0:
        for o in held:
            project(o)
        for o in held:
            near[o].wait_recv()
            project(o ^ 1)
    else:
        for o in held:
            near[o].wait_recv()
        total[...] = jnp.zeros_like(total)

        @pl.loop(0, n)
        def _(at):
            line = lax.broadcasted_iota(jnp.int32, (piece, depth), 0)
            column = lax.broadcasted_iota(jnp.int32, (piece, depth), 1)
            select = (column == line + at * piece).astype(bf16)
            laid = jnp.dot(ctx_held[at], select, preferred_element_type=f32).astype(bf16)

            @pl.loop(0, rows // LANES)
            def _(t):
                here = pl.ds(pl.multiple_of(t * LANES, LANES), LANES)
                total[here, :] += jnp.dot(
                    context_held[here, :], laid, preferred_element_type=f32
                )

    store_ctx = local.start(ctx_held, out_ctx)

    mine = pl.ds(pl.multiple_of(w.core * half, 16), half)
    theirs = pl.ds(pl.multiple_of((1 - w.core) * half, 16), half)
    whole[theirs, :] = total[theirs, :].astype(bf16)
    first = wire.start(whole.at[theirs, :], partner_half, w.along_stream(1))
    first.wait_recv()
    half_sum[...] = (total[mine, :] + partner_half[...].astype(f32)).astype(bf16)
    second = wire.start(half_sum, far_half, w.along_stream(2))
    for mask in w.masks[:1]:
        qkv.relay(mask)
        out.relay(mask)
    second.wait_recv()
    home[mine, :] = (half_sum[...].astype(f32) + far_half[...].astype(f32)).astype(bf16)
    third = wire.start(home.at[mine, :], home.at[mine, :], w.along_stream(1))
    third.wait_recv()
    wire.sent(third)

    @pl.loop(0, rows // step)
    def _(t):
        at = pl.ds(pl.multiple_of(t * step, step), step)
        home[at, :] = (home[at, :].astype(f32) + inputs[at, :].astype(f32)).astype(bf16)

    cross = wire.make(home, resid, w.across())
    cross_grad = wire.make(grad_rows, grad_pair.at[:rows, :], w.across())
    stay = pltpu.make_async_copy(home, resid, local_sem.at[22])
    stay_grad = pltpu.make_async_copy(grad_rows, grad_pair.at[:rows, :], local_sem.at[23])

    @pl.when(crossing)
    def _():
        cross.start()

    @pl.when(jnp.logical_not(crossing))
    def _():
        stay.start()
        stay_grad.start()

    gu.own_near()
    for mask in w.far_masks:
        gu.send(mask)
    for mask in w.masks[1:]:
        qkv.relay(mask)
        out.relay(mask)
    down.own_near()

    @pl.when(crossing)
    def _():
        cross.wait_recv()

    @pl.when(jnp.logical_not(crossing))
    def _():
        stay.wait()

    def normed(source, gain):
        @pl.loop(0, rows // step)
        def _(t):
            at = pl.ds(pl.multiple_of(t * step, step), step)
            values = source[at, :].astype(f32)
            scale = lax.rsqrt(jnp.mean(values * values, axis=-1, keepdims=True) + norm_eps)
            pair[at, :] = (values * scale * gain).astype(bf16)

    normed(resid, gains[0:1, :])
    upper = pair.at[rows:, :]
    first_pair = wire.start(pair.at[:rows, :], upper, w.along_stream(1))
    for copy in owns:
        copy.wait()
    qkv.close()
    out.close()
    quarter = 2 * rows // 4
    width = out_full.shape[1]

    def qkv_of(lo, hi):
        @pl.loop(lo, hi)
        def _(t):
            at = pl.ds(pl.multiple_of(t * quarter, quarter), quarter)
            left = pair[at, :]
            for p in range(3):
                columns = slice(p * width, (p + 1) * width)
                value = jnp.dot(left, qkv_full[:, columns], preferred_element_type=f32)
                qkv_rows[at, columns] = value.astype(bf16)

    qkv_of(0, 2)
    first_pair.wait_recv()
    qkv_of(2, 4)
    mixing = {}

    def rows_of(position):
        return pl.ds(pl.multiple_of(position * quarter, quarter), quarter)

    for mask in (3, 1, 2):
        mixing[mask] = wire.start(
            qkv_rows.at[rows_of(flip(w.position, mask)), :],
            qkv_mixed.at[w.position],
            w.with_position(mask),
        )
    own_quarter = local.start(qkv_rows.at[rows_of(w.position), :], qkv_mixed.at[w.position])
    for mask in w.both_masks:
        gu.send(mask)
    stores = [
        local.start(pair, out_one),
        local.start(qkv_full, out_qkv),
        local.start(out_full, out_out),
        local.start(resid, out_resid),
    ]
    gu_own, down_own = gu.own(local), down.own(local)
    for mask in w.far_masks:
        gu.relay(mask)
    own_quarter.wait()
    for mask in (2, 1, 3):
        mixing[mask].wait_recv()

    fold_held, spread_held = fold[...], spread[...]

    @pl.loop(0, quarter // step)
    def _(t):
        at = pl.ds(pl.multiple_of(t * step, step), step)
        attention_forward_rows(at, qkv_mixed, fold_held, spread_held, probs, mixed_quarter)

    returning = {}
    for mask in (3, 1, 2):
        returning[mask] = wire.start(
            mixed_quarter.at[flip(w.position, mask)],
            mixed.at[rows_of(w.position), :],
            w.with_position(mask),
        )
    own_back = local.start(mixed_quarter.at[w.position], mixed.at[rows_of(w.position), :])
    gu.send(2)
    for mask in w.masks:
        down.send(mask)

    @pl.when(crossing)
    def _():
        cross_grad.start()

    stores += [local.start(qkv_mixed, out_qkv_mixed), local.start(probs, out_probs)]
    for mask in w.both_masks:
        gu.relay(mask)
    own_back.wait()
    for mask in (2, 1, 3):
        returning[mask].wait_recv()
    stores.append(local.start(mixed, out_mixed))
    stores[0].wait()

    @pl.loop(2, 4)
    def _(t):
        at = pl.ds(pl.multiple_of(t * quarter, quarter), quarter)
        to = pl.ds(pl.multiple_of(t * quarter - rows, quarter), quarter)
        away[to, :] = dot_columns(mixed[at, :], out_full[...]).astype(bf16)

    part = wire.start(away, got, w.along_stream(1))

    @pl.loop(0, 2)
    def _(t):
        at = pl.ds(pl.multiple_of(t * quarter, quarter), quarter)
        total[at, :] = dot_columns(mixed[at, :], out_full[...])

    part.wait_recv()
    wire.sent(first_pair)
    gain = gains[1:2, :]

    @pl.loop(0, rows // step)
    def _(t):
        at = pl.ds(pl.multiple_of(t * step, step), step)
        values = resid[at, :].astype(f32) + total[at, :] + got[at, :].astype(f32)
        total[at, :] = values
        scale = lax.rsqrt(jnp.mean(values * values, axis=-1, keepdims=True) + norm_eps)
        pair[at, :] = (values * scale * gain).astype(bf16)

    second_pair = wire.start(pair.at[:rows, :], upper, w.along_stream(1))
    stores.append(local.start(total, out_mid))
    gu.relay(2)
    for mask in w.masks[:-1]:
        down.relay(mask)

    @pl.when(crossing)
    def _():
        cross_grad.wait_recv()

    @pl.when(jnp.logical_not(crossing))
    def _():
        stay_grad.wait()

    grad_copy = wire.start(grad_pair.at[:rows, :], grad_pair.at[rows:, :], w.along_stream(1))
    for mask in w.masks[-1:]:
        down.relay(mask)
    second_pair.wait_recv()
    stores.append(local.start(pair, out_two))
    grad_copy.wait_recv()
    stores.append(local.start(grad_pair, out_grad))
    gu.close()
    down.close()
    for copy in stores[1:]:
        copy.wait()
    for copy in (store_ctx, gu_own, down_own):
        copy.wait()

    @pl.when(crossing)
    def _():
        cross.wait_send()
        cross_grad.wait_send()

    wire.finish()


def front(
    n, context, ctx_weight, inputs, grad_rows, gains,
    qkv_weight, out_weight, gu_weight, down_weight,
):
    rows, depth = inputs.shape
    count = ctx_weight.shape[0] // 4
    wide_q, wide_o = qkv_weight.shape[2], out_weight.shape[2]
    fold, spread = fold_matrices(wide_o)
    quarter = rows // 2
    half = rows // 2
    pairs = len(PAIRS)
    scratch = [
        pltpu.VMEM((n, count, depth // n), bf16),
        pltpu.VMEM((rows, count), bf16),
        pltpu.VMEM((rows, depth), f32),
        pltpu.VMEM((half, depth), bf16),
        pltpu.VMEM((half, depth), bf16),
        pltpu.VMEM((half, depth), bf16),
        pltpu.VMEM((rows, depth), bf16),
        pltpu.VMEM((rows, depth), bf16),
        pltpu.VMEM((rows, depth), bf16),
        pltpu.VMEM((2 * rows, depth), bf16),
        pltpu.VMEM((depth, wide_q), bf16),
        pltpu.VMEM((depth, wide_o), bf16),
        pltpu.VMEM((2 * rows, wide_q), bf16),
        pltpu.VMEM((4, quarter, wide_q), bf16),
        pltpu.VMEM((pairs, quarter, LANES), f32),
        pltpu.VMEM((4, quarter, wide_o), bf16),
        pltpu.VMEM((2 * rows, wide_o), bf16),
        pltpu.VMEM((rows, depth), bf16),
        pltpu.VMEM((rows, depth), bf16),
        pltpu.VMEM((2 * rows, depth), bf16),
        pltpu.SemaphoreType.DMA((24 + 10 * n,)),
        pltpu.SemaphoreType.DMA((24 + 10 * n,)),
        pltpu.SemaphoreType.DMA((24,)),
    ]
    shape = jax.ShapeDtypeStruct
    return pl.pallas_call(
        functools.partial(front_body, n),
        in_specs=[ANY, ANY, VMEM, ANY, VMEM, VMEM, VMEM, ANY, ANY, ANY, ANY],
        out_specs=[ANY] * 13,
        out_shape=[
            shape((depth, wide_q), bf16),
            shape((depth, wide_o), bf16),
            shape((depth, gu_weight.shape[2]), bf16),
            shape((depth, down_weight.shape[2]), bf16),
            shape((n, count, depth // n), bf16),
            shape((rows, depth), bf16),
            shape((rows, depth), f32),
            shape((2 * rows, depth), bf16),
            shape((2 * rows, depth), bf16),
            shape((2 * rows, depth), bf16),
            shape((4, quarter, wide_q), bf16),
            shape((pairs, quarter, LANES), f32),
            shape((2 * rows, wide_o), bf16),
        ],
        scratch_shapes=scratch,
        compiler_params=pltpu.CompilerParams(
            collective_id=3, has_side_effects=True, vmem_limit_bytes=62 << 20
        ),
        name="front",
    )(
        context, ctx_weight, inputs, grad_rows, gains, fold, spread,
        qkv_weight, out_weight, gu_weight, down_weight,
    )


def shards(
    inputs,
    context,
    cotangent,
    live_frames,
    ctx_weight,
    norm_gains,
    qkv_weight,
    out_weight,
    gate_up_weight,
    down_weight,
):
    n = lax.axis_size("frames")
    stream_index = lax.axis_index("stream")
    frame_index = lax.axis_index("frames")
    half_index = stream_index % 2
    place = (frame_index // 2) % 2
    position = (stream_index // 2) * 2 + place
    frame_count = inputs.shape[0]
    width_model = inputs.shape[2]
    offsets = lax.broadcasted_iota(jnp.int32, (frame_count,), 0)
    valid_mask = (offsets % SLOT < jnp.repeat(live_frames, SLOT)).astype(f32)[:, None]
    gain_one = norm_gains[0]
    gain_two = norm_gains[1]

    grad_rows = (cotangent[:, 0] * valid_mask).astype(bf16)
    (
        qkv_full,
        out_full,
        gate_up_full,
        down_full,
        ctx_pieces,
        resid_in,
        resid_mid,
        paired_one,
        paired_two,
        paired_grad_ffn,
        qkv_mixed,
        probs,
        mixed,
    ) = front(
        n,
        context,
        ctx_weight,
        inputs[:, 0],
        grad_rows,
        norm_gains,
        qkv_weight[0],
        out_weight[0],
        gate_up_weight[0],
        down_weight[0],
    )
    ctx_full = ctx_pieces.transpose(1, 0, 2).reshape(-1, width_model)
    near = frame_index % 2

    def paired(mine):
        return jnp.concatenate([mine, swap_stream(mine, 1)], axis=0)

    def own_sum(partial_value):
        return partial_value[:frame_count] + swap_stream(
            partial_value[frame_count:].astype(bf16), 1
        ).astype(f32)

    def rows_times(left, right):
        return jnp.dot(left, right, preferred_element_type=f32)

    def rows_back(left, right):
        return lax.dot_general(left, right, (((1,), (1,)), ((), ())), preferred_element_type=f32)

    def returned(value):
        _, quarter, width = value.shape
        out = jnp.zeros((4, quarter, width), value.dtype)
        own = lax.dynamic_index_in_dim(value, position, 0, keepdims=False)
        out = lax.dynamic_update_index_in_dim(out, own, position, 0)
        for mask in (2, 1, 3):
            there = position ^ mask
            got = peer(lax.dynamic_index_in_dim(value, there, 0, keepdims=False), mask)
            out = lax.dynamic_update_index_in_dim(out, got, there, 0)
        return out.reshape(4 * quarter, width)

    scale_two = norm_scale(resid_mid)
    gate_up = rows_times(paired_two, gate_up_full)
    ffn_half = down_full.shape[1]
    gate_part = gate_up[:, :ffn_half]
    up_part = gate_up[:, ffn_half:]
    sigmoid_gate = jax.nn.sigmoid(gate_part)
    activated = gate_part * sigmoid_gate
    hidden = (activated * up_part).astype(bf16)

    grad_res = paired_grad_ffn[:frame_count]
    sum_down = scattered(halves(paired_grad_ffn, near), hidden, frame_index, place)
    grad_hidden = rows_times(paired_grad_ffn, down_full)
    grad_gate = grad_hidden * up_part * (sigmoid_gate * (1.0 + gate_part * (1.0 - sigmoid_gate)))
    grad_up = grad_hidden * activated
    grad_gu_low = jnp.concatenate([grad_gate, grad_up], axis=-1).astype(bf16)
    grad_normed_two = own_sum(rows_back(grad_gu_low, gate_up_full))
    sum_gate_up = scattered(halves(paired_two, near), grad_gu_low, frame_index, place)
    back_two, grad_gain_two = norm_back(resid_mid, scale_two, gain_two, grad_normed_two)
    grad_mid = grad_res.astype(f32) + back_two
    paired_grad_attn = paired(grad_mid.astype(bf16))
    grad_mixed = rows_times(paired_grad_attn, out_full).astype(bf16)
    grad_qkv_mixed = attention_backward(qkv_mixed, probs, exchange_rows(grad_mixed, position))
    grad_qkv_low = returned(grad_qkv_mixed)
    def parts(left, right):
        away, stay = halves(left, near)
        block = width_model // n
        return [
            dot_rows(part, right).astype(bf16).reshape(n // 2, block, right.shape[1])
            for part in (away, stay)
        ]

    part_away = rows_back(grad_qkv_low[frame_count:], qkv_full).astype(bf16)
    part_stay = rows_back(grad_qkv_low[:frame_count], qkv_full)
    result_rows = (resid_mid + own_sum(rows_back(hidden, down_full))).astype(bf16)
    sum_qkv, sum_out, grad_home, result, sum_context, ctx_total = tail(
        n,
        part_away,
        part_stay,
        resid_in,
        grad_mid,
        norm_gains,
        grad_gain_two[None],
        result_rows,
        *parts(paired_one, grad_qkv_low),
        *parts(paired_grad_attn, mixed),
        context,
        ctx_full,
    )
    result = result.astype(f32) * valid_mask
    ctx_total = ctx_total.T
    sum_ctx = ctx_total[: ctx_weight.shape[0]]
    sum_gains = ctx_total[ctx_weight.shape[0] : ctx_weight.shape[0] + 2]

    return (
        result[:, None],
        grad_home[:, None],
        sum_context,
        sum_ctx,
        sum_gains,
        sum_qkv[None],
        sum_out[None],
        sum_gate_up[None],
        sum_down[None],
    )


def solution(mesh):
    placed = (
        P("frames", "stream", None),
        P("frames", None),
        P("frames", "stream", None),
        P("frames"),
        P(None, "frames"),
        P(),
        P("stream", None, "frames", None),
        P("stream", None, "frames", None),
        P("stream", None, "frames", None),
        P("stream", None, "frames", None),
    )
    return jax.shard_map(
        shards,
        mesh=mesh,
        in_specs=placed,
        out_specs=(
            P("frames", "stream", None),
            P("frames", "stream", None),
            P("frames", "stream"),
            P(None, ("stream", "frames")),
            P(None, ("stream", "frames")),
            P("stream", None, "frames", None),
            P("stream", None, "frames", None),
            P("stream", None, "frames", None),
            P("stream", None, "frames", None),
        ),
        check_vma=False,
    )
```

```python
import functools
import math

import jax
import jax.numpy as jnp
from jax import lax
from jax.experimental import pallas as pl
from jax.experimental.pallas import tpu as pltpu
from jax.sharding import PartitionSpec as P

HD = 64
SLOT = 128
LANES = 128
norm_eps = 1e-05
f32 = jnp.float32
bf16 = jnp.bfloat16

PAIRS = [(q, k) for q in range(4) for k in range(q + 1)]


ANY = pl.BlockSpec(memory_space=pl.ANY)
VMEM = pl.BlockSpec(memory_space=pltpu.VMEM)
EXTRA = 32


def flip(value, mask):
    bit = 1
    while bit <= mask:
        if mask & bit:
            value = value + bit - 2 * bit * ((value // bit) % 2)
        bit *= 2
    return value


class Where:
    def __init__(self, n):
        self.n = n
        self.stream = lax.axis_index("stream")
        self.frame = lax.axis_index("frames")
        self.core = self.stream % 2
        self.place = (self.frame // 2) % 2
        self.position = (self.stream // 2) * 2 + self.place
        self.near = self.frame % 2
        self.at = self.frame // 2
        self.far_masks = [m for m in range(2, n, 2) if not m & 2]
        self.both_masks = [m for m in range(2, n, 2) if m & 2 and m > 2]
        self.masks = self.far_masks + self.both_masks + [2]

    def along_stream(self, mask):
        return (flip(self.stream, mask), self.frame)

    def along_frames(self, mask):
        return (self.stream, flip(self.frame, mask))

    def with_position(self, mask):
        return (flip(self.stream, mask & 2), flip(self.frame, 2 * (mask & 1)))

    def across(self):
        return (flip(self.stream, 1), flip(self.frame, 2))


class Wire:
    def __init__(self, send, recv):
        self.send, self.recv, self.count, self.started = send, recv, 0, []

    def make(self, src, dst, device, index=None):
        k = self.count if index is None else index
        if index is None:
            self.count += 1
        return pltpu.make_async_remote_copy(
            src_ref=src,
            dst_ref=dst,
            send_sem=self.send.at[k],
            recv_sem=self.recv.at[k],
            device_id=device,
            device_id_type=pl.DeviceIdType.MESH,
        )

    def start(self, src, dst, device):
        copy = self.make(src, dst, device)
        copy.start()
        self.started.append(copy)
        return copy

    def sent(self, copy):
        self.started = [c for c in self.started if c is not copy]
        copy.wait_send()

    def finish(self):
        for copy in self.started:
            copy.wait_send()


class Local:
    def __init__(self, sems):
        self.sems, self.count = sems, 0

    def start(self, src, dst):
        copy = pltpu.make_async_copy(src, dst, self.sems.at[self.count])
        self.count += 1
        copy.start()
        return copy


def greet(devices):
    barrier = pltpu.get_barrier_semaphore()
    for device in devices:
        pl.semaphore_signal(
            barrier, inc=1, device_id=device, device_id_type=pl.DeviceIdType.MESH
        )
    pl.semaphore_wait(barrier, len(devices))


def dot_rows(left, right):
    return lax.dot_general(left, right, (((0,), (0,)), ((), ())), preferred_element_type=f32)


def dot_columns(left, right):
    return lax.dot_general(left, right, (((1,), (1,)), ((), ())), preferred_element_type=f32)


class Reduction:
    def __init__(self, w, wire, send, keep, arrived, sums, landed, out):
        self.w, self.wire = w, wire
        self.send, self.keep, self.arrived = send, keep, arrived
        self.sums, self.landed, self.out = sums, landed, out
        self.first, self.second = {}, {}
        self.order = w.masks + [0]

    def begin(self, mask):
        block = flip(self.w.at, mask // 2)
        self.first[mask] = self.wire.start(
            self.send.at[block], self.arrived.at[block], self.w.along_frames(1)
        )

    def forward(self, mask):
        block = flip(self.w.at, mask // 2)
        self.first[mask].wait_recv()
        self.wire.sent(self.first[mask])
        total = self.keep[block].astype(f32) + self.arrived[block].astype(f32)
        self.sums[block] = total.astype(bf16)
        if mask:
            self.second[mask] = self.wire.start(
                self.sums.at[block], self.landed.at[mask // 2 - 1], self.w.along_frames(mask)
            )

    def land(self):
        for copy in self.second.values():
            copy.wait_recv()

    def close(self):
        own, other = self.sums[self.w.at].astype(f32), None
        for mask in self.w.masks:
            self.second[mask].wait_recv()
            got = self.landed[mask // 2 - 1].astype(f32)
            if mask & 2:
                other = got if other is None else other + got
            else:
                own = own + got
        self.out[self.w.place] = own
        self.out[1 - self.w.place] = other


def tail_body(
    n, part_send, part_own, resid, mid, gains, gain_two, result_rows,
    gq_send, gq_keep, go_send, go_keep, context, ctx_full,
    out_q, out_o, out_grad, out_result, out_context, out_ctx,
    part_got, low, home, partner_half, half_sum, far_half, whole, kept_q, kept_o,
    arrived_q, arrived_o, sums_q, sums_o, landed_q, landed_o,
    context_held, ctx_held, term, term_got, term_sum, term_landed, gain_sum,
    send_sem, recv_sem, local_sem,
):
    w = Where(n)
    wire, local = Wire(send_sem, recv_sem), Local(local_sem)
    rows, depth = resid.shape
    crossing = w.core != w.place
    load_q = local.start(gq_keep, kept_q)
    load_o = local.start(go_keep, kept_o)
    load_context = local.start(context, context_held)
    load_ctx = local.start(ctx_full, ctx_held)
    greet(
        [w.along_stream(1), w.along_stream(2), w.along_frames(1)]
        + [w.along_frames(m) for m in w.masks]
        + [w.across()]
    )
    part = wire.start(part_send, part_got, w.along_stream(1))
    red_o = Reduction(w, wire, go_send, kept_o, arrived_o, sums_o, landed_o, out_o)
    red_q = Reduction(w, wire, gq_send, kept_q, arrived_q, sums_q, landed_q, out_q)
    for mask in red_o.order:
        red_o.begin(mask)
    for mask in red_q.order:
        red_q.begin(mask)

    part.wait_recv()
    gain = gains[0:1, :]
    gain_sum[...] = jnp.zeros_like(gain_sum)
    step = 64

    @pl.loop(0, rows // step)
    def _(t):
        at = pl.ds(pl.multiple_of(t * step, step), step)
        grad = part_own[at, :].astype(f32) + part_got[at, :].astype(f32)
        values = resid[at, :].astype(f32)
        scale = lax.rsqrt(jnp.mean(values * values, axis=-1, keepdims=True) + norm_eps)
        weighted = grad * gain
        inner = jnp.mean(weighted * values, axis=-1, keepdims=True)
        back = scale * weighted - values * (scale * scale * scale * inner)
        low[at, :] = (mid[at, :] + back).astype(bf16)
        gain_sum[...] += jnp.sum(grad * values * scale, axis=0, keepdims=True)

    row = lax.broadcasted_iota(jnp.int32, (EXTRA, depth), 0)
    low[rows:, :] = jnp.where(
        row == 0, gain_sum[...], jnp.where(row == 1, gain_two[...], 0.0)
    ).astype(bf16)

    cross = wire.make(low, home, w.across())
    cross_result = wire.make(result_rows, out_result, w.across())

    @pl.when(crossing)
    def _():
        cross.start()

    load_o.wait()
    load_q.wait()
    for mask in red_o.order:
        red_o.forward(mask)

    @pl.when(crossing)
    def _():
        cross_result.start()
        cross.wait_recv()

    stay = pltpu.make_async_copy(low, home, local.sems.at[4])
    stay_result = pltpu.make_async_copy(result_rows, out_result, local.sems.at[5])

    @pl.when(jnp.logical_not(crossing))
    def _():
        stay.start()
        stay_result.start()
        stay.wait()

    half = (rows + EXTRA) // 2
    mine = pl.ds(pl.multiple_of(w.core * half, 16), half)
    theirs = pl.ds(pl.multiple_of((1 - w.core) * half, 16), half)
    first = wire.start(home.at[theirs, :], partner_half, w.along_stream(1))
    out_grad[...] = home[:rows, :].astype(f32)
    first.wait_recv()
    half_sum[...] = (home[mine, :].astype(f32) + partner_half[...].astype(f32)).astype(bf16)
    second = wire.start(half_sum, far_half, w.along_stream(2))
    red_q.forward(red_q.order[0])
    red_q.forward(red_q.order[1])
    second.wait_recv()
    whole[mine, :] = (half_sum[...].astype(f32) + far_half[...].astype(f32)).astype(bf16)
    third = wire.start(whole.at[mine, :], whole.at[mine, :], w.along_stream(1))
    load_context.wait()
    third.wait_recv()

    share = depth // 4
    columns = pl.ds(pl.multiple_of(w.stream * share, LANES), share)
    block = share // n
    wide = context_held.shape[1]
    pieces = 2
    grad_share = whole[:rows, columns]
    firsts, seconds = [], []
    row = lax.broadcasted_iota(jnp.int32, (EXTRA, LANES), 0)
    select = (row == lax.broadcasted_iota(jnp.int32, (EXTRA, LANES), 1)).astype(bf16)
    edges = [wide * p // pieces for p in range(pieces)] + [wide + LANES]
    for p in range(pieces):
        lo, hi = edges[p], edges[p + 1]
        for at in range(lo, min(hi, wide), 1024):
            to = min(at + 1024, wide)
            value = dot_rows(grad_share, context_held[:, at:to]).astype(bf16)
            for k in range(n):
                term[k // 2, k % 2, :, at:to] = value[k * block : (k + 1) * block]
        if hi > wide:
            value = dot_rows(whole[rows:, columns], select).astype(bf16)
            for k in range(n):
                term[k // 2, k % 2, :, wide:hi] = value[k * block : (k + 1) * block]
        firsts.append(
            wire.start(
                term.at[:, 1 - w.near, :, lo:hi], term_got.at[:, :, lo:hi], w.along_frames(1)
            )
        )
    for mask in red_q.order[2:]:
        red_q.forward(mask)
    load_ctx.wait()

    def context_rows(t):
        at = pl.ds(pl.multiple_of(t * LANES, LANES), LANES)
        out_context[at, :] = dot_columns(whole[at, :], ctx_held[...])

    @pl.loop(0, rows // LANES)
    def _(t):
        context_rows(t)

    for p in range(pieces):
        lo, hi = edges[p], edges[p + 1]
        firsts[p].wait_recv()
        for mask in w.masks + [0]:
            to = flip(w.at, mask // 2)
            total = term[to, w.near, :, lo:hi].astype(f32) + term_got[to, :, lo:hi].astype(f32)
            term_sum[to, :, lo:hi] = total.astype(bf16)
            if mask:
                seconds.append(
                    wire.start(
                        term_sum.at[to, :, lo:hi],
                        term_landed.at[mask // 2, :, lo:hi],
                        w.along_frames(mask),
                    )
                )
    red_o.close()
    red_q.close()

    @pl.when(crossing)
    def _():
        cross_result.wait_recv()
        cross.wait_send()
        cross_result.wait_send()

    @pl.when(jnp.logical_not(crossing))
    def _():
        stay_result.wait()

    for copy in seconds:
        copy.wait_recv()
    total = term_sum[w.at].astype(f32)
    for mask in w.masks:
        total = total + term_landed[mask // 2].astype(f32)
    out_ctx[...] = total
    wire.finish()


def tail(
    n, part_send, part_own, resid, mid, gains, gain_two, result_rows,
    gq_send, gq_keep, go_send, go_keep, context, ctx_full,
):
    rows, depth = resid.shape
    halfn, block, wide_q = gq_send.shape
    wide_o = go_send.shape[2]
    share = depth // 4 // n
    wide = context.shape[1] + LANES
    half = (rows + EXTRA) // 2
    count = 64 + 2 * n
    scratch = [
        pltpu.VMEM((rows, depth), bf16),
        pltpu.VMEM((rows + EXTRA, depth), bf16),
        pltpu.VMEM((rows + EXTRA, depth), bf16),
        pltpu.VMEM((half, depth), bf16),
        pltpu.VMEM((half, depth), bf16),
        pltpu.VMEM((half, depth), bf16),
        pltpu.VMEM((rows + EXTRA, depth), bf16),
        pltpu.VMEM((halfn, block, wide_q), bf16),
        pltpu.VMEM((halfn, block, wide_o), bf16),
        pltpu.VMEM((halfn, block, wide_q), bf16),
        pltpu.VMEM((halfn, block, wide_o), bf16),
        pltpu.VMEM((halfn, block, wide_q), bf16),
        pltpu.VMEM((halfn, block, wide_o), bf16),
        pltpu.VMEM((halfn, block, wide_q), bf16),
        pltpu.VMEM((halfn, block, wide_o), bf16),
        pltpu.VMEM(context.shape, bf16),
        pltpu.VMEM(ctx_full.shape, bf16),
        pltpu.VMEM((halfn, 2, share, wide), bf16),
        pltpu.VMEM((halfn, share, wide), bf16),
        pltpu.VMEM((halfn, share, wide), bf16),
        pltpu.VMEM((halfn, share, wide), bf16),
        pltpu.VMEM((1, depth), f32),
        pltpu.SemaphoreType.DMA((count,)),
        pltpu.SemaphoreType.DMA((count,)),
        pltpu.SemaphoreType.DMA((6,)),
    ]
    return pl.pallas_call(
        functools.partial(tail_body, n),
        in_specs=[ANY, VMEM, VMEM, VMEM, VMEM, VMEM, VMEM, ANY, ANY, ANY, ANY, ANY, ANY],
        out_specs=[VMEM, VMEM, VMEM, VMEM, VMEM, VMEM],
        out_shape=[
            jax.ShapeDtypeStruct((2, block, wide_q), f32),
            jax.ShapeDtypeStruct((2, block, wide_o), f32),
            jax.ShapeDtypeStruct((rows, depth), f32),
            jax.ShapeDtypeStruct((rows, depth), bf16),
            jax.ShapeDtypeStruct((rows, ctx_full.shape[0]), f32),
            jax.ShapeDtypeStruct((share, wide), f32),
        ],
        scratch_shapes=scratch,
        compiler_params=pltpu.CompilerParams(
            collective_id=5, has_side_effects=True, vmem_limit_bytes=60 << 20
        ),
        name="tail",
    )(
        part_send, part_own, resid, mid, gains, gain_two, result_rows,
        gq_send, gq_keep, go_send, go_keep, context, ctx_full,
    )


def ending_body(
    n, resid, mid, gains, gain_two, result_rows, valid,
    pair_one, pair_grad, mixed_rows, grad_qkv_rows, qkv_weight, context, ctx_pieces,
    out_q, out_o, landed_q, landed_o, out_grad, out_result, out_context, out_ctx,
    one, grad_two, mixed, grad_qkv, qkv_full, left_away, left_stay, part_send, part_own,
    part_got, low, home, partner_half, half_sum, far_half, whole, result_home,
    send_q, send_o, kept_q, kept_o, arrived_q, arrived_o,
    context_held, ctx_held, term, term_got, term_sum, term_landed, gain_sum,
    send_sem, recv_sem, local_sem,
):
    w = Where(n)
    wire, local = Wire(send_sem, recv_sem), Local(local_sem)
    rows, depth = resid.shape
    piece = depth // n
    crossing = w.core != w.place
    load_grad = local.start(pair_grad, grad_two)
    load_mixed = local.start(mixed_rows, mixed)
    load_qkv = local.start(grad_qkv_rows, grad_qkv)
    load_weight = local.start(qkv_weight, qkv_full)
    load_one = local.start(pair_one, one)
    load_context = local.start(context, context_held)
    load_ctx = [
        local.start(ctx_pieces.at[k], ctx_held.at[:, k * piece : (k + 1) * piece])
        for k in range(n)
    ]
    greet(
        [w.along_stream(1), w.along_stream(2), w.along_frames(1)]
        + [w.along_frames(m) for m in w.masks]
        + [w.across()]
    )
    cross_result = wire.make(result_rows, result_home, w.across())
    stay_result = pltpu.make_async_copy(result_rows, result_home, local.sems.at[30])
    stay = pltpu.make_async_copy(low, home, local.sems.at[31])

    @pl.when(crossing)
    def _():
        cross_result.start()

    @pl.when(jnp.logical_not(crossing))
    def _():
        stay_result.start()

    def split(source, which, into):
        for b in range(n // 2):
            at = pl.ds(pl.multiple_of((2 * b + which) * piece, piece), piece)
            into[:, b * piece : (b + 1) * piece] = source[:, at]

    def product(left, right, into):
        wide = right.shape[1]
        for lo in range(0, wide, 512):
            value = dot_rows(left[...], right[:, lo : lo + 512]).astype(bf16)
            for b in range(n // 2):
                into[b, :, lo : lo + 512] = value[b * piece : (b + 1) * piece]

    def partial(t):
        at = pl.ds(pl.multiple_of(t * 256, 256), 256)
        return dot_columns(grad_qkv[at, :], qkv_full[...])

    load_grad.wait()
    split(grad_two, 1 - w.near, left_away)
    load_mixed.wait()
    product(left_away, mixed, send_o)
    red_o = Reduction(w, wire, send_o, kept_o, arrived_o, send_o, landed_o, out_o)
    for mask in red_o.order:
        red_o.begin(mask)
    load_qkv.wait()
    load_weight.wait()

    @pl.loop(0, rows // 256)
    def _(t):
        to = pl.ds(pl.multiple_of(t * 256, 256), 256)
        part_send[to, :] = partial(rows // 256 + t).astype(bf16)

    part = wire.start(part_send, part_got, w.along_stream(1))
    load_one.wait()
    split(one, 1 - w.near, left_away)
    product(left_away, grad_qkv, send_q)
    red_q = Reduction(w, wire, send_q, kept_q, arrived_q, send_q, landed_q, out_q)
    for mask in red_q.order:
        red_q.begin(mask)

    @pl.loop(0, rows // 256)
    def _(t):
        to = pl.ds(pl.multiple_of(t * 256, 256), 256)
        part_own[to, :] = partial(t)

    part.wait_recv()
    gain = gains[0:1, :]
    gain_sum[...] = jnp.zeros_like(gain_sum)
    step = 64

    @pl.loop(0, rows // step)
    def _(t):
        at = pl.ds(pl.multiple_of(t * step, step), step)
        grad = part_own[at, :].astype(f32) + part_got[at, :].astype(f32)
        values = resid[at, :].astype(f32)
        scale = lax.rsqrt(jnp.mean(values * values, axis=-1, keepdims=True) + norm_eps)
        weighted = grad * gain
        inner = jnp.mean(weighted * values, axis=-1, keepdims=True)
        back = scale * weighted - values * (scale * scale * scale * inner)
        low[at, :] = (mid[at, :] + back).astype(bf16)
        gain_sum[...] += jnp.sum(grad * values * scale, axis=0, keepdims=True)

    row = lax.broadcasted_iota(jnp.int32, (EXTRA, depth), 0)
    low[rows:, :] = jnp.where(
        row == 0, gain_sum[...], jnp.where(row == 1, gain_two[...], 0.0)
    ).astype(bf16)

    cross = wire.make(low, home, w.across())

    @pl.when(crossing)
    def _():
        cross.start()

    split(grad_two, w.near, left_stay)
    product(left_stay, mixed, kept_o)
    for mask in red_o.order:
        red_o.forward(mask)

    @pl.when(crossing)
    def _():
        cross_result.wait_recv()

    @pl.when(jnp.logical_not(crossing))
    def _():
        stay.start()
        stay_result.wait()

    split(one, w.near, left_stay)
    product(left_stay, grad_qkv, kept_q)
    out_result[:, 0, :] = result_home[...].astype(f32) * valid[...]

    @pl.when(crossing)
    def _():
        cross.wait_recv()

    @pl.when(jnp.logical_not(crossing))
    def _():
        stay.wait()

    half = (rows + EXTRA) // 2
    mine = pl.ds(pl.multiple_of(w.core * half, 16), half)
    theirs = pl.ds(pl.multiple_of((1 - w.core) * half, 16), half)
    first = wire.start(home.at[theirs, :], partner_half, w.along_stream(1))
    out_grad[:, 0, :] = home[:rows, :].astype(f32)
    first.wait_recv()
    half_sum[...] = (home[mine, :].astype(f32) + partner_half[...].astype(f32)).astype(bf16)
    second = wire.start(half_sum, far_half, w.along_stream(2))
    red_q.forward(red_q.order[0])
    red_q.forward(red_q.order[1])
    second.wait_recv()
    whole[mine, :] = (half_sum[...].astype(f32) + far_half[...].astype(f32)).astype(bf16)
    third = wire.start(whole.at[mine, :], whole.at[mine, :], w.along_stream(1))
    load_context.wait()
    third.wait_recv()

    share = depth // 4
    columns = pl.ds(pl.multiple_of(w.stream * share, LANES), share)
    block = share // n
    wide = context_held.shape[1]
    pieces = 4
    grad_share = whole[:rows, columns]
    firsts, seconds = [], []
    row = lax.broadcasted_iota(jnp.int32, (EXTRA, LANES), 0)
    select = (row == lax.broadcasted_iota(jnp.int32, (EXTRA, LANES), 1)).astype(bf16)
    edges = [wide * p // pieces for p in range(pieces)] + [wide + LANES]
    for p in range(pieces):
        lo, hi = edges[p], edges[p + 1]
        for at in range(lo, min(hi, wide), 1024):
            to = min(at + 1024, wide)
            value = dot_rows(grad_share, context_held[:, at:to]).astype(bf16)
            for k in range(n):
                term[k // 2, k % 2, :, at:to] = value[k * block : (k + 1) * block]
        if hi > wide:
            value = dot_rows(whole[rows:, columns], select).astype(bf16)
            for k in range(n):
                term[k // 2, k % 2, :, wide:hi] = value[k * block : (k + 1) * block]
        firsts.append(
            wire.start(
                term.at[:, 1 - w.near, :, lo:hi], term_got.at[:, :, lo:hi], w.along_frames(1)
            )
        )
    for mask in red_q.order[2:]:
        red_q.forward(mask)
    for copy in load_ctx:
        copy.wait()

    def context_rows(t):
        at = pl.ds(pl.multiple_of(t * LANES, LANES), LANES)
        out_context[at, :] = dot_columns(whole[at, :], ctx_held[...])

    @pl.loop(0, rows // LANES)
    def _(t):
        context_rows(t)

    for p in range(pieces):
        lo, hi = edges[p], edges[p + 1]
        firsts[p].wait_recv()
        for mask in w.masks + [0]:
            to = flip(w.at, mask // 2)
            total = term[to, w.near, :, lo:hi].astype(f32) + term_got[to, :, lo:hi].astype(f32)
            term_sum[to, :, lo:hi] = total.astype(bf16)
            if mask:
                seconds.append(
                    wire.start(
                        term_sum.at[to, :, lo:hi],
                        term_landed.at[mask // 2, :, lo:hi],
                        w.along_frames(mask),
                    )
                )
    red_o.land()
    red_q.land()
    kept = [local.start(send_o.at[w.at], out_o), local.start(send_q.at[w.at], out_q)]

    @pl.when(crossing)
    def _():
        cross.wait_send()
        cross_result.wait_send()

    for copy in seconds:
        copy.wait_recv()
    total = term_sum[w.at].astype(f32)
    for mask in w.masks:
        total = total + term_landed[mask // 2].astype(f32)
    out_ctx[...] = total
    for copy in kept:
        copy.wait()
    wire.finish()


def ending_scratch(n, rows, depth, context_shape, count, wide_q, wide_o):
    halfn, block, share = n // 2, depth // n, depth // 4 // n
    wide = context_shape[1] + LANES
    half = (rows + EXTRA) // 2
    both = 2 * rows
    shapes = [
        ((both, depth), bf16),
        ((both, depth), bf16),
        ((both, wide_o), bf16),
        ((both, wide_q), bf16),
        ((depth, wide_q), bf16),
        ((both, depth // 2), bf16),
        ((both, depth // 2), bf16),
        ((rows, depth), bf16),
        ((rows, depth), f32),
        ((rows, depth), bf16),
        ((rows + EXTRA, depth), bf16),
        ((rows + EXTRA, depth), bf16),
        ((half, depth), bf16),
        ((half, depth), bf16),
        ((half, depth), bf16),
        ((rows + EXTRA, depth), bf16),
        ((rows, depth), bf16),
        ((halfn, block, wide_q), bf16),
        ((halfn, block, wide_o), bf16),
        ((halfn, block, wide_q), bf16),
        ((halfn, block, wide_o), bf16),
        ((halfn, block, wide_q), bf16),
        ((halfn, block, wide_o), bf16),
        (context_shape, bf16),
        ((count, depth), bf16),
        ((halfn, 2, share, wide), bf16),
        ((halfn, share, wide), bf16),
        ((halfn, share, wide), bf16),
        ((halfn, share, wide), bf16),
        ((1, depth), f32),
    ]
    others = [((rows, depth), f32)] * 4 + [((rows, depth), bf16)] * 2 + [((rows, count), f32)]
    return shapes, sum(math.prod(dims) * jnp.dtype(kind).itemsize for dims, kind in shapes + others)


def ending(
    n, resid, mid, gains, gain_two, result_rows, valid,
    pair_one, pair_grad, mixed, grad_qkv, qkv_full, context, ctx_pieces,
):
    rows, depth = resid.shape
    halfn, block = n // 2, depth // n
    wide_q, wide_o = qkv_full.shape[1], mixed.shape[1]
    count = ctx_pieces.shape[1]
    shapes, _ = ending_scratch(n, rows, depth, context.shape, count, wide_q, wide_o)
    sems = 64 + 2 * n
    shape = jax.ShapeDtypeStruct
    return pl.pallas_call(
        functools.partial(ending_body, n),
        in_specs=[VMEM] * 6 + [ANY] * 7,
        out_specs=[ANY] * 4 + [VMEM] * 4,
        out_shape=[
            shape((block, wide_q), bf16),
            shape((block, wide_o), bf16),
            shape((halfn - 1, block, wide_q), bf16),
            shape((halfn - 1, block, wide_o), bf16),
            shape((rows, 1, depth), f32),
            shape((rows, 1, depth), f32),
            shape((rows, count), f32),
            shape((depth // 4 // n, context.shape[1] + LANES), f32),
        ],
        scratch_shapes=[pltpu.VMEM(dims, kind) for dims, kind in shapes]
        + [
            pltpu.SemaphoreType.DMA((sems,)),
            pltpu.SemaphoreType.DMA((sems,)),
            pltpu.SemaphoreType.DMA((32,)),
        ],
        compiler_params=pltpu.CompilerParams(
            collective_id=6, has_side_effects=True, vmem_limit_bytes=67_000_000
        ),
        name="ending",
    )(
        resid, mid, gains, gain_two, result_rows, valid,
        pair_one, pair_grad, mixed, grad_qkv, qkv_full, context, ctx_pieces,
    )


def swap_frames(value, mask):
    n = lax.axis_size("frames")
    return lax.ppermute(value, "frames", [(d, d ^ mask) for d in range(n)])


def swap_stream(value, mask):
    n = lax.axis_size("stream")
    return lax.ppermute(value, "stream", [(d, d ^ mask) for d in range(n)])


def joint(value, target):
    streams, n = lax.axis_size("stream"), lax.axis_size("frames")
    pairs = []
    for s in range(streams):
        for f in range(n):
            to_s, to_f = target(s, f)
            pairs.append((s * n + f, to_s * n + to_f))
    return lax.ppermute(value, ("stream", "frames"), pairs)


def transposed(value):
    def target(s, f):
        core, place = s % 2, (f // 2) % 2
        return s - core + place, f - 2 * place + 2 * core

    return joint(value, target)


def peer(value, mask):
    return joint(value, lambda s, f: (s ^ (mask & 2), f ^ (2 * (mask & 1))))


def norm_scale(values):
    return lax.rsqrt(jnp.mean(values * values, axis=-1, keepdims=True) + norm_eps)


def norm_back(values, scale, gain, grad):
    weighted = grad * gain
    inner_mean = jnp.mean(weighted * values, axis=-1, keepdims=True)
    grad_values = scale * weighted - values * (scale * scale * scale) * inner_mean
    grad_gain = jnp.sum(grad * values * scale, axis=0)
    return (grad_values, grad_gain)


def exchange_rows(qkv, position):
    rows, width = qkv.shape
    quarter = rows // 4
    parts = qkv.reshape(4, quarter, width)
    out = jnp.zeros((4, quarter, width), qkv.dtype)
    own = lax.dynamic_index_in_dim(parts, position, 0, keepdims=False)
    out = lax.dynamic_update_index_in_dim(out, own, position, 0)
    for mask in (2, 1, 3):
        there = position ^ mask
        got = peer(lax.dynamic_index_in_dim(parts, there, 0, keepdims=False), mask)
        out = lax.dynamic_update_index_in_dim(out, got, there, 0)
    return out


def heads_sum(product, fold):
    high = product.astype(bf16)
    low = (product - high.astype(f32)).astype(bf16)
    return jnp.dot(high, fold, preferred_element_type=f32) + jnp.dot(
        low, fold, preferred_element_type=f32
    )


def attention_forward_rows(at, qkv_ref, fold, spread, probs_ref, out_ref):
    width = out_ref.shape[2]
    for q in range(4):
        query = qkv_ref[q, at, :width].astype(f32)
        scores = []
        for k in range(q + 1):
            key = qkv_ref[k, at, width : 2 * width].astype(f32)
            scores.append(heads_sum(query * key, fold) * HD ** (-0.5))
        top = functools.reduce(jnp.maximum, scores)
        expo = [jnp.exp(s - top) for s in scores]
        total = functools.reduce(jnp.add, expo)
        mixed = None
        for k in range(q + 1):
            prob = expo[k] / total
            probs_ref[PAIRS.index((q, k)), at, :] = prob
            wide = jnp.dot(prob.astype(bf16), spread, preferred_element_type=f32)
            term = wide * qkv_ref[k, at, 2 * width :].astype(f32)
            mixed = term if mixed is None else mixed + term
        out_ref[q, at, :] = mixed.astype(bf16)


def attention_backward_rows(at, qkv_ref, probs_ref, grad_ref, fold, spread, out_ref):
    width = grad_ref.shape[2]
    grad_keys, grad_values = [None] * 4, [None] * 4
    for q in range(4):
        grad = grad_ref[q, at, :].astype(f32)
        query = qkv_ref[q, at, :width].astype(f32)
        probs = [probs_ref[PAIRS.index((q, k)), at, :] for k in range(q + 1)]
        grad_probs = [
            heads_sum(grad * qkv_ref[k, at, 2 * width :].astype(f32), fold) for k in range(q + 1)
        ]
        total = functools.reduce(jnp.add, [p * g for p, g in zip(probs, grad_probs)])
        grad_query = None
        for k in range(q + 1):
            wide = jnp.dot(probs[k].astype(bf16), spread, preferred_element_type=f32)
            term = wide * grad
            grad_values[k] = term if grad_values[k] is None else grad_values[k] + term
            grad_score = (probs[k] * (grad_probs[k] - total)).astype(bf16)
            wide = jnp.dot(grad_score, spread, preferred_element_type=f32)
            term = wide * qkv_ref[k, at, width : 2 * width].astype(f32)
            grad_query = term if grad_query is None else grad_query + term
            term = wide * query
            grad_keys[k] = term if grad_keys[k] is None else grad_keys[k] + term
        out_ref[q, at, :width] = (grad_query * HD ** (-0.5)).astype(bf16)
    for k in range(4):
        out_ref[k, at, width : 2 * width] = (grad_keys[k] * HD ** (-0.5)).astype(bf16)
        out_ref[k, at, 2 * width :] = grad_values[k].astype(bf16)


def attention_backward_body(qkv_ref, probs_ref, grad_ref, fold_ref, spread_ref, out_ref):
    everything = slice(None)
    attention_backward_rows(
        everything, qkv_ref, probs_ref, grad_ref, fold_ref[...], spread_ref[...], out_ref
    )


def fold_matrices(width):
    feature = lax.broadcasted_iota(jnp.int32, (width, LANES), 0) // HD
    head = lax.broadcasted_iota(jnp.int32, (width, LANES), 1)
    fold = (feature == head).astype(bf16)
    return fold, fold.T


def attention_backward(qkv, probs, grad, step=64):
    _, rows, triple = qkv.shape
    width = triple // 3
    fold, spread = fold_matrices(width)
    return pl.pallas_call(
        attention_backward_body,
        grid=(rows // step,),
        in_specs=[
            pl.BlockSpec((4, step, triple), lambda r: (0, r, 0)),
            pl.BlockSpec((len(PAIRS), step, LANES), lambda r: (0, r, 0)),
            pl.BlockSpec((4, step, width), lambda r: (0, r, 0)),
            pl.BlockSpec((width, LANES), lambda r: (0, 0)),
            pl.BlockSpec((LANES, width), lambda r: (0, 0)),
        ],
        out_specs=pl.BlockSpec((4, step, triple), lambda r: (0, r, 0)),
        out_shape=jax.ShapeDtypeStruct((4, rows, triple), bf16),
        name="attention_backward",
    )(qkv, probs, grad, fold, spread)


def after(value, *others):
    return lax.optimization_barrier((value,) + others)[0]


def taken(weights, place):
    own = [lax.dynamic_index_in_dim(w, place, 0, keepdims=False) for w in weights]
    other = [lax.dynamic_index_in_dim(w, 1 - place, 0, keepdims=False) for w in weights]
    if len(weights) == 1:
        return own[0], other[0]
    return jnp.concatenate(own, axis=1), jnp.concatenate(other, axis=1)


def placed_rows(pieces, frame_index, start, width):
    n = lax.axis_size("frames")
    block = pieces[0].shape[0]
    full = jnp.zeros((n, block, width), pieces[0].dtype)
    for mask in range(n):
        part = pieces[mask][:, start : start + width]
        full = lax.dynamic_update_index_in_dim(full, part, frame_index ^ mask, 0)
    return full.reshape(n * block, width)


def halves(left, near):
    n = lax.axis_size("frames")
    rows, depth = left.shape
    block = depth // n
    even = jnp.concatenate([left[:, k * block : (k + 1) * block] for k in range(0, n, 2)], axis=1)
    odd = jnp.concatenate([left[:, k * block : (k + 1) * block] for k in range(1, n, 2)], axis=1)
    return jnp.where(near == 0, odd, even), jnp.where(near == 0, even, odd)


def scattered(left_halves, right, frame_index, place):
    n = lax.axis_size("frames")

    def product(part):
        return lax.dot_general(
            part, right, (((0,), (0,)), ((), ())), preferred_element_type=f32
        ).astype(bf16)

    arrived = swap_frames(product(left_halves[0]), 1)
    half_sum = (product(left_halves[1]).astype(f32) + arrived.astype(f32)).astype(bf16)
    half_sum = half_sum.reshape(n // 2, -1, right.shape[1])
    at = frame_index // 2
    own = lax.dynamic_index_in_dim(half_sum, at, 0, keepdims=False).astype(f32)
    other = None
    for mask in range(2, n, 2):
        got = swap_frames(
            lax.dynamic_index_in_dim(half_sum, at ^ (mask // 2), 0, keepdims=False), mask
        ).astype(f32)
        if mask & 2:
            other = got if other is None else other + got
        else:
            own = own + got
    first = jnp.where(place == 0, own, other)
    second = jnp.where(place == 0, other, own)
    return jnp.stack([first, second], axis=0)


class Spread:
    def __init__(self, w, wire, weight, full):
        self.w, self.wire, self.weight, self.full = w, wire, weight, full
        self.block = full.shape[0] // w.n
        self.far, self.near = {}, {}

    def rows(self, frame):
        return self.full.at[pl.ds(pl.multiple_of(frame * self.block, self.block), self.block), :]

    def own(self, local):
        return local.start(self.weight.at[self.w.place], self.rows(self.w.frame))

    def own_near(self):
        w = self.w
        self.near[0] = self.wire.start(
            self.weight.at[w.place], self.rows(w.frame), w.along_frames(1)
        )

    def send(self, mask):
        w = self.w
        which = 1 - w.place if mask & 2 else w.place
        self.far[mask] = self.wire.start(
            self.weight.at[which], self.rows(w.frame), w.along_frames(mask)
        )

    def relay(self, mask):
        self.far[mask].wait_recv()
        rows = self.rows(flip(self.w.frame, mask))
        self.near[mask] = self.wire.start(rows, rows, self.w.along_frames(1))

    def close(self):
        for copy in self.near.values():
            copy.wait_recv()


def front_body(
    n, context, ctx_weight, inputs, grad_rows, gains, fold, spread,
    qkv_weight, out_weight, gu_weight, down_weight,
    out_qkv, out_out, out_gu, out_down, out_ctx, out_resid, out_mid, out_one, out_two, out_grad,
    out_qkv_mixed, out_probs, out_mixed,
    ctx_held, context_held, total, partner_half, half_sum, far_half, whole, home, resid, pair,
    qkv_full, out_full, qkv_rows, qkv_mixed, probs, mixed_quarter, mixed, away, got, grad_pair,
    send_sem, recv_sem, local_sem,
):
    w = Where(n)
    wire, local = Wire(send_sem, recv_sem), Local(local_sem)
    rows, depth = inputs.shape
    count = ctx_weight.shape[0] // 4
    piece = depth // n
    crossing = w.core != w.place
    half = rows // 2
    step = 64
    quarter_of_context = pl.ds(pl.multiple_of(w.stream * count, LANES), count)
    load_context = local.start(context.at[:, quarter_of_context], context_held)
    load_ctx = local.start(ctx_weight.at[quarter_of_context, :], ctx_held.at[w.frame])
    qkv = Spread(w, wire, qkv_weight, qkv_full)
    out = Spread(w, wire, out_weight, out_full)
    gu = Spread(w, wire, gu_weight, out_gu)
    down = Spread(w, wire, down_weight, out_down)
    owns = [qkv.own(local), out.own(local)]
    greet(
        [w.along_stream(1), w.along_stream(2), w.along_frames(1)]
        + [w.along_frames(m) for m in w.masks]
        + [w.across(), w.with_position(3)]
    )

    load_ctx.wait()
    held, near = [0], {}

    def ctx_near(o):
        at = flip(w.frame, o)
        near[o] = wire.start(ctx_held.at[at], ctx_held.at[at], w.along_frames(1))

    ready = []
    for bit in reversed(range(1, n.bit_length() - 1)):
        copies = []
        for o in held:
            at = flip(w.frame, o)
            copies.append(
                (o, wire.start(ctx_held.at[at], ctx_held.at[at], w.along_frames(1 << bit)))
            )
        if bit == n.bit_length() - 2:
            ctx_near(0)
            qkv.own_near()
            out.own_near()
        if bit == 1:
            for mask in w.masks:
                qkv.send(mask)
                out.send(mask)
        for o, copy in copies:
            copy.wait_recv()
            ctx_near(o ^ (1 << bit))
            held.append(o ^ (1 << bit))

    load_context.wait()

    def project(o):
        at = flip(w.frame, o)
        columns = pl.ds(pl.multiple_of(at * piece, piece), piece)
        value = jnp.dot(context_held[...], ctx_held[at], preferred_element_type=f32)
        total[:, columns] = value

    if piece % LANES == 0:
        for o in held:
            project(o)
        for o in held:
            near[o].wait_recv()
            project(o ^ 1)
    else:
        for o in held:
            near[o].wait_recv()
        total[...] = jnp.zeros_like(total)

        @pl.loop(0, n)
        def _(at):
            line = lax.broadcasted_iota(jnp.int32, (piece, depth), 0)
            column = lax.broadcasted_iota(jnp.int32, (piece, depth), 1)
            select = (column == line + at * piece).astype(bf16)
            laid = jnp.dot(ctx_held[at], select, preferred_element_type=f32).astype(bf16)

            @pl.loop(0, rows // LANES)
            def _(t):
                here = pl.ds(pl.multiple_of(t * LANES, LANES), LANES)
                total[here, :] += jnp.dot(
                    context_held[here, :], laid, preferred_element_type=f32
                )

    store_ctx = local.start(ctx_held, out_ctx)

    mine = pl.ds(pl.multiple_of(w.core * half, 16), half)
    theirs = pl.ds(pl.multiple_of((1 - w.core) * half, 16), half)
    whole[theirs, :] = total[theirs, :].astype(bf16)
    first = wire.start(whole.at[theirs, :], partner_half, w.along_stream(1))
    first.wait_recv()
    half_sum[...] = (total[mine, :] + partner_half[...].astype(f32)).astype(bf16)
    second = wire.start(half_sum, far_half, w.along_stream(2))
    for mask in w.masks[:1]:
        qkv.relay(mask)
        out.relay(mask)
    second.wait_recv()
    home[mine, :] = (half_sum[...].astype(f32) + far_half[...].astype(f32)).astype(bf16)
    third = wire.start(home.at[mine, :], home.at[mine, :], w.along_stream(1))
    third.wait_recv()
    wire.sent(third)

    @pl.loop(0, rows // step)
    def _(t):
        at = pl.ds(pl.multiple_of(t * step, step), step)
        home[at, :] = (home[at, :].astype(f32) + inputs[at, :].astype(f32)).astype(bf16)

    cross = wire.make(home, resid, w.across())
    cross_grad = wire.make(grad_rows, grad_pair.at[:rows, :], w.across())
    stay = pltpu.make_async_copy(home, resid, local_sem.at[22])
    stay_grad = pltpu.make_async_copy(grad_rows, grad_pair.at[:rows, :], local_sem.at[23])

    @pl.when(crossing)
    def _():
        cross.start()

    @pl.when(jnp.logical_not(crossing))
    def _():
        stay.start()
        stay_grad.start()

    gu.own_near()
    for mask in w.far_masks:
        gu.send(mask)
    for mask in w.masks[1:]:
        qkv.relay(mask)
        out.relay(mask)
    down.own_near()

    @pl.when(crossing)
    def _():
        cross.wait_recv()

    @pl.when(jnp.logical_not(crossing))
    def _():
        stay.wait()

    def normed(source, gain):
        @pl.loop(0, rows // step)
        def _(t):
            at = pl.ds(pl.multiple_of(t * step, step), step)
            values = source[at, :].astype(f32)
            scale = lax.rsqrt(jnp.mean(values * values, axis=-1, keepdims=True) + norm_eps)
            pair[at, :] = (values * scale * gain).astype(bf16)

    normed(resid, gains[0:1, :])
    upper = pair.at[rows:, :]
    first_pair = wire.start(pair.at[:rows, :], upper, w.along_stream(1))
    for copy in owns:
        copy.wait()
    qkv.close()
    out.close()
    quarter = 2 * rows // 4
    width = out_full.shape[1]

    def qkv_of(lo, hi):
        @pl.loop(lo, hi)
        def _(t):
            at = pl.ds(pl.multiple_of(t * quarter, quarter), quarter)
            left = pair[at, :]
            for p in range(3):
                columns = slice(p * width, (p + 1) * width)
                value = jnp.dot(left, qkv_full[:, columns], preferred_element_type=f32)
                qkv_rows[at, columns] = value.astype(bf16)

    qkv_of(0, 2)
    first_pair.wait_recv()
    qkv_of(2, 4)
    mixing = {}

    def rows_of(position):
        return pl.ds(pl.multiple_of(position * quarter, quarter), quarter)

    for mask in (3, 1, 2):
        mixing[mask] = wire.start(
            qkv_rows.at[rows_of(flip(w.position, mask)), :],
            qkv_mixed.at[w.position],
            w.with_position(mask),
        )
    own_quarter = local.start(qkv_rows.at[rows_of(w.position), :], qkv_mixed.at[w.position])
    for mask in w.both_masks:
        gu.send(mask)
    stores = [
        local.start(pair, out_one),
        local.start(qkv_full, out_qkv),
        local.start(out_full, out_out),
        local.start(resid, out_resid),
    ]
    gu_own, down_own = gu.own(local), down.own(local)
    for mask in w.far_masks:
        gu.relay(mask)
    own_quarter.wait()
    for mask in (2, 1, 3):
        mixing[mask].wait_recv()

    fold_held, spread_held = fold[...], spread[...]

    @pl.loop(0, quarter // step)
    def _(t):
        at = pl.ds(pl.multiple_of(t * step, step), step)
        attention_forward_rows(at, qkv_mixed, fold_held, spread_held, probs, mixed_quarter)

    returning = {}
    for mask in (3, 1, 2):
        returning[mask] = wire.start(
            mixed_quarter.at[flip(w.position, mask)],
            mixed.at[rows_of(w.position), :],
            w.with_position(mask),
        )
    own_back = local.start(mixed_quarter.at[w.position], mixed.at[rows_of(w.position), :])
    gu.send(2)
    for mask in w.masks:
        down.send(mask)

    @pl.when(crossing)
    def _():
        cross_grad.start()

    stores += [local.start(qkv_mixed, out_qkv_mixed), local.start(probs, out_probs)]
    for mask in w.both_masks:
        gu.relay(mask)
    own_back.wait()
    for mask in (2, 1, 3):
        returning[mask].wait_recv()
    stores.append(local.start(mixed, out_mixed))
    stores[0].wait()

    @pl.loop(2, 4)
    def _(t):
        at = pl.ds(pl.multiple_of(t * quarter, quarter), quarter)
        to = pl.ds(pl.multiple_of(t * quarter - rows, quarter), quarter)
        away[to, :] = dot_columns(mixed[at, :], out_full[...]).astype(bf16)

    part = wire.start(away, got, w.along_stream(1))

    @pl.loop(0, 2)
    def _(t):
        at = pl.ds(pl.multiple_of(t * quarter, quarter), quarter)
        total[at, :] = dot_columns(mixed[at, :], out_full[...])

    part.wait_recv()
    wire.sent(first_pair)
    gain = gains[1:2, :]

    @pl.loop(0, rows // step)
    def _(t):
        at = pl.ds(pl.multiple_of(t * step, step), step)
        values = resid[at, :].astype(f32) + total[at, :] + got[at, :].astype(f32)
        total[at, :] = values
        scale = lax.rsqrt(jnp.mean(values * values, axis=-1, keepdims=True) + norm_eps)
        pair[at, :] = (values * scale * gain).astype(bf16)

    second_pair = wire.start(pair.at[:rows, :], upper, w.along_stream(1))
    stores.append(local.start(total, out_mid))
    gu.relay(2)
    for mask in w.masks[:-1]:
        down.relay(mask)

    @pl.when(crossing)
    def _():
        cross_grad.wait_recv()

    @pl.when(jnp.logical_not(crossing))
    def _():
        stay_grad.wait()

    grad_copy = wire.start(grad_pair.at[:rows, :], grad_pair.at[rows:, :], w.along_stream(1))
    for mask in w.masks[-1:]:
        down.relay(mask)
    second_pair.wait_recv()
    stores.append(local.start(pair, out_two))
    grad_copy.wait_recv()
    stores.append(local.start(grad_pair, out_grad))
    gu.close()
    down.close()
    for copy in stores[1:]:
        copy.wait()
    for copy in (store_ctx, gu_own, down_own):
        copy.wait()

    @pl.when(crossing)
    def _():
        cross.wait_send()
        cross_grad.wait_send()

    wire.finish()


def front(
    n, context, ctx_weight, inputs, grad_rows, gains,
    qkv_weight, out_weight, gu_weight, down_weight,
):
    rows, depth = inputs.shape
    count = ctx_weight.shape[0] // 4
    wide_q, wide_o = qkv_weight.shape[2], out_weight.shape[2]
    fold, spread = fold_matrices(wide_o)
    quarter = rows // 2
    half = rows // 2
    pairs = len(PAIRS)
    scratch = [
        pltpu.VMEM((n, count, depth // n), bf16),
        pltpu.VMEM((rows, count), bf16),
        pltpu.VMEM((rows, depth), f32),
        pltpu.VMEM((half, depth), bf16),
        pltpu.VMEM((half, depth), bf16),
        pltpu.VMEM((half, depth), bf16),
        pltpu.VMEM((rows, depth), bf16),
        pltpu.VMEM((rows, depth), bf16),
        pltpu.VMEM((rows, depth), bf16),
        pltpu.VMEM((2 * rows, depth), bf16),
        pltpu.VMEM((depth, wide_q), bf16),
        pltpu.VMEM((depth, wide_o), bf16),
        pltpu.VMEM((2 * rows, wide_q), bf16),
        pltpu.VMEM((4, quarter, wide_q), bf16),
        pltpu.VMEM((pairs, quarter, LANES), f32),
        pltpu.VMEM((4, quarter, wide_o), bf16),
        pltpu.VMEM((2 * rows, wide_o), bf16),
        pltpu.VMEM((rows, depth), bf16),
        pltpu.VMEM((rows, depth), bf16),
        pltpu.VMEM((2 * rows, depth), bf16),
        pltpu.SemaphoreType.DMA((24 + 10 * n,)),
        pltpu.SemaphoreType.DMA((24 + 10 * n,)),
        pltpu.SemaphoreType.DMA((24,)),
    ]
    shape = jax.ShapeDtypeStruct
    return pl.pallas_call(
        functools.partial(front_body, n),
        in_specs=[ANY, ANY, VMEM, ANY, VMEM, VMEM, VMEM, ANY, ANY, ANY, ANY],
        out_specs=[ANY] * 13,
        out_shape=[
            shape((depth, wide_q), bf16),
            shape((depth, wide_o), bf16),
            shape((depth, gu_weight.shape[2]), bf16),
            shape((depth, down_weight.shape[2]), bf16),
            shape((n, count, depth // n), bf16),
            shape((rows, depth), bf16),
            shape((rows, depth), f32),
            shape((2 * rows, depth), bf16),
            shape((2 * rows, depth), bf16),
            shape((2 * rows, depth), bf16),
            shape((4, quarter, wide_q), bf16),
            shape((pairs, quarter, LANES), f32),
            shape((2 * rows, wide_o), bf16),
        ],
        scratch_shapes=scratch,
        compiler_params=pltpu.CompilerParams(
            collective_id=3, has_side_effects=True, vmem_limit_bytes=62 << 20
        ),
        name="front",
    )(
        context, ctx_weight, inputs, grad_rows, gains, fold, spread,
        qkv_weight, out_weight, gu_weight, down_weight,
    )


def back_body(
    n, pair_two, pair_grad, resid, gu_weight, down_weight, out_weight, qkv_held, probs_held,
    gains, fold, spread,
    out_down, out_gu, landed_down, landed_gu, out_mid, out_gain, out_pair, out_rows, out_qkv,
    two, grad, gu_full, down_full, out_full, two_away, two_stay, grad_away, grad_stay,
    hidden, grad_gu, send_down, send_gu, got_down, got_gu,
    values_mid, away, got, grad_rows, grad_mixed, qkv_mixed, probs, grad_qkv,
    send_sem, recv_sem, tile_send, tile_recv, local_sem,
):
    w = Where(n)
    wire, local = Wire(send_sem, recv_sem), Local(local_sem)
    tiled = Wire(tile_send, tile_recv)
    rows, depth = out_mid.shape
    both = 2 * rows
    piece = depth // n
    halfn = n // 2
    wide = down_full.shape[1]
    tile = 2 * LANES
    whole_tiles = wide // tile
    tiles = whole_tiles + (1 if wide % tile else 0)
    step = 64
    loads = [
        local.start(pair_two, two),
        local.start(gu_weight, gu_full),
        local.start(pair_grad, grad),
        local.start(down_weight, down_full),
    ]
    late = [
        local.start(resid, values_mid),
        local.start(out_weight, out_full),
        local.start(qkv_held, qkv_mixed),
        local.start(probs_held, probs),
    ]
    greet(
        [w.along_stream(1), w.along_stream(2), w.along_frames(1)]
        + [w.along_frames(m) for m in w.masks]
        + [w.with_position(3)]
    )
    neighbour = w.along_frames(1)

    def split(source, into_away, into_stay):
        for b in range(halfn):
            for ref, which in ((into_away, 1 - w.near), (into_stay, w.near)):
                at = pl.ds(pl.multiple_of((2 * b + which) * piece, piece), piece)
                ref[:, b * piece : (b + 1) * piece] = source[:, at]

    loads[0].wait()
    split(two, two_away, two_stay)
    loads[2].wait()
    split(grad, grad_away, grad_stay)
    loads[1].wait()
    loads[3].wait()

    def columns(start, size):
        return pl.ds(pl.multiple_of(start, LANES), size)

    def moves(t, size):
        lo = t * tile
        for j, (ref, into, start) in enumerate(
            ((send_down, got_down, lo), (send_gu, got_gu, lo), (send_gu, got_gu, wide + lo))
        ):
            at = columns(start, size)
            yield tiled.make(ref.at[:, :, at], into.at[:, :, at], neighbour, 3 * t + j)

    def forward(t, size):
        lo = t * tile
        here = columns(lo, size)
        there = columns(wide + lo, size)

        @pl.loop(0, both // 256)
        def _(r):
            at = pl.ds(pl.multiple_of(r * 256, 256), 256)
            left = two[at, :]
            gate = jnp.dot(left, gu_full[:, here], preferred_element_type=f32)
            up = jnp.dot(left, gu_full[:, there], preferred_element_type=f32)
            back = jnp.dot(grad[at, :], down_full[:, here], preferred_element_type=f32)
            sigma = 1.0 / (1.0 + jnp.exp(-gate))
            active = gate * sigma
            hidden[at, here] = (active * up).astype(bf16)
            grad_gu[at, here] = (back * up * (sigma * (1.0 + gate * (1.0 - sigma)))).astype(bf16)
            grad_gu[at, there] = (back * active).astype(bf16)

        for ref, left, right, at in (
            (send_down, grad_away, hidden, here),
            (send_gu, two_away, grad_gu, here),
            (send_gu, two_away, grad_gu, there),
        ):
            value = dot_rows(left[...], right[:, at]).astype(bf16)
            for b in range(halfn):
                ref[b, :, at] = value[b * piece : (b + 1) * piece]
        for move in moves(t, size):
            move.start()

    rest = wide - whole_tiles * tile

    @pl.loop(0, whole_tiles)
    def _(t):
        forward(t, tile)

    if rest:
        forward(whole_tiles, rest)

    def landings(t, size):
        lo = t * tile
        for j, (ref, into, start) in enumerate(
            ((send_down, landed_down, lo), (send_gu, landed_gu, lo), (send_gu, landed_gu, wide + lo))
        ):
            at = columns(start, size)
            for k, mask in enumerate(w.masks):
                yield tiled.make(
                    ref.at[flip(w.at, mask // 2), :, at],
                    into.at[mask // 2 - 1, :, at],
                    w.along_frames(mask),
                    3 * tiles + (3 * t + j) * len(w.masks) + k,
                )

    def reduce(t, size):
        lo = t * tile
        here = columns(lo, size)
        there = columns(wide + lo, size)
        for move in moves(t, size):
            move.wait()
        for ref, into, left, right, at in (
            (send_down, got_down, grad_stay, hidden, here),
            (send_gu, got_gu, two_stay, grad_gu, here),
            (send_gu, got_gu, two_stay, grad_gu, there),
        ):
            value = dot_rows(left[...], right[:, at])
            for b in range(halfn):
                total = value[b * piece : (b + 1) * piece] + into[b, :, at].astype(f32)
                ref[b, :, at] = total.astype(bf16)
        for landing in landings(t, size):
            landing.start()

    def reduce_some(lo, hi):
        if hi - lo == 1:
            reduce(lo, tile)
        elif hi > lo:

            @pl.loop(lo, hi)
            def _(t):
                reduce(t, tile)

    def rows_of(position):
        quarter = both // 4
        return pl.ds(pl.multiple_of(position * quarter, quarter), quarter)

    def partial(left, right, t):
        at = pl.ds(pl.multiple_of(t * 256, 256), 256)
        return dot_columns(left[at, :], right[...])

    @pl.loop(0, rows // 256)
    def _(t):
        to = pl.ds(pl.multiple_of(t * 256, 256), 256)
        away[to, :] = partial(grad_gu, gu_full, rows // 256 + t).astype(bf16)

    first = wire.start(away, got, w.along_stream(1))

    @pl.loop(0, rows // 256)
    def _(t):
        to = pl.ds(pl.multiple_of(t * 256, 256), 256)
        out_mid[to, :] = partial(grad_gu, gu_full, t)

    cuts = [min(c, whole_tiles) for c in (1, 2, 3)]
    reduce_some(0, cuts[0])

    late[0].wait()
    first.wait_recv()
    gain = gains[1:2, :]
    out_gain[...] = jnp.zeros_like(out_gain)

    @pl.loop(0, rows // step)
    def _(t):
        at = pl.ds(pl.multiple_of(t * step, step), step)
        grad_normed = out_mid[at, :] + got[at, :].astype(f32)
        values = values_mid[at, :]
        scale = lax.rsqrt(jnp.mean(values * values, axis=-1, keepdims=True) + norm_eps)
        weighted = grad_normed * gain
        inner = jnp.mean(weighted * values, axis=-1, keepdims=True)
        total = grad[at, :].astype(f32) + scale * weighted
        total = total - values * (scale * scale * scale * inner)
        out_mid[at, :] = total
        two[at, :] = total.astype(bf16)
        out_gain[...] += jnp.sum(grad_normed * values * scale, axis=0, keepdims=True)

    second = wire.start(two.at[:rows, :], two.at[rows:, :], w.along_stream(1))
    late[1].wait()

    def back_rows(lo, hi):
        @pl.loop(lo, hi)
        def _(t):
            at = pl.ds(pl.multiple_of(t * 256, 256), 256)
            value = jnp.dot(two[at, :], out_full[...], preferred_element_type=f32)
            grad_rows[at, :] = value.astype(bf16)

    back_rows(0, rows // 256)
    second.wait_recv()
    back_rows(rows // 256, both // 256)
    mixing = {}
    for mask in (3, 1, 2):
        mixing[mask] = wire.start(
            grad_rows.at[rows_of(flip(w.position, mask)), :],
            grad_mixed.at[w.position],
            w.with_position(mask),
        )
    own = local.start(grad_rows.at[rows_of(w.position), :], grad_mixed.at[w.position])
    store_pair = local.start(two, out_pair)

    reduce_some(cuts[0], cuts[1])
    own.wait()
    late[2].wait()
    late[3].wait()
    for mask in (2, 1, 3):
        mixing[mask].wait_recv()
    fold_held, spread_held = fold[...], spread[...]

    @pl.loop(0, both // 4 // step)
    def _(t):
        at = pl.ds(pl.multiple_of(t * step, step), step)
        attention_backward_rows(
            at, qkv_mixed, probs, grad_mixed, fold_held, spread_held, grad_qkv
        )

    returning = {}
    for mask in (3, 1, 2):
        returning[mask] = wire.start(
            grad_qkv.at[flip(w.position, mask)],
            out_qkv.at[rows_of(w.position), :],
            w.with_position(mask),
        )
    own_back = local.start(grad_qkv.at[w.position], out_qkv.at[rows_of(w.position), :])
    reduce_some(cuts[1], cuts[2])

    wire.sent(first)

    @pl.loop(0, rows // 256)
    def _(t):
        to = pl.ds(pl.multiple_of(t * 256, 256), 256)
        away[to, :] = partial(hidden, down_full, rows // 256 + t).astype(bf16)

    third = wire.start(away, got, w.along_stream(1))

    @pl.loop(0, rows // 256)
    def _(t):
        to = pl.ds(pl.multiple_of(t * 256, 256), 256)
        values_mid[to, :] = values_mid[to, :] + partial(hidden, down_full, t)

    third.wait_recv()

    @pl.loop(0, rows // step)
    def _(t):
        at = pl.ds(pl.multiple_of(t * step, step), step)
        out_rows[at, :] = (values_mid[at, :] + got[at, :].astype(f32)).astype(bf16)

    reduce_some(cuts[2], whole_tiles)
    if rest:
        reduce(whole_tiles, rest)
    kept = [local.start(send_down.at[w.at], out_down), local.start(send_gu.at[w.at], out_gu)]
    own_back.wait()
    store_pair.wait()
    for mask in (2, 1, 3):
        returning[mask].wait_recv()
    for t in range(tiles):
        for landing in landings(t, tile if t < whole_tiles else rest):
            landing.wait()
    for copy in kept:
        copy.wait()
    wire.finish()


def back_scratch(n, rows, depth, wide, head_width):
    both, halfn, piece = 2 * rows, n // 2, depth // n
    pairs = len(PAIRS)
    quarter = both // 4
    shapes = [
        ((both, depth), bf16),
        ((both, depth), bf16),
        ((depth, 2 * wide), bf16),
        ((depth, wide), bf16),
        ((depth, head_width), bf16),
        ((both, depth // 2), bf16),
        ((both, depth // 2), bf16),
        ((both, depth // 2), bf16),
        ((both, depth // 2), bf16),
        ((both, wide), bf16),
        ((both, 2 * wide), bf16),
        ((halfn, piece, wide), bf16),
        ((halfn, piece, 2 * wide), bf16),
        ((halfn, piece, wide), bf16),
        ((halfn, piece, 2 * wide), bf16),
        ((rows, depth), f32),
        ((rows, depth), bf16),
        ((rows, depth), bf16),
        ((both, head_width), bf16),
        ((4, quarter, head_width), bf16),
        ((4, quarter, 3 * head_width), bf16),
        ((pairs, quarter, LANES), f32),
        ((4, quarter, 3 * head_width), bf16),
    ]
    outs = [((rows, depth), f32), ((rows, depth), bf16)]
    return shapes, sum(math.prod(dims) * jnp.dtype(kind).itemsize for dims, kind in shapes + outs)


def back(
    n, pair_two, pair_grad, resid, gu_full, down_full, out_full, qkv_mixed, probs, gains
):
    rows, depth = resid.shape
    wide, head_width = down_full.shape[1], out_full.shape[1]
    shapes, _ = back_scratch(n, rows, depth, wide, head_width)
    tiles = -(-wide // (2 * LANES))
    fold, spread = fold_matrices(head_width)
    shape = jax.ShapeDtypeStruct
    moves = 3 * tiles * (1 + n // 2 - 1)
    return pl.pallas_call(
        functools.partial(back_body, n),
        in_specs=[ANY] * 8 + [VMEM] * 3,
        out_specs=[ANY, ANY, ANY, ANY, VMEM, VMEM, ANY, VMEM, ANY],
        out_shape=[
            shape((depth // n, wide), bf16),
            shape((depth // n, 2 * wide), bf16),
            shape((n // 2 - 1, depth // n, wide), bf16),
            shape((n // 2 - 1, depth // n, 2 * wide), bf16),
            shape((rows, depth), f32),
            shape((1, depth), f32),
            shape((2 * rows, depth), bf16),
            shape((rows, depth), bf16),
            shape((2 * rows, 3 * head_width), bf16),
        ],
        scratch_shapes=[pltpu.VMEM(dims, kind) for dims, kind in shapes]
        + [
            pltpu.SemaphoreType.DMA((12,)),
            pltpu.SemaphoreType.DMA((12,)),
            pltpu.SemaphoreType.DMA((moves,)),
            pltpu.SemaphoreType.DMA((moves,)),
            pltpu.SemaphoreType.DMA((16,)),
        ],
        compiler_params=pltpu.CompilerParams(
            collective_id=4, has_side_effects=True, vmem_limit_bytes=67_000_000
        ),
        name="back",
    )(
        pair_two, pair_grad, resid, gu_full, down_full, out_full, qkv_mixed, probs,
        gains, fold, spread,
    )


def settled(own, landed, place):
    total, other = own.astype(f32), None
    for k in range(landed.shape[0]):
        value = landed[k].astype(f32)
        if (k + 1) & 1:
            other = value if other is None else other + value
        else:
            total = total + value
    return jnp.where(place == 0, jnp.stack([total, other]), jnp.stack([other, total]))


def shards(
    inputs,
    context,
    cotangent,
    live_frames,
    ctx_weight,
    norm_gains,
    qkv_weight,
    out_weight,
    gate_up_weight,
    down_weight,
):
    n = lax.axis_size("frames")
    stream_index = lax.axis_index("stream")
    frame_index = lax.axis_index("frames")
    half_index = stream_index % 2
    place = (frame_index // 2) % 2
    position = (stream_index // 2) * 2 + place
    frame_count = inputs.shape[0]
    width_model = inputs.shape[2]
    offsets = lax.broadcasted_iota(jnp.int32, (frame_count,), 0)
    valid_mask = (offsets % SLOT < jnp.repeat(live_frames, SLOT)).astype(f32)[:, None]
    gain_one = norm_gains[0]
    gain_two = norm_gains[1]

    grad_rows = (cotangent[:, 0] * valid_mask).astype(bf16)
    (
        qkv_full,
        out_full,
        gate_up_full,
        down_full,
        ctx_pieces,
        resid_in,
        resid_mid,
        paired_one,
        paired_two,
        paired_grad_ffn,
        qkv_mixed,
        probs,
        mixed,
    ) = front(
        n,
        context,
        ctx_weight,
        inputs[:, 0],
        grad_rows,
        norm_gains,
        qkv_weight[0],
        out_weight[0],
        gate_up_weight[0],
        down_weight[0],
    )
    near = frame_index % 2

    def paired(mine):
        return jnp.concatenate([mine, swap_stream(mine, 1)], axis=0)

    def own_sum(partial_value):
        return partial_value[:frame_count] + swap_stream(
            partial_value[frame_count:].astype(bf16), 1
        ).astype(f32)

    def rows_times(left, right):
        return jnp.dot(left, right, preferred_element_type=f32)

    def rows_back(left, right):
        return lax.dot_general(left, right, (((1,), (1,)), ((), ())), preferred_element_type=f32)

    def returned(value):
        _, quarter, width = value.shape
        out = jnp.zeros((4, quarter, width), value.dtype)
        own = lax.dynamic_index_in_dim(value, position, 0, keepdims=False)
        out = lax.dynamic_update_index_in_dim(out, own, position, 0)
        for mask in (2, 1, 3):
            there = position ^ mask
            got = peer(lax.dynamic_index_in_dim(value, there, 0, keepdims=False), mask)
            out = lax.dynamic_update_index_in_dim(out, got, there, 0)
        return out.reshape(4 * quarter, width)

    head_width = out_full.shape[1]
    _, needed = back_scratch(n, frame_count, width_model, down_full.shape[1], head_width)
    if needed <= 66_000_000 and (width_model // n) % LANES == 0:
        (
            own_down,
            own_gate_up,
            landed_down,
            landed_gate_up,
            grad_mid,
            grad_gain_two,
            paired_grad_attn,
            result_rows,
            grad_qkv_low,
        ) = back(
            n,
            paired_two,
            paired_grad_ffn,
            resid_mid,
            gate_up_full,
            down_full,
            out_full,
            qkv_mixed,
            probs,
            norm_gains,
        )
        sum_down = settled(own_down, landed_down, place)
        sum_gate_up = settled(own_gate_up, landed_gate_up, place)
    else:
        scale_two = norm_scale(resid_mid)
        gate_up = rows_times(paired_two, gate_up_full)
        ffn_half = down_full.shape[1]
        gate_part = gate_up[:, :ffn_half]
        up_part = gate_up[:, ffn_half:]
        sigmoid_gate = jax.nn.sigmoid(gate_part)
        activated = gate_part * sigmoid_gate
        hidden = (activated * up_part).astype(bf16)

        grad_res = paired_grad_ffn[:frame_count]
        sum_down = scattered(halves(paired_grad_ffn, near), hidden, frame_index, place)
        grad_hidden = rows_times(paired_grad_ffn, down_full)
        grad_gate = grad_hidden * up_part * (sigmoid_gate * (1.0 + gate_part * (1.0 - sigmoid_gate)))
        grad_up = grad_hidden * activated
        grad_gu_low = jnp.concatenate([grad_gate, grad_up], axis=-1).astype(bf16)
        grad_normed_two = own_sum(rows_back(grad_gu_low, gate_up_full))
        sum_gate_up = scattered(halves(paired_two, near), grad_gu_low, frame_index, place)
        back_two, grad_gain_two = norm_back(resid_mid, scale_two, gain_two, grad_normed_two)
        grad_mid = grad_res.astype(f32) + back_two
        paired_grad_attn = paired(grad_mid.astype(bf16))
        grad_mixed = rows_times(paired_grad_attn, out_full).astype(bf16)
        grad_qkv_mixed = attention_backward(qkv_mixed, probs, exchange_rows(grad_mixed, position))
        grad_qkv_low = returned(grad_qkv_mixed)
        result_rows = (resid_mid + own_sum(rows_back(hidden, down_full))).astype(bf16)
        grad_gain_two = grad_gain_two[None]

    wide_q = qkv_full.shape[1]
    count = ctx_pieces.shape[1]
    _, needed = ending_scratch(
        n, frame_count, width_model, context.shape, count, wide_q, head_width
    )
    if needed <= 66_000_000 and (width_model // n) % LANES == 0:
        own_qkv, own_out, landed_qkv, landed_out, grad_home, result, sum_context, ctx_total = ending(
            n,
            resid_in,
            grad_mid,
            norm_gains,
            grad_gain_two,
            result_rows,
            valid_mask,
            paired_one,
            paired_grad_attn,
            mixed,
            grad_qkv_low,
            qkv_full,
            context,
            ctx_pieces,
        )
        sum_qkv = settled(own_qkv, landed_qkv, place)
        sum_out = settled(own_out, landed_out, place)
    else:

        def parts(left, right):
            away, stay = halves(left, near)
            block = width_model // n
            return [
                dot_rows(part, right).astype(bf16).reshape(n // 2, block, right.shape[1])
                for part in (away, stay)
            ]

        part_away = rows_back(grad_qkv_low[frame_count:], qkv_full).astype(bf16)
        part_stay = rows_back(grad_qkv_low[:frame_count], qkv_full)
        sum_qkv, sum_out, grad_home, result, sum_context, ctx_total = tail(
            n,
            part_away,
            part_stay,
            resid_in,
            grad_mid,
            norm_gains,
            grad_gain_two,
            result_rows,
            *parts(paired_one, grad_qkv_low),
            *parts(paired_grad_attn, mixed),
            context,
            ctx_pieces.transpose(1, 0, 2).reshape(-1, width_model),
        )
        result = (result.astype(f32) * valid_mask)[:, None]
        grad_home = grad_home[:, None]
    ctx_total = ctx_total.T
    sum_ctx = ctx_total[: ctx_weight.shape[0]]
    sum_gains = ctx_total[ctx_weight.shape[0] : ctx_weight.shape[0] + 2]

    return (
        result,
        grad_home,
        sum_context,
        sum_ctx,
        sum_gains,
        sum_qkv[None],
        sum_out[None],
        sum_gate_up[None],
        sum_down[None],
    )


def solution(mesh):
    placed = (
        P("frames", "stream", None),
        P("frames", None),
        P("frames", "stream", None),
        P("frames"),
        P(None, "frames"),
        P(),
        P("stream", None, "frames", None),
        P("stream", None, "frames", None),
        P("stream", None, "frames", None),
        P("stream", None, "frames", None),
    )
    return jax.shard_map(
        shards,
        mesh=mesh,
        in_specs=placed,
        out_specs=(
            P("frames", "stream", None),
            P("frames", "stream", None),
            P("frames", "stream"),
            P(None, ("stream", "frames")),
            P(None, ("stream", "frames")),
            P("stream", None, "frames", None),
            P("stream", None, "frames", None),
            P("stream", None, "frames", None),
            P("stream", None, "frames", None),
        ),
        check_vma=False,
    )
```

```python
import functools
import math

import jax
import jax.numpy as jnp
from jax import lax
from jax.experimental import pallas as pl
from jax.experimental.pallas import tpu as pltpu
from jax.sharding import PartitionSpec as P

HD = 64
SLOT = 128
LANES = 128
norm_eps = 1e-05
f32 = jnp.float32
bf16 = jnp.bfloat16

PAIRS = [(q, k) for q in range(4) for k in range(q + 1)]


ANY = pl.BlockSpec(memory_space=pl.ANY)
VMEM = pl.BlockSpec(memory_space=pltpu.VMEM)
EXTRA = 32


def flip(value, mask):
    bit = 1
    while bit <= mask:
        if mask & bit:
            value = value + bit - 2 * bit * ((value // bit) % 2)
        bit *= 2
    return value


class Where:
    def __init__(self, n):
        self.n = n
        self.stream = lax.axis_index("stream")
        self.frame = lax.axis_index("frames")
        self.core = self.stream % 2
        self.place = (self.frame // 2) % 2
        self.position = (self.stream // 2) * 2 + self.place
        self.near = self.frame % 2
        self.at = self.frame // 2
        self.far_masks = [m for m in range(2, n, 2) if not m & 2]
        self.both_masks = [m for m in range(2, n, 2) if m & 2 and m > 2]
        self.masks = self.far_masks + self.both_masks + [2]

    def along_stream(self, mask):
        return (flip(self.stream, mask), self.frame)

    def along_frames(self, mask):
        return (self.stream, flip(self.frame, mask))

    def with_position(self, mask):
        return (flip(self.stream, mask & 2), flip(self.frame, 2 * (mask & 1)))

    def across(self):
        return (flip(self.stream, 1), flip(self.frame, 2))


class Wire:
    def __init__(self, send, recv):
        self.send, self.recv, self.count, self.started = send, recv, 0, []

    def make(self, src, dst, device, index=None):
        k = self.count if index is None else index
        if index is None:
            self.count += 1
        return pltpu.make_async_remote_copy(
            src_ref=src,
            dst_ref=dst,
            send_sem=self.send.at[k],
            recv_sem=self.recv.at[k],
            device_id=device,
            device_id_type=pl.DeviceIdType.MESH,
        )

    def start(self, src, dst, device):
        copy = self.make(src, dst, device)
        copy.start()
        self.started.append(copy)
        return copy

    def sent(self, copy):
        self.started = [c for c in self.started if c is not copy]
        copy.wait_send()

    def finish(self):
        for copy in self.started:
            copy.wait_send()


class Local:
    def __init__(self, sems):
        self.sems, self.count = sems, 0

    def start(self, src, dst):
        copy = pltpu.make_async_copy(src, dst, self.sems.at[self.count])
        self.count += 1
        copy.start()
        return copy


def greet(devices):
    barrier = pltpu.get_barrier_semaphore()
    for device in devices:
        pl.semaphore_signal(
            barrier, inc=1, device_id=device, device_id_type=pl.DeviceIdType.MESH
        )
    pl.semaphore_wait(barrier, len(devices))


def dot_rows(left, right):
    return lax.dot_general(left, right, (((0,), (0,)), ((), ())), preferred_element_type=f32)


def dot_columns(left, right):
    return lax.dot_general(left, right, (((1,), (1,)), ((), ())), preferred_element_type=f32)


class Reduction:
    def __init__(self, w, wire, send, keep, arrived, sums, landed, out):
        self.w, self.wire = w, wire
        self.send, self.keep, self.arrived = send, keep, arrived
        self.sums, self.landed, self.out = sums, landed, out
        self.first, self.second = {}, {}
        self.order = w.masks + [0]

    def begin(self, mask):
        block = flip(self.w.at, mask // 2)
        self.first[mask] = self.wire.start(
            self.send.at[block], self.arrived.at[block], self.w.along_frames(1)
        )

    def forward(self, mask):
        block = flip(self.w.at, mask // 2)
        self.first[mask].wait_recv()
        self.wire.sent(self.first[mask])
        total = self.keep[block].astype(f32) + self.arrived[block].astype(f32)
        self.sums[block] = total.astype(bf16)
        if mask:
            self.second[mask] = self.wire.start(
                self.sums.at[block], self.landed.at[mask // 2 - 1], self.w.along_frames(mask)
            )

    def land(self):
        for copy in self.second.values():
            copy.wait_recv()

    def close(self):
        own, other = self.sums[self.w.at].astype(f32), None
        for mask in self.w.masks:
            self.second[mask].wait_recv()
            got = self.landed[mask // 2 - 1].astype(f32)
            if mask & 2:
                other = got if other is None else other + got
            else:
                own = own + got
        self.out[self.w.place] = own
        self.out[1 - self.w.place] = other


def tail_body(
    n, part_send, part_own, resid, mid, gains, gain_two, result_rows,
    gq_send, gq_keep, go_send, go_keep, context, ctx_full,
    out_q, out_o, out_grad, out_result, out_context, out_ctx,
    part_got, low, home, partner_half, half_sum, far_half, whole, kept_q, kept_o,
    arrived_q, arrived_o, sums_q, sums_o, landed_q, landed_o,
    context_held, ctx_held, term, term_got, term_sum, term_landed, gain_sum,
    send_sem, recv_sem, local_sem,
):
    w = Where(n)
    wire, local = Wire(send_sem, recv_sem), Local(local_sem)
    rows, depth = resid.shape
    crossing = w.core != w.place
    load_q = local.start(gq_keep, kept_q)
    load_o = local.start(go_keep, kept_o)
    load_context = local.start(context, context_held)
    load_ctx = local.start(ctx_full, ctx_held)
    greet(
        [w.along_stream(1), w.along_stream(2), w.along_frames(1)]
        + [w.along_frames(m) for m in w.masks]
        + [w.across()]
    )
    part = wire.start(part_send, part_got, w.along_stream(1))
    red_o = Reduction(w, wire, go_send, kept_o, arrived_o, sums_o, landed_o, out_o)
    red_q = Reduction(w, wire, gq_send, kept_q, arrived_q, sums_q, landed_q, out_q)
    for mask in red_o.order:
        red_o.begin(mask)
    for mask in red_q.order:
        red_q.begin(mask)

    part.wait_recv()
    gain = gains[0:1, :]
    gain_sum[...] = jnp.zeros_like(gain_sum)
    step = 64

    @pl.loop(0, rows // step)
    def _(t):
        at = pl.ds(pl.multiple_of(t * step, step), step)
        grad = part_own[at, :].astype(f32) + part_got[at, :].astype(f32)
        values = resid[at, :].astype(f32)
        scale = lax.rsqrt(jnp.mean(values * values, axis=-1, keepdims=True) + norm_eps)
        weighted = grad * gain
        inner = jnp.mean(weighted * values, axis=-1, keepdims=True)
        back = scale * weighted - values * (scale * scale * scale * inner)
        low[at, :] = (mid[at, :] + back).astype(bf16)
        gain_sum[...] += jnp.sum(grad * values * scale, axis=0, keepdims=True)

    row = lax.broadcasted_iota(jnp.int32, (EXTRA, depth), 0)
    low[rows:, :] = jnp.where(
        row == 0, gain_sum[...], jnp.where(row == 1, gain_two[...], 0.0)
    ).astype(bf16)

    cross = wire.make(low, home, w.across())
    cross_result = wire.make(result_rows, out_result, w.across())

    @pl.when(crossing)
    def _():
        cross.start()

    load_o.wait()
    load_q.wait()
    for mask in red_o.order:
        red_o.forward(mask)

    @pl.when(crossing)
    def _():
        cross_result.start()
        cross.wait_recv()

    stay = pltpu.make_async_copy(low, home, local.sems.at[4])
    stay_result = pltpu.make_async_copy(result_rows, out_result, local.sems.at[5])

    @pl.when(jnp.logical_not(crossing))
    def _():
        stay.start()
        stay_result.start()
        stay.wait()

    half = (rows + EXTRA) // 2
    mine = pl.ds(pl.multiple_of(w.core * half, 16), half)
    theirs = pl.ds(pl.multiple_of((1 - w.core) * half, 16), half)
    first = wire.start(home.at[theirs, :], partner_half, w.along_stream(1))
    out_grad[...] = home[:rows, :].astype(f32)
    first.wait_recv()
    half_sum[...] = (home[mine, :].astype(f32) + partner_half[...].astype(f32)).astype(bf16)
    second = wire.start(half_sum, far_half, w.along_stream(2))
    red_q.forward(red_q.order[0])
    red_q.forward(red_q.order[1])
    second.wait_recv()
    whole[mine, :] = (half_sum[...].astype(f32) + far_half[...].astype(f32)).astype(bf16)
    third = wire.start(whole.at[mine, :], whole.at[mine, :], w.along_stream(1))
    load_context.wait()
    third.wait_recv()

    share = depth // 4
    columns = pl.ds(pl.multiple_of(w.stream * share, LANES), share)
    block = share // n
    wide = context_held.shape[1]
    pieces = 2
    grad_share = whole[:rows, columns]
    firsts, seconds = [], []
    row = lax.broadcasted_iota(jnp.int32, (EXTRA, LANES), 0)
    select = (row == lax.broadcasted_iota(jnp.int32, (EXTRA, LANES), 1)).astype(bf16)
    edges = [wide * p // pieces for p in range(pieces)] + [wide + LANES]
    for p in range(pieces):
        lo, hi = edges[p], edges[p + 1]
        for at in range(lo, min(hi, wide), 1024):
            to = min(at + 1024, wide)
            value = dot_rows(grad_share, context_held[:, at:to]).astype(bf16)
            for k in range(n):
                term[k // 2, k % 2, :, at:to] = value[k * block : (k + 1) * block]
        if hi > wide:
            value = dot_rows(whole[rows:, columns], select).astype(bf16)
            for k in range(n):
                term[k // 2, k % 2, :, wide:hi] = value[k * block : (k + 1) * block]
        firsts.append(
            wire.start(
                term.at[:, 1 - w.near, :, lo:hi], term_got.at[:, :, lo:hi], w.along_frames(1)
            )
        )
    for mask in red_q.order[2:]:
        red_q.forward(mask)
    load_ctx.wait()

    def context_rows(t):
        at = pl.ds(pl.multiple_of(t * LANES, LANES), LANES)
        out_context[at, :] = dot_columns(whole[at, :], ctx_held[...])

    @pl.loop(0, rows // LANES)
    def _(t):
        context_rows(t)

    for p in range(pieces):
        lo, hi = edges[p], edges[p + 1]
        firsts[p].wait_recv()
        for mask in w.masks + [0]:
            to = flip(w.at, mask // 2)
            total = term[to, w.near, :, lo:hi].astype(f32) + term_got[to, :, lo:hi].astype(f32)
            term_sum[to, :, lo:hi] = total.astype(bf16)
            if mask:
                seconds.append(
                    wire.start(
                        term_sum.at[to, :, lo:hi],
                        term_landed.at[mask // 2, :, lo:hi],
                        w.along_frames(mask),
                    )
                )
    red_o.close()
    red_q.close()

    @pl.when(crossing)
    def _():
        cross_result.wait_recv()
        cross.wait_send()
        cross_result.wait_send()

    @pl.when(jnp.logical_not(crossing))
    def _():
        stay_result.wait()

    for copy in seconds:
        copy.wait_recv()
    total = term_sum[w.at].astype(f32)
    for mask in w.masks:
        total = total + term_landed[mask // 2].astype(f32)
    out_ctx[...] = total
    wire.finish()


def tail(
    n, part_send, part_own, resid, mid, gains, gain_two, result_rows,
    gq_send, gq_keep, go_send, go_keep, context, ctx_full,
):
    rows, depth = resid.shape
    halfn, block, wide_q = gq_send.shape
    wide_o = go_send.shape[2]
    share = depth // 4 // n
    wide = context.shape[1] + LANES
    half = (rows + EXTRA) // 2
    count = 64 + 2 * n
    scratch = [
        pltpu.VMEM((rows, depth), bf16),
        pltpu.VMEM((rows + EXTRA, depth), bf16),
        pltpu.VMEM((rows + EXTRA, depth), bf16),
        pltpu.VMEM((half, depth), bf16),
        pltpu.VMEM((half, depth), bf16),
        pltpu.VMEM((half, depth), bf16),
        pltpu.VMEM((rows + EXTRA, depth), bf16),
        pltpu.VMEM((halfn, block, wide_q), bf16),
        pltpu.VMEM((halfn, block, wide_o), bf16),
        pltpu.VMEM((halfn, block, wide_q), bf16),
        pltpu.VMEM((halfn, block, wide_o), bf16),
        pltpu.VMEM((halfn, block, wide_q), bf16),
        pltpu.VMEM((halfn, block, wide_o), bf16),
        pltpu.VMEM((halfn, block, wide_q), bf16),
        pltpu.VMEM((halfn, block, wide_o), bf16),
        pltpu.VMEM(context.shape, bf16),
        pltpu.VMEM(ctx_full.shape, bf16),
        pltpu.VMEM((halfn, 2, share, wide), bf16),
        pltpu.VMEM((halfn, share, wide), bf16),
        pltpu.VMEM((halfn, share, wide), bf16),
        pltpu.VMEM((halfn, share, wide), bf16),
        pltpu.VMEM((1, depth), f32),
        pltpu.SemaphoreType.DMA((count,)),
        pltpu.SemaphoreType.DMA((count,)),
        pltpu.SemaphoreType.DMA((6,)),
    ]
    return pl.pallas_call(
        functools.partial(tail_body, n),
        in_specs=[ANY, VMEM, VMEM, VMEM, VMEM, VMEM, VMEM, ANY, ANY, ANY, ANY, ANY, ANY],
        out_specs=[VMEM, VMEM, VMEM, VMEM, VMEM, VMEM],
        out_shape=[
            jax.ShapeDtypeStruct((2, block, wide_q), f32),
            jax.ShapeDtypeStruct((2, block, wide_o), f32),
            jax.ShapeDtypeStruct((rows, depth), f32),
            jax.ShapeDtypeStruct((rows, depth), bf16),
            jax.ShapeDtypeStruct((rows, ctx_full.shape[0]), f32),
            jax.ShapeDtypeStruct((share, wide), f32),
        ],
        scratch_shapes=scratch,
        compiler_params=pltpu.CompilerParams(
            collective_id=5, has_side_effects=True, vmem_limit_bytes=60 << 20
        ),
        name="tail",
    )(
        part_send, part_own, resid, mid, gains, gain_two, result_rows,
        gq_send, gq_keep, go_send, go_keep, context, ctx_full,
    )


def ending_body(
    n, resid, mid, gains, gain_two, result_rows, valid,
    pair_one, pair_grad, mixed_rows, grad_qkv_rows, qkv_weight, context, ctx_pieces, up_send, up_stay,
    out_q, out_o, out_up, landed_q, landed_o, landed_up, out_grad, out_result, out_context, out_ctx,
    one, grad_two, mixed, grad_qkv, qkv_full, left_away, left_stay, part_send, part_own,
    part_got, low, home, partner_half, half_sum, far_half, whole, result_home,
    send_q, send_o, kept_q, kept_o, arrived_q, arrived_o, send_up, kept_up, arrived_up,
    context_held, ctx_held, term, term_got, term_sum, term_landed, gain_sum,
    send_sem, recv_sem, local_sem,
):
    w = Where(n)
    wire, local = Wire(send_sem, recv_sem), Local(local_sem)
    rows, depth = resid.shape
    piece = depth // n
    crossing = w.core != w.place
    load_up = local.start(up_send, send_up)
    load_grad = local.start(pair_grad, grad_two)
    load_mixed = local.start(mixed_rows, mixed)
    load_qkv = local.start(grad_qkv_rows, grad_qkv)
    load_weight = local.start(qkv_weight, qkv_full)
    load_one = local.start(pair_one, one)
    load_up_stay = local.start(up_stay, kept_up)
    load_context = local.start(context, context_held)
    load_ctx = [
        local.start(ctx_pieces.at[k], ctx_held.at[:, k * piece : (k + 1) * piece])
        for k in range(n)
    ]
    greet(
        [w.along_stream(1), w.along_stream(2), w.along_frames(1)]
        + [w.along_frames(m) for m in w.masks]
        + [w.across()]
    )
    cross_result = wire.make(result_rows, result_home, w.across())
    stay_result = pltpu.make_async_copy(result_rows, result_home, local.sems.at[30])
    stay = pltpu.make_async_copy(low, home, local.sems.at[31])

    @pl.when(crossing)
    def _():
        cross_result.start()

    @pl.when(jnp.logical_not(crossing))
    def _():
        stay_result.start()

    def split(source, which, into):
        for b in range(n // 2):
            at = pl.ds(pl.multiple_of((2 * b + which) * piece, piece), piece)
            into[:, b * piece : (b + 1) * piece] = source[:, at]

    def product(left, right, into):
        wide = right.shape[1]
        for lo in range(0, wide, 512):
            value = dot_rows(left[...], right[:, lo : lo + 512]).astype(bf16)
            for b in range(n // 2):
                into[b, :, lo : lo + 512] = value[b * piece : (b + 1) * piece]

    def partial(t):
        at = pl.ds(pl.multiple_of(t * 256, 256), 256)
        return dot_columns(grad_qkv[at, :], qkv_full[...])

    load_up.wait()
    red_up = Reduction(w, wire, send_up, kept_up, arrived_up, send_up, landed_up, out_up)
    for mask in red_up.order:
        red_up.begin(mask)
    load_grad.wait()
    split(grad_two, 1 - w.near, left_away)
    load_mixed.wait()
    product(left_away, mixed, send_o)
    red_o = Reduction(w, wire, send_o, kept_o, arrived_o, send_o, landed_o, out_o)
    for mask in red_o.order:
        red_o.begin(mask)
    load_qkv.wait()
    load_weight.wait()

    @pl.loop(0, rows // 256)
    def _(t):
        to = pl.ds(pl.multiple_of(t * 256, 256), 256)
        part_send[to, :] = partial(rows // 256 + t).astype(bf16)

    part = wire.start(part_send, part_got, w.along_stream(1))
    load_one.wait()
    split(one, 1 - w.near, left_away)
    product(left_away, grad_qkv, send_q)
    red_q = Reduction(w, wire, send_q, kept_q, arrived_q, send_q, landed_q, out_q)
    for mask in red_q.order:
        red_q.begin(mask)

    @pl.loop(0, rows // 256)
    def _(t):
        to = pl.ds(pl.multiple_of(t * 256, 256), 256)
        part_own[to, :] = partial(t)

    part.wait_recv()
    gain = gains[0:1, :]
    gain_sum[...] = jnp.zeros_like(gain_sum)
    step = 64

    @pl.loop(0, rows // step)
    def _(t):
        at = pl.ds(pl.multiple_of(t * step, step), step)
        grad = part_own[at, :].astype(f32) + part_got[at, :].astype(f32)
        values = resid[at, :].astype(f32)
        scale = lax.rsqrt(jnp.mean(values * values, axis=-1, keepdims=True) + norm_eps)
        weighted = grad * gain
        inner = jnp.mean(weighted * values, axis=-1, keepdims=True)
        back = scale * weighted - values * (scale * scale * scale * inner)
        low[at, :] = (mid[at, :] + back).astype(bf16)
        gain_sum[...] += jnp.sum(grad * values * scale, axis=0, keepdims=True)

    row = lax.broadcasted_iota(jnp.int32, (EXTRA, depth), 0)
    low[rows:, :] = jnp.where(
        row == 0, gain_sum[...], jnp.where(row == 1, gain_two[...], 0.0)
    ).astype(bf16)

    cross = wire.make(low, home, w.across())

    @pl.when(crossing)
    def _():
        cross.start()

    split(grad_two, w.near, left_stay)
    product(left_stay, mixed, kept_o)
    load_up_stay.wait()
    for mask in red_up.order[:2]:
        red_up.forward(mask)
    for mask in red_o.order:
        red_o.forward(mask)

    @pl.when(crossing)
    def _():
        cross_result.wait_recv()

    @pl.when(jnp.logical_not(crossing))
    def _():
        stay.start()
        stay_result.wait()

    split(one, w.near, left_stay)
    product(left_stay, grad_qkv, kept_q)
    out_result[:, 0, :] = result_home[...].astype(f32) * valid[...]

    @pl.when(crossing)
    def _():
        cross.wait_recv()

    @pl.when(jnp.logical_not(crossing))
    def _():
        stay.wait()

    half = (rows + EXTRA) // 2
    mine = pl.ds(pl.multiple_of(w.core * half, 16), half)
    theirs = pl.ds(pl.multiple_of((1 - w.core) * half, 16), half)
    first = wire.start(home.at[theirs, :], partner_half, w.along_stream(1))
    out_grad[:, 0, :] = home[:rows, :].astype(f32)
    for mask in red_up.order[2:]:
        red_up.forward(mask)
    first.wait_recv()
    half_sum[...] = (home[mine, :].astype(f32) + partner_half[...].astype(f32)).astype(bf16)
    second = wire.start(half_sum, far_half, w.along_stream(2))
    red_q.forward(red_q.order[0])
    red_q.forward(red_q.order[1])
    second.wait_recv()
    whole[mine, :] = (half_sum[...].astype(f32) + far_half[...].astype(f32)).astype(bf16)
    third = wire.start(whole.at[mine, :], whole.at[mine, :], w.along_stream(1))
    load_context.wait()
    third.wait_recv()

    share = depth // 4
    columns = pl.ds(pl.multiple_of(w.stream * share, LANES), share)
    block = share // n
    wide = context_held.shape[1]
    pieces = 4
    grad_share = whole[:rows, columns]
    firsts, seconds = [], []
    row = lax.broadcasted_iota(jnp.int32, (EXTRA, LANES), 0)
    select = (row == lax.broadcasted_iota(jnp.int32, (EXTRA, LANES), 1)).astype(bf16)
    edges = [wide * p // pieces for p in range(pieces)] + [wide + LANES]
    for p in range(pieces):
        lo, hi = edges[p], edges[p + 1]
        for at in range(lo, min(hi, wide), 1024):
            to = min(at + 1024, wide)
            value = dot_rows(grad_share, context_held[:, at:to]).astype(bf16)
            for k in range(n):
                term[k // 2, k % 2, :, at:to] = value[k * block : (k + 1) * block]
        if hi > wide:
            value = dot_rows(whole[rows:, columns], select).astype(bf16)
            for k in range(n):
                term[k // 2, k % 2, :, wide:hi] = value[k * block : (k + 1) * block]
        firsts.append(
            wire.start(
                term.at[:, 1 - w.near, :, lo:hi], term_got.at[:, :, lo:hi], w.along_frames(1)
            )
        )
    for mask in red_q.order[2:]:
        red_q.forward(mask)
    for copy in load_ctx:
        copy.wait()

    def context_rows(t):
        at = pl.ds(pl.multiple_of(t * LANES, LANES), LANES)
        out_context[at, :] = dot_columns(whole[at, :], ctx_held[...])

    @pl.loop(0, rows // LANES)
    def _(t):
        context_rows(t)

    for p in range(pieces):
        lo, hi = edges[p], edges[p + 1]
        firsts[p].wait_recv()
        for mask in w.masks + [0]:
            to = flip(w.at, mask // 2)
            total = term[to, w.near, :, lo:hi].astype(f32) + term_got[to, :, lo:hi].astype(f32)
            term_sum[to, :, lo:hi] = total.astype(bf16)
            if mask:
                seconds.append(
                    wire.start(
                        term_sum.at[to, :, lo:hi],
                        term_landed.at[mask // 2, :, lo:hi],
                        w.along_frames(mask),
                    )
                )
    red_up.land()
    red_o.land()
    red_q.land()
    kept = [
        local.start(send_o.at[w.at], out_o),
        local.start(send_q.at[w.at], out_q),
        local.start(send_up.at[w.at], out_up),
    ]

    @pl.when(crossing)
    def _():
        cross.wait_send()
        cross_result.wait_send()

    for copy in seconds:
        copy.wait_recv()
    total = term_sum[w.at].astype(f32)
    for mask in w.masks:
        total = total + term_landed[mask // 2].astype(f32)
    out_ctx[...] = total
    for copy in kept:
        copy.wait()
    wire.finish()


def ending_scratch(n, rows, depth, context_shape, count, wide_q, wide_o, wide_up):
    halfn, block, share = n // 2, depth // n, depth // 4 // n
    wide = context_shape[1] + LANES
    half = (rows + EXTRA) // 2
    both = 2 * rows
    shapes = [
        ((both, depth), bf16),
        ((both, depth), bf16),
        ((both, wide_o), bf16),
        ((both, wide_q), bf16),
        ((depth, wide_q), bf16),
        ((both, depth // 2), bf16),
        ((both, depth // 2), bf16),
        ((rows, depth), bf16),
        ((rows, depth), f32),
        ((rows, depth), bf16),
        ((rows + EXTRA, depth), bf16),
        ((rows + EXTRA, depth), bf16),
        ((half, depth), bf16),
        ((half, depth), bf16),
        ((half, depth), bf16),
        ((rows + EXTRA, depth), bf16),
        ((rows, depth), bf16),
        ((halfn, block, wide_q), bf16),
        ((halfn, block, wide_o), bf16),
        ((halfn, block, wide_q), bf16),
        ((halfn, block, wide_o), bf16),
        ((halfn, block, wide_q), bf16),
        ((halfn, block, wide_o), bf16),
        ((halfn, block, wide_up), bf16),
        ((halfn, block, wide_up), bf16),
        ((halfn, block, wide_up), bf16),
        (context_shape, bf16),
        ((count, depth), bf16),
        ((halfn, 2, share, wide), bf16),
        ((halfn, share, wide), bf16),
        ((halfn, share, wide), bf16),
        ((halfn, share, wide), bf16),
        ((1, depth), f32),
    ]
    others = [((rows, depth), f32)] * 4 + [((rows, depth), bf16)] * 2 + [((rows, count), f32)]
    return shapes, sum(math.prod(dims) * jnp.dtype(kind).itemsize for dims, kind in shapes + others)


def ending(
    n, resid, mid, gains, gain_two, result_rows, valid,
    pair_one, pair_grad, mixed, grad_qkv, qkv_full, context, ctx_pieces, up_send, up_stay,
):
    rows, depth = resid.shape
    halfn, block = n // 2, depth // n
    wide_q, wide_o = qkv_full.shape[1], mixed.shape[1]
    count = ctx_pieces.shape[1]
    wide_up = up_send.shape[2]
    shapes, _ = ending_scratch(n, rows, depth, context.shape, count, wide_q, wide_o, wide_up)
    sems = 64 + 2 * n
    shape = jax.ShapeDtypeStruct
    return pl.pallas_call(
        functools.partial(ending_body, n),
        in_specs=[VMEM] * 6 + [ANY] * 9,
        out_specs=[ANY] * 6 + [VMEM] * 4,
        out_shape=[
            shape((block, wide_q), bf16),
            shape((block, wide_o), bf16),
            shape((block, wide_up), bf16),
            shape((halfn - 1, block, wide_q), bf16),
            shape((halfn - 1, block, wide_o), bf16),
            shape((halfn - 1, block, wide_up), bf16),
            shape((rows, 1, depth), f32),
            shape((rows, 1, depth), f32),
            shape((rows, count), f32),
            shape((depth // 4 // n, context.shape[1] + LANES), f32),
        ],
        scratch_shapes=[pltpu.VMEM(dims, kind) for dims, kind in shapes]
        + [
            pltpu.SemaphoreType.DMA((sems,)),
            pltpu.SemaphoreType.DMA((sems,)),
            pltpu.SemaphoreType.DMA((32,)),
        ],
        compiler_params=pltpu.CompilerParams(
            collective_id=6, has_side_effects=True, vmem_limit_bytes=67_000_000
        ),
        name="ending",
    )(
        resid, mid, gains, gain_two, result_rows, valid,
        pair_one, pair_grad, mixed, grad_qkv, qkv_full, context, ctx_pieces, up_send, up_stay,
    )


def swap_frames(value, mask):
    n = lax.axis_size("frames")
    return lax.ppermute(value, "frames", [(d, d ^ mask) for d in range(n)])


def swap_stream(value, mask):
    n = lax.axis_size("stream")
    return lax.ppermute(value, "stream", [(d, d ^ mask) for d in range(n)])


def joint(value, target):
    streams, n = lax.axis_size("stream"), lax.axis_size("frames")
    pairs = []
    for s in range(streams):
        for f in range(n):
            to_s, to_f = target(s, f)
            pairs.append((s * n + f, to_s * n + to_f))
    return lax.ppermute(value, ("stream", "frames"), pairs)


def transposed(value):
    def target(s, f):
        core, place = s % 2, (f // 2) % 2
        return s - core + place, f - 2 * place + 2 * core

    return joint(value, target)


def peer(value, mask):
    return joint(value, lambda s, f: (s ^ (mask & 2), f ^ (2 * (mask & 1))))


def norm_scale(values):
    return lax.rsqrt(jnp.mean(values * values, axis=-1, keepdims=True) + norm_eps)


def norm_back(values, scale, gain, grad):
    weighted = grad * gain
    inner_mean = jnp.mean(weighted * values, axis=-1, keepdims=True)
    grad_values = scale * weighted - values * (scale * scale * scale) * inner_mean
    grad_gain = jnp.sum(grad * values * scale, axis=0)
    return (grad_values, grad_gain)


def exchange_rows(qkv, position):
    rows, width = qkv.shape
    quarter = rows // 4
    parts = qkv.reshape(4, quarter, width)
    out = jnp.zeros((4, quarter, width), qkv.dtype)
    own = lax.dynamic_index_in_dim(parts, position, 0, keepdims=False)
    out = lax.dynamic_update_index_in_dim(out, own, position, 0)
    for mask in (2, 1, 3):
        there = position ^ mask
        got = peer(lax.dynamic_index_in_dim(parts, there, 0, keepdims=False), mask)
        out = lax.dynamic_update_index_in_dim(out, got, there, 0)
    return out


def heads_sum(product, fold):
    high = product.astype(bf16)
    low = (product - high.astype(f32)).astype(bf16)
    return jnp.dot(high, fold, preferred_element_type=f32) + jnp.dot(
        low, fold, preferred_element_type=f32
    )


def attention_forward_rows(at, qkv_ref, fold, spread, probs_ref, out_ref):
    width = out_ref.shape[2]
    for q in range(4):
        query = qkv_ref[q, at, :width].astype(f32)
        scores = []
        for k in range(q + 1):
            key = qkv_ref[k, at, width : 2 * width].astype(f32)
            scores.append(heads_sum(query * key, fold) * HD ** (-0.5))
        top = functools.reduce(jnp.maximum, scores)
        expo = [jnp.exp(s - top) for s in scores]
        total = functools.reduce(jnp.add, expo)
        mixed = None
        for k in range(q + 1):
            prob = expo[k] / total
            probs_ref[PAIRS.index((q, k)), at, :] = prob
            wide = jnp.dot(prob.astype(bf16), spread, preferred_element_type=f32)
            term = wide * qkv_ref[k, at, 2 * width :].astype(f32)
            mixed = term if mixed is None else mixed + term
        out_ref[q, at, :] = mixed.astype(bf16)


def attention_backward_rows(at, qkv_ref, probs_ref, grad_ref, fold, spread, out_ref):
    width = grad_ref.shape[2]
    grad_keys, grad_values = [None] * 4, [None] * 4
    for q in range(4):
        grad = grad_ref[q, at, :].astype(f32)
        query = qkv_ref[q, at, :width].astype(f32)
        probs = [probs_ref[PAIRS.index((q, k)), at, :] for k in range(q + 1)]
        grad_probs = [
            heads_sum(grad * qkv_ref[k, at, 2 * width :].astype(f32), fold) for k in range(q + 1)
        ]
        total = functools.reduce(jnp.add, [p * g for p, g in zip(probs, grad_probs)])
        grad_query = None
        for k in range(q + 1):
            wide = jnp.dot(probs[k].astype(bf16), spread, preferred_element_type=f32)
            term = wide * grad
            grad_values[k] = term if grad_values[k] is None else grad_values[k] + term
            grad_score = (probs[k] * (grad_probs[k] - total)).astype(bf16)
            wide = jnp.dot(grad_score, spread, preferred_element_type=f32)
            term = wide * qkv_ref[k, at, width : 2 * width].astype(f32)
            grad_query = term if grad_query is None else grad_query + term
            term = wide * query
            grad_keys[k] = term if grad_keys[k] is None else grad_keys[k] + term
        out_ref[q, at, :width] = (grad_query * HD ** (-0.5)).astype(bf16)
    for k in range(4):
        out_ref[k, at, width : 2 * width] = (grad_keys[k] * HD ** (-0.5)).astype(bf16)
        out_ref[k, at, 2 * width :] = grad_values[k].astype(bf16)


def attention_backward_body(qkv_ref, probs_ref, grad_ref, fold_ref, spread_ref, out_ref):
    everything = slice(None)
    attention_backward_rows(
        everything, qkv_ref, probs_ref, grad_ref, fold_ref[...], spread_ref[...], out_ref
    )


def fold_matrices(width):
    feature = lax.broadcasted_iota(jnp.int32, (width, LANES), 0) // HD
    head = lax.broadcasted_iota(jnp.int32, (width, LANES), 1)
    fold = (feature == head).astype(bf16)
    return fold, fold.T


def attention_backward(qkv, probs, grad, step=64):
    _, rows, triple = qkv.shape
    width = triple // 3
    fold, spread = fold_matrices(width)
    return pl.pallas_call(
        attention_backward_body,
        grid=(rows // step,),
        in_specs=[
            pl.BlockSpec((4, step, triple), lambda r: (0, r, 0)),
            pl.BlockSpec((len(PAIRS), step, LANES), lambda r: (0, r, 0)),
            pl.BlockSpec((4, step, width), lambda r: (0, r, 0)),
            pl.BlockSpec((width, LANES), lambda r: (0, 0)),
            pl.BlockSpec((LANES, width), lambda r: (0, 0)),
        ],
        out_specs=pl.BlockSpec((4, step, triple), lambda r: (0, r, 0)),
        out_shape=jax.ShapeDtypeStruct((4, rows, triple), bf16),
        name="attention_backward",
    )(qkv, probs, grad, fold, spread)


def after(value, *others):
    return lax.optimization_barrier((value,) + others)[0]


def taken(weights, place):
    own = [lax.dynamic_index_in_dim(w, place, 0, keepdims=False) for w in weights]
    other = [lax.dynamic_index_in_dim(w, 1 - place, 0, keepdims=False) for w in weights]
    if len(weights) == 1:
        return own[0], other[0]
    return jnp.concatenate(own, axis=1), jnp.concatenate(other, axis=1)


def placed_rows(pieces, frame_index, start, width):
    n = lax.axis_size("frames")
    block = pieces[0].shape[0]
    full = jnp.zeros((n, block, width), pieces[0].dtype)
    for mask in range(n):
        part = pieces[mask][:, start : start + width]
        full = lax.dynamic_update_index_in_dim(full, part, frame_index ^ mask, 0)
    return full.reshape(n * block, width)


def halves(left, near):
    n = lax.axis_size("frames")
    rows, depth = left.shape
    block = depth // n
    even = jnp.concatenate([left[:, k * block : (k + 1) * block] for k in range(0, n, 2)], axis=1)
    odd = jnp.concatenate([left[:, k * block : (k + 1) * block] for k in range(1, n, 2)], axis=1)
    return jnp.where(near == 0, odd, even), jnp.where(near == 0, even, odd)


def scattered(left_halves, right, frame_index, place):
    n = lax.axis_size("frames")

    def product(part):
        return lax.dot_general(
            part, right, (((0,), (0,)), ((), ())), preferred_element_type=f32
        ).astype(bf16)

    arrived = swap_frames(product(left_halves[0]), 1)
    half_sum = (product(left_halves[1]).astype(f32) + arrived.astype(f32)).astype(bf16)
    half_sum = half_sum.reshape(n // 2, -1, right.shape[1])
    at = frame_index // 2
    own = lax.dynamic_index_in_dim(half_sum, at, 0, keepdims=False).astype(f32)
    other = None
    for mask in range(2, n, 2):
        got = swap_frames(
            lax.dynamic_index_in_dim(half_sum, at ^ (mask // 2), 0, keepdims=False), mask
        ).astype(f32)
        if mask & 2:
            other = got if other is None else other + got
        else:
            own = own + got
    first = jnp.where(place == 0, own, other)
    second = jnp.where(place == 0, other, own)
    return jnp.stack([first, second], axis=0)


class Spread:
    def __init__(self, w, wire, weight, full):
        self.w, self.wire, self.weight, self.full = w, wire, weight, full
        self.block = full.shape[0] // w.n
        self.far, self.near = {}, {}

    def rows(self, frame):
        return self.full.at[pl.ds(pl.multiple_of(frame * self.block, self.block), self.block), :]

    def own(self, local):
        return local.start(self.weight.at[self.w.place], self.rows(self.w.frame))

    def own_near(self):
        w = self.w
        self.near[0] = self.wire.start(
            self.weight.at[w.place], self.rows(w.frame), w.along_frames(1)
        )

    def send(self, masks):
        w = self.w
        for mask in masks:
            which = 1 - w.place if mask & 2 else w.place
            self.far[mask] = self.wire.start(
                self.weight.at[which], self.rows(w.frame), w.along_frames(mask)
            )

    def relay(self, mask):
        self.far[mask].wait_recv()
        rows = self.rows(flip(self.w.frame, mask))
        self.near[mask] = self.wire.start(rows, rows, self.w.along_frames(1))

    def close(self):
        for copy in self.near.values():
            copy.wait_recv()


def front_body(
    n, context, ctx_weight, inputs, gains, fold, spread,
    qkv_weight, out_weight, gu_weight, down_weight,
    out_qkv, out_out, out_gu, out_down, out_ctx, out_resid, out_mid, out_one, out_two,
    out_qkv_mixed, out_probs, out_mixed,
    ctx_held, context_held, total, partner_half, half_sum, far_half, whole, home, resid, pair,
    qkv_full, out_full, qkv_rows, qkv_mixed, probs, mixed_quarter, mixed, away, got,
    send_sem, recv_sem, local_sem,
):
    w = Where(n)
    wire, local = Wire(send_sem, recv_sem), Local(local_sem)
    rows, depth = inputs.shape
    count = ctx_weight.shape[0] // 4
    piece = depth // n
    crossing = w.core != w.place
    half = rows // 2
    step = 64
    quarter_of_context = pl.ds(pl.multiple_of(w.stream * count, LANES), count)
    load_context = local.start(context.at[:, quarter_of_context], context_held)
    load_ctx = local.start(ctx_weight.at[quarter_of_context, :], ctx_held.at[w.frame])
    qkv = Spread(w, wire, qkv_weight, qkv_full)
    out = Spread(w, wire, out_weight, out_full)
    gu = Spread(w, wire, gu_weight, out_gu)
    down = Spread(w, wire, down_weight, out_down)
    owns = [qkv.own(local), out.own(local)]
    greet(
        [w.along_stream(1), w.along_stream(2), w.along_frames(1)]
        + [w.along_frames(m) for m in w.masks]
        + [w.across(), w.with_position(3)]
    )

    load_ctx.wait()
    held, near = [0], {}

    def ctx_near(o):
        at = flip(w.frame, o)
        near[o] = wire.start(ctx_held.at[at], ctx_held.at[at], w.along_frames(1))

    ready = []
    for bit in reversed(range(1, n.bit_length() - 1)):
        copies = []
        for o in held:
            at = flip(w.frame, o)
            copies.append(
                (o, wire.start(ctx_held.at[at], ctx_held.at[at], w.along_frames(1 << bit)))
            )
        if bit == n.bit_length() - 2:
            ctx_near(0)
            qkv.own_near()
            out.own_near()
        if bit == 1:
            for mask in w.masks:
                qkv.send([mask])
                out.send([mask])
        for o, copy in copies:
            copy.wait_recv()
            ctx_near(o ^ (1 << bit))
            held.append(o ^ (1 << bit))

    load_context.wait()

    def project(o):
        at = flip(w.frame, o)
        columns = pl.ds(pl.multiple_of(at * piece, piece), piece)
        value = jnp.dot(context_held[...], ctx_held[at], preferred_element_type=f32)
        total[:, columns] = value

    def relay_attention(k):
        for mask in w.masks[k : k + 1]:
            qkv.relay(mask)
            out.relay(mask)

    if piece % LANES == 0:
        for o in held:
            project(o)
        for o in held:
            if o == held[-1]:
                relay_attention(0)
            near[o].wait_recv()
            project(o ^ 1)
    else:
        for o in held:
            near[o].wait_recv()
        relay_attention(0)
        total[...] = jnp.zeros_like(total)

        @pl.loop(0, n)
        def _(at):
            line = lax.broadcasted_iota(jnp.int32, (piece, depth), 0)
            column = lax.broadcasted_iota(jnp.int32, (piece, depth), 1)
            select = (column == line + at * piece).astype(bf16)
            laid = jnp.dot(ctx_held[at], select, preferred_element_type=f32).astype(bf16)

            @pl.loop(0, rows // LANES)
            def _(t):
                here = pl.ds(pl.multiple_of(t * LANES, LANES), LANES)
                total[here, :] += jnp.dot(
                    context_held[here, :], laid, preferred_element_type=f32
                )

    store_ctx = local.start(ctx_held, out_ctx)

    mine = pl.ds(pl.multiple_of(w.core * half, 16), half)
    theirs = pl.ds(pl.multiple_of((1 - w.core) * half, 16), half)
    whole[theirs, :] = total[theirs, :].astype(bf16)
    first = wire.start(whole.at[theirs, :], partner_half, w.along_stream(1))
    first.wait_recv()
    half_sum[...] = (total[mine, :] + partner_half[...].astype(f32)).astype(bf16)
    second = wire.start(half_sum, far_half, w.along_stream(2))
    relay_attention(1)
    second.wait_recv()
    home[mine, :] = (half_sum[...].astype(f32) + far_half[...].astype(f32)).astype(bf16)
    third = wire.start(home.at[mine, :], home.at[mine, :], w.along_stream(1))
    third.wait_recv()
    wire.sent(third)

    @pl.loop(0, rows // step)
    def _(t):
        at = pl.ds(pl.multiple_of(t * step, step), step)
        home[at, :] = (home[at, :].astype(f32) + inputs[at, :].astype(f32)).astype(bf16)

    cross = wire.make(home, resid, w.across())
    stay = pltpu.make_async_copy(home, resid, local_sem.at[22])

    @pl.when(crossing)
    def _():
        cross.start()

    @pl.when(jnp.logical_not(crossing))
    def _():
        stay.start()

    gu.own_near()
    gu.send(w.far_masks + w.both_masks)
    for k in range(2, len(w.masks)):
        relay_attention(k)

    @pl.when(crossing)
    def _():
        cross.wait_recv()

    @pl.when(jnp.logical_not(crossing))
    def _():
        stay.wait()

    def normed(source, gain):
        @pl.loop(0, rows // step)
        def _(t):
            at = pl.ds(pl.multiple_of(t * step, step), step)
            values = source[at, :].astype(f32)
            scale = lax.rsqrt(jnp.mean(values * values, axis=-1, keepdims=True) + norm_eps)
            pair[at, :] = (values * scale * gain).astype(bf16)

    normed(resid, gains[0:1, :])
    upper = pair.at[rows:, :]
    first_pair = wire.start(pair.at[:rows, :], upper, w.along_stream(1))
    for copy in owns:
        copy.wait()
    qkv.close()
    out.close()
    quarter = 2 * rows // 4
    width = out_full.shape[1]

    def qkv_of(lo, hi):
        @pl.loop(lo, hi)
        def _(t):
            at = pl.ds(pl.multiple_of(t * quarter, quarter), quarter)
            left = pair[at, :]
            for p in range(3):
                columns = slice(p * width, (p + 1) * width)
                value = jnp.dot(left, qkv_full[:, columns], preferred_element_type=f32)
                qkv_rows[at, columns] = value.astype(bf16)

    qkv_of(0, 2)
    first_pair.wait_recv()
    qkv_of(2, 4)
    mixing = {}

    def rows_of(position):
        return pl.ds(pl.multiple_of(position * quarter, quarter), quarter)

    for mask in (3, 1, 2):
        mixing[mask] = wire.start(
            qkv_rows.at[rows_of(flip(w.position, mask)), :],
            qkv_mixed.at[w.position],
            w.with_position(mask),
        )
    own_quarter = local.start(qkv_rows.at[rows_of(w.position), :], qkv_mixed.at[w.position])
    gu.send([2])
    down.send(w.far_masks)
    stores = [
        local.start(pair, out_one),
        local.start(qkv_full, out_qkv),
        local.start(out_full, out_out),
        local.start(resid, out_resid),
    ]
    gu_own, down_own = gu.own(local), down.own(local)
    for mask in w.far_masks:
        gu.relay(mask)
    own_quarter.wait()
    for mask in (2, 1, 3):
        mixing[mask].wait_recv()
    for mask in w.both_masks:
        gu.relay(mask)
    fold_held, spread_held = fold[...], spread[...]

    @pl.loop(0, quarter // step)
    def _(t):
        at = pl.ds(pl.multiple_of(t * step, step), step)
        attention_forward_rows(at, qkv_mixed, fold_held, spread_held, probs, mixed_quarter)

    returning = {}
    for mask in (3, 1, 2):
        returning[mask] = wire.start(
            mixed_quarter.at[flip(w.position, mask)],
            mixed.at[rows_of(w.position), :],
            w.with_position(mask),
        )
    own_back = local.start(mixed_quarter.at[w.position], mixed.at[rows_of(w.position), :])
    down.send(w.both_masks + [2])
    stores += [local.start(qkv_mixed, out_qkv_mixed), local.start(probs, out_probs)]
    gu.relay(2)
    own_back.wait()
    for mask in (2, 1, 3):
        returning[mask].wait_recv()
    stores.append(local.start(mixed, out_mixed))
    stores[0].wait()

    @pl.loop(2, 4)
    def _(t):
        at = pl.ds(pl.multiple_of(t * quarter, quarter), quarter)
        to = pl.ds(pl.multiple_of(t * quarter - rows, quarter), quarter)
        away[to, :] = dot_columns(mixed[at, :], out_full[...]).astype(bf16)

    part = wire.start(away, got, w.along_stream(1))

    @pl.loop(0, 2)
    def _(t):
        at = pl.ds(pl.multiple_of(t * quarter, quarter), quarter)
        total[at, :] = dot_columns(mixed[at, :], out_full[...])

    part.wait_recv()
    wire.sent(first_pair)
    gain = gains[1:2, :]

    @pl.loop(0, rows // step)
    def _(t):
        at = pl.ds(pl.multiple_of(t * step, step), step)
        values = resid[at, :].astype(f32) + total[at, :] + got[at, :].astype(f32)
        total[at, :] = values
        scale = lax.rsqrt(jnp.mean(values * values, axis=-1, keepdims=True) + norm_eps)
        pair[at, :] = (values * scale * gain).astype(bf16)

    second_pair = wire.start(pair.at[:rows, :], upper, w.along_stream(1))
    stores.append(local.start(total, out_mid))
    second_pair.wait_recv()
    stores.append(local.start(pair, out_two))
    gu.close()
    for copy in down.far.values():
        copy.wait_recv()
    for copy in stores[1:]:
        copy.wait()
    for copy in (store_ctx, gu_own, down_own):
        copy.wait()

    @pl.when(crossing)
    def _():
        cross.wait_send()

    wire.finish()


def front(
    n, context, ctx_weight, inputs, gains, qkv_weight, out_weight, gu_weight, down_weight,
):
    rows, depth = inputs.shape
    count = ctx_weight.shape[0] // 4
    wide_q, wide_o = qkv_weight.shape[2], out_weight.shape[2]
    fold, spread = fold_matrices(wide_o)
    quarter = rows // 2
    half = rows // 2
    pairs = len(PAIRS)
    scratch = [
        pltpu.VMEM((n, count, depth // n), bf16),
        pltpu.VMEM((rows, count), bf16),
        pltpu.VMEM((rows, depth), f32),
        pltpu.VMEM((half, depth), bf16),
        pltpu.VMEM((half, depth), bf16),
        pltpu.VMEM((half, depth), bf16),
        pltpu.VMEM((rows, depth), bf16),
        pltpu.VMEM((rows, depth), bf16),
        pltpu.VMEM((rows, depth), bf16),
        pltpu.VMEM((2 * rows, depth), bf16),
        pltpu.VMEM((depth, wide_q), bf16),
        pltpu.VMEM((depth, wide_o), bf16),
        pltpu.VMEM((2 * rows, wide_q), bf16),
        pltpu.VMEM((4, quarter, wide_q), bf16),
        pltpu.VMEM((pairs, quarter, LANES), f32),
        pltpu.VMEM((4, quarter, wide_o), bf16),
        pltpu.VMEM((2 * rows, wide_o), bf16),
        pltpu.VMEM((rows, depth), bf16),
        pltpu.VMEM((rows, depth), bf16),
        pltpu.SemaphoreType.DMA((24 + 10 * n,)),
        pltpu.SemaphoreType.DMA((24 + 10 * n,)),
        pltpu.SemaphoreType.DMA((24,)),
    ]
    shape = jax.ShapeDtypeStruct
    return pl.pallas_call(
        functools.partial(front_body, n),
        in_specs=[ANY, ANY, VMEM, VMEM, VMEM, VMEM, ANY, ANY, ANY, ANY],
        out_specs=[ANY] * 12,
        out_shape=[
            shape((depth, wide_q), bf16),
            shape((depth, wide_o), bf16),
            shape((depth, gu_weight.shape[2]), bf16),
            shape((depth, down_weight.shape[2]), bf16),
            shape((n, count, depth // n), bf16),
            shape((rows, depth), bf16),
            shape((rows, depth), f32),
            shape((2 * rows, depth), bf16),
            shape((2 * rows, depth), bf16),
            shape((4, quarter, wide_q), bf16),
            shape((pairs, quarter, LANES), f32),
            shape((2 * rows, wide_o), bf16),
        ],
        scratch_shapes=scratch,
        compiler_params=pltpu.CompilerParams(
            collective_id=3, has_side_effects=True, vmem_limit_bytes=62 << 20
        ),
        name="front",
    )(
        context, ctx_weight, inputs, gains, fold, spread,
        qkv_weight, out_weight, gu_weight, down_weight,
    )


def back_body(
    n, pair_two, home_grad, resid, gu_weight, down_half, out_weight, qkv_held, probs_held,
    gains, fold, spread,
    out_down, out_gate, out_up, out_up_stay, landed_down, landed_gate, out_mid, out_gain, out_pair, out_rows, out_qkv,
    two, grad, gu_full, down_full, out_full, two_away, two_stay, grad_away, grad_stay,
    hidden, grad_gu, send_down, send_gu, got_down, got_gu,
    values_mid, away, got, grad_rows, grad_mixed, qkv_mixed, probs, grad_qkv,
    send_sem, recv_sem, tile_send, tile_recv, local_sem,
):
    w = Where(n)
    wire, local = Wire(send_sem, recv_sem), Local(local_sem)
    tiled = Wire(tile_send, tile_recv)
    rows, depth = out_mid.shape
    both = 2 * rows
    piece = depth // n
    halfn = n // 2
    wide = down_full.shape[1]
    tile = 2 * LANES
    whole_tiles = wide // tile
    tiles = whole_tiles + (1 if wide % tile else 0)
    step = 64
    loads = [
        local.start(pair_two, two),
        local.start(gu_weight, gu_full),
    ]
    blocks = [
        pl.ds(pl.multiple_of((2 * b + w.near) * piece, piece), piece) for b in range(halfn)
    ]
    down_own = [local.start(down_half.at[at, :], down_full.at[at, :]) for at in blocks]
    late = [
        local.start(resid, values_mid),
        local.start(out_weight, out_full),
        local.start(qkv_held, qkv_mixed),
        local.start(probs_held, probs),
    ]
    greet(
        [w.along_stream(1), w.along_stream(2), w.along_frames(1)]
        + [w.along_frames(m) for m in w.masks]
        + [w.with_position(3), w.across()]
    )
    crossing = w.core != w.place
    cross = wire.make(home_grad, grad.at[:rows, :], w.across())
    stay = pltpu.make_async_copy(home_grad, grad.at[:rows, :], local_sem.at[15 + n])

    @pl.when(crossing)
    def _():
        cross.start()

    @pl.when(jnp.logical_not(crossing))
    def _():
        stay.start()

    neighbour = w.along_frames(1)
    down_near = [wire.start(down_half.at[at, :], down_full.at[at, :], neighbour) for at in blocks]

    def split(source, into_away, into_stay):
        for b in range(halfn):
            for ref, which in ((into_away, 1 - w.near), (into_stay, w.near)):
                at = pl.ds(pl.multiple_of((2 * b + which) * piece, piece), piece)
                ref[:, b * piece : (b + 1) * piece] = source[:, at]

    loads[0].wait()
    split(two, two_away, two_stay)
    loads[1].wait()

    def columns(start, size):
        return pl.ds(pl.multiple_of(start, LANES), size)

    def tile_parts(t):
        lo = t * tile
        return ((send_down, got_down, lo), (send_gu, got_gu, lo), (send_gu, got_gu, wide + lo))

    def move(t, size, j):
        ref, into, start = tile_parts(t)[j]
        at = columns(start, size)
        return tiled.make(ref.at[:, :, at], into.at[:, :, at], neighbour, 3 * t + j)

    def forward(t, size):
        lo = t * tile
        here = columns(lo, size)
        there = columns(wide + lo, size)

        @pl.loop(0, both // 256)
        def _(r):
            at = pl.ds(pl.multiple_of(r * 256, 256), 256)
            left = two[at, :]
            gate = jnp.dot(left, gu_full[:, here], preferred_element_type=f32)
            up = jnp.dot(left, gu_full[:, there], preferred_element_type=f32)
            hidden[at, here] = (gate / (1.0 + jnp.exp(-gate)) * up).astype(bf16)
            grad_gu[at, here] = gate.astype(bf16)
            grad_gu[at, there] = up.astype(bf16)

    def store_away(ref, left, right, at):
        value = dot_rows(left[...], right[:, at]).astype(bf16)
        for b in range(halfn):
            ref[b, :, at] = value[b * piece : (b + 1) * piece]

    def away_down(t, size):
        store_away(send_down, grad_away, hidden, columns(t * tile, size))
        move(t, size, 0).start()

    def backward(t, size):
        lo = t * tile
        here = columns(lo, size)
        there = columns(wide + lo, size)

        @pl.loop(0, both // 256)
        def _(r):
            at = pl.ds(pl.multiple_of(r * 256, 256), 256)
            gate = grad_gu[at, here].astype(f32)
            up = grad_gu[at, there].astype(f32)
            back = jnp.dot(grad[at, :], down_full[:, here], preferred_element_type=f32)
            sigma = 1.0 / (1.0 + jnp.exp(-gate))
            grad_gu[at, here] = (back * up * (sigma * (1.0 + gate * (1.0 - sigma)))).astype(bf16)
            grad_gu[at, there] = (back * (gate * sigma)).astype(bf16)

        store_away(send_gu, two_away, grad_gu, here)
        store_away(send_gu, two_away, grad_gu, there)
        move(t, size, 1).start()

    rest = wide - whole_tiles * tile

    def every(step_of):
        @pl.loop(0, whole_tiles)
        def _(t):
            step_of(t, tile)

        if rest:
            step_of(whole_tiles, rest)

    every(forward)

    @pl.when(crossing)
    def _():
        cross.wait_recv()

    @pl.when(jnp.logical_not(crossing))
    def _():
        stay.wait()

    grad_pair = wire.start(grad.at[:rows, :], grad.at[rows:, :], w.along_stream(1))
    grad_pair.wait_recv()
    split(grad, grad_away, grad_stay)
    every(away_down)
    for copy in down_own:
        copy.wait()
    for copy in down_near:
        copy.wait_recv()
    every(backward)

    landed = (landed_down, landed_gate)

    def landing(t, size, j, k):
        ref, _, start = tile_parts(t)[j]
        mask = w.masks[k]
        at = columns(start, size)
        return tiled.make(
            ref.at[flip(w.at, mask // 2), :, at],
            landed[j].at[mask // 2 - 1, :, columns(t * tile, size)],
            w.along_frames(mask),
            3 * tiles + (3 * t + j) * len(w.masks) + k,
        )

    lefts = (grad_stay, two_stay, two_stay)
    rights = (hidden, grad_gu, grad_gu)

    def reduce_part(t, size, j):
        ref, into, start = tile_parts(t)[j]
        at = columns(start, size)
        move(t, size, j).wait()
        value = dot_rows(lefts[j][...], rights[j][:, at])
        for b in range(halfn):
            total = value[b * piece : (b + 1) * piece] + into[b, :, at].astype(f32)
            ref[b, :, at] = total.astype(bf16)
        for k in range(len(w.masks)):
            landing(t, size, j, k).start()

    def reduce_down(t, size):
        reduce_part(t, size, 0)

    def reduce_gu(t, size):
        reduce_part(t, size, 1)

    def stay_up(t, size):
        at = columns(wide + t * tile, size)
        store_away(got_gu, two_stay, grad_gu, at)

    def some(step_of, lo, hi):
        top = min(hi, whole_tiles)
        if top > lo:

            @pl.loop(lo, top)
            def _(t):
                step_of(t, tile)

        if hi > whole_tiles and rest:
            step_of(whole_tiles, rest)

    cut = min(3, whole_tiles)

    def rows_of(position):
        quarter = both // 4
        return pl.ds(pl.multiple_of(position * quarter, quarter), quarter)

    def partial(left, right, t):
        at = pl.ds(pl.multiple_of(t * 256, 256), 256)
        return dot_columns(left[at, :], right[...])

    @pl.loop(0, rows // 256)
    def _(t):
        to = pl.ds(pl.multiple_of(t * 256, 256), 256)
        away[to, :] = partial(grad_gu, gu_full, rows // 256 + t).astype(bf16)

    first = wire.start(away, got, w.along_stream(1))

    @pl.loop(0, rows // 256)
    def _(t):
        to = pl.ds(pl.multiple_of(t * 256, 256), 256)
        out_mid[to, :] = partial(grad_gu, gu_full, t)

    some(reduce_down, 0, cut)

    late[0].wait()
    first.wait_recv()
    gain = gains[1:2, :]
    out_gain[...] = jnp.zeros_like(out_gain)

    @pl.loop(0, rows // step)
    def _(t):
        at = pl.ds(pl.multiple_of(t * step, step), step)
        grad_normed = out_mid[at, :] + got[at, :].astype(f32)
        values = values_mid[at, :]
        scale = lax.rsqrt(jnp.mean(values * values, axis=-1, keepdims=True) + norm_eps)
        weighted = grad_normed * gain
        inner = jnp.mean(weighted * values, axis=-1, keepdims=True)
        total = grad[at, :].astype(f32) + scale * weighted
        total = total - values * (scale * scale * scale * inner)
        out_mid[at, :] = total
        two[at, :] = total.astype(bf16)
        out_gain[...] += jnp.sum(grad_normed * values * scale, axis=0, keepdims=True)

    second = wire.start(two.at[:rows, :], two.at[rows:, :], w.along_stream(1))
    late[1].wait()

    def back_rows(lo, hi):
        @pl.loop(lo, hi)
        def _(t):
            at = pl.ds(pl.multiple_of(t * 256, 256), 256)
            value = jnp.dot(two[at, :], out_full[...], preferred_element_type=f32)
            grad_rows[at, :] = value.astype(bf16)

    back_rows(0, rows // 256)
    second.wait_recv()
    back_rows(rows // 256, both // 256)
    mixing = {}
    for mask in (3, 1, 2):
        mixing[mask] = wire.start(
            grad_rows.at[rows_of(flip(w.position, mask)), :],
            grad_mixed.at[w.position],
            w.with_position(mask),
        )
    own = local.start(grad_rows.at[rows_of(w.position), :], grad_mixed.at[w.position])
    store_pair = local.start(two, out_pair)

    some(reduce_down, cut, tiles)
    own.wait()
    late[2].wait()
    late[3].wait()
    for mask in (2, 1, 3):
        mixing[mask].wait_recv()
    fold_held, spread_held = fold[...], spread[...]

    @pl.loop(0, both // 4 // step)
    def _(t):
        at = pl.ds(pl.multiple_of(t * step, step), step)
        attention_backward_rows(
            at, qkv_mixed, probs, grad_mixed, fold_held, spread_held, grad_qkv
        )

    returning = {}
    for mask in (3, 1, 2):
        returning[mask] = wire.start(
            grad_qkv.at[flip(w.position, mask)],
            out_qkv.at[rows_of(w.position), :],
            w.with_position(mask),
        )
    own_back = local.start(grad_qkv.at[w.position], out_qkv.at[rows_of(w.position), :])
    early = min(2, whole_tiles)
    some(reduce_gu, 0, early)
    some(stay_up, 0, tiles)

    wire.sent(first)

    @pl.loop(0, rows // 256)
    def _(t):
        to = pl.ds(pl.multiple_of(t * 256, 256), 256)
        away[to, :] = partial(hidden, down_full, rows // 256 + t).astype(bf16)

    third = wire.start(away, got, w.along_stream(1))

    @pl.loop(0, rows // 256)
    def _(t):
        to = pl.ds(pl.multiple_of(t * 256, 256), 256)
        values_mid[to, :] = values_mid[to, :] + partial(hidden, down_full, t)

    third.wait_recv()

    @pl.loop(0, rows // step)
    def _(t):
        at = pl.ds(pl.multiple_of(t * step, step), step)
        out_rows[at, :] = (values_mid[at, :] + got[at, :].astype(f32)).astype(bf16)

    some(reduce_gu, early, tiles)
    kept = [
        local.start(send_down.at[w.at], out_down),
        local.start(send_gu.at[w.at, :, :wide], out_gate),
        local.start(send_gu.at[:, :, wide:], out_up),
        local.start(got_gu.at[:, :, wide:], out_up_stay),
    ]
    own_back.wait()
    store_pair.wait()
    for mask in (2, 1, 3):
        returning[mask].wait_recv()
    for t in range(tiles):
        for j in range(2):
            for k in range(len(w.masks)):
                landing(t, tile if t < whole_tiles else rest, j, k).wait()
    for copy in kept:
        copy.wait()

    @pl.when(crossing)
    def _():
        cross.wait_send()

    wire.finish()


def back_scratch(n, rows, depth, wide, head_width):
    both, halfn, piece = 2 * rows, n // 2, depth // n
    pairs = len(PAIRS)
    quarter = both // 4
    shapes = [
        ((both, depth), bf16),
        ((both, depth), bf16),
        ((depth, 2 * wide), bf16),
        ((depth, wide), bf16),
        ((depth, head_width), bf16),
        ((both, depth // 2), bf16),
        ((both, depth // 2), bf16),
        ((both, depth // 2), bf16),
        ((both, depth // 2), bf16),
        ((both, wide), bf16),
        ((both, 2 * wide), bf16),
        ((halfn, piece, wide), bf16),
        ((halfn, piece, 2 * wide), bf16),
        ((halfn, piece, wide), bf16),
        ((halfn, piece, 2 * wide), bf16),
        ((rows, depth), f32),
        ((rows, depth), bf16),
        ((rows, depth), bf16),
        ((both, head_width), bf16),
        ((4, quarter, head_width), bf16),
        ((4, quarter, 3 * head_width), bf16),
        ((pairs, quarter, LANES), f32),
        ((4, quarter, 3 * head_width), bf16),
    ]
    outs = [((rows, depth), f32), ((rows, depth), bf16)]
    return shapes, sum(math.prod(dims) * jnp.dtype(kind).itemsize for dims, kind in shapes + outs)


def back(
    n, pair_two, home_grad, resid, gu_full, down_half, out_full, qkv_mixed, probs, gains
):
    rows, depth = resid.shape
    wide, head_width = down_half.shape[1], out_full.shape[1]
    shapes, _ = back_scratch(n, rows, depth, wide, head_width)
    tiles = -(-wide // (2 * LANES))
    fold, spread = fold_matrices(head_width)
    shape = jax.ShapeDtypeStruct
    moves = 3 * tiles * (1 + n // 2 - 1)
    return pl.pallas_call(
        functools.partial(back_body, n),
        in_specs=[ANY] * 8 + [VMEM] * 3,
        out_specs=[ANY, ANY, ANY, ANY, ANY, ANY, VMEM, VMEM, ANY, VMEM, ANY],
        out_shape=[
            shape((depth // n, wide), bf16),
            shape((depth // n, wide), bf16),
            shape((n // 2, depth // n, wide), bf16),
            shape((n // 2, depth // n, wide), bf16),
            shape((n // 2 - 1, depth // n, wide), bf16),
            shape((n // 2 - 1, depth // n, wide), bf16),
            shape((rows, depth), f32),
            shape((1, depth), f32),
            shape((2 * rows, depth), bf16),
            shape((rows, depth), bf16),
            shape((2 * rows, 3 * head_width), bf16),
        ],
        scratch_shapes=[pltpu.VMEM(dims, kind) for dims, kind in shapes]
        + [
            pltpu.SemaphoreType.DMA((16 + 2 * n,)),
            pltpu.SemaphoreType.DMA((16 + 2 * n,)),
            pltpu.SemaphoreType.DMA((moves,)),
            pltpu.SemaphoreType.DMA((moves,)),
            pltpu.SemaphoreType.DMA((16 + n,)),
        ],
        compiler_params=pltpu.CompilerParams(
            collective_id=4, has_side_effects=True, vmem_limit_bytes=67_000_000
        ),
        name="back",
    )(
        pair_two, home_grad, resid, gu_full, down_half, out_full, qkv_mixed, probs,
        gains, fold, spread,
    )


def settled(own, landed, place):
    total, other = own.astype(f32), None
    for k in range(landed.shape[0]):
        value = landed[k].astype(f32)
        if (k + 1) & 1:
            other = value if other is None else other + value
        else:
            total = total + value
    return jnp.where(place == 0, jnp.stack([total, other]), jnp.stack([other, total]))


def shards(
    inputs,
    context,
    cotangent,
    live_frames,
    ctx_weight,
    norm_gains,
    qkv_weight,
    out_weight,
    gate_up_weight,
    down_weight,
):
    n = lax.axis_size("frames")
    stream_index = lax.axis_index("stream")
    frame_index = lax.axis_index("frames")
    half_index = stream_index % 2
    place = (frame_index // 2) % 2
    position = (stream_index // 2) * 2 + place
    frame_count = inputs.shape[0]
    width_model = inputs.shape[2]
    offsets = lax.broadcasted_iota(jnp.int32, (frame_count,), 0)
    valid_mask = (offsets % SLOT < jnp.repeat(live_frames, SLOT)).astype(f32)[:, None]
    gain_one = norm_gains[0]
    gain_two = norm_gains[1]

    grad_rows = (cotangent[:, 0] * valid_mask).astype(bf16)
    (
        qkv_full,
        out_full,
        gate_up_full,
        down_half,
        ctx_pieces,
        resid_in,
        resid_mid,
        paired_one,
        paired_two,
        qkv_mixed,
        probs,
        mixed,
    ) = front(
        n,
        context,
        ctx_weight,
        inputs[:, 0],
        norm_gains,
        qkv_weight[0],
        out_weight[0],
        gate_up_weight[0],
        down_weight[0],
    )
    near = frame_index % 2

    def paired(mine):
        return jnp.concatenate([mine, swap_stream(mine, 1)], axis=0)

    def own_sum(partial_value):
        return partial_value[:frame_count] + swap_stream(
            partial_value[frame_count:].astype(bf16), 1
        ).astype(f32)

    def rows_times(left, right):
        return jnp.dot(left, right, preferred_element_type=f32)

    def rows_back(left, right):
        return lax.dot_general(left, right, (((1,), (1,)), ((), ())), preferred_element_type=f32)

    def returned(value):
        _, quarter, width = value.shape
        out = jnp.zeros((4, quarter, width), value.dtype)
        own = lax.dynamic_index_in_dim(value, position, 0, keepdims=False)
        out = lax.dynamic_update_index_in_dim(out, own, position, 0)
        for mask in (2, 1, 3):
            there = position ^ mask
            got = peer(lax.dynamic_index_in_dim(value, there, 0, keepdims=False), mask)
            out = lax.dynamic_update_index_in_dim(out, got, there, 0)
        return out.reshape(4 * quarter, width)

    head_width = out_full.shape[1]
    _, needed = back_scratch(n, frame_count, width_model, down_weight.shape[3], head_width)
    if needed <= 66_000_000 and (width_model // n) % LANES == 0:
        (
            own_down,
            own_gate,
            up_send,
            up_stay,
            landed_down,
            landed_gate,
            grad_mid,
            grad_gain_two,
            paired_grad_attn,
            result_rows,
            grad_qkv_low,
        ) = back(
            n,
            paired_two,
            grad_rows,
            resid_mid,
            gate_up_full,
            down_half,
            out_full,
            qkv_mixed,
            probs,
            norm_gains,
        )
        sum_down = settled(own_down, landed_down, place)
    else:
        paired_grad_ffn = paired(transposed(grad_rows))
        blocks = down_half.reshape(n // 2, 2, -1, down_half.shape[1])
        blocks = lax.dynamic_index_in_dim(blocks, near, 1, keepdims=False)
        others = swap_frames(blocks, 1)
        even, odd = jnp.where(near == 0, blocks, others), jnp.where(near == 0, others, blocks)
        down_full = jnp.stack([even, odd], axis=1).reshape(down_half.shape)
        scale_two = norm_scale(resid_mid)
        gate_up = rows_times(paired_two, gate_up_full)
        ffn_half = down_full.shape[1]
        gate_part = gate_up[:, :ffn_half]
        up_part = gate_up[:, ffn_half:]
        sigmoid_gate = jax.nn.sigmoid(gate_part)
        activated = gate_part * sigmoid_gate
        hidden = (activated * up_part).astype(bf16)

        grad_res = paired_grad_ffn[:frame_count]
        sum_down = scattered(halves(paired_grad_ffn, near), hidden, frame_index, place)
        grad_hidden = rows_times(paired_grad_ffn, down_full)
        grad_gate = grad_hidden * up_part * (sigmoid_gate * (1.0 + gate_part * (1.0 - sigmoid_gate)))
        grad_up = grad_hidden * activated
        grad_gu_low = jnp.concatenate([grad_gate, grad_up], axis=-1).astype(bf16)
        grad_normed_two = own_sum(rows_back(grad_gu_low, gate_up_full))
        sum_gate_up = scattered(halves(paired_two, near), grad_gu_low, frame_index, place)
        back_two, grad_gain_two = norm_back(resid_mid, scale_two, gain_two, grad_normed_two)
        grad_mid = grad_res.astype(f32) + back_two
        paired_grad_attn = paired(grad_mid.astype(bf16))
        grad_mixed = rows_times(paired_grad_attn, out_full).astype(bf16)
        grad_qkv_mixed = attention_backward(qkv_mixed, probs, exchange_rows(grad_mixed, position))
        grad_qkv_low = returned(grad_qkv_mixed)
        result_rows = (resid_mid + own_sum(rows_back(hidden, down_full))).astype(bf16)
        grad_gain_two = grad_gain_two[None]

    wide_q = qkv_full.shape[1]
    count = ctx_pieces.shape[1]
    _, needed = ending_scratch(
        n, frame_count, width_model, context.shape, count, wide_q, head_width, down_half.shape[1]
    )
    if needed <= 66_000_000 and (width_model // n) % LANES == 0:
        (
            own_qkv,
            own_out,
            own_up,
            landed_qkv,
            landed_out,
            landed_up,
            grad_home,
            result,
            sum_context,
            ctx_total,
        ) = ending(
            n,
            resid_in,
            grad_mid,
            norm_gains,
            grad_gain_two,
            result_rows,
            valid_mask,
            paired_one,
            paired_grad_attn,
            mixed,
            grad_qkv_low,
            qkv_full,
            context,
            ctx_pieces,
            up_send,
            up_stay,
        )
        sum_gate_up = jnp.concatenate(
            [settled(own_gate, landed_gate, place), settled(own_up, landed_up, place)], axis=-1
        )
        sum_qkv = settled(own_qkv, landed_qkv, place)
        sum_out = settled(own_out, landed_out, place)
    else:

        def parts(left, right):
            away, stay = halves(left, near)
            block = width_model // n
            return [
                dot_rows(part, right).astype(bf16).reshape(n // 2, block, right.shape[1])
                for part in (away, stay)
            ]

        part_away = rows_back(grad_qkv_low[frame_count:], qkv_full).astype(bf16)
        part_stay = rows_back(grad_qkv_low[:frame_count], qkv_full)
        sum_qkv, sum_out, grad_home, result, sum_context, ctx_total = tail(
            n,
            part_away,
            part_stay,
            resid_in,
            grad_mid,
            norm_gains,
            grad_gain_two,
            result_rows,
            *parts(paired_one, grad_qkv_low),
            *parts(paired_grad_attn, mixed),
            context,
            ctx_pieces.transpose(1, 0, 2).reshape(-1, width_model),
        )
        result = (result.astype(f32) * valid_mask)[:, None]
        grad_home = grad_home[:, None]
    ctx_total = ctx_total.T
    sum_ctx = ctx_total[: ctx_weight.shape[0]]
    sum_gains = ctx_total[ctx_weight.shape[0] : ctx_weight.shape[0] + 2]

    return (
        result,
        grad_home,
        sum_context,
        sum_ctx,
        sum_gains,
        sum_qkv[None],
        sum_out[None],
        sum_gate_up[None],
        sum_down[None],
    )


def solution(mesh):
    placed = (
        P("frames", "stream", None),
        P("frames", None),
        P("frames", "stream", None),
        P("frames"),
        P(None, "frames"),
        P(),
        P("stream", None, "frames", None),
        P("stream", None, "frames", None),
        P("stream", None, "frames", None),
        P("stream", None, "frames", None),
    )
    return jax.shard_map(
        shards,
        mesh=mesh,
        in_specs=placed,
        out_specs=(
            P("frames", "stream", None),
            P("frames", "stream", None),
            P("frames", "stream"),
            P(None, ("stream", "frames")),
            P(None, ("stream", "frames")),
            P("stream", None, "frames", None),
            P("stream", None, "frames", None),
            P("stream", None, "frames", None),
            P("stream", None, "frames", None),
        ),
        check_vma=False,
    )
```

```python
import functools
import math

import jax
import jax.numpy as jnp
import numpy as np
from jax import lax
from jax.experimental import pallas as pl
from jax.experimental.pallas import tpu as pltpu
from jax.sharding import PartitionSpec as P

HD = 64
SLOT = 128
LANES = 128
norm_eps = 1e-05
f32 = jnp.float32
bf16 = jnp.bfloat16

PAIRS = [(q, k) for q in range(4) for k in range(q + 1)]


ANY = pl.BlockSpec(memory_space=pl.ANY)
VMEM = pl.BlockSpec(memory_space=pltpu.VMEM)
EXTRA = 32


def flip(value, mask):
    bit = 1
    while bit <= mask:
        if mask & bit:
            value = value + bit - 2 * bit * ((value // bit) % 2)
        bit *= 2
    return value


class Where:
    def __init__(self, n):
        self.n = n
        self.stream = lax.axis_index("stream")
        self.frame = lax.axis_index("frames")
        self.core = self.stream % 2
        self.place = (self.frame // 2) % 2
        self.position = (self.stream // 2) * 2 + self.place
        self.near = self.frame % 2
        self.at = self.frame // 2
        self.far_masks = [m for m in range(2, n, 2) if not m & 2]
        self.both_masks = [m for m in range(2, n, 2) if m & 2 and m > 2]
        self.masks = self.far_masks + self.both_masks + [2]

    def along_stream(self, mask):
        return (flip(self.stream, mask), self.frame)

    def along_frames(self, mask):
        return (self.stream, flip(self.frame, mask))

    def with_position(self, mask):
        return (flip(self.stream, mask & 2), flip(self.frame, 2 * (mask & 1)))

    def across(self):
        return (flip(self.stream, 1), flip(self.frame, 2))


class Wire:
    def __init__(self, send, recv):
        self.send, self.recv, self.count, self.started = send, recv, 0, []

    def make(self, src, dst, device, index=None):
        k = self.count if index is None else index
        if index is None:
            self.count += 1
        return pltpu.make_async_remote_copy(
            src_ref=src,
            dst_ref=dst,
            send_sem=self.send.at[k],
            recv_sem=self.recv.at[k],
            device_id=device,
            device_id_type=pl.DeviceIdType.MESH,
        )

    def start(self, src, dst, device):
        copy = self.make(src, dst, device)
        copy.start()
        self.started.append(copy)
        return copy

    def sent(self, copy):
        self.started = [c for c in self.started if c is not copy]
        copy.wait_send()

    def finish(self):
        for copy in self.started:
            copy.wait_send()


class Local:
    def __init__(self, sems):
        self.sems, self.count = sems, 0

    def start(self, src, dst):
        copy = pltpu.make_async_copy(src, dst, self.sems.at[self.count])
        self.count += 1
        copy.start()
        return copy


def greet(devices):
    barrier = pltpu.get_barrier_semaphore()
    for device in devices:
        pl.semaphore_signal(
            barrier, inc=1, device_id=device, device_id_type=pl.DeviceIdType.MESH
        )
    pl.semaphore_wait(barrier, len(devices))


def dot_rows(left, right):
    return lax.dot_general(left, right, (((0,), (0,)), ((), ())), preferred_element_type=f32)


def dot_columns(left, right):
    return lax.dot_general(left, right, (((1,), (1,)), ((), ())), preferred_element_type=f32)


class Reduction:
    def __init__(self, w, wire, send, keep, arrived, sums, landed, out):
        self.w, self.wire = w, wire
        self.send, self.keep, self.arrived = send, keep, arrived
        self.sums, self.landed, self.out = sums, landed, out
        self.first, self.second = {}, {}
        self.order = w.masks + [0]

    def begin(self, mask):
        block = flip(self.w.at, mask // 2)
        self.first[mask] = self.wire.start(
            self.send.at[block], self.arrived.at[block], self.w.along_frames(1)
        )

    def forward(self, mask):
        block = flip(self.w.at, mask // 2)
        self.first[mask].wait_recv()
        self.wire.sent(self.first[mask])
        total = self.keep[block].astype(f32) + self.arrived[block].astype(f32)
        self.sums[block] = total.astype(bf16)
        if mask:
            self.second[mask] = self.wire.start(
                self.sums.at[block], self.landed.at[mask // 2 - 1], self.w.along_frames(mask)
            )

    def land(self):
        for copy in self.second.values():
            copy.wait_recv()

    def close(self):
        own, other = self.sums[self.w.at].astype(f32), None
        for mask in self.w.masks:
            self.second[mask].wait_recv()
            got = self.landed[mask // 2 - 1].astype(f32)
            if mask & 2:
                other = got if other is None else other + got
            else:
                own = own + got
        self.out[self.w.place] = own
        self.out[1 - self.w.place] = other


def tail_body(
    n, part_send, part_own, resid, mid, gains, gain_two, result_rows,
    gq_send, gq_keep, go_send, go_keep, context, ctx_full,
    out_q, out_o, out_grad, out_result, out_context, out_ctx,
    part_got, low, home, partner_half, half_sum, far_half, whole, kept_q, kept_o,
    arrived_q, arrived_o, sums_q, sums_o, landed_q, landed_o,
    context_held, ctx_held, term, term_got, term_sum, term_landed, gain_sum,
    send_sem, recv_sem, local_sem,
):
    w = Where(n)
    wire, local = Wire(send_sem, recv_sem), Local(local_sem)
    rows, depth = resid.shape
    crossing = w.core != w.place
    load_q = local.start(gq_keep, kept_q)
    load_o = local.start(go_keep, kept_o)
    load_context = local.start(context, context_held)
    load_ctx = local.start(ctx_full, ctx_held)
    greet(
        [w.along_stream(1), w.along_stream(2), w.along_frames(1)]
        + [w.along_frames(m) for m in w.masks]
        + [w.across()]
    )
    part = wire.start(part_send, part_got, w.along_stream(1))
    red_o = Reduction(w, wire, go_send, kept_o, arrived_o, sums_o, landed_o, out_o)
    red_q = Reduction(w, wire, gq_send, kept_q, arrived_q, sums_q, landed_q, out_q)
    for mask in red_o.order:
        red_o.begin(mask)
    for mask in red_q.order:
        red_q.begin(mask)

    part.wait_recv()
    gain = gains[0:1, :]
    gain_sum[...] = jnp.zeros_like(gain_sum)
    step = 64

    @pl.loop(0, rows // step)
    def _(t):
        at = pl.ds(pl.multiple_of(t * step, step), step)
        grad = part_own[at, :].astype(f32) + part_got[at, :].astype(f32)
        values = resid[at, :].astype(f32)
        scale = lax.rsqrt(jnp.mean(values * values, axis=-1, keepdims=True) + norm_eps)
        weighted = grad * gain
        inner = jnp.mean(weighted * values, axis=-1, keepdims=True)
        back = scale * weighted - values * (scale * scale * scale * inner)
        low[at, :] = (mid[at, :] + back).astype(bf16)
        gain_sum[...] += jnp.sum(grad * values * scale, axis=0, keepdims=True)

    row = lax.broadcasted_iota(jnp.int32, (EXTRA, depth), 0)
    low[rows:, :] = jnp.where(
        row == 0, gain_sum[...], jnp.where(row == 1, gain_two[...], 0.0)
    ).astype(bf16)

    cross = wire.make(low, home, w.across())
    cross_result = wire.make(result_rows, out_result, w.across())

    @pl.when(crossing)
    def _():
        cross.start()

    load_o.wait()
    load_q.wait()
    for mask in red_o.order:
        red_o.forward(mask)

    @pl.when(crossing)
    def _():
        cross_result.start()
        cross.wait_recv()

    stay = pltpu.make_async_copy(low, home, local.sems.at[4])
    stay_result = pltpu.make_async_copy(result_rows, out_result, local.sems.at[5])

    @pl.when(jnp.logical_not(crossing))
    def _():
        stay.start()
        stay_result.start()
        stay.wait()

    half = (rows + EXTRA) // 2
    mine = pl.ds(pl.multiple_of(w.core * half, 16), half)
    theirs = pl.ds(pl.multiple_of((1 - w.core) * half, 16), half)
    first = wire.start(home.at[theirs, :], partner_half, w.along_stream(1))
    out_grad[...] = home[:rows, :].astype(f32)
    first.wait_recv()
    half_sum[...] = (home[mine, :].astype(f32) + partner_half[...].astype(f32)).astype(bf16)
    second = wire.start(half_sum, far_half, w.along_stream(2))
    red_q.forward(red_q.order[0])
    red_q.forward(red_q.order[1])
    second.wait_recv()
    whole[mine, :] = (half_sum[...].astype(f32) + far_half[...].astype(f32)).astype(bf16)
    third = wire.start(whole.at[mine, :], whole.at[mine, :], w.along_stream(1))
    load_context.wait()
    third.wait_recv()

    share = depth // 4
    columns = pl.ds(pl.multiple_of(w.stream * share, LANES), share)
    block = share // n
    wide = context_held.shape[1]
    pieces = 2
    grad_share = whole[:rows, columns]
    firsts, seconds = [], []
    row = lax.broadcasted_iota(jnp.int32, (EXTRA, LANES), 0)
    select = (row == lax.broadcasted_iota(jnp.int32, (EXTRA, LANES), 1)).astype(bf16)
    edges = [wide * p // pieces for p in range(pieces)] + [wide + LANES]
    for p in range(pieces):
        lo, hi = edges[p], edges[p + 1]
        for at in range(lo, min(hi, wide), 1024):
            to = min(at + 1024, wide)
            value = dot_rows(grad_share, context_held[:, at:to]).astype(bf16)
            for k in range(n):
                term[k // 2, k % 2, :, at:to] = value[k * block : (k + 1) * block]
        if hi > wide:
            value = dot_rows(whole[rows:, columns], select).astype(bf16)
            for k in range(n):
                term[k // 2, k % 2, :, wide:hi] = value[k * block : (k + 1) * block]
        firsts.append(
            wire.start(
                term.at[:, 1 - w.near, :, lo:hi], term_got.at[:, :, lo:hi], w.along_frames(1)
            )
        )
    for mask in red_q.order[2:]:
        red_q.forward(mask)
    load_ctx.wait()

    def context_rows(t):
        at = pl.ds(pl.multiple_of(t * LANES, LANES), LANES)
        out_context[at, :] = dot_columns(whole[at, :], ctx_held[...])

    @pl.loop(0, rows // LANES)
    def _(t):
        context_rows(t)

    for p in range(pieces):
        lo, hi = edges[p], edges[p + 1]
        firsts[p].wait_recv()
        for mask in w.masks + [0]:
            to = flip(w.at, mask // 2)
            total = term[to, w.near, :, lo:hi].astype(f32) + term_got[to, :, lo:hi].astype(f32)
            term_sum[to, :, lo:hi] = total.astype(bf16)
            if mask:
                seconds.append(
                    wire.start(
                        term_sum.at[to, :, lo:hi],
                        term_landed.at[mask // 2, :, lo:hi],
                        w.along_frames(mask),
                    )
                )
    red_o.close()
    red_q.close()

    @pl.when(crossing)
    def _():
        cross_result.wait_recv()
        cross.wait_send()
        cross_result.wait_send()

    @pl.when(jnp.logical_not(crossing))
    def _():
        stay_result.wait()

    for copy in seconds:
        copy.wait_recv()
    total = term_sum[w.at].astype(f32)
    for mask in w.masks:
        total = total + term_landed[mask // 2].astype(f32)
    out_ctx[...] = total
    wire.finish()


def tail(
    n, part_send, part_own, resid, mid, gains, gain_two, result_rows,
    gq_send, gq_keep, go_send, go_keep, context, ctx_full,
):
    rows, depth = resid.shape
    halfn, block, wide_q = gq_send.shape
    wide_o = go_send.shape[2]
    share = depth // 4 // n
    wide = context.shape[1] + LANES
    half = (rows + EXTRA) // 2
    count = 64 + 2 * n
    scratch = [
        pltpu.VMEM((rows, depth), bf16),
        pltpu.VMEM((rows + EXTRA, depth), bf16),
        pltpu.VMEM((rows + EXTRA, depth), bf16),
        pltpu.VMEM((half, depth), bf16),
        pltpu.VMEM((half, depth), bf16),
        pltpu.VMEM((half, depth), bf16),
        pltpu.VMEM((rows + EXTRA, depth), bf16),
        pltpu.VMEM((halfn, block, wide_q), bf16),
        pltpu.VMEM((halfn, block, wide_o), bf16),
        pltpu.VMEM((halfn, block, wide_q), bf16),
        pltpu.VMEM((halfn, block, wide_o), bf16),
        pltpu.VMEM((halfn, block, wide_q), bf16),
        pltpu.VMEM((halfn, block, wide_o), bf16),
        pltpu.VMEM((halfn, block, wide_q), bf16),
        pltpu.VMEM((halfn, block, wide_o), bf16),
        pltpu.VMEM(context.shape, bf16),
        pltpu.VMEM(ctx_full.shape, bf16),
        pltpu.VMEM((halfn, 2, share, wide), bf16),
        pltpu.VMEM((halfn, share, wide), bf16),
        pltpu.VMEM((halfn, share, wide), bf16),
        pltpu.VMEM((halfn, share, wide), bf16),
        pltpu.VMEM((1, depth), f32),
        pltpu.SemaphoreType.DMA((count,)),
        pltpu.SemaphoreType.DMA((count,)),
        pltpu.SemaphoreType.DMA((6,)),
    ]
    return pl.pallas_call(
        functools.partial(tail_body, n),
        in_specs=[ANY, VMEM, VMEM, VMEM, VMEM, VMEM, VMEM, ANY, ANY, ANY, ANY, ANY, ANY],
        out_specs=[VMEM, VMEM, VMEM, VMEM, VMEM, VMEM],
        out_shape=[
            jax.ShapeDtypeStruct((2, block, wide_q), f32),
            jax.ShapeDtypeStruct((2, block, wide_o), f32),
            jax.ShapeDtypeStruct((rows, depth), f32),
            jax.ShapeDtypeStruct((rows, depth), bf16),
            jax.ShapeDtypeStruct((rows, ctx_full.shape[0]), f32),
            jax.ShapeDtypeStruct((share, wide), f32),
        ],
        scratch_shapes=scratch,
        compiler_params=pltpu.CompilerParams(
            collective_id=5, has_side_effects=True, vmem_limit_bytes=60 << 20
        ),
        name="tail",
    )(
        part_send, part_own, resid, mid, gains, gain_two, result_rows,
        gq_send, gq_keep, go_send, go_keep, context, ctx_full,
    )


def ending_body(
    n, resid, mid, gains, gain_two, result_rows,
    pair_one, pair_grad, mixed_rows, grad_qkv_rows, qkv_weight, context, ctx_pieces, up_send, up_stay,
    out_q, out_o, out_up, landed_q, landed_o, landed_up, out_grad, out_result, out_context, out_ctx,
    one, grad_two, mixed, grad_qkv, qkv_full, left_away, left_stay, part_send, part_own,
    part_got, low, home, partner_half, half_sum, far_half, whole, result_home,
    send_q, send_o, kept_q, kept_o, arrived_q, arrived_o, send_up, kept_up, arrived_up,
    context_held, ctx_held, term, term_got, term_sum, term_landed, gain_sum,
    send_sem, recv_sem, local_sem,
):
    w = Where(n)
    wire, local = Wire(send_sem, recv_sem), Local(local_sem)
    rows, depth = resid.shape
    piece = depth // n
    crossing = w.core != w.place
    load_up = local.start(up_send, send_up)
    load_grad = local.start(pair_grad, grad_two)
    load_mixed = local.start(mixed_rows, mixed)
    load_qkv = local.start(grad_qkv_rows, grad_qkv)
    load_weight = local.start(qkv_weight, qkv_full)
    load_one = local.start(pair_one, one)
    load_up_stay = local.start(up_stay, kept_up)
    load_context = local.start(context, context_held)
    load_ctx = [
        local.start(ctx_pieces.at[k], ctx_held.at[:, k * piece : (k + 1) * piece])
        for k in range(n)
    ]
    greet(
        [w.along_stream(1), w.along_stream(2), w.along_frames(1)]
        + [w.along_frames(m) for m in w.masks]
        + [w.across()]
    )
    cross_result = wire.make(result_rows, result_home, w.across())
    stay_result = pltpu.make_async_copy(result_rows, result_home, local.sems.at[30])
    stay = pltpu.make_async_copy(low, home, local.sems.at[31])

    @pl.when(crossing)
    def _():
        cross_result.start()

    @pl.when(jnp.logical_not(crossing))
    def _():
        stay_result.start()

    def split(source, which, into):
        for b in range(n // 2):
            at = pl.ds(pl.multiple_of((2 * b + which) * piece, piece), piece)
            into[:, b * piece : (b + 1) * piece] = source[:, at]

    def product(left, right, into):
        wide = right.shape[1]
        for lo in range(0, wide, 512):
            value = dot_rows(left[...], right[:, lo : lo + 512]).astype(bf16)
            for b in range(n // 2):
                into[b, :, lo : lo + 512] = value[b * piece : (b + 1) * piece]

    def partial(t):
        at = pl.ds(pl.multiple_of(t * 256, 256), 256)
        return dot_columns(grad_qkv[at, :], qkv_full[...])

    load_up.wait()
    red_up = Reduction(w, wire, send_up, kept_up, arrived_up, send_up, landed_up, out_up)
    for mask in red_up.order:
        red_up.begin(mask)
    load_grad.wait()
    split(grad_two, 1 - w.near, left_away)
    load_mixed.wait()
    product(left_away, mixed, send_o)
    red_o = Reduction(w, wire, send_o, kept_o, arrived_o, send_o, landed_o, out_o)
    for mask in red_o.order:
        red_o.begin(mask)
    load_qkv.wait()
    load_weight.wait()

    @pl.loop(0, rows // 256)
    def _(t):
        to = pl.ds(pl.multiple_of(t * 256, 256), 256)
        part_send[to, :] = partial(rows // 256 + t).astype(bf16)

    part = wire.start(part_send, part_got, w.along_stream(1))
    load_one.wait()
    split(one, 1 - w.near, left_away)
    product(left_away, grad_qkv, send_q)
    red_q = Reduction(w, wire, send_q, kept_q, arrived_q, send_q, landed_q, out_q)
    for mask in red_q.order:
        red_q.begin(mask)

    @pl.loop(0, rows // 256)
    def _(t):
        to = pl.ds(pl.multiple_of(t * 256, 256), 256)
        part_own[to, :] = partial(t)

    part.wait_recv()
    gain = gains[0:1, :]
    gain_sum[...] = jnp.zeros_like(gain_sum)
    step = 64

    @pl.loop(0, rows // step)
    def _(t):
        at = pl.ds(pl.multiple_of(t * step, step), step)
        grad = part_own[at, :].astype(f32) + part_got[at, :].astype(f32)
        values = resid[at, :].astype(f32)
        scale = lax.rsqrt(jnp.mean(values * values, axis=-1, keepdims=True) + norm_eps)
        weighted = grad * gain
        inner = jnp.mean(weighted * values, axis=-1, keepdims=True)
        back = scale * weighted - values * (scale * scale * scale * inner)
        low[at, :] = (mid[at, :] + back).astype(bf16)
        gain_sum[...] += jnp.sum(grad * values * scale, axis=0, keepdims=True)

    row = lax.broadcasted_iota(jnp.int32, (EXTRA, depth), 0)
    low[rows:, :] = jnp.where(
        row == 0, gain_sum[...], jnp.where(row == 1, gain_two[...], 0.0)
    ).astype(bf16)

    cross = wire.make(low, home, w.across())

    @pl.when(crossing)
    def _():
        cross.start()

    split(grad_two, w.near, left_stay)
    product(left_stay, mixed, kept_o)
    load_up_stay.wait()
    for mask in red_up.order[:2]:
        red_up.forward(mask)
    for mask in red_o.order:
        red_o.forward(mask)

    @pl.when(crossing)
    def _():
        cross_result.wait_recv()

    @pl.when(jnp.logical_not(crossing))
    def _():
        stay.start()
        stay_result.wait()

    split(one, w.near, left_stay)
    product(left_stay, grad_qkv, kept_q)
    store_result = local.start(result_home, out_result)

    @pl.when(crossing)
    def _():
        cross.wait_recv()

    @pl.when(jnp.logical_not(crossing))
    def _():
        stay.wait()

    half = (rows + EXTRA) // 2
    mine = pl.ds(pl.multiple_of(w.core * half, 16), half)
    theirs = pl.ds(pl.multiple_of((1 - w.core) * half, 16), half)
    first = wire.start(home.at[theirs, :], partner_half, w.along_stream(1))
    store_grad = local.start(home.at[:rows, :], out_grad)
    for mask in red_up.order[2:]:
        red_up.forward(mask)
    first.wait_recv()
    half_sum[...] = (home[mine, :].astype(f32) + partner_half[...].astype(f32)).astype(bf16)
    second = wire.start(half_sum, far_half, w.along_stream(2))
    red_q.forward(red_q.order[0])
    red_q.forward(red_q.order[1])
    second.wait_recv()
    whole[mine, :] = (half_sum[...].astype(f32) + far_half[...].astype(f32)).astype(bf16)
    third = wire.start(whole.at[mine, :], whole.at[mine, :], w.along_stream(1))
    load_context.wait()
    third.wait_recv()

    share = depth // 4
    columns = pl.ds(pl.multiple_of(w.stream * share, LANES), share)
    block = share // n
    wide = context_held.shape[1]
    pieces = 4
    grad_share = whole[:rows, columns]
    firsts, seconds = [], []
    row = lax.broadcasted_iota(jnp.int32, (EXTRA, LANES), 0)
    select = (row == lax.broadcasted_iota(jnp.int32, (EXTRA, LANES), 1)).astype(bf16)
    edges = [wide * p // pieces for p in range(pieces)] + [wide + LANES]
    for p in range(pieces):
        lo, hi = edges[p], edges[p + 1]
        for at in range(lo, min(hi, wide), 1024):
            to = min(at + 1024, wide)
            value = dot_rows(grad_share, context_held[:, at:to]).astype(bf16)
            for k in range(n):
                term[k // 2, k % 2, :, at:to] = value[k * block : (k + 1) * block]
        if hi > wide:
            value = dot_rows(whole[rows:, columns], select).astype(bf16)
            for k in range(n):
                term[k // 2, k % 2, :, wide:hi] = value[k * block : (k + 1) * block]
        firsts.append(
            wire.start(
                term.at[:, 1 - w.near, :, lo:hi], term_got.at[:, :, lo:hi], w.along_frames(1)
            )
        )
    for mask in red_q.order[2:]:
        red_q.forward(mask)
    for copy in load_ctx:
        copy.wait()

    def context_rows(t):
        at = pl.ds(pl.multiple_of(t * LANES, LANES), LANES)
        out_context[at, :] = dot_columns(whole[at, :], ctx_held[...])

    @pl.loop(0, rows // LANES)
    def _(t):
        context_rows(t)

    for p in range(pieces):
        lo, hi = edges[p], edges[p + 1]
        firsts[p].wait_recv()
        for mask in w.masks + [0]:
            to = flip(w.at, mask // 2)
            total = term[to, w.near, :, lo:hi].astype(f32) + term_got[to, :, lo:hi].astype(f32)
            term_sum[to, :, lo:hi] = total.astype(bf16)
            if mask:
                seconds.append(
                    wire.start(
                        term_sum.at[to, :, lo:hi],
                        term_landed.at[mask // 2, :, lo:hi],
                        w.along_frames(mask),
                    )
                )
    red_up.land()
    red_o.land()
    red_q.land()
    kept = [
        store_result,
        store_grad,
        local.start(send_o.at[w.at], out_o),
        local.start(send_q.at[w.at], out_q),
        local.start(send_up.at[w.at], out_up),
    ]

    @pl.when(crossing)
    def _():
        cross.wait_send()
        cross_result.wait_send()

    for copy in seconds:
        copy.wait_recv()
    total = term_sum[w.at].astype(f32)
    for mask in w.masks:
        total = total + term_landed[mask // 2].astype(f32)
    out_ctx[...] = total
    for copy in kept:
        copy.wait()
    wire.finish()


def ending_scratch(n, rows, depth, context_shape, count, wide_q, wide_o, wide_up):
    halfn, block, share = n // 2, depth // n, depth // 4 // n
    wide = context_shape[1] + LANES
    half = (rows + EXTRA) // 2
    both = 2 * rows
    shapes = [
        ((both, depth), bf16),
        ((both, depth), bf16),
        ((both, wide_o), bf16),
        ((both, wide_q), bf16),
        ((depth, wide_q), bf16),
        ((both, depth // 2), bf16),
        ((both, depth // 2), bf16),
        ((rows, depth), bf16),
        ((rows, depth), f32),
        ((rows, depth), bf16),
        ((rows + EXTRA, depth), bf16),
        ((rows + EXTRA, depth), bf16),
        ((half, depth), bf16),
        ((half, depth), bf16),
        ((half, depth), bf16),
        ((rows + EXTRA, depth), bf16),
        ((rows, depth), bf16),
        ((halfn, block, wide_q), bf16),
        ((halfn, block, wide_o), bf16),
        ((halfn, block, wide_q), bf16),
        ((halfn, block, wide_o), bf16),
        ((halfn, block, wide_q), bf16),
        ((halfn, block, wide_o), bf16),
        ((halfn, block, wide_up), bf16),
        ((halfn, block, wide_up), bf16),
        ((halfn, block, wide_up), bf16),
        (context_shape, bf16),
        ((count, depth), bf16),
        ((halfn, 2, share, wide), bf16),
        ((halfn, share, wide), bf16),
        ((halfn, share, wide), bf16),
        ((halfn, share, wide), bf16),
        ((1, depth), f32),
    ]
    others = [((rows, depth), f32)] * 4 + [((rows, depth), bf16)] * 2 + [((rows, count), f32)]
    return shapes, sum(math.prod(dims) * jnp.dtype(kind).itemsize for dims, kind in shapes + others)


def ending(
    n, resid, mid, gains, gain_two, result_rows,
    pair_one, pair_grad, mixed, grad_qkv, qkv_full, context, ctx_pieces, up_send, up_stay,
):
    rows, depth = resid.shape
    halfn, block = n // 2, depth // n
    wide_q, wide_o = qkv_full.shape[1], mixed.shape[1]
    count = ctx_pieces.shape[1]
    wide_up = up_send.shape[2]
    shapes, _ = ending_scratch(n, rows, depth, context.shape, count, wide_q, wide_o, wide_up)
    sems = 64 + 2 * n
    shape = jax.ShapeDtypeStruct
    return pl.pallas_call(
        functools.partial(ending_body, n),
        in_specs=[VMEM] * 5 + [ANY] * 9,
        out_specs=[ANY] * 8 + [VMEM] * 2,
        out_shape=[
            shape((block, wide_q), bf16),
            shape((block, wide_o), bf16),
            shape((block, wide_up), bf16),
            shape((halfn - 1, block, wide_q), bf16),
            shape((halfn - 1, block, wide_o), bf16),
            shape((halfn - 1, block, wide_up), bf16),
            shape((rows, depth), bf16),
            shape((rows, depth), bf16),
            shape((rows, count), f32),
            shape((depth // 4 // n, context.shape[1] + LANES), f32),
        ],
        scratch_shapes=[pltpu.VMEM(dims, kind) for dims, kind in shapes]
        + [
            pltpu.SemaphoreType.DMA((sems,)),
            pltpu.SemaphoreType.DMA((sems,)),
            pltpu.SemaphoreType.DMA((32,)),
        ],
        compiler_params=pltpu.CompilerParams(
            collective_id=6, has_side_effects=True, vmem_limit_bytes=67_000_000
        ),
        name="ending",
    )(
        resid, mid, gains, gain_two, result_rows,
        pair_one, pair_grad, mixed, grad_qkv, qkv_full, context, ctx_pieces, up_send, up_stay,
    )


def finish_body(
    own_q, own_o, own_gate, own_up, own_down, far_q, far_o, far_gate, far_up, far_down,
    grad, result, valid, out_q, out_o, out_gu, out_down, out_grad, out_result,
):
    place = (lax.axis_index("frames") // 2) % 2

    def settle(own, far, out, columns):
        total, other = own[...].astype(f32), None
        for k in range(far.shape[0]):
            value = far[k].astype(f32)
            if (k + 1) & 1:
                other = value if other is None else other + value
            else:
                total = total + value
        out[place, :, columns] = total
        out[1 - place, :, columns] = other

    wide = own_gate.shape[1]
    settle(own_q, far_q, out_q, slice(None))
    settle(own_o, far_o, out_o, slice(None))
    settle(own_gate, far_gate, out_gu, slice(0, wide))
    settle(own_up, far_up, out_gu, slice(wide, 2 * wide))
    settle(own_down, far_down, out_down, slice(None))
    out_grad[:, 0, :] = grad[...].astype(f32)
    out_result[:, 0, :] = result[...].astype(f32) * valid[...]


def finish(owns, fars, grad, result, valid, steps=4):
    block = owns[0].shape[0] // steps
    rows, depth = grad.shape
    shape = jax.ShapeDtypeStruct
    q, o, gate, up, down = [own.shape[1] for own in owns]
    here = rows // steps

    def own_spec(wide):
        return pl.BlockSpec((block, wide), lambda t: (t, 0))

    def far_spec(count, wide):
        return pl.BlockSpec((count, block, wide), lambda t: (0, t, 0))

    widths = (q, o, gate + up, down)
    row_out = pl.BlockSpec((here, 1, depth), lambda t: (t, 0, 0))
    return pl.pallas_call(
        finish_body,
        grid=(steps,),
        in_specs=[own_spec(x.shape[1]) for x in owns]
        + [far_spec(x.shape[0], x.shape[2]) for x in fars]
        + [pl.BlockSpec((here, depth), lambda t: (t, 0))] * 2
        + [pl.BlockSpec((here, 1), lambda t: (t, 0))],
        out_specs=[far_spec(2, wide) for wide in widths] + [row_out, row_out],
        out_shape=[shape((2, owns[0].shape[0], wide), f32) for wide in widths]
        + [shape((rows, 1, depth), f32)] * 2,
        compiler_params=pltpu.CompilerParams(vmem_limit_bytes=60 << 20),
        name="finish",
    )(*owns, *fars, grad, result, valid)


def swap_frames(value, mask):
    n = lax.axis_size("frames")
    return lax.ppermute(value, "frames", [(d, d ^ mask) for d in range(n)])


def swap_stream(value, mask):
    n = lax.axis_size("stream")
    return lax.ppermute(value, "stream", [(d, d ^ mask) for d in range(n)])


def joint(value, target):
    streams, n = lax.axis_size("stream"), lax.axis_size("frames")
    pairs = []
    for s in range(streams):
        for f in range(n):
            to_s, to_f = target(s, f)
            pairs.append((s * n + f, to_s * n + to_f))
    return lax.ppermute(value, ("stream", "frames"), pairs)


def transposed(value):
    def target(s, f):
        core, place = s % 2, (f // 2) % 2
        return s - core + place, f - 2 * place + 2 * core

    return joint(value, target)


def peer(value, mask):
    return joint(value, lambda s, f: (s ^ (mask & 2), f ^ (2 * (mask & 1))))


def norm_scale(values):
    return lax.rsqrt(jnp.mean(values * values, axis=-1, keepdims=True) + norm_eps)


def norm_back(values, scale, gain, grad):
    weighted = grad * gain
    inner_mean = jnp.mean(weighted * values, axis=-1, keepdims=True)
    grad_values = scale * weighted - values * (scale * scale * scale) * inner_mean
    grad_gain = jnp.sum(grad * values * scale, axis=0)
    return (grad_values, grad_gain)


def exchange_rows(qkv, position):
    rows, width = qkv.shape
    quarter = rows // 4
    parts = qkv.reshape(4, quarter, width)
    out = jnp.zeros((4, quarter, width), qkv.dtype)
    own = lax.dynamic_index_in_dim(parts, position, 0, keepdims=False)
    out = lax.dynamic_update_index_in_dim(out, own, position, 0)
    for mask in (2, 1, 3):
        there = position ^ mask
        got = peer(lax.dynamic_index_in_dim(parts, there, 0, keepdims=False), mask)
        out = lax.dynamic_update_index_in_dim(out, got, there, 0)
    return out


def heads_sum(product, fold):
    high = product.astype(bf16)
    low = (product - high.astype(f32)).astype(bf16)
    return jnp.dot(high, fold, preferred_element_type=f32) + jnp.dot(
        low, fold, preferred_element_type=f32
    )


def attention_forward_rows(at, qkv_ref, fold, spread, probs_ref, out_ref):
    width = out_ref.shape[2]
    for q in range(4):
        query = qkv_ref[q, at, :width].astype(f32)
        scores = []
        for k in range(q + 1):
            key = qkv_ref[k, at, width : 2 * width].astype(f32)
            scores.append(heads_sum(query * key, fold) * HD ** (-0.5))
        top = functools.reduce(jnp.maximum, scores)
        expo = [jnp.exp(s - top) for s in scores]
        total = functools.reduce(jnp.add, expo)
        mixed = None
        for k in range(q + 1):
            prob = expo[k] / total
            probs_ref[PAIRS.index((q, k)), at, :] = prob
            wide = jnp.dot(prob.astype(bf16), spread, preferred_element_type=f32)
            term = wide * qkv_ref[k, at, 2 * width :].astype(f32)
            mixed = term if mixed is None else mixed + term
        out_ref[q, at, :] = mixed.astype(bf16)


def attention_backward_rows(at, qkv_ref, probs_ref, grad_ref, fold, spread, out_ref):
    width = grad_ref.shape[2]
    grad_keys, grad_values = [None] * 4, [None] * 4
    for q in range(4):
        grad = grad_ref[q, at, :].astype(f32)
        query = qkv_ref[q, at, :width].astype(f32)
        probs = [probs_ref[PAIRS.index((q, k)), at, :] for k in range(q + 1)]
        grad_probs = [
            heads_sum(grad * qkv_ref[k, at, 2 * width :].astype(f32), fold) for k in range(q + 1)
        ]
        total = functools.reduce(jnp.add, [p * g for p, g in zip(probs, grad_probs)])
        grad_query = None
        for k in range(q + 1):
            wide = jnp.dot(probs[k].astype(bf16), spread, preferred_element_type=f32)
            term = wide * grad
            grad_values[k] = term if grad_values[k] is None else grad_values[k] + term
            grad_score = (probs[k] * (grad_probs[k] - total)).astype(bf16)
            wide = jnp.dot(grad_score, spread, preferred_element_type=f32)
            term = wide * qkv_ref[k, at, width : 2 * width].astype(f32)
            grad_query = term if grad_query is None else grad_query + term
            term = wide * query
            grad_keys[k] = term if grad_keys[k] is None else grad_keys[k] + term
        out_ref[q, at, :width] = (grad_query * HD ** (-0.5)).astype(bf16)
    for k in range(4):
        out_ref[k, at, width : 2 * width] = (grad_keys[k] * HD ** (-0.5)).astype(bf16)
        out_ref[k, at, 2 * width :] = grad_values[k].astype(bf16)


def attention_backward_body(qkv_ref, probs_ref, grad_ref, fold_ref, spread_ref, out_ref):
    everything = slice(None)
    attention_backward_rows(
        everything, qkv_ref, probs_ref, grad_ref, fold_ref[...], spread_ref[...], out_ref
    )


def fold_matrices(width):
    fold = np.arange(width)[:, None] // HD == np.arange(LANES)[None, :]
    return jnp.asarray(fold, bf16), jnp.asarray(fold.T, bf16)


def attention_backward(qkv, probs, grad, step=64):
    _, rows, triple = qkv.shape
    width = triple // 3
    fold, spread = fold_matrices(width)
    return pl.pallas_call(
        attention_backward_body,
        grid=(rows // step,),
        in_specs=[
            pl.BlockSpec((4, step, triple), lambda r: (0, r, 0)),
            pl.BlockSpec((len(PAIRS), step, LANES), lambda r: (0, r, 0)),
            pl.BlockSpec((4, step, width), lambda r: (0, r, 0)),
            pl.BlockSpec((width, LANES), lambda r: (0, 0)),
            pl.BlockSpec((LANES, width), lambda r: (0, 0)),
        ],
        out_specs=pl.BlockSpec((4, step, triple), lambda r: (0, r, 0)),
        out_shape=jax.ShapeDtypeStruct((4, rows, triple), bf16),
        name="attention_backward",
    )(qkv, probs, grad, fold, spread)


def after(value, *others):
    return lax.optimization_barrier((value,) + others)[0]


def taken(weights, place):
    own = [lax.dynamic_index_in_dim(w, place, 0, keepdims=False) for w in weights]
    other = [lax.dynamic_index_in_dim(w, 1 - place, 0, keepdims=False) for w in weights]
    if len(weights) == 1:
        return own[0], other[0]
    return jnp.concatenate(own, axis=1), jnp.concatenate(other, axis=1)


def placed_rows(pieces, frame_index, start, width):
    n = lax.axis_size("frames")
    block = pieces[0].shape[0]
    full = jnp.zeros((n, block, width), pieces[0].dtype)
    for mask in range(n):
        part = pieces[mask][:, start : start + width]
        full = lax.dynamic_update_index_in_dim(full, part, frame_index ^ mask, 0)
    return full.reshape(n * block, width)


def halves(left, near):
    n = lax.axis_size("frames")
    rows, depth = left.shape
    block = depth // n
    even = jnp.concatenate([left[:, k * block : (k + 1) * block] for k in range(0, n, 2)], axis=1)
    odd = jnp.concatenate([left[:, k * block : (k + 1) * block] for k in range(1, n, 2)], axis=1)
    return jnp.where(near == 0, odd, even), jnp.where(near == 0, even, odd)


def scattered(left_halves, right, frame_index, place):
    n = lax.axis_size("frames")

    def product(part):
        return lax.dot_general(
            part, right, (((0,), (0,)), ((), ())), preferred_element_type=f32
        ).astype(bf16)

    arrived = swap_frames(product(left_halves[0]), 1)
    half_sum = (product(left_halves[1]).astype(f32) + arrived.astype(f32)).astype(bf16)
    half_sum = half_sum.reshape(n // 2, -1, right.shape[1])
    at = frame_index // 2
    own = lax.dynamic_index_in_dim(half_sum, at, 0, keepdims=False).astype(f32)
    other = None
    for mask in range(2, n, 2):
        got = swap_frames(
            lax.dynamic_index_in_dim(half_sum, at ^ (mask // 2), 0, keepdims=False), mask
        ).astype(f32)
        if mask & 2:
            other = got if other is None else other + got
        else:
            own = own + got
    first = jnp.where(place == 0, own, other)
    second = jnp.where(place == 0, other, own)
    return jnp.stack([first, second], axis=0)


class Spread:
    def __init__(self, w, wire, weight, full):
        self.w, self.wire, self.weight, self.full = w, wire, weight, full
        self.block = full.shape[0] // w.n
        self.far, self.near = {}, {}

    def rows(self, frame):
        return self.full.at[pl.ds(pl.multiple_of(frame * self.block, self.block), self.block), :]

    def own(self, local):
        return local.start(self.weight.at[self.w.place], self.rows(self.w.frame))

    def own_near(self):
        w = self.w
        self.near[0] = self.wire.start(
            self.weight.at[w.place], self.rows(w.frame), w.along_frames(1)
        )

    def send(self, masks):
        w = self.w
        for mask in masks:
            which = 1 - w.place if mask & 2 else w.place
            self.far[mask] = self.wire.start(
                self.weight.at[which], self.rows(w.frame), w.along_frames(mask)
            )

    def relay(self, mask):
        self.far[mask].wait_recv()
        rows = self.rows(flip(self.w.frame, mask))
        self.near[mask] = self.wire.start(rows, rows, self.w.along_frames(1))

    def close(self):
        for copy in self.near.values():
            copy.wait_recv()


def front_body(
    n, context, ctx_weight, inputs, cotangent, valid, gains, fold, spread,
    qkv_weight, out_weight, gu_weight, down_weight,
    out_qkv, out_out, out_gu, out_down, out_ctx, out_resid, out_mid, out_one, out_two, out_grad,
    out_qkv_mixed, out_probs, out_mixed,
    ctx_held, context_held, total, partner_half, half_sum, far_half, whole, home, resid, pair,
    qkv_full, out_full, qkv_rows, qkv_mixed, probs, mixed_quarter, mixed, away, got, grad_low,
    send_sem, recv_sem, local_sem,
):
    w = Where(n)
    wire, local = Wire(send_sem, recv_sem), Local(local_sem)
    rows, depth = inputs.shape
    count = ctx_weight.shape[0] // 4
    piece = depth // n
    crossing = w.core != w.place
    half = rows // 2
    step = 64
    quarter_of_context = pl.ds(pl.multiple_of(w.stream * count, LANES), count)
    load_context = local.start(context.at[:, quarter_of_context], context_held)
    load_ctx = local.start(ctx_weight.at[quarter_of_context, :], ctx_held.at[w.frame])
    qkv = Spread(w, wire, qkv_weight, qkv_full)
    out = Spread(w, wire, out_weight, out_full)
    gu = Spread(w, wire, gu_weight, out_gu)
    down = Spread(w, wire, down_weight, out_down)
    owns = [qkv.own(local), out.own(local)]
    greet(
        [w.along_stream(1), w.along_stream(2), w.along_frames(1)]
        + [w.along_frames(m) for m in w.masks]
        + [w.across(), w.with_position(3)]
    )

    load_ctx.wait()
    held, near = [0], {}

    def ctx_near(o):
        at = flip(w.frame, o)
        near[o] = wire.start(ctx_held.at[at], ctx_held.at[at], w.along_frames(1))

    ready = []
    for bit in reversed(range(1, n.bit_length() - 1)):
        copies = []
        for o in held:
            at = flip(w.frame, o)
            copies.append(
                (o, wire.start(ctx_held.at[at], ctx_held.at[at], w.along_frames(1 << bit)))
            )
        if bit == n.bit_length() - 2:
            ctx_near(0)
            qkv.own_near()
            out.own_near()
        if bit == 1:
            for mask in w.masks:
                qkv.send([mask])
                out.send([mask])
        for o, copy in copies:
            copy.wait_recv()
            ctx_near(o ^ (1 << bit))
            held.append(o ^ (1 << bit))

    load_context.wait()

    def project(o):
        at = flip(w.frame, o)
        columns = pl.ds(pl.multiple_of(at * piece, piece), piece)
        value = jnp.dot(context_held[...], ctx_held[at], preferred_element_type=f32)
        total[:, columns] = value

    def relay_attention(k):
        for mask in w.masks[k : k + 1]:
            qkv.relay(mask)
            out.relay(mask)

    if piece % LANES == 0:
        for o in held:
            project(o)
        for o in held:
            if o == held[-1]:
                relay_attention(0)
            near[o].wait_recv()
            project(o ^ 1)
    else:
        for o in held:
            near[o].wait_recv()
        relay_attention(0)
        total[...] = jnp.zeros_like(total)

        @pl.loop(0, n)
        def _(at):
            line = lax.broadcasted_iota(jnp.int32, (piece, depth), 0)
            column = lax.broadcasted_iota(jnp.int32, (piece, depth), 1)
            select = (column == line + at * piece).astype(bf16)
            laid = jnp.dot(ctx_held[at], select, preferred_element_type=f32).astype(bf16)

            @pl.loop(0, rows // LANES)
            def _(t):
                here = pl.ds(pl.multiple_of(t * LANES, LANES), LANES)
                total[here, :] += jnp.dot(
                    context_held[here, :], laid, preferred_element_type=f32
                )

    store_ctx = local.start(ctx_held, out_ctx)

    mine = pl.ds(pl.multiple_of(w.core * half, 16), half)
    theirs = pl.ds(pl.multiple_of((1 - w.core) * half, 16), half)
    whole[theirs, :] = total[theirs, :].astype(bf16)
    first = wire.start(whole.at[theirs, :], partner_half, w.along_stream(1))
    first.wait_recv()
    half_sum[...] = (total[mine, :] + partner_half[...].astype(f32)).astype(bf16)
    second = wire.start(half_sum, far_half, w.along_stream(2))
    relay_attention(1)
    second.wait_recv()
    home[mine, :] = (half_sum[...].astype(f32) + far_half[...].astype(f32)).astype(bf16)
    third = wire.start(home.at[mine, :], home.at[mine, :], w.along_stream(1))
    third.wait_recv()
    wire.sent(third)

    @pl.loop(0, rows // step)
    def _(t):
        at = pl.ds(pl.multiple_of(t * step, step), step)
        home[at, :] = (home[at, :].astype(f32) + inputs[at, :].astype(f32)).astype(bf16)

    cross = wire.make(home, resid, w.across())
    stay = pltpu.make_async_copy(home, resid, local_sem.at[22])

    @pl.when(crossing)
    def _():
        cross.start()

    @pl.when(jnp.logical_not(crossing))
    def _():
        stay.start()

    gu.own_near()
    gu.send(w.far_masks + w.both_masks)
    for k in range(2, len(w.masks)):
        relay_attention(k)

    @pl.when(crossing)
    def _():
        cross.wait_recv()

    @pl.when(jnp.logical_not(crossing))
    def _():
        stay.wait()

    def normed(source, gain):
        @pl.loop(0, rows // step)
        def _(t):
            at = pl.ds(pl.multiple_of(t * step, step), step)
            values = source[at, :].astype(f32)
            scale = lax.rsqrt(jnp.mean(values * values, axis=-1, keepdims=True) + norm_eps)
            pair[at, :] = (values * scale * gain).astype(bf16)

    normed(resid, gains[0:1, :])
    upper = pair.at[rows:, :]
    first_pair = wire.start(pair.at[:rows, :], upper, w.along_stream(1))
    for copy in owns:
        copy.wait()
    qkv.close()
    out.close()
    quarter = 2 * rows // 4
    width = out_full.shape[1]

    def qkv_of(lo, hi):
        @pl.loop(lo, hi)
        def _(t):
            at = pl.ds(pl.multiple_of(t * quarter, quarter), quarter)
            left = pair[at, :]
            for p in range(3):
                columns = slice(p * width, (p + 1) * width)
                value = jnp.dot(left, qkv_full[:, columns], preferred_element_type=f32)
                qkv_rows[at, columns] = value.astype(bf16)

    qkv_of(0, 2)
    first_pair.wait_recv()
    qkv_of(2, 4)
    mixing = {}

    def rows_of(position):
        return pl.ds(pl.multiple_of(position * quarter, quarter), quarter)

    for mask in (3, 1, 2):
        mixing[mask] = wire.start(
            qkv_rows.at[rows_of(flip(w.position, mask)), :],
            qkv_mixed.at[w.position],
            w.with_position(mask),
        )
    own_quarter = local.start(qkv_rows.at[rows_of(w.position), :], qkv_mixed.at[w.position])
    gu.send([2])
    down.send(w.far_masks)
    @pl.loop(0, rows // step)
    def _(t):
        at = pl.ds(pl.multiple_of(t * step, step), step)
        grad_low[at, :] = (cotangent[at, 0, :] * valid[at, :]).astype(bf16)

    stores = [
        local.start(pair, out_one),
        local.start(qkv_full, out_qkv),
        local.start(out_full, out_out),
        local.start(resid, out_resid),
        local.start(grad_low, out_grad),
    ]
    gu_own, down_own = gu.own(local), down.own(local)
    for mask in w.far_masks:
        gu.relay(mask)
    own_quarter.wait()
    for mask in (2, 1, 3):
        mixing[mask].wait_recv()
    for mask in w.both_masks:
        gu.relay(mask)
    fold_held, spread_held = fold[...], spread[...]

    @pl.loop(0, quarter // step)
    def _(t):
        at = pl.ds(pl.multiple_of(t * step, step), step)
        attention_forward_rows(at, qkv_mixed, fold_held, spread_held, probs, mixed_quarter)

    returning = {}
    for mask in (3, 1, 2):
        returning[mask] = wire.start(
            mixed_quarter.at[flip(w.position, mask)],
            mixed.at[rows_of(w.position), :],
            w.with_position(mask),
        )
    own_back = local.start(mixed_quarter.at[w.position], mixed.at[rows_of(w.position), :])
    down.send(w.both_masks + [2])
    stores += [local.start(qkv_mixed, out_qkv_mixed), local.start(probs, out_probs)]
    gu.relay(2)
    own_back.wait()
    for mask in (2, 1, 3):
        returning[mask].wait_recv()
    stores.append(local.start(mixed, out_mixed))
    stores[0].wait()

    @pl.loop(2, 4)
    def _(t):
        at = pl.ds(pl.multiple_of(t * quarter, quarter), quarter)
        to = pl.ds(pl.multiple_of(t * quarter - rows, quarter), quarter)
        away[to, :] = dot_columns(mixed[at, :], out_full[...]).astype(bf16)

    part = wire.start(away, got, w.along_stream(1))

    @pl.loop(0, 2)
    def _(t):
        at = pl.ds(pl.multiple_of(t * quarter, quarter), quarter)
        total[at, :] = dot_columns(mixed[at, :], out_full[...])

    part.wait_recv()
    wire.sent(first_pair)
    gain = gains[1:2, :]

    @pl.loop(0, rows // step)
    def _(t):
        at = pl.ds(pl.multiple_of(t * step, step), step)
        values = resid[at, :].astype(f32) + total[at, :] + got[at, :].astype(f32)
        total[at, :] = values
        scale = lax.rsqrt(jnp.mean(values * values, axis=-1, keepdims=True) + norm_eps)
        pair[at, :] = (values * scale * gain).astype(bf16)

    second_pair = wire.start(pair.at[:rows, :], upper, w.along_stream(1))
    stores.append(local.start(total, out_mid))
    second_pair.wait_recv()
    stores.append(local.start(pair, out_two))
    gu.close()
    for copy in down.far.values():
        copy.wait_recv()
    for copy in stores[1:]:
        copy.wait()
    for copy in (store_ctx, gu_own, down_own):
        copy.wait()

    @pl.when(crossing)
    def _():
        cross.wait_send()

    wire.finish()


def front(
    n, context, ctx_weight, inputs, cotangent, valid, gains,
    qkv_weight, out_weight, gu_weight, down_weight,
):
    rows, depth = inputs.shape
    count = ctx_weight.shape[0] // 4
    wide_q, wide_o = qkv_weight.shape[2], out_weight.shape[2]
    fold, spread = fold_matrices(wide_o)
    quarter = rows // 2
    half = rows // 2
    pairs = len(PAIRS)
    scratch = [
        pltpu.VMEM((n, count, depth // n), bf16),
        pltpu.VMEM((rows, count), bf16),
        pltpu.VMEM((rows, depth), f32),
        pltpu.VMEM((half, depth), bf16),
        pltpu.VMEM((half, depth), bf16),
        pltpu.VMEM((half, depth), bf16),
        pltpu.VMEM((rows, depth), bf16),
        pltpu.VMEM((rows, depth), bf16),
        pltpu.VMEM((rows, depth), bf16),
        pltpu.VMEM((2 * rows, depth), bf16),
        pltpu.VMEM((depth, wide_q), bf16),
        pltpu.VMEM((depth, wide_o), bf16),
        pltpu.VMEM((2 * rows, wide_q), bf16),
        pltpu.VMEM((4, quarter, wide_q), bf16),
        pltpu.VMEM((pairs, quarter, LANES), f32),
        pltpu.VMEM((4, quarter, wide_o), bf16),
        pltpu.VMEM((2 * rows, wide_o), bf16),
        pltpu.VMEM((rows, depth), bf16),
        pltpu.VMEM((rows, depth), bf16),
        pltpu.VMEM((rows, depth), bf16),
        pltpu.SemaphoreType.DMA((24 + 10 * n,)),
        pltpu.SemaphoreType.DMA((24 + 10 * n,)),
        pltpu.SemaphoreType.DMA((24,)),
    ]
    shape = jax.ShapeDtypeStruct
    return pl.pallas_call(
        functools.partial(front_body, n),
        in_specs=[ANY, ANY, VMEM, VMEM, VMEM, VMEM, VMEM, VMEM, ANY, ANY, ANY, ANY],
        out_specs=[ANY] * 13,
        out_shape=[
            shape((depth, wide_q), bf16),
            shape((depth, wide_o), bf16),
            shape((depth, gu_weight.shape[2]), bf16),
            shape((depth, down_weight.shape[2]), bf16),
            shape((n, count, depth // n), bf16),
            shape((rows, depth), bf16),
            shape((rows, depth), f32),
            shape((2 * rows, depth), bf16),
            shape((2 * rows, depth), bf16),
            shape((rows, depth), bf16),
            shape((4, quarter, wide_q), bf16),
            shape((pairs, quarter, LANES), f32),
            shape((2 * rows, wide_o), bf16),
        ],
        scratch_shapes=scratch,
        compiler_params=pltpu.CompilerParams(
            collective_id=3, has_side_effects=True, vmem_limit_bytes=62 << 20
        ),
        name="front",
    )(
        context, ctx_weight, inputs, cotangent, valid, gains, fold, spread,
        qkv_weight, out_weight, gu_weight, down_weight,
    )


def back_body(
    n, pair_two, home_grad, resid, gu_weight, down_half, out_weight, qkv_held, probs_held,
    gains, fold, spread,
    out_down, out_gate, out_up, out_up_stay, landed_down, landed_gate, out_mid, out_gain, out_pair, out_rows, out_qkv,
    two, grad, gu_full, down_full, out_full, two_away, two_stay, grad_away, grad_stay,
    hidden, grad_gu, send_down, send_gu, got_down, got_gu,
    values_mid, away, got, grad_rows, grad_mixed, qkv_mixed, probs, grad_qkv,
    send_sem, recv_sem, tile_send, tile_recv, local_sem,
):
    w = Where(n)
    wire, local = Wire(send_sem, recv_sem), Local(local_sem)
    tiled = Wire(tile_send, tile_recv)
    rows, depth = out_mid.shape
    both = 2 * rows
    piece = depth // n
    halfn = n // 2
    wide = down_full.shape[1]
    tile = 2 * LANES
    whole_tiles = wide // tile
    tiles = whole_tiles + (1 if wide % tile else 0)
    step = 64
    loads = [
        local.start(pair_two, two),
        local.start(gu_weight, gu_full),
    ]
    blocks = [
        pl.ds(pl.multiple_of((2 * b + w.near) * piece, piece), piece) for b in range(halfn)
    ]
    down_own = [local.start(down_half.at[at, :], down_full.at[at, :]) for at in blocks]
    late = [
        local.start(resid, values_mid),
        local.start(out_weight, out_full),
        local.start(qkv_held, qkv_mixed),
        local.start(probs_held, probs),
    ]
    greet(
        [w.along_stream(1), w.along_stream(2), w.along_frames(1)]
        + [w.along_frames(m) for m in w.masks]
        + [w.with_position(3), w.across()]
    )
    crossing = w.core != w.place
    cross = wire.make(home_grad, grad.at[:rows, :], w.across())
    stay = pltpu.make_async_copy(home_grad, grad.at[:rows, :], local_sem.at[15 + n])

    @pl.when(crossing)
    def _():
        cross.start()

    @pl.when(jnp.logical_not(crossing))
    def _():
        stay.start()

    neighbour = w.along_frames(1)
    down_near = [wire.start(down_half.at[at, :], down_full.at[at, :], neighbour) for at in blocks]

    def split(source, into_away, into_stay):
        for b in range(halfn):
            for ref, which in ((into_away, 1 - w.near), (into_stay, w.near)):
                at = pl.ds(pl.multiple_of((2 * b + which) * piece, piece), piece)
                ref[:, b * piece : (b + 1) * piece] = source[:, at]

    loads[0].wait()
    split(two, two_away, two_stay)
    loads[1].wait()

    def columns(start, size):
        return pl.ds(pl.multiple_of(start, LANES), size)

    def tile_parts(t):
        lo = t * tile
        return ((send_down, got_down, lo), (send_gu, got_gu, lo), (send_gu, got_gu, wide + lo))

    def move(t, size, j):
        ref, into, start = tile_parts(t)[j]
        at = columns(start, size)
        return tiled.make(ref.at[:, :, at], into.at[:, :, at], neighbour, 3 * t + j)

    def forward(t, size):
        lo = t * tile
        here = columns(lo, size)
        there = columns(wide + lo, size)

        @pl.loop(0, both // 256)
        def _(r):
            at = pl.ds(pl.multiple_of(r * 256, 256), 256)
            left = two[at, :]
            gate = jnp.dot(left, gu_full[:, here], preferred_element_type=f32)
            up = jnp.dot(left, gu_full[:, there], preferred_element_type=f32)
            hidden[at, here] = (gate / (1.0 + jnp.exp(-gate)) * up).astype(bf16)
            grad_gu[at, here] = gate.astype(bf16)
            grad_gu[at, there] = up.astype(bf16)

    def store_away(ref, left, right, at):
        value = dot_rows(left[...], right[:, at]).astype(bf16)
        for b in range(halfn):
            ref[b, :, at] = value[b * piece : (b + 1) * piece]

    def away_down(t, size):
        store_away(send_down, grad_away, hidden, columns(t * tile, size))
        move(t, size, 0).start()

    def backward(t, size):
        lo = t * tile
        here = columns(lo, size)
        there = columns(wide + lo, size)

        @pl.loop(0, both // 256)
        def _(r):
            at = pl.ds(pl.multiple_of(r * 256, 256), 256)
            gate = grad_gu[at, here].astype(f32)
            up = grad_gu[at, there].astype(f32)
            back = jnp.dot(grad[at, :], down_full[:, here], preferred_element_type=f32)
            sigma = 1.0 / (1.0 + jnp.exp(-gate))
            grad_gu[at, here] = (back * up * (sigma * (1.0 + gate * (1.0 - sigma)))).astype(bf16)
            grad_gu[at, there] = (back * (gate * sigma)).astype(bf16)

        store_away(send_gu, two_away, grad_gu, here)
        store_away(send_gu, two_away, grad_gu, there)
        move(t, size, 1).start()

    rest = wide - whole_tiles * tile

    def every(step_of):
        @pl.loop(0, whole_tiles)
        def _(t):
            step_of(t, tile)

        if rest:
            step_of(whole_tiles, rest)

    every(forward)

    @pl.when(crossing)
    def _():
        cross.wait_recv()

    @pl.when(jnp.logical_not(crossing))
    def _():
        stay.wait()

    grad_pair = wire.start(grad.at[:rows, :], grad.at[rows:, :], w.along_stream(1))
    grad_pair.wait_recv()
    split(grad, grad_away, grad_stay)
    every(away_down)
    for copy in down_own:
        copy.wait()
    for copy in down_near:
        copy.wait_recv()
    every(backward)

    landed = (landed_down, landed_gate)

    def landing(t, size, j, k):
        ref, _, start = tile_parts(t)[j]
        mask = w.masks[k]
        at = columns(start, size)
        return tiled.make(
            ref.at[flip(w.at, mask // 2), :, at],
            landed[j].at[mask // 2 - 1, :, columns(t * tile, size)],
            w.along_frames(mask),
            3 * tiles + (3 * t + j) * len(w.masks) + k,
        )

    lefts = (grad_stay, two_stay, two_stay)
    rights = (hidden, grad_gu, grad_gu)

    def reduce_part(t, size, j):
        ref, into, start = tile_parts(t)[j]
        at = columns(start, size)
        move(t, size, j).wait()
        value = dot_rows(lefts[j][...], rights[j][:, at])
        for b in range(halfn):
            total = value[b * piece : (b + 1) * piece] + into[b, :, at].astype(f32)
            ref[b, :, at] = total.astype(bf16)
        for k in range(len(w.masks)):
            landing(t, size, j, k).start()

    def reduce_down(t, size):
        reduce_part(t, size, 0)

    def reduce_gu(t, size):
        reduce_part(t, size, 1)

    def stay_up(t, size):
        at = columns(wide + t * tile, size)
        store_away(got_gu, two_stay, grad_gu, at)

    def some(step_of, lo, hi):
        top = min(hi, whole_tiles)
        if top > lo:

            @pl.loop(lo, top)
            def _(t):
                step_of(t, tile)

        if hi > whole_tiles and rest:
            step_of(whole_tiles, rest)

    cut = min(3, whole_tiles)

    def rows_of(position):
        quarter = both // 4
        return pl.ds(pl.multiple_of(position * quarter, quarter), quarter)

    def partial(left, right, t):
        at = pl.ds(pl.multiple_of(t * 256, 256), 256)
        return dot_columns(left[at, :], right[...])

    @pl.loop(0, rows // 256)
    def _(t):
        to = pl.ds(pl.multiple_of(t * 256, 256), 256)
        away[to, :] = partial(grad_gu, gu_full, rows // 256 + t).astype(bf16)

    first = wire.start(away, got, w.along_stream(1))

    @pl.loop(0, rows // 256)
    def _(t):
        to = pl.ds(pl.multiple_of(t * 256, 256), 256)
        out_mid[to, :] = partial(grad_gu, gu_full, t)

    some(reduce_down, 0, cut)

    late[0].wait()
    first.wait_recv()
    gain = gains[1:2, :]
    out_gain[...] = jnp.zeros_like(out_gain)

    @pl.loop(0, rows // step)
    def _(t):
        at = pl.ds(pl.multiple_of(t * step, step), step)
        grad_normed = out_mid[at, :] + got[at, :].astype(f32)
        values = values_mid[at, :]
        scale = lax.rsqrt(jnp.mean(values * values, axis=-1, keepdims=True) + norm_eps)
        weighted = grad_normed * gain
        inner = jnp.mean(weighted * values, axis=-1, keepdims=True)
        total = grad[at, :].astype(f32) + scale * weighted
        total = total - values * (scale * scale * scale * inner)
        out_mid[at, :] = total
        two[at, :] = total.astype(bf16)
        out_gain[...] += jnp.sum(grad_normed * values * scale, axis=0, keepdims=True)

    second = wire.start(two.at[:rows, :], two.at[rows:, :], w.along_stream(1))
    late[1].wait()

    def back_rows(lo, hi):
        @pl.loop(lo, hi)
        def _(t):
            at = pl.ds(pl.multiple_of(t * 256, 256), 256)
            value = jnp.dot(two[at, :], out_full[...], preferred_element_type=f32)
            grad_rows[at, :] = value.astype(bf16)

    back_rows(0, rows // 256)
    second.wait_recv()
    back_rows(rows // 256, both // 256)
    mixing = {}
    for mask in (3, 1, 2):
        mixing[mask] = wire.start(
            grad_rows.at[rows_of(flip(w.position, mask)), :],
            grad_mixed.at[w.position],
            w.with_position(mask),
        )
    own = local.start(grad_rows.at[rows_of(w.position), :], grad_mixed.at[w.position])
    store_pair = local.start(two, out_pair)

    some(reduce_down, cut, tiles)
    own.wait()
    late[2].wait()
    late[3].wait()
    for mask in (2, 1, 3):
        mixing[mask].wait_recv()
    fold_held, spread_held = fold[...], spread[...]

    @pl.loop(0, both // 4 // step)
    def _(t):
        at = pl.ds(pl.multiple_of(t * step, step), step)
        attention_backward_rows(
            at, qkv_mixed, probs, grad_mixed, fold_held, spread_held, grad_qkv
        )

    returning = {}
    for mask in (3, 1, 2):
        returning[mask] = wire.start(
            grad_qkv.at[flip(w.position, mask)],
            out_qkv.at[rows_of(w.position), :],
            w.with_position(mask),
        )
    own_back = local.start(grad_qkv.at[w.position], out_qkv.at[rows_of(w.position), :])
    early = min(2, whole_tiles)
    some(reduce_gu, 0, early)
    some(stay_up, 0, tiles)

    wire.sent(first)

    @pl.loop(0, rows // 256)
    def _(t):
        to = pl.ds(pl.multiple_of(t * 256, 256), 256)
        away[to, :] = partial(hidden, down_full, rows // 256 + t).astype(bf16)

    third = wire.start(away, got, w.along_stream(1))

    @pl.loop(0, rows // 256)
    def _(t):
        to = pl.ds(pl.multiple_of(t * 256, 256), 256)
        values_mid[to, :] = values_mid[to, :] + partial(hidden, down_full, t)

    third.wait_recv()

    @pl.loop(0, rows // step)
    def _(t):
        at = pl.ds(pl.multiple_of(t * step, step), step)
        out_rows[at, :] = (values_mid[at, :] + got[at, :].astype(f32)).astype(bf16)

    some(reduce_gu, early, tiles)
    kept = [
        local.start(send_down.at[w.at], out_down),
        local.start(send_gu.at[w.at, :, :wide], out_gate),
        local.start(send_gu.at[:, :, wide:], out_up),
        local.start(got_gu.at[:, :, wide:], out_up_stay),
    ]
    own_back.wait()
    store_pair.wait()
    for mask in (2, 1, 3):
        returning[mask].wait_recv()
    for t in range(tiles):
        for j in range(2):
            for k in range(len(w.masks)):
                landing(t, tile if t < whole_tiles else rest, j, k).wait()
    for copy in kept:
        copy.wait()

    @pl.when(crossing)
    def _():
        cross.wait_send()

    wire.finish()


def back_scratch(n, rows, depth, wide, head_width):
    both, halfn, piece = 2 * rows, n // 2, depth // n
    pairs = len(PAIRS)
    quarter = both // 4
    shapes = [
        ((both, depth), bf16),
        ((both, depth), bf16),
        ((depth, 2 * wide), bf16),
        ((depth, wide), bf16),
        ((depth, head_width), bf16),
        ((both, depth // 2), bf16),
        ((both, depth // 2), bf16),
        ((both, depth // 2), bf16),
        ((both, depth // 2), bf16),
        ((both, wide), bf16),
        ((both, 2 * wide), bf16),
        ((halfn, piece, wide), bf16),
        ((halfn, piece, 2 * wide), bf16),
        ((halfn, piece, wide), bf16),
        ((halfn, piece, 2 * wide), bf16),
        ((rows, depth), f32),
        ((rows, depth), bf16),
        ((rows, depth), bf16),
        ((both, head_width), bf16),
        ((4, quarter, head_width), bf16),
        ((4, quarter, 3 * head_width), bf16),
        ((pairs, quarter, LANES), f32),
        ((4, quarter, 3 * head_width), bf16),
    ]
    outs = [((rows, depth), f32), ((rows, depth), bf16)]
    return shapes, sum(math.prod(dims) * jnp.dtype(kind).itemsize for dims, kind in shapes + outs)


def back(
    n, pair_two, home_grad, resid, gu_full, down_half, out_full, qkv_mixed, probs, gains
):
    rows, depth = resid.shape
    wide, head_width = down_half.shape[1], out_full.shape[1]
    shapes, _ = back_scratch(n, rows, depth, wide, head_width)
    tiles = -(-wide // (2 * LANES))
    fold, spread = fold_matrices(head_width)
    shape = jax.ShapeDtypeStruct
    moves = 3 * tiles * (1 + n // 2 - 1)
    return pl.pallas_call(
        functools.partial(back_body, n),
        in_specs=[ANY] * 8 + [VMEM] * 3,
        out_specs=[ANY, ANY, ANY, ANY, ANY, ANY, VMEM, VMEM, ANY, VMEM, ANY],
        out_shape=[
            shape((depth // n, wide), bf16),
            shape((depth // n, wide), bf16),
            shape((n // 2, depth // n, wide), bf16),
            shape((n // 2, depth // n, wide), bf16),
            shape((n // 2 - 1, depth // n, wide), bf16),
            shape((n // 2 - 1, depth // n, wide), bf16),
            shape((rows, depth), f32),
            shape((1, depth), f32),
            shape((2 * rows, depth), bf16),
            shape((rows, depth), bf16),
            shape((2 * rows, 3 * head_width), bf16),
        ],
        scratch_shapes=[pltpu.VMEM(dims, kind) for dims, kind in shapes]
        + [
            pltpu.SemaphoreType.DMA((16 + 2 * n,)),
            pltpu.SemaphoreType.DMA((16 + 2 * n,)),
            pltpu.SemaphoreType.DMA((moves,)),
            pltpu.SemaphoreType.DMA((moves,)),
            pltpu.SemaphoreType.DMA((16 + n,)),
        ],
        compiler_params=pltpu.CompilerParams(
            collective_id=4, has_side_effects=True, vmem_limit_bytes=67_000_000
        ),
        name="back",
    )(
        pair_two, home_grad, resid, gu_full, down_half, out_full, qkv_mixed, probs,
        gains, fold, spread,
    )


def shards(
    inputs,
    context,
    cotangent,
    live_frames,
    ctx_weight,
    norm_gains,
    qkv_weight,
    out_weight,
    gate_up_weight,
    down_weight,
):
    n = lax.axis_size("frames")
    stream_index = lax.axis_index("stream")
    frame_index = lax.axis_index("frames")
    half_index = stream_index % 2
    place = (frame_index // 2) % 2
    position = (stream_index // 2) * 2 + place
    frame_count = inputs.shape[0]
    width_model = inputs.shape[2]
    offsets = lax.broadcasted_iota(jnp.int32, (frame_count,), 0)
    valid_mask = (offsets % SLOT < jnp.repeat(live_frames, SLOT)).astype(f32)[:, None]
    gain_one = norm_gains[0]
    gain_two = norm_gains[1]

    (
        qkv_full,
        out_full,
        gate_up_full,
        down_half,
        ctx_pieces,
        resid_in,
        resid_mid,
        paired_one,
        paired_two,
        grad_rows,
        qkv_mixed,
        probs,
        mixed,
    ) = front(
        n,
        context,
        ctx_weight,
        inputs[:, 0],
        cotangent,
        valid_mask,
        norm_gains,
        qkv_weight[0],
        out_weight[0],
        gate_up_weight[0],
        down_weight[0],
    )
    near = frame_index % 2

    def paired(mine):
        return jnp.concatenate([mine, swap_stream(mine, 1)], axis=0)

    def own_sum(partial_value):
        return partial_value[:frame_count] + swap_stream(
            partial_value[frame_count:].astype(bf16), 1
        ).astype(f32)

    def rows_times(left, right):
        return jnp.dot(left, right, preferred_element_type=f32)

    def rows_back(left, right):
        return lax.dot_general(left, right, (((1,), (1,)), ((), ())), preferred_element_type=f32)

    def returned(value):
        _, quarter, width = value.shape
        out = jnp.zeros((4, quarter, width), value.dtype)
        own = lax.dynamic_index_in_dim(value, position, 0, keepdims=False)
        out = lax.dynamic_update_index_in_dim(out, own, position, 0)
        for mask in (2, 1, 3):
            there = position ^ mask
            got = peer(lax.dynamic_index_in_dim(value, there, 0, keepdims=False), mask)
            out = lax.dynamic_update_index_in_dim(out, got, there, 0)
        return out.reshape(4 * quarter, width)

    head_width = out_full.shape[1]
    _, needed = back_scratch(n, frame_count, width_model, down_weight.shape[3], head_width)
    if needed <= 66_000_000 and (width_model // n) % LANES == 0:
        (
            own_down,
            own_gate,
            up_send,
            up_stay,
            landed_down,
            landed_gate,
            grad_mid,
            grad_gain_two,
            paired_grad_attn,
            result_rows,
            grad_qkv_low,
        ) = back(
            n,
            paired_two,
            grad_rows,
            resid_mid,
            gate_up_full,
            down_half,
            out_full,
            qkv_mixed,
            probs,
            norm_gains,
        )
    else:
        paired_grad_ffn = paired(transposed(grad_rows))
        blocks = down_half.reshape(n // 2, 2, -1, down_half.shape[1])
        blocks = lax.dynamic_index_in_dim(blocks, near, 1, keepdims=False)
        others = swap_frames(blocks, 1)
        even, odd = jnp.where(near == 0, blocks, others), jnp.where(near == 0, others, blocks)
        down_full = jnp.stack([even, odd], axis=1).reshape(down_half.shape)
        scale_two = norm_scale(resid_mid)
        gate_up = rows_times(paired_two, gate_up_full)
        ffn_half = down_full.shape[1]
        gate_part = gate_up[:, :ffn_half]
        up_part = gate_up[:, ffn_half:]
        sigmoid_gate = jax.nn.sigmoid(gate_part)
        activated = gate_part * sigmoid_gate
        hidden = (activated * up_part).astype(bf16)

        grad_res = paired_grad_ffn[:frame_count]
        sum_down = scattered(halves(paired_grad_ffn, near), hidden, frame_index, place)
        grad_hidden = rows_times(paired_grad_ffn, down_full)
        grad_gate = grad_hidden * up_part * (sigmoid_gate * (1.0 + gate_part * (1.0 - sigmoid_gate)))
        grad_up = grad_hidden * activated
        grad_gu_low = jnp.concatenate([grad_gate, grad_up], axis=-1).astype(bf16)
        grad_normed_two = own_sum(rows_back(grad_gu_low, gate_up_full))
        sum_gate_up = scattered(halves(paired_two, near), grad_gu_low, frame_index, place)
        back_two, grad_gain_two = norm_back(resid_mid, scale_two, gain_two, grad_normed_two)
        grad_mid = grad_res.astype(f32) + back_two
        paired_grad_attn = paired(grad_mid.astype(bf16))
        grad_mixed = rows_times(paired_grad_attn, out_full).astype(bf16)
        grad_qkv_mixed = attention_backward(qkv_mixed, probs, exchange_rows(grad_mixed, position))
        grad_qkv_low = returned(grad_qkv_mixed)
        result_rows = (resid_mid + own_sum(rows_back(hidden, down_full))).astype(bf16)
        grad_gain_two = grad_gain_two[None]

    wide_q = qkv_full.shape[1]
    count = ctx_pieces.shape[1]
    _, needed = ending_scratch(
        n, frame_count, width_model, context.shape, count, wide_q, head_width, down_half.shape[1]
    )
    if needed <= 66_000_000 and (width_model // n) % LANES == 0:
        (
            own_qkv,
            own_out,
            own_up,
            landed_qkv,
            landed_out,
            landed_up,
            grad_home,
            result,
            sum_context,
            ctx_total,
        ) = ending(
            n,
            resid_in,
            grad_mid,
            norm_gains,
            grad_gain_two,
            result_rows,
            paired_one,
            paired_grad_attn,
            mixed,
            grad_qkv_low,
            qkv_full,
            context,
            ctx_pieces,
            up_send,
            up_stay,
        )
        sum_qkv, sum_out, sum_gate_up, sum_down, grad_home, result = finish(
            (own_qkv, own_out, own_gate, own_up, own_down),
            (landed_qkv, landed_out, landed_gate, landed_up, landed_down),
            grad_home,
            result,
            valid_mask,
        )
    else:

        def parts(left, right):
            away, stay = halves(left, near)
            block = width_model // n
            return [
                dot_rows(part, right).astype(bf16).reshape(n // 2, block, right.shape[1])
                for part in (away, stay)
            ]

        part_away = rows_back(grad_qkv_low[frame_count:], qkv_full).astype(bf16)
        part_stay = rows_back(grad_qkv_low[:frame_count], qkv_full)
        sum_qkv, sum_out, grad_home, result, sum_context, ctx_total = tail(
            n,
            part_away,
            part_stay,
            resid_in,
            grad_mid,
            norm_gains,
            grad_gain_two,
            result_rows,
            *parts(paired_one, grad_qkv_low),
            *parts(paired_grad_attn, mixed),
            context,
            ctx_pieces.transpose(1, 0, 2).reshape(-1, width_model),
        )
        result = (result.astype(f32) * valid_mask)[:, None]
        grad_home = grad_home[:, None]
    ctx_total = ctx_total.T
    sum_ctx = ctx_total[: ctx_weight.shape[0]]
    sum_gains = ctx_total[ctx_weight.shape[0] : ctx_weight.shape[0] + 2]

    return (
        result,
        grad_home,
        sum_context,
        sum_ctx,
        sum_gains,
        sum_qkv[None],
        sum_out[None],
        sum_gate_up[None],
        sum_down[None],
    )


def solution(mesh):
    placed = (
        P("frames", "stream", None),
        P("frames", None),
        P("frames", "stream", None),
        P("frames"),
        P(None, "frames"),
        P(),
        P("stream", None, "frames", None),
        P("stream", None, "frames", None),
        P("stream", None, "frames", None),
        P("stream", None, "frames", None),
    )
    return jax.shard_map(
        shards,
        mesh=mesh,
        in_specs=placed,
        out_specs=(
            P("frames", "stream", None),
            P("frames", "stream", None),
            P("frames", "stream"),
            P(None, ("stream", "frames")),
            P(None, ("stream", "frames")),
            P("stream", None, "frames", None),
            P("stream", None, "frames", None),
            P("stream", None, "frames", None),
            P("stream", None, "frames", None),
        ),
        check_vma=False,
    )
```

```python
import functools
import math

import jax
import jax.numpy as jnp
import numpy as np
from jax import lax
from jax.experimental import pallas as pl
from jax.experimental.pallas import tpu as pltpu
from jax.sharding import PartitionSpec as P

HD = 64
SLOT = 128
LANES = 128
norm_eps = 1e-05
f32 = jnp.float32
bf16 = jnp.bfloat16

PAIRS = [(q, k) for q in range(4) for k in range(q + 1)]


ANY = pl.BlockSpec(memory_space=pl.ANY)
VMEM = pl.BlockSpec(memory_space=pltpu.VMEM)
EXTRA = 32


def flip(value, mask):
    bit = 1
    while bit <= mask:
        if mask & bit:
            value = value + bit - 2 * bit * ((value // bit) % 2)
        bit *= 2
    return value


class Where:
    def __init__(self, n):
        self.n = n
        self.stream = lax.axis_index("stream")
        self.frame = lax.axis_index("frames")
        self.core = self.stream % 2
        self.place = (self.frame // 2) % 2
        self.position = (self.stream // 2) * 2 + self.place
        self.near = self.frame % 2
        self.at = self.frame // 2
        self.far_masks = [m for m in range(2, n, 2) if not m & 2]
        self.both_masks = [m for m in range(2, n, 2) if m & 2 and m > 2]
        self.masks = self.far_masks + self.both_masks + [2]

    def along_stream(self, mask):
        return (flip(self.stream, mask), self.frame)

    def along_frames(self, mask):
        return (self.stream, flip(self.frame, mask))

    def with_position(self, mask):
        return (flip(self.stream, mask & 2), flip(self.frame, 2 * (mask & 1)))

    def across(self):
        return (flip(self.stream, 1), flip(self.frame, 2))


class Wire:
    def __init__(self, send, recv):
        self.send, self.recv, self.count, self.started = send, recv, 0, []

    def make(self, src, dst, device, index=None):
        k = self.count if index is None else index
        if index is None:
            self.count += 1
        return pltpu.make_async_remote_copy(
            src_ref=src,
            dst_ref=dst,
            send_sem=self.send.at[k],
            recv_sem=self.recv.at[k],
            device_id=device,
            device_id_type=pl.DeviceIdType.MESH,
        )

    def start(self, src, dst, device):
        copy = self.make(src, dst, device)
        copy.start()
        self.started.append(copy)
        return copy

    def sent(self, copy):
        self.started = [c for c in self.started if c is not copy]
        copy.wait_send()

    def finish(self):
        for copy in self.started:
            copy.wait_send()


class Local:
    def __init__(self, sems):
        self.sems, self.count = sems, 0

    def start(self, src, dst):
        copy = pltpu.make_async_copy(src, dst, self.sems.at[self.count])
        self.count += 1
        copy.start()
        return copy


def greet(devices):
    barrier = pltpu.get_barrier_semaphore()
    for device in devices:
        pl.semaphore_signal(
            barrier, inc=1, device_id=device, device_id_type=pl.DeviceIdType.MESH
        )
    pl.semaphore_wait(barrier, len(devices))


def dot_rows(left, right):
    return lax.dot_general(left, right, (((0,), (0,)), ((), ())), preferred_element_type=f32)


def dot_columns(left, right):
    return lax.dot_general(left, right, (((1,), (1,)), ((), ())), preferred_element_type=f32)


class Reduction:
    def __init__(self, w, wire, send, keep, arrived, sums, landed, out):
        self.w, self.wire = w, wire
        self.send, self.keep, self.arrived = send, keep, arrived
        self.sums, self.landed, self.out = sums, landed, out
        self.first, self.second = {}, {}
        self.order = w.masks + [0]

    def begin(self, mask):
        block = flip(self.w.at, mask // 2)
        self.first[mask] = self.wire.start(
            self.send.at[block], self.arrived.at[block], self.w.along_frames(1)
        )

    def forward(self, mask):
        block = flip(self.w.at, mask // 2)
        self.first[mask].wait_recv()
        self.wire.sent(self.first[mask])
        total = self.keep[block].astype(f32) + self.arrived[block].astype(f32)
        self.sums[block] = total.astype(bf16)
        if mask:
            self.second[mask] = self.wire.start(
                self.sums.at[block], self.landed.at[mask // 2 - 1], self.w.along_frames(mask)
            )

    def land(self):
        for copy in self.second.values():
            copy.wait_recv()

    def close(self):
        own, other = self.sums[self.w.at].astype(f32), None
        for mask in self.w.masks:
            self.second[mask].wait_recv()
            got = self.landed[mask // 2 - 1].astype(f32)
            if mask & 2:
                other = got if other is None else other + got
            else:
                own = own + got
        self.out[self.w.place] = own
        self.out[1 - self.w.place] = other


def tail_body(
    n, part_send, part_own, resid, mid, gains, gain_two, result_rows,
    gq_send, gq_keep, go_send, go_keep, context, ctx_full,
    out_q, out_o, out_grad, out_result, out_context, out_ctx,
    part_got, low, home, partner_half, half_sum, far_half, whole, kept_q, kept_o,
    arrived_q, arrived_o, sums_q, sums_o, landed_q, landed_o,
    context_held, ctx_held, term, term_got, term_sum, term_landed, gain_sum,
    send_sem, recv_sem, local_sem,
):
    w = Where(n)
    wire, local = Wire(send_sem, recv_sem), Local(local_sem)
    rows, depth = resid.shape
    crossing = w.core != w.place
    load_q = local.start(gq_keep, kept_q)
    load_o = local.start(go_keep, kept_o)
    load_context = local.start(context, context_held)
    load_ctx = local.start(ctx_full, ctx_held)
    greet(
        [w.along_stream(1), w.along_stream(2), w.along_frames(1)]
        + [w.along_frames(m) for m in w.masks]
        + [w.across()]
    )
    part = wire.start(part_send, part_got, w.along_stream(1))
    red_o = Reduction(w, wire, go_send, kept_o, arrived_o, sums_o, landed_o, out_o)
    red_q = Reduction(w, wire, gq_send, kept_q, arrived_q, sums_q, landed_q, out_q)
    for mask in red_o.order:
        red_o.begin(mask)
    for mask in red_q.order:
        red_q.begin(mask)

    part.wait_recv()
    gain = gains[0:1, :]
    gain_sum[...] = jnp.zeros_like(gain_sum)
    step = 64

    @pl.loop(0, rows // step)
    def _(t):
        at = pl.ds(pl.multiple_of(t * step, step), step)
        grad = part_own[at, :].astype(f32) + part_got[at, :].astype(f32)
        values = resid[at, :].astype(f32)
        scale = lax.rsqrt(jnp.mean(values * values, axis=-1, keepdims=True) + norm_eps)
        weighted = grad * gain
        inner = jnp.mean(weighted * values, axis=-1, keepdims=True)
        back = scale * weighted - values * (scale * scale * scale * inner)
        low[at, :] = (mid[at, :] + back).astype(bf16)
        gain_sum[...] += jnp.sum(grad * values * scale, axis=0, keepdims=True)

    row = lax.broadcasted_iota(jnp.int32, (EXTRA, depth), 0)
    low[rows:, :] = jnp.where(
        row == 0, gain_sum[...], jnp.where(row == 1, gain_two[...], 0.0)
    ).astype(bf16)

    cross = wire.make(low, home, w.across())
    cross_result = wire.make(result_rows, out_result, w.across())

    @pl.when(crossing)
    def _():
        cross.start()

    load_o.wait()
    load_q.wait()
    for mask in red_o.order:
        red_o.forward(mask)

    @pl.when(crossing)
    def _():
        cross_result.start()
        cross.wait_recv()

    stay = pltpu.make_async_copy(low, home, local.sems.at[4])
    stay_result = pltpu.make_async_copy(result_rows, out_result, local.sems.at[5])

    @pl.when(jnp.logical_not(crossing))
    def _():
        stay.start()
        stay_result.start()
        stay.wait()

    half = (rows + EXTRA) // 2
    mine = pl.ds(pl.multiple_of(w.core * half, 16), half)
    theirs = pl.ds(pl.multiple_of((1 - w.core) * half, 16), half)
    first = wire.start(home.at[theirs, :], partner_half, w.along_stream(1))
    out_grad[...] = home[:rows, :].astype(f32)
    first.wait_recv()
    half_sum[...] = (home[mine, :].astype(f32) + partner_half[...].astype(f32)).astype(bf16)
    second = wire.start(half_sum, far_half, w.along_stream(2))
    red_q.forward(red_q.order[0])
    red_q.forward(red_q.order[1])
    second.wait_recv()
    whole[mine, :] = (half_sum[...].astype(f32) + far_half[...].astype(f32)).astype(bf16)
    third = wire.start(whole.at[mine, :], whole.at[mine, :], w.along_stream(1))
    load_context.wait()
    third.wait_recv()

    share = depth // 4
    columns = pl.ds(pl.multiple_of(w.stream * share, LANES), share)
    block = share // n
    wide = context_held.shape[1]
    pieces = 2
    grad_share = whole[:rows, columns]
    firsts, seconds = [], []
    row = lax.broadcasted_iota(jnp.int32, (EXTRA, LANES), 0)
    select = (row == lax.broadcasted_iota(jnp.int32, (EXTRA, LANES), 1)).astype(bf16)
    edges = [wide * p // pieces for p in range(pieces)] + [wide + LANES]
    for p in range(pieces):
        lo, hi = edges[p], edges[p + 1]
        for at in range(lo, min(hi, wide), 1024):
            to = min(at + 1024, wide)
            value = dot_rows(grad_share, context_held[:, at:to]).astype(bf16)
            for k in range(n):
                term[k // 2, k % 2, :, at:to] = value[k * block : (k + 1) * block]
        if hi > wide:
            value = dot_rows(whole[rows:, columns], select).astype(bf16)
            for k in range(n):
                term[k // 2, k % 2, :, wide:hi] = value[k * block : (k + 1) * block]
        firsts.append(
            wire.start(
                term.at[:, 1 - w.near, :, lo:hi], term_got.at[:, :, lo:hi], w.along_frames(1)
            )
        )
    for mask in red_q.order[2:]:
        red_q.forward(mask)
    load_ctx.wait()

    def context_rows(t):
        at = pl.ds(pl.multiple_of(t * LANES, LANES), LANES)
        out_context[at, :] = dot_columns(whole[at, :], ctx_held[...])

    @pl.loop(0, rows // LANES)
    def _(t):
        context_rows(t)

    for p in range(pieces):
        lo, hi = edges[p], edges[p + 1]
        firsts[p].wait_recv()
        for mask in w.masks + [0]:
            to = flip(w.at, mask // 2)
            total = term[to, w.near, :, lo:hi].astype(f32) + term_got[to, :, lo:hi].astype(f32)
            term_sum[to, :, lo:hi] = total.astype(bf16)
            if mask:
                seconds.append(
                    wire.start(
                        term_sum.at[to, :, lo:hi],
                        term_landed.at[mask // 2, :, lo:hi],
                        w.along_frames(mask),
                    )
                )
    red_o.close()
    red_q.close()

    @pl.when(crossing)
    def _():
        cross_result.wait_recv()
        cross.wait_send()
        cross_result.wait_send()

    @pl.when(jnp.logical_not(crossing))
    def _():
        stay_result.wait()

    for copy in seconds:
        copy.wait_recv()
    total = term_sum[w.at].astype(f32)
    for mask in w.masks:
        total = total + term_landed[mask // 2].astype(f32)
    out_ctx[...] = total
    wire.finish()


def tail(
    n, part_send, part_own, resid, mid, gains, gain_two, result_rows,
    gq_send, gq_keep, go_send, go_keep, context, ctx_full,
):
    rows, depth = resid.shape
    halfn, block, wide_q = gq_send.shape
    wide_o = go_send.shape[2]
    share = depth // 4 // n
    wide = context.shape[1] + LANES
    half = (rows + EXTRA) // 2
    count = 64 + 2 * n
    scratch = [
        pltpu.VMEM((rows, depth), bf16),
        pltpu.VMEM((rows + EXTRA, depth), bf16),
        pltpu.VMEM((rows + EXTRA, depth), bf16),
        pltpu.VMEM((half, depth), bf16),
        pltpu.VMEM((half, depth), bf16),
        pltpu.VMEM((half, depth), bf16),
        pltpu.VMEM((rows + EXTRA, depth), bf16),
        pltpu.VMEM((halfn, block, wide_q), bf16),
        pltpu.VMEM((halfn, block, wide_o), bf16),
        pltpu.VMEM((halfn, block, wide_q), bf16),
        pltpu.VMEM((halfn, block, wide_o), bf16),
        pltpu.VMEM((halfn, block, wide_q), bf16),
        pltpu.VMEM((halfn, block, wide_o), bf16),
        pltpu.VMEM((halfn, block, wide_q), bf16),
        pltpu.VMEM((halfn, block, wide_o), bf16),
        pltpu.VMEM(context.shape, bf16),
        pltpu.VMEM(ctx_full.shape, bf16),
        pltpu.VMEM((halfn, 2, share, wide), bf16),
        pltpu.VMEM((halfn, share, wide), bf16),
        pltpu.VMEM((halfn, share, wide), bf16),
        pltpu.VMEM((halfn, share, wide), bf16),
        pltpu.VMEM((1, depth), f32),
        pltpu.SemaphoreType.DMA((count,)),
        pltpu.SemaphoreType.DMA((count,)),
        pltpu.SemaphoreType.DMA((6,)),
    ]
    return pl.pallas_call(
        functools.partial(tail_body, n),
        in_specs=[ANY, VMEM, VMEM, VMEM, VMEM, VMEM, VMEM, ANY, ANY, ANY, ANY, ANY, ANY],
        out_specs=[VMEM, VMEM, VMEM, VMEM, VMEM, VMEM],
        out_shape=[
            jax.ShapeDtypeStruct((2, block, wide_q), f32),
            jax.ShapeDtypeStruct((2, block, wide_o), f32),
            jax.ShapeDtypeStruct((rows, depth), f32),
            jax.ShapeDtypeStruct((rows, depth), bf16),
            jax.ShapeDtypeStruct((rows, ctx_full.shape[0]), f32),
            jax.ShapeDtypeStruct((share, wide), f32),
        ],
        scratch_shapes=scratch,
        compiler_params=pltpu.CompilerParams(
            collective_id=5, has_side_effects=True, vmem_limit_bytes=60 << 20
        ),
        name="tail",
    )(
        part_send, part_own, resid, mid, gains, gain_two, result_rows,
        gq_send, gq_keep, go_send, go_keep, context, ctx_full,
    )


def ending_body(
    n, resid, mid, gains, gain_two, result_rows,
    pair_one, pair_grad, mixed_rows, grad_qkv_rows, qkv_weight, context, ctx_pieces, up_send, up_stay,
    out_q, out_o, out_up, landed_q, landed_o, landed_up, out_grad, out_result, out_context, out_ctx,
    one, grad_two, mixed, grad_qkv, qkv_full, left_away, left_stay, part_send, part_own,
    part_got, low, home, partner_half, half_sum, far_half, whole, result_home,
    send_q, send_o, kept_q, kept_o, arrived_q, arrived_o, send_up, kept_up, arrived_up,
    context_held, ctx_held, term, term_got, term_sum, term_landed, gain_sum,
    send_sem, recv_sem, local_sem,
):
    w = Where(n)
    wire, local = Wire(send_sem, recv_sem), Local(local_sem)
    rows, depth = resid.shape
    piece = depth // n
    crossing = w.core != w.place
    load_up = local.start(up_send, send_up)
    load_grad = local.start(pair_grad, grad_two)
    load_mixed = local.start(mixed_rows, mixed)
    load_qkv = local.start(grad_qkv_rows, grad_qkv)
    load_weight = local.start(qkv_weight, qkv_full)
    load_one = local.start(pair_one, one)
    load_up_stay = local.start(up_stay, kept_up)
    load_context = local.start(context, context_held)
    load_ctx = [
        local.start(ctx_pieces.at[k], ctx_held.at[:, k * piece : (k + 1) * piece])
        for k in range(n)
    ]
    greet(
        [w.along_stream(1), w.along_stream(2), w.along_frames(1)]
        + [w.along_frames(m) for m in w.masks]
        + [w.across()]
    )
    cross_result = wire.make(result_rows, result_home, w.across())
    stay_result = pltpu.make_async_copy(result_rows, result_home, local.sems.at[30])
    stay = pltpu.make_async_copy(low, home, local.sems.at[31])

    @pl.when(crossing)
    def _():
        cross_result.start()

    @pl.when(jnp.logical_not(crossing))
    def _():
        stay_result.start()

    def split(source, which, into):
        for b in range(n // 2):
            at = pl.ds(pl.multiple_of((2 * b + which) * piece, piece), piece)
            into[:, b * piece : (b + 1) * piece] = source[:, at]

    def product(left, right, into):
        wide = right.shape[1]
        for lo in range(0, wide, 512):
            value = dot_rows(left[...], right[:, lo : lo + 512]).astype(bf16)
            for b in range(n // 2):
                into[b, :, lo : lo + 512] = value[b * piece : (b + 1) * piece]

    def partial(t):
        at = pl.ds(pl.multiple_of(t * 256, 256), 256)
        return dot_columns(grad_qkv[at, :], qkv_full[...])

    load_up.wait()
    red_up = Reduction(w, wire, send_up, kept_up, arrived_up, send_up, landed_up, out_up)
    for mask in red_up.order:
        red_up.begin(mask)
    load_grad.wait()
    split(grad_two, 1 - w.near, left_away)
    load_mixed.wait()
    product(left_away, mixed, send_o)
    red_o = Reduction(w, wire, send_o, kept_o, arrived_o, send_o, landed_o, out_o)
    for mask in red_o.order:
        red_o.begin(mask)
    load_qkv.wait()
    load_weight.wait()

    @pl.loop(0, rows // 256)
    def _(t):
        to = pl.ds(pl.multiple_of(t * 256, 256), 256)
        part_send[to, :] = partial(rows // 256 + t).astype(bf16)

    part = wire.start(part_send, part_got, w.along_stream(1))
    load_one.wait()
    split(one, 1 - w.near, left_away)
    product(left_away, grad_qkv, send_q)
    red_q = Reduction(w, wire, send_q, kept_q, arrived_q, send_q, landed_q, out_q)
    for mask in red_q.order:
        red_q.begin(mask)

    @pl.loop(0, rows // 256)
    def _(t):
        to = pl.ds(pl.multiple_of(t * 256, 256), 256)
        part_own[to, :] = partial(t)

    part.wait_recv()
    gain = gains[0:1, :]
    gain_sum[...] = jnp.zeros_like(gain_sum)
    step = 64

    @pl.loop(0, rows // step)
    def _(t):
        at = pl.ds(pl.multiple_of(t * step, step), step)
        grad = part_own[at, :].astype(f32) + part_got[at, :].astype(f32)
        values = resid[at, :].astype(f32)
        scale = lax.rsqrt(jnp.mean(values * values, axis=-1, keepdims=True) + norm_eps)
        weighted = grad * gain
        inner = jnp.mean(weighted * values, axis=-1, keepdims=True)
        back = scale * weighted - values * (scale * scale * scale * inner)
        low[at, :] = (mid[at, :] + back).astype(bf16)
        gain_sum[...] += jnp.sum(grad * values * scale, axis=0, keepdims=True)

    row = lax.broadcasted_iota(jnp.int32, (EXTRA, depth), 0)
    low[rows:, :] = jnp.where(
        row == 0, gain_sum[...], jnp.where(row == 1, gain_two[...], 0.0)
    ).astype(bf16)

    cross = wire.make(low, home, w.across())

    @pl.when(crossing)
    def _():
        cross.start()

    split(grad_two, w.near, left_stay)
    product(left_stay, mixed, kept_o)
    load_up_stay.wait()
    for mask in red_up.order[:2]:
        red_up.forward(mask)
    for mask in red_o.order:
        red_o.forward(mask)

    @pl.when(crossing)
    def _():
        cross_result.wait_recv()

    @pl.when(jnp.logical_not(crossing))
    def _():
        stay.start()
        stay_result.wait()

    split(one, w.near, left_stay)
    product(left_stay, grad_qkv, kept_q)
    store_result = local.start(result_home, out_result)

    @pl.when(crossing)
    def _():
        cross.wait_recv()

    @pl.when(jnp.logical_not(crossing))
    def _():
        stay.wait()

    half = (rows + EXTRA) // 2
    mine = pl.ds(pl.multiple_of(w.core * half, 16), half)
    theirs = pl.ds(pl.multiple_of((1 - w.core) * half, 16), half)
    first = wire.start(home.at[theirs, :], partner_half, w.along_stream(1))
    store_grad = local.start(home.at[:rows, :], out_grad)
    for mask in red_up.order[2:]:
        red_up.forward(mask)
    first.wait_recv()
    half_sum[...] = (home[mine, :].astype(f32) + partner_half[...].astype(f32)).astype(bf16)
    second = wire.start(half_sum, far_half, w.along_stream(2))
    red_q.forward(red_q.order[0])
    red_q.forward(red_q.order[1])
    second.wait_recv()
    whole[mine, :] = (half_sum[...].astype(f32) + far_half[...].astype(f32)).astype(bf16)
    third = wire.start(whole.at[mine, :], whole.at[mine, :], w.along_stream(1))
    load_context.wait()
    third.wait_recv()

    share = depth // 4
    columns = pl.ds(pl.multiple_of(w.stream * share, LANES), share)
    block = share // n
    wide = context_held.shape[1]
    pieces = 4
    grad_share = whole[:rows, columns]
    firsts, seconds = [], []
    row = lax.broadcasted_iota(jnp.int32, (EXTRA, LANES), 0)
    select = (row == lax.broadcasted_iota(jnp.int32, (EXTRA, LANES), 1)).astype(bf16)
    edges = [wide * p // pieces for p in range(pieces)] + [wide + LANES]
    for p in range(pieces):
        lo, hi = edges[p], edges[p + 1]
        for at in range(lo, min(hi, wide), 1024):
            to = min(at + 1024, wide)
            value = dot_rows(grad_share, context_held[:, at:to]).astype(bf16)
            for k in range(n):
                term[k // 2, k % 2, :, at:to] = value[k * block : (k + 1) * block]
        if hi > wide:
            value = dot_rows(whole[rows:, columns], select).astype(bf16)
            for k in range(n):
                term[k // 2, k % 2, :, wide:hi] = value[k * block : (k + 1) * block]
        firsts.append(
            wire.start(
                term.at[:, 1 - w.near, :, lo:hi], term_got.at[:, :, lo:hi], w.along_frames(1)
            )
        )
    for mask in red_q.order[2:]:
        red_q.forward(mask)
    for copy in load_ctx:
        copy.wait()

    def context_rows(t):
        at = pl.ds(pl.multiple_of(t * LANES, LANES), LANES)
        out_context[at, :] = dot_columns(whole[at, :], ctx_held[...])

    @pl.loop(0, rows // LANES)
    def _(t):
        context_rows(t)

    for p in range(pieces):
        lo, hi = edges[p], edges[p + 1]
        firsts[p].wait_recv()
        for mask in w.masks + [0]:
            to = flip(w.at, mask // 2)
            total = term[to, w.near, :, lo:hi].astype(f32) + term_got[to, :, lo:hi].astype(f32)
            term_sum[to, :, lo:hi] = total.astype(bf16)
            if mask:
                seconds.append(
                    wire.start(
                        term_sum.at[to, :, lo:hi],
                        term_landed.at[mask // 2, :, lo:hi],
                        w.along_frames(mask),
                    )
                )
    red_up.land()
    red_o.land()
    red_q.land()
    kept = [
        store_result,
        store_grad,
        local.start(send_o.at[w.at], out_o),
        local.start(send_q.at[w.at], out_q),
        local.start(send_up.at[w.at], out_up),
    ]

    @pl.when(crossing)
    def _():
        cross.wait_send()
        cross_result.wait_send()

    for copy in seconds:
        copy.wait_recv()
    total = term_sum[w.at].astype(f32)
    for mask in w.masks:
        total = total + term_landed[mask // 2].astype(f32)
    out_ctx[...] = total
    for copy in kept:
        copy.wait()
    wire.finish()


def ending_scratch(n, rows, depth, context_shape, count, wide_q, wide_o, wide_up):
    halfn, block, share = n // 2, depth // n, depth // 4 // n
    wide = context_shape[1] + LANES
    half = (rows + EXTRA) // 2
    both = 2 * rows
    shapes = [
        ((both, depth), bf16),
        ((both, depth), bf16),
        ((both, wide_o), bf16),
        ((both, wide_q), bf16),
        ((depth, wide_q), bf16),
        ((both, depth // 2), bf16),
        ((both, depth // 2), bf16),
        ((rows, depth), bf16),
        ((rows, depth), f32),
        ((rows, depth), bf16),
        ((rows + EXTRA, depth), bf16),
        ((rows + EXTRA, depth), bf16),
        ((half, depth), bf16),
        ((half, depth), bf16),
        ((half, depth), bf16),
        ((rows + EXTRA, depth), bf16),
        ((rows, depth), bf16),
        ((halfn, block, wide_q), bf16),
        ((halfn, block, wide_o), bf16),
        ((halfn, block, wide_q), bf16),
        ((halfn, block, wide_o), bf16),
        ((halfn, block, wide_q), bf16),
        ((halfn, block, wide_o), bf16),
        ((halfn, block, wide_up), bf16),
        ((halfn, block, wide_up), bf16),
        ((halfn, block, wide_up), bf16),
        (context_shape, bf16),
        ((count, depth), bf16),
        ((halfn, 2, share, wide), bf16),
        ((halfn, share, wide), bf16),
        ((halfn, share, wide), bf16),
        ((halfn, share, wide), bf16),
        ((1, depth), f32),
    ]
    others = [((rows, depth), f32)] * 4 + [((rows, depth), bf16)] * 2 + [((rows, count), f32)]
    return shapes, sum(math.prod(dims) * jnp.dtype(kind).itemsize for dims, kind in shapes + others)


def ending(
    n, resid, mid, gains, gain_two, result_rows,
    pair_one, pair_grad, mixed, grad_qkv, qkv_full, context, ctx_pieces, up_send, up_stay,
):
    rows, depth = resid.shape
    halfn, block = n // 2, depth // n
    wide_q, wide_o = qkv_full.shape[1], mixed.shape[1]
    count = ctx_pieces.shape[1]
    wide_up = up_send.shape[2]
    shapes, _ = ending_scratch(n, rows, depth, context.shape, count, wide_q, wide_o, wide_up)
    sems = 64 + 2 * n
    shape = jax.ShapeDtypeStruct
    return pl.pallas_call(
        functools.partial(ending_body, n),
        in_specs=[VMEM] * 5 + [ANY] * 9,
        out_specs=[ANY] * 8 + [VMEM] * 2,
        out_shape=[
            shape((block, wide_q), bf16),
            shape((block, wide_o), bf16),
            shape((block, wide_up), bf16),
            shape((halfn - 1, block, wide_q), bf16),
            shape((halfn - 1, block, wide_o), bf16),
            shape((halfn - 1, block, wide_up), bf16),
            shape((rows, depth), bf16),
            shape((rows, depth), bf16),
            shape((rows, count), f32),
            shape((depth // 4 // n, context.shape[1] + LANES), f32),
        ],
        scratch_shapes=[pltpu.VMEM(dims, kind) for dims, kind in shapes]
        + [
            pltpu.SemaphoreType.DMA((sems,)),
            pltpu.SemaphoreType.DMA((sems,)),
            pltpu.SemaphoreType.DMA((32,)),
        ],
        compiler_params=pltpu.CompilerParams(
            collective_id=6, has_side_effects=True, vmem_limit_bytes=67_000_000
        ),
        name="ending",
    )(
        resid, mid, gains, gain_two, result_rows,
        pair_one, pair_grad, mixed, grad_qkv, qkv_full, context, ctx_pieces, up_send, up_stay,
    )


def finish_body(
    own_q, own_o, own_gate, own_up, own_down, far_q, far_o, far_gate, far_up, far_down,
    grad, result, valid, out_q, out_o, out_gu, out_down, out_grad, out_result,
):
    place = (lax.axis_index("frames") // 2) % 2

    def settle(own, far, out, columns):
        total, other = own[...].astype(f32), None
        for k in range(far.shape[0]):
            value = far[k].astype(f32)
            if (k + 1) & 1:
                other = value if other is None else other + value
            else:
                total = total + value
        out[place, :, columns] = total
        out[1 - place, :, columns] = other

    wide = own_gate.shape[1]
    settle(own_q, far_q, out_q, slice(None))
    settle(own_o, far_o, out_o, slice(None))
    settle(own_gate, far_gate, out_gu, slice(0, wide))
    settle(own_up, far_up, out_gu, slice(wide, 2 * wide))
    settle(own_down, far_down, out_down, slice(None))
    out_grad[:, 0, :] = grad[...].astype(f32)
    out_result[:, 0, :] = result[...].astype(f32) * valid[...]


def finish(owns, fars, grad, result, valid, steps=4):
    block = owns[0].shape[0] // steps
    rows, depth = grad.shape
    shape = jax.ShapeDtypeStruct
    q, o, gate, up, down = [own.shape[1] for own in owns]
    here = rows // steps

    def own_spec(wide):
        return pl.BlockSpec((block, wide), lambda t: (t, 0))

    def far_spec(count, wide):
        return pl.BlockSpec((count, block, wide), lambda t: (0, t, 0))

    widths = (q, o, gate + up, down)
    row_out = pl.BlockSpec((here, 1, depth), lambda t: (t, 0, 0))
    return pl.pallas_call(
        finish_body,
        grid=(steps,),
        in_specs=[own_spec(x.shape[1]) for x in owns]
        + [far_spec(x.shape[0], x.shape[2]) for x in fars]
        + [pl.BlockSpec((here, depth), lambda t: (t, 0))] * 2
        + [pl.BlockSpec((here, 1), lambda t: (t, 0))],
        out_specs=[far_spec(2, wide) for wide in widths] + [row_out, row_out],
        out_shape=[shape((2, owns[0].shape[0], wide), f32) for wide in widths]
        + [shape((rows, 1, depth), f32)] * 2,
        compiler_params=pltpu.CompilerParams(vmem_limit_bytes=60 << 20),
        name="finish",
    )(*owns, *fars, grad, result, valid)


def swap_frames(value, mask):
    n = lax.axis_size("frames")
    return lax.ppermute(value, "frames", [(d, d ^ mask) for d in range(n)])


def swap_stream(value, mask):
    n = lax.axis_size("stream")
    return lax.ppermute(value, "stream", [(d, d ^ mask) for d in range(n)])


def joint(value, target):
    streams, n = lax.axis_size("stream"), lax.axis_size("frames")
    pairs = []
    for s in range(streams):
        for f in range(n):
            to_s, to_f = target(s, f)
            pairs.append((s * n + f, to_s * n + to_f))
    return lax.ppermute(value, ("stream", "frames"), pairs)


def transposed(value):
    def target(s, f):
        core, place = s % 2, (f // 2) % 2
        return s - core + place, f - 2 * place + 2 * core

    return joint(value, target)


def peer(value, mask):
    return joint(value, lambda s, f: (s ^ (mask & 2), f ^ (2 * (mask & 1))))


def norm_scale(values):
    return lax.rsqrt(jnp.mean(values * values, axis=-1, keepdims=True) + norm_eps)


def norm_back(values, scale, gain, grad):
    weighted = grad * gain
    inner_mean = jnp.mean(weighted * values, axis=-1, keepdims=True)
    grad_values = scale * weighted - values * (scale * scale * scale) * inner_mean
    grad_gain = jnp.sum(grad * values * scale, axis=0)
    return (grad_values, grad_gain)


def exchange_rows(qkv, position):
    rows, width = qkv.shape
    quarter = rows // 4
    parts = qkv.reshape(4, quarter, width)
    out = jnp.zeros((4, quarter, width), qkv.dtype)
    own = lax.dynamic_index_in_dim(parts, position, 0, keepdims=False)
    out = lax.dynamic_update_index_in_dim(out, own, position, 0)
    for mask in (2, 1, 3):
        there = position ^ mask
        got = peer(lax.dynamic_index_in_dim(parts, there, 0, keepdims=False), mask)
        out = lax.dynamic_update_index_in_dim(out, got, there, 0)
    return out


def heads_sum(product, fold):
    high = product.astype(bf16)
    low = (product - high.astype(f32)).astype(bf16)
    return jnp.dot(high, fold, preferred_element_type=f32) + jnp.dot(
        low, fold, preferred_element_type=f32
    )


def attention_forward_rows(at, qkv_ref, fold, spread, probs_ref, out_ref):
    width = out_ref.shape[2]
    for q in range(4):
        query = qkv_ref[q, at, :width].astype(f32)
        scores = []
        for k in range(q + 1):
            key = qkv_ref[k, at, width : 2 * width].astype(f32)
            scores.append(heads_sum(query * key, fold) * HD ** (-0.5))
        top = functools.reduce(jnp.maximum, scores)
        expo = [jnp.exp(s - top) for s in scores]
        total = functools.reduce(jnp.add, expo)
        mixed = None
        for k in range(q + 1):
            prob = expo[k] / total
            probs_ref[PAIRS.index((q, k)), at, :] = prob
            wide = jnp.dot(prob.astype(bf16), spread, preferred_element_type=f32)
            term = wide * qkv_ref[k, at, 2 * width :].astype(f32)
            mixed = term if mixed is None else mixed + term
        out_ref[q, at, :] = mixed.astype(bf16)


def attention_backward_rows(at, qkv_ref, probs_ref, grad_ref, fold, spread, out_ref):
    width = grad_ref.shape[2]
    grad_keys, grad_values = [None] * 4, [None] * 4
    for q in range(4):
        grad = grad_ref[q, at, :].astype(f32)
        query = qkv_ref[q, at, :width].astype(f32)
        probs = [probs_ref[PAIRS.index((q, k)), at, :] for k in range(q + 1)]
        grad_probs = [
            heads_sum(grad * qkv_ref[k, at, 2 * width :].astype(f32), fold) for k in range(q + 1)
        ]
        total = functools.reduce(jnp.add, [p * g for p, g in zip(probs, grad_probs)])
        grad_query = None
        for k in range(q + 1):
            wide = jnp.dot(probs[k].astype(bf16), spread, preferred_element_type=f32)
            term = wide * grad
            grad_values[k] = term if grad_values[k] is None else grad_values[k] + term
            grad_score = (probs[k] * (grad_probs[k] - total)).astype(bf16)
            wide = jnp.dot(grad_score, spread, preferred_element_type=f32)
            term = wide * qkv_ref[k, at, width : 2 * width].astype(f32)
            grad_query = term if grad_query is None else grad_query + term
            term = wide * query
            grad_keys[k] = term if grad_keys[k] is None else grad_keys[k] + term
        out_ref[q, at, :width] = (grad_query * HD ** (-0.5)).astype(bf16)
    for k in range(4):
        out_ref[k, at, width : 2 * width] = (grad_keys[k] * HD ** (-0.5)).astype(bf16)
        out_ref[k, at, 2 * width :] = grad_values[k].astype(bf16)


def attention_backward_body(qkv_ref, probs_ref, grad_ref, fold_ref, spread_ref, out_ref):
    everything = slice(None)
    attention_backward_rows(
        everything, qkv_ref, probs_ref, grad_ref, fold_ref[...], spread_ref[...], out_ref
    )


def fold_matrices(width):
    fold = np.arange(width)[:, None] // HD == np.arange(LANES)[None, :]
    return jnp.asarray(fold, bf16), jnp.asarray(fold.T, bf16)


def attention_backward(qkv, probs, grad, step=64):
    _, rows, triple = qkv.shape
    width = triple // 3
    fold, spread = fold_matrices(width)
    return pl.pallas_call(
        attention_backward_body,
        grid=(rows // step,),
        in_specs=[
            pl.BlockSpec((4, step, triple), lambda r: (0, r, 0)),
            pl.BlockSpec((len(PAIRS), step, LANES), lambda r: (0, r, 0)),
            pl.BlockSpec((4, step, width), lambda r: (0, r, 0)),
            pl.BlockSpec((width, LANES), lambda r: (0, 0)),
            pl.BlockSpec((LANES, width), lambda r: (0, 0)),
        ],
        out_specs=pl.BlockSpec((4, step, triple), lambda r: (0, r, 0)),
        out_shape=jax.ShapeDtypeStruct((4, rows, triple), bf16),
        name="attention_backward",
    )(qkv, probs, grad, fold, spread)


def after(value, *others):
    return lax.optimization_barrier((value,) + others)[0]


def taken(weights, place):
    own = [lax.dynamic_index_in_dim(w, place, 0, keepdims=False) for w in weights]
    other = [lax.dynamic_index_in_dim(w, 1 - place, 0, keepdims=False) for w in weights]
    if len(weights) == 1:
        return own[0], other[0]
    return jnp.concatenate(own, axis=1), jnp.concatenate(other, axis=1)


def placed_rows(pieces, frame_index, start, width):
    n = lax.axis_size("frames")
    block = pieces[0].shape[0]
    full = jnp.zeros((n, block, width), pieces[0].dtype)
    for mask in range(n):
        part = pieces[mask][:, start : start + width]
        full = lax.dynamic_update_index_in_dim(full, part, frame_index ^ mask, 0)
    return full.reshape(n * block, width)


def halves(left, near):
    n = lax.axis_size("frames")
    rows, depth = left.shape
    block = depth // n
    even = jnp.concatenate([left[:, k * block : (k + 1) * block] for k in range(0, n, 2)], axis=1)
    odd = jnp.concatenate([left[:, k * block : (k + 1) * block] for k in range(1, n, 2)], axis=1)
    return jnp.where(near == 0, odd, even), jnp.where(near == 0, even, odd)


def scattered(left_halves, right, frame_index, place):
    n = lax.axis_size("frames")

    def product(part):
        return lax.dot_general(
            part, right, (((0,), (0,)), ((), ())), preferred_element_type=f32
        ).astype(bf16)

    arrived = swap_frames(product(left_halves[0]), 1)
    half_sum = (product(left_halves[1]).astype(f32) + arrived.astype(f32)).astype(bf16)
    half_sum = half_sum.reshape(n // 2, -1, right.shape[1])
    at = frame_index // 2
    own = lax.dynamic_index_in_dim(half_sum, at, 0, keepdims=False).astype(f32)
    other = None
    for mask in range(2, n, 2):
        got = swap_frames(
            lax.dynamic_index_in_dim(half_sum, at ^ (mask // 2), 0, keepdims=False), mask
        ).astype(f32)
        if mask & 2:
            other = got if other is None else other + got
        else:
            own = own + got
    first = jnp.where(place == 0, own, other)
    second = jnp.where(place == 0, other, own)
    return jnp.stack([first, second], axis=0)


class Spread:
    def __init__(self, w, wire, weight, full):
        self.w, self.wire, self.weight, self.full = w, wire, weight, full
        self.block = full.shape[0] // w.n
        self.far, self.near = {}, {}

    def rows(self, frame):
        return self.full.at[pl.ds(pl.multiple_of(frame * self.block, self.block), self.block), :]

    def own(self, local):
        return local.start(self.weight.at[self.w.place], self.rows(self.w.frame))

    def own_near(self):
        w = self.w
        self.near[0] = self.wire.start(
            self.weight.at[w.place], self.rows(w.frame), w.along_frames(1)
        )

    def send(self, masks):
        w = self.w
        for mask in masks:
            which = 1 - w.place if mask & 2 else w.place
            self.far[mask] = self.wire.start(
                self.weight.at[which], self.rows(w.frame), w.along_frames(mask)
            )

    def relay(self, mask):
        self.far[mask].wait_recv()
        rows = self.rows(flip(self.w.frame, mask))
        self.near[mask] = self.wire.start(rows, rows, self.w.along_frames(1))

    def close(self):
        for copy in self.near.values():
            copy.wait_recv()


def front_body(
    n, context, ctx_weight, inputs, cotangent, valid, gains, fold, spread,
    qkv_weight, out_weight, gu_weight, down_weight,
    out_qkv, out_out, out_gu, out_down, out_ctx, out_resid, out_mid, out_one, out_two, out_grad,
    out_qkv_mixed, out_probs, out_mixed,
    ctx_held, context_held, total, partner_half, half_sum, far_half, whole, home, resid, pair,
    qkv_full, out_full, qkv_rows, qkv_mixed, probs, mixed_quarter, mixed, away, got, grad_low,
    send_sem, recv_sem, local_sem,
):
    w = Where(n)
    wire, local = Wire(send_sem, recv_sem), Local(local_sem)
    rows, depth = inputs.shape
    count = ctx_weight.shape[0] // 4
    piece = depth // n
    crossing = w.core != w.place
    half = rows // 2
    step = 64
    quarter_of_context = pl.ds(pl.multiple_of(w.stream * count, LANES), count)
    load_context = local.start(context.at[:, quarter_of_context], context_held)
    load_ctx = local.start(ctx_weight.at[quarter_of_context, :], ctx_held.at[w.frame])
    qkv = Spread(w, wire, qkv_weight, qkv_full)
    out = Spread(w, wire, out_weight, out_full)
    gu = Spread(w, wire, gu_weight, out_gu)
    down = Spread(w, wire, down_weight, out_down)
    owns = [qkv.own(local), out.own(local)]
    greet(
        [w.along_stream(1), w.along_stream(2), w.along_frames(1)]
        + [w.along_frames(m) for m in w.masks]
        + [w.across(), w.with_position(3)]
    )

    load_ctx.wait()
    held, near = [0], {}

    def ctx_near(o):
        at = flip(w.frame, o)
        near[o] = wire.start(ctx_held.at[at], ctx_held.at[at], w.along_frames(1))

    ready = []
    for bit in reversed(range(1, n.bit_length() - 1)):
        copies = []
        for o in held:
            at = flip(w.frame, o)
            copies.append(
                (o, wire.start(ctx_held.at[at], ctx_held.at[at], w.along_frames(1 << bit)))
            )
        if bit == n.bit_length() - 2:
            ctx_near(0)
            qkv.own_near()
            out.own_near()
        if bit == 1:
            for mask in w.masks:
                qkv.send([mask])
                out.send([mask])
        for o, copy in copies:
            copy.wait_recv()
            ctx_near(o ^ (1 << bit))
            held.append(o ^ (1 << bit))

    load_context.wait()

    def project(o):
        at = flip(w.frame, o)
        columns = pl.ds(pl.multiple_of(at * piece, piece), piece)
        value = jnp.dot(context_held[...], ctx_held[at], preferred_element_type=f32)
        total[:, columns] = value

    def relay_attention(k):
        for mask in w.masks[k : k + 1]:
            qkv.relay(mask)
            out.relay(mask)

    if piece % LANES == 0:
        for o in held:
            project(o)
        for o in held:
            if o == held[-1]:
                relay_attention(0)
            near[o].wait_recv()
            project(o ^ 1)
    else:
        for o in held:
            near[o].wait_recv()
        relay_attention(0)
        total[...] = jnp.zeros_like(total)

        @pl.loop(0, n)
        def _(at):
            line = lax.broadcasted_iota(jnp.int32, (piece, depth), 0)
            column = lax.broadcasted_iota(jnp.int32, (piece, depth), 1)
            select = (column == line + at * piece).astype(bf16)
            laid = jnp.dot(ctx_held[at], select, preferred_element_type=f32).astype(bf16)

            @pl.loop(0, rows // LANES)
            def _(t):
                here = pl.ds(pl.multiple_of(t * LANES, LANES), LANES)
                total[here, :] += jnp.dot(
                    context_held[here, :], laid, preferred_element_type=f32
                )

    store_ctx = local.start(ctx_held, out_ctx)

    mine = pl.ds(pl.multiple_of(w.core * half, 16), half)
    theirs = pl.ds(pl.multiple_of((1 - w.core) * half, 16), half)
    whole[theirs, :] = total[theirs, :].astype(bf16)
    first = wire.start(whole.at[theirs, :], partner_half, w.along_stream(1))
    first.wait_recv()
    half_sum[...] = (total[mine, :] + partner_half[...].astype(f32)).astype(bf16)
    second = wire.start(half_sum, far_half, w.along_stream(2))
    relay_attention(1)
    second.wait_recv()
    home[mine, :] = (half_sum[...].astype(f32) + far_half[...].astype(f32)).astype(bf16)
    third = wire.start(home.at[mine, :], home.at[mine, :], w.along_stream(1))
    third.wait_recv()
    wire.sent(third)

    @pl.loop(0, rows // step)
    def _(t):
        at = pl.ds(pl.multiple_of(t * step, step), step)
        home[at, :] = (home[at, :].astype(f32) + inputs[at, :].astype(f32)).astype(bf16)

    cross = wire.make(home, resid, w.across())
    stay = pltpu.make_async_copy(home, resid, local_sem.at[22])

    @pl.when(crossing)
    def _():
        cross.start()

    @pl.when(jnp.logical_not(crossing))
    def _():
        stay.start()

    gu.own_near()
    gu.send(w.far_masks + w.both_masks)
    for k in range(2, len(w.masks)):
        relay_attention(k)

    @pl.when(crossing)
    def _():
        cross.wait_recv()

    @pl.when(jnp.logical_not(crossing))
    def _():
        stay.wait()

    def normed(source, gain):
        @pl.loop(0, rows // step)
        def _(t):
            at = pl.ds(pl.multiple_of(t * step, step), step)
            values = source[at, :].astype(f32)
            scale = lax.rsqrt(jnp.mean(values * values, axis=-1, keepdims=True) + norm_eps)
            pair[at, :] = (values * scale * gain).astype(bf16)

    normed(resid, gains[0:1, :])
    upper = pair.at[rows:, :]
    first_pair = wire.start(pair.at[:rows, :], upper, w.along_stream(1))
    for copy in owns:
        copy.wait()
    qkv.close()
    out.close()
    quarter = 2 * rows // 4
    width = out_full.shape[1]

    def qkv_of(lo, hi):
        @pl.loop(lo, hi)
        def _(t):
            at = pl.ds(pl.multiple_of(t * quarter, quarter), quarter)
            left = pair[at, :]
            for p in range(3):
                columns = slice(p * width, (p + 1) * width)
                value = jnp.dot(left, qkv_full[:, columns], preferred_element_type=f32)
                qkv_rows[at, columns] = value.astype(bf16)

    qkv_of(0, 2)
    first_pair.wait_recv()
    qkv_of(2, 4)
    mixing = {}

    def rows_of(position):
        return pl.ds(pl.multiple_of(position * quarter, quarter), quarter)

    for mask in (3, 1, 2):
        mixing[mask] = wire.start(
            qkv_rows.at[rows_of(flip(w.position, mask)), :],
            qkv_mixed.at[w.position],
            w.with_position(mask),
        )
    own_quarter = local.start(qkv_rows.at[rows_of(w.position), :], qkv_mixed.at[w.position])
    gu.send([2])
    down.send(w.far_masks)
    @pl.loop(0, rows // step)
    def _(t):
        at = pl.ds(pl.multiple_of(t * step, step), step)
        grad_low[at, :] = (cotangent[at, 0, :] * valid[at, :]).astype(bf16)

    stores = [
        local.start(pair, out_one),
        local.start(qkv_full, out_qkv),
        local.start(out_full, out_out),
        local.start(resid, out_resid),
        local.start(grad_low, out_grad),
    ]
    gu_own, down_own = gu.own(local), down.own(local)
    for mask in w.far_masks:
        gu.relay(mask)
    own_quarter.wait()
    for mask in (2, 1, 3):
        mixing[mask].wait_recv()
    for mask in w.both_masks:
        gu.relay(mask)
    fold_held, spread_held = fold[...], spread[...]

    @pl.loop(0, quarter // step)
    def _(t):
        at = pl.ds(pl.multiple_of(t * step, step), step)
        attention_forward_rows(at, qkv_mixed, fold_held, spread_held, probs, mixed_quarter)

    returning = {}
    for mask in (3, 1, 2):
        returning[mask] = wire.start(
            mixed_quarter.at[flip(w.position, mask)],
            mixed.at[rows_of(w.position), :],
            w.with_position(mask),
        )
    own_back = local.start(mixed_quarter.at[w.position], mixed.at[rows_of(w.position), :])
    down.send(w.both_masks + [2])
    stores += [local.start(qkv_mixed, out_qkv_mixed), local.start(probs, out_probs)]
    gu.relay(2)
    own_back.wait()
    for mask in (2, 1, 3):
        returning[mask].wait_recv()
    stores.append(local.start(mixed, out_mixed))
    stores[0].wait()

    @pl.loop(2, 4)
    def _(t):
        at = pl.ds(pl.multiple_of(t * quarter, quarter), quarter)
        to = pl.ds(pl.multiple_of(t * quarter - rows, quarter), quarter)
        away[to, :] = dot_columns(mixed[at, :], out_full[...]).astype(bf16)

    part = wire.start(away, got, w.along_stream(1))

    @pl.loop(0, 2)
    def _(t):
        at = pl.ds(pl.multiple_of(t * quarter, quarter), quarter)
        total[at, :] = dot_columns(mixed[at, :], out_full[...])

    part.wait_recv()
    wire.sent(first_pair)
    gain = gains[1:2, :]

    @pl.loop(0, rows // step)
    def _(t):
        at = pl.ds(pl.multiple_of(t * step, step), step)
        values = resid[at, :].astype(f32) + total[at, :] + got[at, :].astype(f32)
        total[at, :] = values
        scale = lax.rsqrt(jnp.mean(values * values, axis=-1, keepdims=True) + norm_eps)
        pair[at, :] = (values * scale * gain).astype(bf16)

    second_pair = wire.start(pair.at[:rows, :], upper, w.along_stream(1))
    stores.append(local.start(total, out_mid))
    second_pair.wait_recv()
    stores.append(local.start(pair, out_two))
    gu.close()
    for copy in down.far.values():
        copy.wait_recv()
    for copy in stores[1:]:
        copy.wait()
    for copy in (store_ctx, gu_own, down_own):
        copy.wait()

    @pl.when(crossing)
    def _():
        cross.wait_send()

    wire.finish()


def front(
    n, context, ctx_weight, inputs, cotangent, valid, gains,
    qkv_weight, out_weight, gu_weight, down_weight,
):
    rows, depth = inputs.shape
    count = ctx_weight.shape[0] // 4
    wide_q, wide_o = qkv_weight.shape[2], out_weight.shape[2]
    fold, spread = fold_matrices(wide_o)
    quarter = rows // 2
    half = rows // 2
    pairs = len(PAIRS)
    scratch = [
        pltpu.VMEM((n, count, depth // n), bf16),
        pltpu.VMEM((rows, count), bf16),
        pltpu.VMEM((rows, depth), f32),
        pltpu.VMEM((half, depth), bf16),
        pltpu.VMEM((half, depth), bf16),
        pltpu.VMEM((half, depth), bf16),
        pltpu.VMEM((rows, depth), bf16),
        pltpu.VMEM((rows, depth), bf16),
        pltpu.VMEM((rows, depth), bf16),
        pltpu.VMEM((2 * rows, depth), bf16),
        pltpu.VMEM((depth, wide_q), bf16),
        pltpu.VMEM((depth, wide_o), bf16),
        pltpu.VMEM((2 * rows, wide_q), bf16),
        pltpu.VMEM((4, quarter, wide_q), bf16),
        pltpu.VMEM((pairs, quarter, LANES), f32),
        pltpu.VMEM((4, quarter, wide_o), bf16),
        pltpu.VMEM((2 * rows, wide_o), bf16),
        pltpu.VMEM((rows, depth), bf16),
        pltpu.VMEM((rows, depth), bf16),
        pltpu.VMEM((rows, depth), bf16),
        pltpu.SemaphoreType.DMA((24 + 10 * n,)),
        pltpu.SemaphoreType.DMA((24 + 10 * n,)),
        pltpu.SemaphoreType.DMA((24,)),
    ]
    shape = jax.ShapeDtypeStruct
    return pl.pallas_call(
        functools.partial(front_body, n),
        in_specs=[ANY, ANY, VMEM, VMEM, VMEM, VMEM, VMEM, VMEM, ANY, ANY, ANY, ANY],
        out_specs=[ANY] * 13,
        out_shape=[
            shape((depth, wide_q), bf16),
            shape((depth, wide_o), bf16),
            shape((depth, gu_weight.shape[2]), bf16),
            shape((depth, down_weight.shape[2]), bf16),
            shape((n, count, depth // n), bf16),
            shape((rows, depth), bf16),
            shape((rows, depth), f32),
            shape((2 * rows, depth), bf16),
            shape((2 * rows, depth), bf16),
            shape((rows, depth), bf16),
            shape((4, quarter, wide_q), bf16),
            shape((pairs, quarter, LANES), f32),
            shape((2 * rows, wide_o), bf16),
        ],
        scratch_shapes=scratch,
        compiler_params=pltpu.CompilerParams(
            collective_id=3, has_side_effects=True, vmem_limit_bytes=62 << 20
        ),
        name="front",
    )(
        context, ctx_weight, inputs, cotangent, valid, gains, fold, spread,
        qkv_weight, out_weight, gu_weight, down_weight,
    )


def back_body(
    n, pair_two, home_grad, resid, gu_weight, down_half, out_weight, qkv_held, probs_held,
    gains, fold, spread,
    out_down, out_gate, out_up, out_up_stay, landed_down, landed_gate, out_mid, out_gain, out_pair, out_rows, out_qkv,
    two, grad, gu_full, down_full, out_full, two_away, two_stay, grad_away, grad_stay,
    hidden, grad_gu, send_down, send_gu, got_down, got_gu,
    values_mid, away, got, grad_rows, grad_mixed, qkv_mixed, probs, grad_qkv,
    send_sem, recv_sem, tile_send, tile_recv, local_sem,
):
    w = Where(n)
    wire, local = Wire(send_sem, recv_sem), Local(local_sem)
    tiled = Wire(tile_send, tile_recv)
    rows, depth = out_mid.shape
    both = 2 * rows
    piece = depth // n
    halfn = n // 2
    wide = down_full.shape[1]
    tile = 2 * LANES
    whole_tiles = wide // tile
    tiles = whole_tiles + (1 if wide % tile else 0)
    step = 64
    loads = [
        local.start(pair_two, two),
        local.start(gu_weight, gu_full),
    ]
    blocks = [
        pl.ds(pl.multiple_of((2 * b + w.near) * piece, piece), piece) for b in range(halfn)
    ]
    down_own = [local.start(down_half.at[at, :], down_full.at[at, :]) for at in blocks]
    late = [
        local.start(resid, values_mid),
        local.start(out_weight, out_full),
        local.start(qkv_held, qkv_mixed),
        local.start(probs_held, probs),
    ]
    greet(
        [w.along_stream(1), w.along_stream(2), w.along_frames(1)]
        + [w.along_frames(m) for m in w.masks]
        + [w.with_position(3), w.across()]
    )
    crossing = w.core != w.place
    cross = wire.make(home_grad, grad.at[:rows, :], w.across())
    stay = pltpu.make_async_copy(home_grad, grad.at[:rows, :], local_sem.at[15 + n])

    @pl.when(crossing)
    def _():
        cross.start()

    @pl.when(jnp.logical_not(crossing))
    def _():
        stay.start()

    neighbour = w.along_frames(1)
    cut = min(3, whole_tiles)
    down_near = [
        [
            wire.start(down_half.at[at, span], down_full.at[at, span], neighbour)
            for at in blocks
        ]
        for span in (slice(0, cut * tile), slice(cut * tile, wide))
    ]

    def split(source, into_away, into_stay):
        for b in range(halfn):
            for ref, which in ((into_away, 1 - w.near), (into_stay, w.near)):
                at = pl.ds(pl.multiple_of((2 * b + which) * piece, piece), piece)
                ref[:, b * piece : (b + 1) * piece] = source[:, at]

    loads[0].wait()
    split(two, two_away, two_stay)
    loads[1].wait()

    def columns(start, size):
        return pl.ds(pl.multiple_of(start, LANES), size)

    def tile_parts(t):
        lo = t * tile
        return ((send_down, got_down, lo), (send_gu, got_gu, lo), (send_gu, got_gu, wide + lo))

    def move(t, size, j):
        ref, into, start = tile_parts(t)[j]
        at = columns(start, size)
        return tiled.make(ref.at[:, :, at], into.at[:, :, at], neighbour, 3 * t + j)

    def forward(t, size):
        lo = t * tile
        here = columns(lo, size)
        there = columns(wide + lo, size)

        @pl.loop(0, both // 256)
        def _(r):
            at = pl.ds(pl.multiple_of(r * 256, 256), 256)
            left = two[at, :]
            gate = jnp.dot(left, gu_full[:, here], preferred_element_type=f32)
            up = jnp.dot(left, gu_full[:, there], preferred_element_type=f32)
            hidden[at, here] = (gate / (1.0 + jnp.exp(-gate)) * up).astype(bf16)
            grad_gu[at, here] = gate.astype(bf16)
            grad_gu[at, there] = up.astype(bf16)

    def store_away(ref, left, right, at):
        value = dot_rows(left[...], right[:, at]).astype(bf16)
        for b in range(halfn):
            ref[b, :, at] = value[b * piece : (b + 1) * piece]

    def away_down(t, size):
        store_away(send_down, grad_away, hidden, columns(t * tile, size))
        move(t, size, 0).start()

    def backward(t, size):
        lo = t * tile
        here = columns(lo, size)
        there = columns(wide + lo, size)

        @pl.loop(0, both // 256)
        def _(r):
            at = pl.ds(pl.multiple_of(r * 256, 256), 256)
            gate = grad_gu[at, here].astype(f32)
            up = grad_gu[at, there].astype(f32)
            back = jnp.dot(grad[at, :], down_full[:, here], preferred_element_type=f32)
            sigma = 1.0 / (1.0 + jnp.exp(-gate))
            grad_gu[at, here] = (back * up * (sigma * (1.0 + gate * (1.0 - sigma)))).astype(bf16)
            grad_gu[at, there] = (back * (gate * sigma)).astype(bf16)

        store_away(send_gu, two_away, grad_gu, here)
        store_away(send_gu, two_away, grad_gu, there)
        move(t, size, 1).start()

    rest = wide - whole_tiles * tile

    def some(step_of, lo, hi):
        top = min(hi, whole_tiles)
        if top > lo:

            @pl.loop(lo, top)
            def _(t):
                step_of(t, tile)

        if hi > whole_tiles and rest:
            step_of(whole_tiles, rest)

    def every(step_of):
        @pl.loop(0, whole_tiles)
        def _(t):
            step_of(t, tile)

        if rest:
            step_of(whole_tiles, rest)

    every(forward)

    @pl.when(crossing)
    def _():
        cross.wait_recv()

    @pl.when(jnp.logical_not(crossing))
    def _():
        stay.wait()

    grad_pair = wire.start(grad.at[:rows, :], grad.at[rows:, :], w.along_stream(1))
    grad_pair.wait_recv()
    split(grad, grad_away, grad_stay)
    every(away_down)
    for copy in down_own:
        copy.wait()
    for copy in down_near[0]:
        copy.wait_recv()
    some(backward, 0, cut)
    for copy in down_near[1]:
        copy.wait_recv()
    some(backward, cut, tiles)

    landed = (landed_down, landed_gate)

    def landing(t, size, j, k):
        ref, _, start = tile_parts(t)[j]
        mask = w.masks[k]
        at = columns(start, size)
        return tiled.make(
            ref.at[flip(w.at, mask // 2), :, at],
            landed[j].at[mask // 2 - 1, :, columns(t * tile, size)],
            w.along_frames(mask),
            3 * tiles + (3 * t + j) * len(w.masks) + k,
        )

    lefts = (grad_stay, two_stay, two_stay)
    rights = (hidden, grad_gu, grad_gu)

    def reduce_part(t, size, j):
        ref, into, start = tile_parts(t)[j]
        at = columns(start, size)
        move(t, size, j).wait()
        value = dot_rows(lefts[j][...], rights[j][:, at])
        for b in range(halfn):
            total = value[b * piece : (b + 1) * piece] + into[b, :, at].astype(f32)
            ref[b, :, at] = total.astype(bf16)
        for k in range(len(w.masks)):
            landing(t, size, j, k).start()

    def reduce_down(t, size):
        reduce_part(t, size, 0)

    def reduce_gu(t, size):
        reduce_part(t, size, 1)

    def stay_up(t, size):
        at = columns(wide + t * tile, size)
        store_away(got_gu, two_stay, grad_gu, at)

    def rows_of(position):
        quarter = both // 4
        return pl.ds(pl.multiple_of(position * quarter, quarter), quarter)

    def partial(left, right, t):
        at = pl.ds(pl.multiple_of(t * 256, 256), 256)
        return dot_columns(left[at, :], right[...])

    @pl.loop(0, rows // 256)
    def _(t):
        to = pl.ds(pl.multiple_of(t * 256, 256), 256)
        away[to, :] = partial(grad_gu, gu_full, rows // 256 + t).astype(bf16)

    first = wire.start(away, got, w.along_stream(1))

    @pl.loop(0, rows // 256)
    def _(t):
        to = pl.ds(pl.multiple_of(t * 256, 256), 256)
        out_mid[to, :] = partial(grad_gu, gu_full, t)

    some(reduce_down, 0, min(2, whole_tiles))

    late[0].wait()
    first.wait_recv()
    gain = gains[1:2, :]
    out_gain[...] = jnp.zeros_like(out_gain)

    @pl.loop(0, rows // step)
    def _(t):
        at = pl.ds(pl.multiple_of(t * step, step), step)
        grad_normed = out_mid[at, :] + got[at, :].astype(f32)
        values = values_mid[at, :]
        scale = lax.rsqrt(jnp.mean(values * values, axis=-1, keepdims=True) + norm_eps)
        weighted = grad_normed * gain
        inner = jnp.mean(weighted * values, axis=-1, keepdims=True)
        total = grad[at, :].astype(f32) + scale * weighted
        total = total - values * (scale * scale * scale * inner)
        out_mid[at, :] = total
        two[at, :] = total.astype(bf16)
        out_gain[...] += jnp.sum(grad_normed * values * scale, axis=0, keepdims=True)

    second = wire.start(two.at[:rows, :], two.at[rows:, :], w.along_stream(1))
    late[1].wait()

    def back_rows(lo, hi):
        @pl.loop(lo, hi)
        def _(t):
            at = pl.ds(pl.multiple_of(t * 256, 256), 256)
            value = jnp.dot(two[at, :], out_full[...], preferred_element_type=f32)
            grad_rows[at, :] = value.astype(bf16)

    back_rows(0, rows // 256)
    second.wait_recv()
    back_rows(rows // 256, both // 256)
    mixing = {}
    for mask in (3, 1, 2):
        mixing[mask] = wire.start(
            grad_rows.at[rows_of(flip(w.position, mask)), :],
            grad_mixed.at[w.position],
            w.with_position(mask),
        )
    own = local.start(grad_rows.at[rows_of(w.position), :], grad_mixed.at[w.position])
    store_pair = local.start(two, out_pair)

    some(reduce_down, min(2, whole_tiles), tiles)
    own.wait()
    late[2].wait()
    late[3].wait()
    for mask in (2, 1, 3):
        mixing[mask].wait_recv()
    fold_held, spread_held = fold[...], spread[...]

    @pl.loop(0, both // 4 // step)
    def _(t):
        at = pl.ds(pl.multiple_of(t * step, step), step)
        attention_backward_rows(
            at, qkv_mixed, probs, grad_mixed, fold_held, spread_held, grad_qkv
        )

    returning = {}
    for mask in (3, 1, 2):
        returning[mask] = wire.start(
            grad_qkv.at[flip(w.position, mask)],
            out_qkv.at[rows_of(w.position), :],
            w.with_position(mask),
        )
    own_back = local.start(grad_qkv.at[w.position], out_qkv.at[rows_of(w.position), :])
    early = min(2, whole_tiles)
    some(reduce_gu, 0, early)
    some(stay_up, 0, tiles)

    wire.sent(first)

    @pl.loop(0, rows // 256)
    def _(t):
        to = pl.ds(pl.multiple_of(t * 256, 256), 256)
        away[to, :] = partial(hidden, down_full, rows // 256 + t).astype(bf16)

    third = wire.start(away, got, w.along_stream(1))

    @pl.loop(0, rows // 256)
    def _(t):
        to = pl.ds(pl.multiple_of(t * 256, 256), 256)
        values_mid[to, :] = values_mid[to, :] + partial(hidden, down_full, t)

    third.wait_recv()

    @pl.loop(0, rows // step)
    def _(t):
        at = pl.ds(pl.multiple_of(t * step, step), step)
        out_rows[at, :] = (values_mid[at, :] + got[at, :].astype(f32)).astype(bf16)

    some(reduce_gu, early, tiles)
    kept = [
        local.start(send_down.at[w.at], out_down),
        local.start(send_gu.at[w.at, :, :wide], out_gate),
        local.start(send_gu.at[:, :, wide:], out_up),
        local.start(got_gu.at[:, :, wide:], out_up_stay),
    ]
    own_back.wait()
    store_pair.wait()
    for mask in (2, 1, 3):
        returning[mask].wait_recv()
    for t in range(tiles):
        for j in range(2):
            for k in range(len(w.masks)):
                landing(t, tile if t < whole_tiles else rest, j, k).wait()
    for copy in kept:
        copy.wait()

    @pl.when(crossing)
    def _():
        cross.wait_send()

    wire.finish()


def back_scratch(n, rows, depth, wide, head_width):
    both, halfn, piece = 2 * rows, n // 2, depth // n
    pairs = len(PAIRS)
    quarter = both // 4
    shapes = [
        ((both, depth), bf16),
        ((both, depth), bf16),
        ((depth, 2 * wide), bf16),
        ((depth, wide), bf16),
        ((depth, head_width), bf16),
        ((both, depth // 2), bf16),
        ((both, depth // 2), bf16),
        ((both, depth // 2), bf16),
        ((both, depth // 2), bf16),
        ((both, wide), bf16),
        ((both, 2 * wide), bf16),
        ((halfn, piece, wide), bf16),
        ((halfn, piece, 2 * wide), bf16),
        ((halfn, piece, wide), bf16),
        ((halfn, piece, 2 * wide), bf16),
        ((rows, depth), f32),
        ((rows, depth), bf16),
        ((rows, depth), bf16),
        ((both, head_width), bf16),
        ((4, quarter, head_width), bf16),
        ((4, quarter, 3 * head_width), bf16),
        ((pairs, quarter, LANES), f32),
        ((4, quarter, 3 * head_width), bf16),
    ]
    outs = [((rows, depth), f32), ((rows, depth), bf16)]
    return shapes, sum(math.prod(dims) * jnp.dtype(kind).itemsize for dims, kind in shapes + outs)


def back(
    n, pair_two, home_grad, resid, gu_full, down_half, out_full, qkv_mixed, probs, gains
):
    rows, depth = resid.shape
    wide, head_width = down_half.shape[1], out_full.shape[1]
    shapes, _ = back_scratch(n, rows, depth, wide, head_width)
    tiles = -(-wide // (2 * LANES))
    fold, spread = fold_matrices(head_width)
    shape = jax.ShapeDtypeStruct
    moves = 3 * tiles * (1 + n // 2 - 1)
    return pl.pallas_call(
        functools.partial(back_body, n),
        in_specs=[ANY] * 8 + [VMEM] * 3,
        out_specs=[ANY, ANY, ANY, ANY, ANY, ANY, VMEM, VMEM, ANY, VMEM, ANY],
        out_shape=[
            shape((depth // n, wide), bf16),
            shape((depth // n, wide), bf16),
            shape((n // 2, depth // n, wide), bf16),
            shape((n // 2, depth // n, wide), bf16),
            shape((n // 2 - 1, depth // n, wide), bf16),
            shape((n // 2 - 1, depth // n, wide), bf16),
            shape((rows, depth), f32),
            shape((1, depth), f32),
            shape((2 * rows, depth), bf16),
            shape((rows, depth), bf16),
            shape((2 * rows, 3 * head_width), bf16),
        ],
        scratch_shapes=[pltpu.VMEM(dims, kind) for dims, kind in shapes]
        + [
            pltpu.SemaphoreType.DMA((16 + 2 * n,)),
            pltpu.SemaphoreType.DMA((16 + 2 * n,)),
            pltpu.SemaphoreType.DMA((moves,)),
            pltpu.SemaphoreType.DMA((moves,)),
            pltpu.SemaphoreType.DMA((16 + n,)),
        ],
        compiler_params=pltpu.CompilerParams(
            collective_id=4, has_side_effects=True, vmem_limit_bytes=67_000_000
        ),
        name="back",
    )(
        pair_two, home_grad, resid, gu_full, down_half, out_full, qkv_mixed, probs,
        gains, fold, spread,
    )


def shards(
    inputs,
    context,
    cotangent,
    live_frames,
    ctx_weight,
    norm_gains,
    qkv_weight,
    out_weight,
    gate_up_weight,
    down_weight,
):
    n = lax.axis_size("frames")
    stream_index = lax.axis_index("stream")
    frame_index = lax.axis_index("frames")
    half_index = stream_index % 2
    place = (frame_index // 2) % 2
    position = (stream_index // 2) * 2 + place
    frame_count = inputs.shape[0]
    width_model = inputs.shape[2]
    offsets = lax.broadcasted_iota(jnp.int32, (frame_count,), 0)
    valid_mask = (offsets % SLOT < jnp.repeat(live_frames, SLOT)).astype(f32)[:, None]
    gain_one = norm_gains[0]
    gain_two = norm_gains[1]

    (
        qkv_full,
        out_full,
        gate_up_full,
        down_half,
        ctx_pieces,
        resid_in,
        resid_mid,
        paired_one,
        paired_two,
        grad_rows,
        qkv_mixed,
        probs,
        mixed,
    ) = front(
        n,
        context,
        ctx_weight,
        inputs[:, 0],
        cotangent,
        valid_mask,
        norm_gains,
        qkv_weight[0],
        out_weight[0],
        gate_up_weight[0],
        down_weight[0],
    )
    near = frame_index % 2

    def paired(mine):
        return jnp.concatenate([mine, swap_stream(mine, 1)], axis=0)

    def own_sum(partial_value):
        return partial_value[:frame_count] + swap_stream(
            partial_value[frame_count:].astype(bf16), 1
        ).astype(f32)

    def rows_times(left, right):
        return jnp.dot(left, right, preferred_element_type=f32)

    def rows_back(left, right):
        return lax.dot_general(left, right, (((1,), (1,)), ((), ())), preferred_element_type=f32)

    def returned(value):
        _, quarter, width = value.shape
        out = jnp.zeros((4, quarter, width), value.dtype)
        own = lax.dynamic_index_in_dim(value, position, 0, keepdims=False)
        out = lax.dynamic_update_index_in_dim(out, own, position, 0)
        for mask in (2, 1, 3):
            there = position ^ mask
            got = peer(lax.dynamic_index_in_dim(value, there, 0, keepdims=False), mask)
            out = lax.dynamic_update_index_in_dim(out, got, there, 0)
        return out.reshape(4 * quarter, width)

    head_width = out_full.shape[1]
    _, needed = back_scratch(n, frame_count, width_model, down_weight.shape[3], head_width)
    if needed <= 66_000_000 and (width_model // n) % LANES == 0:
        (
            own_down,
            own_gate,
            up_send,
            up_stay,
            landed_down,
            landed_gate,
            grad_mid,
            grad_gain_two,
            paired_grad_attn,
            result_rows,
            grad_qkv_low,
        ) = back(
            n,
            paired_two,
            grad_rows,
            resid_mid,
            gate_up_full,
            down_half,
            out_full,
            qkv_mixed,
            probs,
            norm_gains,
        )
    else:
        paired_grad_ffn = paired(transposed(grad_rows))
        blocks = down_half.reshape(n // 2, 2, -1, down_half.shape[1])
        blocks = lax.dynamic_index_in_dim(blocks, near, 1, keepdims=False)
        others = swap_frames(blocks, 1)
        even, odd = jnp.where(near == 0, blocks, others), jnp.where(near == 0, others, blocks)
        down_full = jnp.stack([even, odd], axis=1).reshape(down_half.shape)
        scale_two = norm_scale(resid_mid)
        gate_up = rows_times(paired_two, gate_up_full)
        ffn_half = down_full.shape[1]
        gate_part = gate_up[:, :ffn_half]
        up_part = gate_up[:, ffn_half:]
        sigmoid_gate = jax.nn.sigmoid(gate_part)
        activated = gate_part * sigmoid_gate
        hidden = (activated * up_part).astype(bf16)

        grad_res = paired_grad_ffn[:frame_count]
        sum_down = scattered(halves(paired_grad_ffn, near), hidden, frame_index, place)
        grad_hidden = rows_times(paired_grad_ffn, down_full)
        grad_gate = grad_hidden * up_part * (sigmoid_gate * (1.0 + gate_part * (1.0 - sigmoid_gate)))
        grad_up = grad_hidden * activated
        grad_gu_low = jnp.concatenate([grad_gate, grad_up], axis=-1).astype(bf16)
        grad_normed_two = own_sum(rows_back(grad_gu_low, gate_up_full))
        sum_gate_up = scattered(halves(paired_two, near), grad_gu_low, frame_index, place)
        back_two, grad_gain_two = norm_back(resid_mid, scale_two, gain_two, grad_normed_two)
        grad_mid = grad_res.astype(f32) + back_two
        paired_grad_attn = paired(grad_mid.astype(bf16))
        grad_mixed = rows_times(paired_grad_attn, out_full).astype(bf16)
        grad_qkv_mixed = attention_backward(qkv_mixed, probs, exchange_rows(grad_mixed, position))
        grad_qkv_low = returned(grad_qkv_mixed)
        result_rows = (resid_mid + own_sum(rows_back(hidden, down_full))).astype(bf16)
        grad_gain_two = grad_gain_two[None]

    wide_q = qkv_full.shape[1]
    count = ctx_pieces.shape[1]
    _, needed = ending_scratch(
        n, frame_count, width_model, context.shape, count, wide_q, head_width, down_half.shape[1]
    )
    if needed <= 66_000_000 and (width_model // n) % LANES == 0:
        (
            own_qkv,
            own_out,
            own_up,
            landed_qkv,
            landed_out,
            landed_up,
            grad_home,
            result,
            sum_context,
            ctx_total,
        ) = ending(
            n,
            resid_in,
            grad_mid,
            norm_gains,
            grad_gain_two,
            result_rows,
            paired_one,
            paired_grad_attn,
            mixed,
            grad_qkv_low,
            qkv_full,
            context,
            ctx_pieces,
            up_send,
            up_stay,
        )
        sum_qkv, sum_out, sum_gate_up, sum_down, grad_home, result = finish(
            (own_qkv, own_out, own_gate, own_up, own_down),
            (landed_qkv, landed_out, landed_gate, landed_up, landed_down),
            grad_home,
            result,
            valid_mask,
        )
    else:

        def parts(left, right):
            away, stay = halves(left, near)
            block = width_model // n
            return [
                dot_rows(part, right).astype(bf16).reshape(n // 2, block, right.shape[1])
                for part in (away, stay)
            ]

        part_away = rows_back(grad_qkv_low[frame_count:], qkv_full).astype(bf16)
        part_stay = rows_back(grad_qkv_low[:frame_count], qkv_full)
        sum_qkv, sum_out, grad_home, result, sum_context, ctx_total = tail(
            n,
            part_away,
            part_stay,
            resid_in,
            grad_mid,
            norm_gains,
            grad_gain_two,
            result_rows,
            *parts(paired_one, grad_qkv_low),
            *parts(paired_grad_attn, mixed),
            context,
            ctx_pieces.transpose(1, 0, 2).reshape(-1, width_model),
        )
        result = (result.astype(f32) * valid_mask)[:, None]
        grad_home = grad_home[:, None]
    ctx_total = ctx_total.T
    sum_ctx = ctx_total[: ctx_weight.shape[0]]
    sum_gains = ctx_total[ctx_weight.shape[0] : ctx_weight.shape[0] + 2]

    return (
        result,
        grad_home,
        sum_context,
        sum_ctx,
        sum_gains,
        sum_qkv[None],
        sum_out[None],
        sum_gate_up[None],
        sum_down[None],
    )


def solution(mesh):
    placed = (
        P("frames", "stream", None),
        P("frames", None),
        P("frames", "stream", None),
        P("frames"),
        P(None, "frames"),
        P(),
        P("stream", None, "frames", None),
        P("stream", None, "frames", None),
        P("stream", None, "frames", None),
        P("stream", None, "frames", None),
    )
    return jax.shard_map(
        shards,
        mesh=mesh,
        in_specs=placed,
        out_specs=(
            P("frames", "stream", None),
            P("frames", "stream", None),
            P("frames", "stream"),
            P(None, ("stream", "frames")),
            P(None, ("stream", "frames")),
            P("stream", None, "frames", None),
            P("stream", None, "frames", None),
            P("stream", None, "frames", None),
            P("stream", None, "frames", None),
        ),
        check_vma=False,
    )
```

```python
import functools
import math

import jax
import jax.numpy as jnp
import numpy as np
from jax import lax
from jax.experimental import pallas as pl
from jax.experimental.pallas import tpu as pltpu
from jax.sharding import PartitionSpec as P

HD = 64
SLOT = 128
LANES = 128
norm_eps = 1e-05
f32 = jnp.float32
bf16 = jnp.bfloat16

PAIRS = [(q, k) for q in range(4) for k in range(q + 1)]


ANY = pl.BlockSpec(memory_space=pl.ANY)
VMEM = pl.BlockSpec(memory_space=pltpu.VMEM)
EXTRA = 32


def flip(value, mask):
    bit = 1
    while bit <= mask:
        if mask & bit:
            value = value + bit - 2 * bit * ((value // bit) % 2)
        bit *= 2
    return value


class Where:
    def __init__(self, n):
        self.n = n
        self.stream = lax.axis_index("stream")
        self.frame = lax.axis_index("frames")
        self.core = self.stream % 2
        self.place = (self.frame // 2) % 2
        self.position = (self.stream // 2) * 2 + self.place
        self.near = self.frame % 2
        self.at = self.frame // 2
        self.far_masks = [m for m in range(2, n, 2) if not m & 2]
        self.both_masks = [m for m in range(2, n, 2) if m & 2 and m > 2]
        self.masks = self.far_masks + self.both_masks + [2]

    def along_stream(self, mask):
        return (flip(self.stream, mask), self.frame)

    def along_frames(self, mask):
        return (self.stream, flip(self.frame, mask))

    def with_position(self, mask):
        return (flip(self.stream, mask & 2), flip(self.frame, 2 * (mask & 1)))

    def across(self):
        return (flip(self.stream, 1), flip(self.frame, 2))


class Wire:
    def __init__(self, send, recv):
        self.send, self.recv, self.count, self.started = send, recv, 0, []

    def make(self, src, dst, device, index=None):
        k = self.count if index is None else index
        if index is None:
            self.count += 1
        return pltpu.make_async_remote_copy(
            src_ref=src,
            dst_ref=dst,
            send_sem=self.send.at[k],
            recv_sem=self.recv.at[k],
            device_id=device,
            device_id_type=pl.DeviceIdType.MESH,
        )

    def start(self, src, dst, device):
        copy = self.make(src, dst, device)
        copy.start()
        self.started.append(copy)
        return copy

    def sent(self, copy):
        self.started = [c for c in self.started if c is not copy]
        copy.wait_send()

    def finish(self):
        for copy in self.started:
            copy.wait_send()


class Local:
    def __init__(self, sems):
        self.sems, self.count = sems, 0

    def start(self, src, dst):
        copy = pltpu.make_async_copy(src, dst, self.sems.at[self.count])
        self.count += 1
        copy.start()
        return copy


def greet(devices):
    barrier = pltpu.get_barrier_semaphore()
    for device in devices:
        pl.semaphore_signal(
            barrier, inc=1, device_id=device, device_id_type=pl.DeviceIdType.MESH
        )
    pl.semaphore_wait(barrier, len(devices))


def dot_rows(left, right):
    return lax.dot_general(left, right, (((0,), (0,)), ((), ())), preferred_element_type=f32)


def dot_columns(left, right):
    return lax.dot_general(left, right, (((1,), (1,)), ((), ())), preferred_element_type=f32)


class Reduction:
    def __init__(self, w, wire, send, keep, arrived, sums, landed, out):
        self.w, self.wire = w, wire
        self.send, self.keep, self.arrived = send, keep, arrived
        self.sums, self.landed, self.out = sums, landed, out
        self.first, self.second = {}, {}
        self.order = w.masks + [0]

    def begin(self, mask):
        block = flip(self.w.at, mask // 2)
        self.first[mask] = self.wire.start(
            self.send.at[block], self.arrived.at[block], self.w.along_frames(1)
        )

    def forward(self, mask):
        block = flip(self.w.at, mask // 2)
        self.first[mask].wait_recv()
        self.wire.sent(self.first[mask])
        total = self.keep[block].astype(f32) + self.arrived[block].astype(f32)
        self.sums[block] = total.astype(bf16)
        if mask:
            self.second[mask] = self.wire.start(
                self.sums.at[block], self.landed.at[mask // 2 - 1], self.w.along_frames(mask)
            )

    def land(self):
        for copy in self.second.values():
            copy.wait_recv()

    def close(self):
        own, other = self.sums[self.w.at].astype(f32), None
        for mask in self.w.masks:
            self.second[mask].wait_recv()
            got = self.landed[mask // 2 - 1].astype(f32)
            if mask & 2:
                other = got if other is None else other + got
            else:
                own = own + got
        self.out[self.w.place] = own
        self.out[1 - self.w.place] = other


def tail_body(
    n, part_send, part_own, resid, mid, gains, gain_two, result_rows,
    gq_send, gq_keep, go_send, go_keep, context, ctx_full,
    out_q, out_o, out_grad, out_result, out_context, out_ctx,
    part_got, low, home, partner_half, half_sum, far_half, whole, kept_q, kept_o,
    arrived_q, arrived_o, sums_q, sums_o, landed_q, landed_o,
    context_held, ctx_held, term, term_got, term_sum, term_landed, gain_sum,
    send_sem, recv_sem, local_sem,
):
    w = Where(n)
    wire, local = Wire(send_sem, recv_sem), Local(local_sem)
    rows, depth = resid.shape
    crossing = w.core != w.place
    load_q = local.start(gq_keep, kept_q)
    load_o = local.start(go_keep, kept_o)
    load_context = local.start(context, context_held)
    load_ctx = local.start(ctx_full, ctx_held)
    greet(
        [w.along_stream(1), w.along_stream(2), w.along_frames(1)]
        + [w.along_frames(m) for m in w.masks]
        + [w.across()]
    )
    part = wire.start(part_send, part_got, w.along_stream(1))
    red_o = Reduction(w, wire, go_send, kept_o, arrived_o, sums_o, landed_o, out_o)
    red_q = Reduction(w, wire, gq_send, kept_q, arrived_q, sums_q, landed_q, out_q)
    for mask in red_o.order:
        red_o.begin(mask)
    for mask in red_q.order:
        red_q.begin(mask)

    part.wait_recv()
    gain = gains[0:1, :]
    gain_sum[...] = jnp.zeros_like(gain_sum)
    step = 64

    @pl.loop(0, rows // step)
    def _(t):
        at = pl.ds(pl.multiple_of(t * step, step), step)
        grad = part_own[at, :].astype(f32) + part_got[at, :].astype(f32)
        values = resid[at, :].astype(f32)
        scale = lax.rsqrt(jnp.mean(values * values, axis=-1, keepdims=True) + norm_eps)
        weighted = grad * gain
        inner = jnp.mean(weighted * values, axis=-1, keepdims=True)
        back = scale * weighted - values * (scale * scale * scale * inner)
        low[at, :] = (mid[at, :] + back).astype(bf16)
        gain_sum[...] += jnp.sum(grad * values * scale, axis=0, keepdims=True)

    row = lax.broadcasted_iota(jnp.int32, (EXTRA, depth), 0)
    low[rows:, :] = jnp.where(
        row == 0, gain_sum[...], jnp.where(row == 1, gain_two[...], 0.0)
    ).astype(bf16)

    cross = wire.make(low, home, w.across())
    cross_result = wire.make(result_rows, out_result, w.across())

    @pl.when(crossing)
    def _():
        cross.start()

    load_o.wait()
    load_q.wait()
    for mask in red_o.order:
        red_o.forward(mask)

    @pl.when(crossing)
    def _():
        cross_result.start()
        cross.wait_recv()

    stay = pltpu.make_async_copy(low, home, local.sems.at[4])
    stay_result = pltpu.make_async_copy(result_rows, out_result, local.sems.at[5])

    @pl.when(jnp.logical_not(crossing))
    def _():
        stay.start()
        stay_result.start()
        stay.wait()

    half = (rows + EXTRA) // 2
    mine = pl.ds(pl.multiple_of(w.core * half, 16), half)
    theirs = pl.ds(pl.multiple_of((1 - w.core) * half, 16), half)
    first = wire.start(home.at[theirs, :], partner_half, w.along_stream(1))
    out_grad[...] = home[:rows, :].astype(f32)
    first.wait_recv()
    half_sum[...] = (home[mine, :].astype(f32) + partner_half[...].astype(f32)).astype(bf16)
    second = wire.start(half_sum, far_half, w.along_stream(2))
    red_q.forward(red_q.order[0])
    red_q.forward(red_q.order[1])
    second.wait_recv()
    whole[mine, :] = (half_sum[...].astype(f32) + far_half[...].astype(f32)).astype(bf16)
    third = wire.start(whole.at[mine, :], whole.at[mine, :], w.along_stream(1))
    load_context.wait()
    third.wait_recv()

    share = depth // 4
    columns = pl.ds(pl.multiple_of(w.stream * share, LANES), share)
    block = share // n
    wide = context_held.shape[1]
    pieces = 2
    grad_share = whole[:rows, columns]
    firsts, seconds = [], []
    row = lax.broadcasted_iota(jnp.int32, (EXTRA, LANES), 0)
    select = (row == lax.broadcasted_iota(jnp.int32, (EXTRA, LANES), 1)).astype(bf16)
    edges = [wide * p // pieces for p in range(pieces)] + [wide + LANES]
    for p in range(pieces):
        lo, hi = edges[p], edges[p + 1]
        for at in range(lo, min(hi, wide), 1024):
            to = min(at + 1024, wide)
            value = dot_rows(grad_share, context_held[:, at:to]).astype(bf16)
            for k in range(n):
                term[k // 2, k % 2, :, at:to] = value[k * block : (k + 1) * block]
        if hi > wide:
            value = dot_rows(whole[rows:, columns], select).astype(bf16)
            for k in range(n):
                term[k // 2, k % 2, :, wide:hi] = value[k * block : (k + 1) * block]
        firsts.append(
            wire.start(
                term.at[:, 1 - w.near, :, lo:hi], term_got.at[:, :, lo:hi], w.along_frames(1)
            )
        )
    for mask in red_q.order[2:]:
        red_q.forward(mask)
    load_ctx.wait()

    def context_rows(t):
        at = pl.ds(pl.multiple_of(t * LANES, LANES), LANES)
        out_context[at, :] = dot_columns(whole[at, :], ctx_held[...])

    @pl.loop(0, rows // LANES)
    def _(t):
        context_rows(t)

    for p in range(pieces):
        lo, hi = edges[p], edges[p + 1]
        firsts[p].wait_recv()
        for mask in w.masks + [0]:
            to = flip(w.at, mask // 2)
            total = term[to, w.near, :, lo:hi].astype(f32) + term_got[to, :, lo:hi].astype(f32)
            term_sum[to, :, lo:hi] = total.astype(bf16)
            if mask:
                seconds.append(
                    wire.start(
                        term_sum.at[to, :, lo:hi],
                        term_landed.at[mask // 2, :, lo:hi],
                        w.along_frames(mask),
                    )
                )
    red_o.close()
    red_q.close()

    @pl.when(crossing)
    def _():
        cross_result.wait_recv()
        cross.wait_send()
        cross_result.wait_send()

    @pl.when(jnp.logical_not(crossing))
    def _():
        stay_result.wait()

    for copy in seconds:
        copy.wait_recv()
    total = term_sum[w.at].astype(f32)
    for mask in w.masks:
        total = total + term_landed[mask // 2].astype(f32)
    out_ctx[...] = total
    wire.finish()


def tail(
    n, part_send, part_own, resid, mid, gains, gain_two, result_rows,
    gq_send, gq_keep, go_send, go_keep, context, ctx_full,
):
    rows, depth = resid.shape
    halfn, block, wide_q = gq_send.shape
    wide_o = go_send.shape[2]
    share = depth // 4 // n
    wide = context.shape[1] + LANES
    half = (rows + EXTRA) // 2
    count = 64 + 2 * n
    scratch = [
        pltpu.VMEM((rows, depth), bf16),
        pltpu.VMEM((rows + EXTRA, depth), bf16),
        pltpu.VMEM((rows + EXTRA, depth), bf16),
        pltpu.VMEM((half, depth), bf16),
        pltpu.VMEM((half, depth), bf16),
        pltpu.VMEM((half, depth), bf16),
        pltpu.VMEM((rows + EXTRA, depth), bf16),
        pltpu.VMEM((halfn, block, wide_q), bf16),
        pltpu.VMEM((halfn, block, wide_o), bf16),
        pltpu.VMEM((halfn, block, wide_q), bf16),
        pltpu.VMEM((halfn, block, wide_o), bf16),
        pltpu.VMEM((halfn, block, wide_q), bf16),
        pltpu.VMEM((halfn, block, wide_o), bf16),
        pltpu.VMEM((halfn, block, wide_q), bf16),
        pltpu.VMEM((halfn, block, wide_o), bf16),
        pltpu.VMEM(context.shape, bf16),
        pltpu.VMEM(ctx_full.shape, bf16),
        pltpu.VMEM((halfn, 2, share, wide), bf16),
        pltpu.VMEM((halfn, share, wide), bf16),
        pltpu.VMEM((halfn, share, wide), bf16),
        pltpu.VMEM((halfn, share, wide), bf16),
        pltpu.VMEM((1, depth), f32),
        pltpu.SemaphoreType.DMA((count,)),
        pltpu.SemaphoreType.DMA((count,)),
        pltpu.SemaphoreType.DMA((6,)),
    ]
    return pl.pallas_call(
        functools.partial(tail_body, n),
        in_specs=[ANY, VMEM, VMEM, VMEM, VMEM, VMEM, VMEM, ANY, ANY, ANY, ANY, ANY, ANY],
        out_specs=[VMEM, VMEM, VMEM, VMEM, VMEM, VMEM],
        out_shape=[
            jax.ShapeDtypeStruct((2, block, wide_q), f32),
            jax.ShapeDtypeStruct((2, block, wide_o), f32),
            jax.ShapeDtypeStruct((rows, depth), f32),
            jax.ShapeDtypeStruct((rows, depth), bf16),
            jax.ShapeDtypeStruct((rows, ctx_full.shape[0]), f32),
            jax.ShapeDtypeStruct((share, wide), f32),
        ],
        scratch_shapes=scratch,
        compiler_params=pltpu.CompilerParams(
            collective_id=5, has_side_effects=True, vmem_limit_bytes=60 << 20
        ),
        name="tail",
    )(
        part_send, part_own, resid, mid, gains, gain_two, result_rows,
        gq_send, gq_keep, go_send, go_keep, context, ctx_full,
    )


def ending_body(
    n, resid, mid, gains, gain_two, result_rows,
    pair_one, pair_grad, mixed_rows, grad_qkv_rows, qkv_weight, context, ctx_pieces, up_send, up_stay,
    out_q, out_o, out_up, landed_q, landed_o, landed_up, out_grad, out_result, out_context, out_ctx, out_gains,
    one, grad_two, mixed, grad_qkv, qkv_full, left_away, left_stay, part_send, part_own,
    part_got, low, home, partner_half, half_sum, far_half, whole, result_home,
    send_q, send_o, kept_q, kept_o, arrived_q, arrived_o, send_up, kept_up, arrived_up,
    context_held, ctx_held, term, term_got, term_sum, term_landed, gain_sum,
    send_sem, recv_sem, local_sem,
):
    w = Where(n)
    wire, local = Wire(send_sem, recv_sem), Local(local_sem)
    rows, depth = resid.shape
    piece = depth // n
    crossing = w.core != w.place
    load_up = local.start(up_send, send_up)
    load_grad = local.start(pair_grad, grad_two)
    load_mixed = local.start(mixed_rows, mixed)
    load_qkv = local.start(grad_qkv_rows, grad_qkv)
    load_weight = local.start(qkv_weight, qkv_full)
    load_one = local.start(pair_one, one)
    load_up_stay = local.start(up_stay, kept_up)
    load_context = local.start(context, context_held)
    load_ctx = [
        local.start(ctx_pieces.at[k], ctx_held.at[:, k * piece : (k + 1) * piece])
        for k in range(n)
    ]
    greet(
        [w.along_stream(1), w.along_stream(2), w.along_frames(1)]
        + [w.along_frames(m) for m in w.masks]
        + [w.across()]
    )
    cross_result = wire.make(result_rows, result_home, w.across())
    stay_result = pltpu.make_async_copy(result_rows, result_home, local.sems.at[30])
    stay = pltpu.make_async_copy(low, home, local.sems.at[31])

    @pl.when(crossing)
    def _():
        cross_result.start()

    @pl.when(jnp.logical_not(crossing))
    def _():
        stay_result.start()

    def split(source, which, into):
        for b in range(n // 2):
            at = pl.ds(pl.multiple_of((2 * b + which) * piece, piece), piece)
            into[:, b * piece : (b + 1) * piece] = source[:, at]

    def product(left, right, into):
        wide = right.shape[1]
        for lo in range(0, wide, 512):
            value = dot_rows(left[...], right[:, lo : lo + 512]).astype(bf16)
            for b in range(n // 2):
                into[b, :, lo : lo + 512] = value[b * piece : (b + 1) * piece]

    def partial(t):
        at = pl.ds(pl.multiple_of(t * 256, 256), 256)
        return dot_columns(grad_qkv[at, :], qkv_full[...])

    load_up.wait()
    red_up = Reduction(w, wire, send_up, kept_up, arrived_up, send_up, landed_up, out_up)
    for mask in red_up.order:
        red_up.begin(mask)
    load_grad.wait()
    split(grad_two, 1 - w.near, left_away)
    load_mixed.wait()
    product(left_away, mixed, send_o)
    red_o = Reduction(w, wire, send_o, kept_o, arrived_o, send_o, landed_o, out_o)
    for mask in red_o.order:
        red_o.begin(mask)
    load_qkv.wait()
    load_weight.wait()

    @pl.loop(0, rows // 256)
    def _(t):
        to = pl.ds(pl.multiple_of(t * 256, 256), 256)
        part_send[to, :] = partial(rows // 256 + t).astype(bf16)

    part = wire.start(part_send, part_got, w.along_stream(1))
    load_one.wait()
    split(one, 1 - w.near, left_away)
    product(left_away, grad_qkv, send_q)
    red_q = Reduction(w, wire, send_q, kept_q, arrived_q, send_q, landed_q, out_q)
    for mask in red_q.order:
        red_q.begin(mask)

    @pl.loop(0, rows // 256)
    def _(t):
        to = pl.ds(pl.multiple_of(t * 256, 256), 256)
        part_own[to, :] = partial(t)

    part.wait_recv()
    gain = gains[0:1, :]
    gain_sum[...] = jnp.zeros_like(gain_sum)
    step = 64

    @pl.loop(0, rows // step)
    def _(t):
        at = pl.ds(pl.multiple_of(t * step, step), step)
        grad = part_own[at, :].astype(f32) + part_got[at, :].astype(f32)
        values = resid[at, :].astype(f32)
        scale = lax.rsqrt(jnp.mean(values * values, axis=-1, keepdims=True) + norm_eps)
        weighted = grad * gain
        inner = jnp.mean(weighted * values, axis=-1, keepdims=True)
        back = scale * weighted - values * (scale * scale * scale * inner)
        low[at, :] = (mid[at, :] + back).astype(bf16)
        gain_sum[...] += jnp.sum(grad * values * scale, axis=0, keepdims=True)

    row = lax.broadcasted_iota(jnp.int32, (EXTRA, depth), 0)
    low[rows:, :] = jnp.where(
        row == 0, gain_sum[...], jnp.where(row == 1, gain_two[...], 0.0)
    ).astype(bf16)

    cross = wire.make(low, home, w.across())

    @pl.when(crossing)
    def _():
        cross.start()

    split(grad_two, w.near, left_stay)
    product(left_stay, mixed, kept_o)
    load_up_stay.wait()
    for mask in red_up.order[:2]:
        red_up.forward(mask)
    for mask in red_o.order:
        red_o.forward(mask)

    @pl.when(crossing)
    def _():
        cross_result.wait_recv()

    @pl.when(jnp.logical_not(crossing))
    def _():
        stay.start()
        stay_result.wait()

    split(one, w.near, left_stay)
    product(left_stay, grad_qkv, kept_q)
    store_result = local.start(result_home, out_result)

    @pl.when(crossing)
    def _():
        cross.wait_recv()

    @pl.when(jnp.logical_not(crossing))
    def _():
        stay.wait()

    half = (rows + EXTRA) // 2
    mine = pl.ds(pl.multiple_of(w.core * half, 16), half)
    theirs = pl.ds(pl.multiple_of((1 - w.core) * half, 16), half)
    first = wire.start(home.at[theirs, :], partner_half, w.along_stream(1))
    store_grad = local.start(home.at[:rows, :], out_grad)
    for mask in red_up.order[2:]:
        red_up.forward(mask)
    first.wait_recv()
    half_sum[...] = (home[mine, :].astype(f32) + partner_half[...].astype(f32)).astype(bf16)
    second = wire.start(half_sum, far_half, w.along_stream(2))
    red_q.forward(red_q.order[0])
    red_q.forward(red_q.order[1])
    second.wait_recv()
    whole[mine, :] = (half_sum[...].astype(f32) + far_half[...].astype(f32)).astype(bf16)
    third = wire.start(whole.at[mine, :], whole.at[mine, :], w.along_stream(1))
    load_context.wait()
    third.wait_recv()

    share = depth // 4
    columns = pl.ds(pl.multiple_of(w.stream * share, LANES), share)
    block = share // n
    wide = context_held.shape[1]
    pieces = 4
    grad_share = whole[:rows, columns]
    firsts, seconds = [], []
    row = lax.broadcasted_iota(jnp.int32, (EXTRA, LANES), 0)
    select = (row == lax.broadcasted_iota(jnp.int32, (EXTRA, LANES), 1)).astype(bf16)
    edges = [wide * p // pieces for p in range(pieces)] + [wide + LANES]
    for p in range(pieces):
        lo, hi = edges[p], edges[p + 1]
        for at in range(lo, min(hi, wide), 1024):
            to = min(at + 1024, wide)
            value = dot_rows(grad_share, context_held[:, at:to]).astype(bf16)
            for k in range(n):
                term[k // 2, k % 2, :, at:to] = value[k * block : (k + 1) * block]
        if hi > wide:
            value = dot_rows(whole[rows:, columns], select).astype(bf16)
            for k in range(n):
                term[k // 2, k % 2, :, wide:hi] = value[k * block : (k + 1) * block]
        firsts.append(
            wire.start(
                term.at[:, 1 - w.near, :, lo:hi], term_got.at[:, :, lo:hi], w.along_frames(1)
            )
        )
    for mask in red_q.order[2:]:
        red_q.forward(mask)
    for copy in load_ctx:
        copy.wait()

    def context_rows(t):
        at = pl.ds(pl.multiple_of(t * LANES, LANES), LANES)
        out_context[at, :] = dot_columns(whole[at, :], ctx_held[...])

    @pl.loop(0, rows // LANES)
    def _(t):
        context_rows(t)

    for p in range(pieces):
        lo, hi = edges[p], edges[p + 1]
        firsts[p].wait_recv()
        for mask in w.masks + [0]:
            to = flip(w.at, mask // 2)
            total = term[to, w.near, :, lo:hi].astype(f32) + term_got[to, :, lo:hi].astype(f32)
            term_sum[to, :, lo:hi] = total.astype(bf16)
            if mask:
                seconds.append(
                    wire.start(
                        term_sum.at[to, :, lo:hi],
                        term_landed.at[mask // 2, :, lo:hi],
                        w.along_frames(mask),
                    )
                )
    red_up.land()
    red_o.land()
    red_q.land()
    kept = [
        store_result,
        store_grad,
        local.start(send_o.at[w.at], out_o),
        local.start(send_q.at[w.at], out_q),
        local.start(send_up.at[w.at], out_up),
    ]

    @pl.when(crossing)
    def _():
        cross.wait_send()
        cross_result.wait_send()

    for copy in seconds:
        copy.wait_recv()
    total = term_sum[w.at].astype(f32)
    for mask in w.masks:
        total = total + term_landed[mask // 2].astype(f32)
    out_ctx[...] = total[:, :wide]
    out_gains[...] = total[:, wide:]
    for copy in kept:
        copy.wait()
    wire.finish()


def ending_scratch(n, rows, depth, context_shape, count, wide_q, wide_o, wide_up):
    halfn, block, share = n // 2, depth // n, depth // 4 // n
    wide = context_shape[1] + LANES
    half = (rows + EXTRA) // 2
    both = 2 * rows
    shapes = [
        ((both, depth), bf16),
        ((both, depth), bf16),
        ((both, wide_o), bf16),
        ((both, wide_q), bf16),
        ((depth, wide_q), bf16),
        ((both, depth // 2), bf16),
        ((both, depth // 2), bf16),
        ((rows, depth), bf16),
        ((rows, depth), f32),
        ((rows, depth), bf16),
        ((rows + EXTRA, depth), bf16),
        ((rows + EXTRA, depth), bf16),
        ((half, depth), bf16),
        ((half, depth), bf16),
        ((half, depth), bf16),
        ((rows + EXTRA, depth), bf16),
        ((rows, depth), bf16),
        ((halfn, block, wide_q), bf16),
        ((halfn, block, wide_o), bf16),
        ((halfn, block, wide_q), bf16),
        ((halfn, block, wide_o), bf16),
        ((halfn, block, wide_q), bf16),
        ((halfn, block, wide_o), bf16),
        ((halfn, block, wide_up), bf16),
        ((halfn, block, wide_up), bf16),
        ((halfn, block, wide_up), bf16),
        (context_shape, bf16),
        ((count, depth), bf16),
        ((halfn, 2, share, wide), bf16),
        ((halfn, share, wide), bf16),
        ((halfn, share, wide), bf16),
        ((halfn, share, wide), bf16),
        ((1, depth), f32),
    ]
    others = [((rows, depth), f32)] * 4 + [((rows, depth), bf16)] * 2 + [((rows, count), f32)]
    return shapes, sum(math.prod(dims) * jnp.dtype(kind).itemsize for dims, kind in shapes + others)


def ending(
    n, resid, mid, gains, gain_two, result_rows,
    pair_one, pair_grad, mixed, grad_qkv, qkv_full, context, ctx_pieces, up_send, up_stay,
):
    rows, depth = resid.shape
    halfn, block = n // 2, depth // n
    wide_q, wide_o = qkv_full.shape[1], mixed.shape[1]
    count = ctx_pieces.shape[1]
    wide_up = up_send.shape[2]
    shapes, _ = ending_scratch(n, rows, depth, context.shape, count, wide_q, wide_o, wide_up)
    sems = 64 + 2 * n
    shape = jax.ShapeDtypeStruct
    return pl.pallas_call(
        functools.partial(ending_body, n),
        in_specs=[VMEM] * 5 + [ANY] * 9,
        out_specs=[ANY] * 8 + [VMEM] * 3,
        out_shape=[
            shape((block, wide_q), bf16),
            shape((block, wide_o), bf16),
            shape((block, wide_up), bf16),
            shape((halfn - 1, block, wide_q), bf16),
            shape((halfn - 1, block, wide_o), bf16),
            shape((halfn - 1, block, wide_up), bf16),
            shape((rows, depth), bf16),
            shape((rows, depth), bf16),
            shape((rows, count), f32),
            shape((depth // 4 // n, context.shape[1]), f32),
            shape((depth // 4 // n, LANES), f32),
        ],
        scratch_shapes=[pltpu.VMEM(dims, kind) for dims, kind in shapes]
        + [
            pltpu.SemaphoreType.DMA((sems,)),
            pltpu.SemaphoreType.DMA((sems,)),
            pltpu.SemaphoreType.DMA((32,)),
        ],
        compiler_params=pltpu.CompilerParams(
            collective_id=6, has_side_effects=True, vmem_limit_bytes=67_000_000
        ),
        name="ending",
    )(
        resid, mid, gains, gain_two, result_rows,
        pair_one, pair_grad, mixed, grad_qkv, qkv_full, context, ctx_pieces, up_send, up_stay,
    )


def finish_body(
    own_q, own_o, own_gate, own_up, own_down, far_q, far_o, far_gate, far_up, far_down,
    grad, result, valid, out_q, out_o, out_gu, out_down, out_grad, out_result,
):
    place = (lax.axis_index("frames") // 2) % 2

    def settle(own, far, out, columns):
        total, other = own[...].astype(f32), None
        for k in range(far.shape[0]):
            value = far[k].astype(f32)
            if (k + 1) & 1:
                other = value if other is None else other + value
            else:
                total = total + value
        out[place, :, columns] = total
        out[1 - place, :, columns] = other

    wide = own_gate.shape[1]
    settle(own_q, far_q, out_q, slice(None))
    settle(own_o, far_o, out_o, slice(None))
    settle(own_gate, far_gate, out_gu, slice(0, wide))
    settle(own_up, far_up, out_gu, slice(wide, 2 * wide))
    settle(own_down, far_down, out_down, slice(None))
    out_grad[:, 0, :] = grad[...].astype(f32)
    out_result[:, 0, :] = result[...].astype(f32) * valid[...]


def finish(owns, fars, grad, result, valid, steps=4):
    block = owns[0].shape[0] // steps
    rows, depth = grad.shape
    shape = jax.ShapeDtypeStruct
    q, o, gate, up, down = [own.shape[1] for own in owns]
    here = rows // steps

    def own_spec(wide):
        return pl.BlockSpec((block, wide), lambda t: (t, 0))

    def far_spec(count, wide):
        return pl.BlockSpec((count, block, wide), lambda t: (0, t, 0))

    widths = (q, o, gate + up, down)
    row_out = pl.BlockSpec((here, 1, depth), lambda t: (t, 0, 0))
    return pl.pallas_call(
        finish_body,
        grid=(steps,),
        in_specs=[own_spec(x.shape[1]) for x in owns]
        + [far_spec(x.shape[0], x.shape[2]) for x in fars]
        + [pl.BlockSpec((here, depth), lambda t: (t, 0))] * 2
        + [pl.BlockSpec((here, 1), lambda t: (t, 0))],
        out_specs=[far_spec(2, wide) for wide in widths] + [row_out, row_out],
        out_shape=[shape((2, owns[0].shape[0], wide), f32) for wide in widths]
        + [shape((rows, 1, depth), f32)] * 2,
        compiler_params=pltpu.CompilerParams(vmem_limit_bytes=60 << 20),
        name="finish",
    )(*owns, *fars, grad, result, valid)


def swap_frames(value, mask):
    n = lax.axis_size("frames")
    return lax.ppermute(value, "frames", [(d, d ^ mask) for d in range(n)])


def swap_stream(value, mask):
    n = lax.axis_size("stream")
    return lax.ppermute(value, "stream", [(d, d ^ mask) for d in range(n)])


def joint(value, target):
    streams, n = lax.axis_size("stream"), lax.axis_size("frames")
    pairs = []
    for s in range(streams):
        for f in range(n):
            to_s, to_f = target(s, f)
            pairs.append((s * n + f, to_s * n + to_f))
    return lax.ppermute(value, ("stream", "frames"), pairs)


def transposed(value):
    def target(s, f):
        core, place = s % 2, (f // 2) % 2
        return s - core + place, f - 2 * place + 2 * core

    return joint(value, target)


def peer(value, mask):
    return joint(value, lambda s, f: (s ^ (mask & 2), f ^ (2 * (mask & 1))))


def norm_scale(values):
    return lax.rsqrt(jnp.mean(values * values, axis=-1, keepdims=True) + norm_eps)


def norm_back(values, scale, gain, grad):
    weighted = grad * gain
    inner_mean = jnp.mean(weighted * values, axis=-1, keepdims=True)
    grad_values = scale * weighted - values * (scale * scale * scale) * inner_mean
    grad_gain = jnp.sum(grad * values * scale, axis=0)
    return (grad_values, grad_gain)


def exchange_rows(qkv, position):
    rows, width = qkv.shape
    quarter = rows // 4
    parts = qkv.reshape(4, quarter, width)
    out = jnp.zeros((4, quarter, width), qkv.dtype)
    own = lax.dynamic_index_in_dim(parts, position, 0, keepdims=False)
    out = lax.dynamic_update_index_in_dim(out, own, position, 0)
    for mask in (2, 1, 3):
        there = position ^ mask
        got = peer(lax.dynamic_index_in_dim(parts, there, 0, keepdims=False), mask)
        out = lax.dynamic_update_index_in_dim(out, got, there, 0)
    return out


def heads_sum(product, fold):
    high = product.astype(bf16)
    low = (product - high.astype(f32)).astype(bf16)
    return jnp.dot(high, fold, preferred_element_type=f32) + jnp.dot(
        low, fold, preferred_element_type=f32
    )


def attention_forward_rows(at, qkv_ref, fold, spread, probs_ref, out_ref):
    width = out_ref.shape[2]
    for q in range(4):
        query = qkv_ref[q, at, :width].astype(f32)
        scores = []
        for k in range(q + 1):
            key = qkv_ref[k, at, width : 2 * width].astype(f32)
            scores.append(heads_sum(query * key, fold) * HD ** (-0.5))
        top = functools.reduce(jnp.maximum, scores)
        expo = [jnp.exp(s - top) for s in scores]
        total = functools.reduce(jnp.add, expo)
        mixed = None
        for k in range(q + 1):
            prob = expo[k] / total
            probs_ref[PAIRS.index((q, k)), at, :] = prob
            wide = jnp.dot(prob.astype(bf16), spread, preferred_element_type=f32)
            term = wide * qkv_ref[k, at, 2 * width :].astype(f32)
            mixed = term if mixed is None else mixed + term
        out_ref[q, at, :] = mixed.astype(bf16)


def attention_backward_rows(at, qkv_ref, probs_ref, grad_ref, fold, spread, out_ref):
    width = grad_ref.shape[2]
    grad_keys, grad_values = [None] * 4, [None] * 4
    for q in range(4):
        grad = grad_ref[q, at, :].astype(f32)
        query = qkv_ref[q, at, :width].astype(f32)
        probs = [probs_ref[PAIRS.index((q, k)), at, :] for k in range(q + 1)]
        grad_probs = [
            heads_sum(grad * qkv_ref[k, at, 2 * width :].astype(f32), fold) for k in range(q + 1)
        ]
        total = functools.reduce(jnp.add, [p * g for p, g in zip(probs, grad_probs)])
        grad_query = None
        for k in range(q + 1):
            wide = jnp.dot(probs[k].astype(bf16), spread, preferred_element_type=f32)
            term = wide * grad
            grad_values[k] = term if grad_values[k] is None else grad_values[k] + term
            grad_score = (probs[k] * (grad_probs[k] - total)).astype(bf16)
            wide = jnp.dot(grad_score, spread, preferred_element_type=f32)
            term = wide * qkv_ref[k, at, width : 2 * width].astype(f32)
            grad_query = term if grad_query is None else grad_query + term
            term = wide * query
            grad_keys[k] = term if grad_keys[k] is None else grad_keys[k] + term
        out_ref[q, at, :width] = (grad_query * HD ** (-0.5)).astype(bf16)
    for k in range(4):
        out_ref[k, at, width : 2 * width] = (grad_keys[k] * HD ** (-0.5)).astype(bf16)
        out_ref[k, at, 2 * width :] = grad_values[k].astype(bf16)


def attention_backward_body(qkv_ref, probs_ref, grad_ref, fold_ref, spread_ref, out_ref):
    everything = slice(None)
    attention_backward_rows(
        everything, qkv_ref, probs_ref, grad_ref, fold_ref[...], spread_ref[...], out_ref
    )


def fold_matrices(width):
    fold = np.arange(width)[:, None] // HD == np.arange(LANES)[None, :]
    return jnp.asarray(fold, bf16), jnp.asarray(fold.T, bf16)


def attention_backward(qkv, probs, grad, step=64):
    _, rows, triple = qkv.shape
    width = triple // 3
    fold, spread = fold_matrices(width)
    return pl.pallas_call(
        attention_backward_body,
        grid=(rows // step,),
        in_specs=[
            pl.BlockSpec((4, step, triple), lambda r: (0, r, 0)),
            pl.BlockSpec((len(PAIRS), step, LANES), lambda r: (0, r, 0)),
            pl.BlockSpec((4, step, width), lambda r: (0, r, 0)),
            pl.BlockSpec((width, LANES), lambda r: (0, 0)),
            pl.BlockSpec((LANES, width), lambda r: (0, 0)),
        ],
        out_specs=pl.BlockSpec((4, step, triple), lambda r: (0, r, 0)),
        out_shape=jax.ShapeDtypeStruct((4, rows, triple), bf16),
        name="attention_backward",
    )(qkv, probs, grad, fold, spread)


def after(value, *others):
    return lax.optimization_barrier((value,) + others)[0]


def taken(weights, place):
    own = [lax.dynamic_index_in_dim(w, place, 0, keepdims=False) for w in weights]
    other = [lax.dynamic_index_in_dim(w, 1 - place, 0, keepdims=False) for w in weights]
    if len(weights) == 1:
        return own[0], other[0]
    return jnp.concatenate(own, axis=1), jnp.concatenate(other, axis=1)


def placed_rows(pieces, frame_index, start, width):
    n = lax.axis_size("frames")
    block = pieces[0].shape[0]
    full = jnp.zeros((n, block, width), pieces[0].dtype)
    for mask in range(n):
        part = pieces[mask][:, start : start + width]
        full = lax.dynamic_update_index_in_dim(full, part, frame_index ^ mask, 0)
    return full.reshape(n * block, width)


def halves(left, near):
    n = lax.axis_size("frames")
    rows, depth = left.shape
    block = depth // n
    even = jnp.concatenate([left[:, k * block : (k + 1) * block] for k in range(0, n, 2)], axis=1)
    odd = jnp.concatenate([left[:, k * block : (k + 1) * block] for k in range(1, n, 2)], axis=1)
    return jnp.where(near == 0, odd, even), jnp.where(near == 0, even, odd)


def scattered(left_halves, right, frame_index, place):
    n = lax.axis_size("frames")

    def product(part):
        return lax.dot_general(
            part, right, (((0,), (0,)), ((), ())), preferred_element_type=f32
        ).astype(bf16)

    arrived = swap_frames(product(left_halves[0]), 1)
    half_sum = (product(left_halves[1]).astype(f32) + arrived.astype(f32)).astype(bf16)
    half_sum = half_sum.reshape(n // 2, -1, right.shape[1])
    at = frame_index // 2
    own = lax.dynamic_index_in_dim(half_sum, at, 0, keepdims=False).astype(f32)
    other = None
    for mask in range(2, n, 2):
        got = swap_frames(
            lax.dynamic_index_in_dim(half_sum, at ^ (mask // 2), 0, keepdims=False), mask
        ).astype(f32)
        if mask & 2:
            other = got if other is None else other + got
        else:
            own = own + got
    first = jnp.where(place == 0, own, other)
    second = jnp.where(place == 0, other, own)
    return jnp.stack([first, second], axis=0)


class Spread:
    def __init__(self, w, wire, weight, full):
        self.w, self.wire, self.weight, self.full = w, wire, weight, full
        self.block = full.shape[0] // w.n
        self.far, self.near = {}, {}

    def rows(self, frame):
        return self.full.at[pl.ds(pl.multiple_of(frame * self.block, self.block), self.block), :]

    def own(self, local):
        return local.start(self.weight.at[self.w.place], self.rows(self.w.frame))

    def own_near(self):
        w = self.w
        self.near[0] = self.wire.start(
            self.weight.at[w.place], self.rows(w.frame), w.along_frames(1)
        )

    def send(self, masks):
        w = self.w
        for mask in masks:
            which = 1 - w.place if mask & 2 else w.place
            self.far[mask] = self.wire.start(
                self.weight.at[which], self.rows(w.frame), w.along_frames(mask)
            )

    def relay(self, mask):
        self.far[mask].wait_recv()
        rows = self.rows(flip(self.w.frame, mask))
        self.near[mask] = self.wire.start(rows, rows, self.w.along_frames(1))

    def close(self):
        for copy in self.near.values():
            copy.wait_recv()


def front_body(
    n, context, ctx_weight, inputs, cotangent, valid, gains, fold, spread,
    qkv_weight, out_weight, gu_weight, down_weight,
    out_qkv, out_out, out_gu, out_down, out_ctx, out_resid, out_mid, out_one, out_two, out_grad,
    out_qkv_mixed, out_probs, out_mixed,
    ctx_held, context_held, total, partner_half, half_sum, far_half, whole, home, resid, pair,
    qkv_full, out_full, qkv_rows, qkv_mixed, probs, mixed_quarter, mixed, away, got, grad_low,
    send_sem, recv_sem, local_sem,
):
    w = Where(n)
    wire, local = Wire(send_sem, recv_sem), Local(local_sem)
    rows, depth = inputs.shape
    count = ctx_weight.shape[0] // 4
    piece = depth // n
    crossing = w.core != w.place
    half = rows // 2
    step = 64
    quarter_of_context = pl.ds(pl.multiple_of(w.stream * count, LANES), count)
    load_context = local.start(context.at[:, quarter_of_context], context_held)
    load_ctx = local.start(ctx_weight.at[quarter_of_context, :], ctx_held.at[w.frame])
    qkv = Spread(w, wire, qkv_weight, qkv_full)
    out = Spread(w, wire, out_weight, out_full)
    gu = Spread(w, wire, gu_weight, out_gu)
    down = Spread(w, wire, down_weight, out_down)
    owns = [qkv.own(local), out.own(local)]
    greet(
        [w.along_stream(1), w.along_stream(2), w.along_frames(1)]
        + [w.along_frames(m) for m in w.masks]
        + [w.across(), w.with_position(3)]
    )

    load_ctx.wait()
    held, near = [0], {}

    def ctx_near(o):
        at = flip(w.frame, o)
        near[o] = wire.start(ctx_held.at[at], ctx_held.at[at], w.along_frames(1))

    ready = []
    for bit in reversed(range(1, n.bit_length() - 1)):
        copies = []
        for o in held:
            at = flip(w.frame, o)
            copies.append(
                (o, wire.start(ctx_held.at[at], ctx_held.at[at], w.along_frames(1 << bit)))
            )
        if bit == n.bit_length() - 2:
            ctx_near(0)
            qkv.own_near()
            out.own_near()
        if bit == 1:
            for mask in w.masks:
                qkv.send([mask])
                out.send([mask])
        for o, copy in copies:
            copy.wait_recv()
            ctx_near(o ^ (1 << bit))
            held.append(o ^ (1 << bit))

    load_context.wait()

    def project(o):
        at = flip(w.frame, o)
        columns = pl.ds(pl.multiple_of(at * piece, piece), piece)
        value = jnp.dot(context_held[...], ctx_held[at], preferred_element_type=f32)
        total[:, columns] = value

    def relay_attention(k):
        for mask in w.masks[k : k + 1]:
            qkv.relay(mask)
            out.relay(mask)

    if piece % LANES == 0:
        for o in held:
            project(o)
        for o in held:
            if o == held[-1]:
                relay_attention(0)
            near[o].wait_recv()
            project(o ^ 1)
    else:
        for o in held:
            near[o].wait_recv()
        relay_attention(0)
        total[...] = jnp.zeros_like(total)

        @pl.loop(0, n)
        def _(at):
            line = lax.broadcasted_iota(jnp.int32, (piece, depth), 0)
            column = lax.broadcasted_iota(jnp.int32, (piece, depth), 1)
            select = (column == line + at * piece).astype(bf16)
            laid = jnp.dot(ctx_held[at], select, preferred_element_type=f32).astype(bf16)

            @pl.loop(0, rows // LANES)
            def _(t):
                here = pl.ds(pl.multiple_of(t * LANES, LANES), LANES)
                total[here, :] += jnp.dot(
                    context_held[here, :], laid, preferred_element_type=f32
                )

    store_ctx = local.start(ctx_held, out_ctx)

    mine = pl.ds(pl.multiple_of(w.core * half, 16), half)
    theirs = pl.ds(pl.multiple_of((1 - w.core) * half, 16), half)
    whole[theirs, :] = total[theirs, :].astype(bf16)
    first = wire.start(whole.at[theirs, :], partner_half, w.along_stream(1))
    first.wait_recv()
    half_sum[...] = (total[mine, :] + partner_half[...].astype(f32)).astype(bf16)
    second = wire.start(half_sum, far_half, w.along_stream(2))
    relay_attention(1)
    second.wait_recv()
    home[mine, :] = (half_sum[...].astype(f32) + far_half[...].astype(f32)).astype(bf16)
    third = wire.start(home.at[mine, :], home.at[mine, :], w.along_stream(1))
    third.wait_recv()
    wire.sent(third)

    @pl.loop(0, rows // step)
    def _(t):
        at = pl.ds(pl.multiple_of(t * step, step), step)
        home[at, :] = (home[at, :].astype(f32) + inputs[at, :].astype(f32)).astype(bf16)

    cross = wire.make(home, resid, w.across())
    stay = pltpu.make_async_copy(home, resid, local_sem.at[22])

    @pl.when(crossing)
    def _():
        cross.start()

    @pl.when(jnp.logical_not(crossing))
    def _():
        stay.start()

    gu.own_near()
    gu.send(w.far_masks + w.both_masks)
    for k in range(2, len(w.masks)):
        relay_attention(k)

    @pl.when(crossing)
    def _():
        cross.wait_recv()

    @pl.when(jnp.logical_not(crossing))
    def _():
        stay.wait()

    def normed(source, gain):
        @pl.loop(0, rows // step)
        def _(t):
            at = pl.ds(pl.multiple_of(t * step, step), step)
            values = source[at, :].astype(f32)
            scale = lax.rsqrt(jnp.mean(values * values, axis=-1, keepdims=True) + norm_eps)
            pair[at, :] = (values * scale * gain).astype(bf16)

    normed(resid, gains[0:1, :])
    upper = pair.at[rows:, :]
    first_pair = wire.start(pair.at[:rows, :], upper, w.along_stream(1))
    for copy in owns:
        copy.wait()
    qkv.close()
    out.close()
    quarter = 2 * rows // 4
    width = out_full.shape[1]

    def qkv_of(lo, hi):
        @pl.loop(lo, hi)
        def _(t):
            at = pl.ds(pl.multiple_of(t * quarter, quarter), quarter)
            left = pair[at, :]
            for p in range(3):
                columns = slice(p * width, (p + 1) * width)
                value = jnp.dot(left, qkv_full[:, columns], preferred_element_type=f32)
                qkv_rows[at, columns] = value.astype(bf16)

    qkv_of(0, 2)
    first_pair.wait_recv()
    qkv_of(2, 4)
    mixing = {}

    def rows_of(position):
        return pl.ds(pl.multiple_of(position * quarter, quarter), quarter)

    for mask in (3, 1, 2):
        mixing[mask] = wire.start(
            qkv_rows.at[rows_of(flip(w.position, mask)), :],
            qkv_mixed.at[w.position],
            w.with_position(mask),
        )
    own_quarter = local.start(qkv_rows.at[rows_of(w.position), :], qkv_mixed.at[w.position])
    gu.send([2])
    down.send(w.far_masks)
    @pl.loop(0, rows // step)
    def _(t):
        at = pl.ds(pl.multiple_of(t * step, step), step)
        grad_low[at, :] = (cotangent[at, 0, :] * valid[at, :]).astype(bf16)

    stores = [
        local.start(pair, out_one),
        local.start(qkv_full, out_qkv),
        local.start(out_full, out_out),
        local.start(resid, out_resid),
        local.start(grad_low, out_grad),
    ]
    gu_own, down_own = gu.own(local), down.own(local)
    for mask in w.far_masks:
        gu.relay(mask)
    own_quarter.wait()
    for mask in (2, 1, 3):
        mixing[mask].wait_recv()
    for mask in w.both_masks:
        gu.relay(mask)
    fold_held, spread_held = fold[...], spread[...]

    @pl.loop(0, quarter // step)
    def _(t):
        at = pl.ds(pl.multiple_of(t * step, step), step)
        attention_forward_rows(at, qkv_mixed, fold_held, spread_held, probs, mixed_quarter)

    returning = {}
    for mask in (3, 1, 2):
        returning[mask] = wire.start(
            mixed_quarter.at[flip(w.position, mask)],
            mixed.at[rows_of(w.position), :],
            w.with_position(mask),
        )
    own_back = local.start(mixed_quarter.at[w.position], mixed.at[rows_of(w.position), :])
    down.send(w.both_masks + [2])
    stores += [local.start(qkv_mixed, out_qkv_mixed), local.start(probs, out_probs)]
    gu.relay(2)
    own_back.wait()
    for mask in (2, 1, 3):
        returning[mask].wait_recv()
    stores.append(local.start(mixed, out_mixed))
    stores[0].wait()

    @pl.loop(2, 4)
    def _(t):
        at = pl.ds(pl.multiple_of(t * quarter, quarter), quarter)
        to = pl.ds(pl.multiple_of(t * quarter - rows, quarter), quarter)
        away[to, :] = dot_columns(mixed[at, :], out_full[...]).astype(bf16)

    part = wire.start(away, got, w.along_stream(1))

    @pl.loop(0, 2)
    def _(t):
        at = pl.ds(pl.multiple_of(t * quarter, quarter), quarter)
        total[at, :] = dot_columns(mixed[at, :], out_full[...])

    part.wait_recv()
    wire.sent(first_pair)
    gain = gains[1:2, :]

    @pl.loop(0, rows // step)
    def _(t):
        at = pl.ds(pl.multiple_of(t * step, step), step)
        values = resid[at, :].astype(f32) + total[at, :] + got[at, :].astype(f32)
        total[at, :] = values
        scale = lax.rsqrt(jnp.mean(values * values, axis=-1, keepdims=True) + norm_eps)
        pair[at, :] = (values * scale * gain).astype(bf16)

    second_pair = wire.start(pair.at[:rows, :], upper, w.along_stream(1))
    stores.append(local.start(total, out_mid))
    second_pair.wait_recv()
    stores.append(local.start(pair, out_two))
    gu.close()
    for copy in down.far.values():
        copy.wait_recv()
    for copy in stores[1:]:
        copy.wait()
    for copy in (store_ctx, gu_own, down_own):
        copy.wait()

    @pl.when(crossing)
    def _():
        cross.wait_send()

    wire.finish()


def front(
    n, context, ctx_weight, inputs, cotangent, valid, gains,
    qkv_weight, out_weight, gu_weight, down_weight,
):
    rows, depth = inputs.shape
    count = ctx_weight.shape[0] // 4
    wide_q, wide_o = qkv_weight.shape[2], out_weight.shape[2]
    fold, spread = fold_matrices(wide_o)
    quarter = rows // 2
    half = rows // 2
    pairs = len(PAIRS)
    scratch = [
        pltpu.VMEM((n, count, depth // n), bf16),
        pltpu.VMEM((rows, count), bf16),
        pltpu.VMEM((rows, depth), f32),
        pltpu.VMEM((half, depth), bf16),
        pltpu.VMEM((half, depth), bf16),
        pltpu.VMEM((half, depth), bf16),
        pltpu.VMEM((rows, depth), bf16),
        pltpu.VMEM((rows, depth), bf16),
        pltpu.VMEM((rows, depth), bf16),
        pltpu.VMEM((2 * rows, depth), bf16),
        pltpu.VMEM((depth, wide_q), bf16),
        pltpu.VMEM((depth, wide_o), bf16),
        pltpu.VMEM((2 * rows, wide_q), bf16),
        pltpu.VMEM((4, quarter, wide_q), bf16),
        pltpu.VMEM((pairs, quarter, LANES), f32),
        pltpu.VMEM((4, quarter, wide_o), bf16),
        pltpu.VMEM((2 * rows, wide_o), bf16),
        pltpu.VMEM((rows, depth), bf16),
        pltpu.VMEM((rows, depth), bf16),
        pltpu.VMEM((rows, depth), bf16),
        pltpu.SemaphoreType.DMA((24 + 10 * n,)),
        pltpu.SemaphoreType.DMA((24 + 10 * n,)),
        pltpu.SemaphoreType.DMA((24,)),
    ]
    shape = jax.ShapeDtypeStruct
    return pl.pallas_call(
        functools.partial(front_body, n),
        in_specs=[ANY, ANY, VMEM, VMEM, VMEM, VMEM, VMEM, VMEM, ANY, ANY, ANY, ANY],
        out_specs=[ANY] * 13,
        out_shape=[
            shape((depth, wide_q), bf16),
            shape((depth, wide_o), bf16),
            shape((depth, gu_weight.shape[2]), bf16),
            shape((depth, down_weight.shape[2]), bf16),
            shape((n, count, depth // n), bf16),
            shape((rows, depth), bf16),
            shape((rows, depth), f32),
            shape((2 * rows, depth), bf16),
            shape((2 * rows, depth), bf16),
            shape((rows, depth), bf16),
            shape((4, quarter, wide_q), bf16),
            shape((pairs, quarter, LANES), f32),
            shape((2 * rows, wide_o), bf16),
        ],
        scratch_shapes=scratch,
        compiler_params=pltpu.CompilerParams(
            collective_id=3, has_side_effects=True, vmem_limit_bytes=62 << 20
        ),
        name="front",
    )(
        context, ctx_weight, inputs, cotangent, valid, gains, fold, spread,
        qkv_weight, out_weight, gu_weight, down_weight,
    )


def back_body(
    n, pair_two, home_grad, resid, gu_weight, down_half, out_weight, qkv_held, probs_held,
    gains, fold, spread,
    out_down, out_gate, out_up, out_up_stay, landed_down, landed_gate, out_mid, out_gain, out_pair, out_rows, out_qkv,
    two, grad, gu_full, down_full, out_full, two_away, two_stay, grad_away, grad_stay,
    hidden, grad_gu, send_down, send_gu, got_down, got_gu,
    values_mid, away, got, grad_rows, grad_mixed, qkv_mixed, probs, grad_qkv,
    send_sem, recv_sem, tile_send, tile_recv, local_sem,
):
    w = Where(n)
    wire, local = Wire(send_sem, recv_sem), Local(local_sem)
    tiled = Wire(tile_send, tile_recv)
    rows, depth = out_mid.shape
    both = 2 * rows
    piece = depth // n
    halfn = n // 2
    wide = down_full.shape[1]
    tile = 2 * LANES
    whole_tiles = wide // tile
    tiles = whole_tiles + (1 if wide % tile else 0)
    step = 64
    loads = [
        local.start(pair_two, two),
        local.start(gu_weight, gu_full),
    ]
    blocks = [
        pl.ds(pl.multiple_of((2 * b + w.near) * piece, piece), piece) for b in range(halfn)
    ]
    down_own = [local.start(down_half.at[at, :], down_full.at[at, :]) for at in blocks]
    late = [
        local.start(resid, values_mid),
        local.start(out_weight, out_full),
        local.start(qkv_held, qkv_mixed),
        local.start(probs_held, probs),
    ]
    greet(
        [w.along_stream(1), w.along_stream(2), w.along_frames(1)]
        + [w.along_frames(m) for m in w.masks]
        + [w.with_position(3), w.across()]
    )
    crossing = w.core != w.place
    cross = wire.make(home_grad, grad.at[:rows, :], w.across())
    stay = pltpu.make_async_copy(home_grad, grad.at[:rows, :], local_sem.at[15 + n])

    @pl.when(crossing)
    def _():
        cross.start()

    @pl.when(jnp.logical_not(crossing))
    def _():
        stay.start()

    neighbour = w.along_frames(1)
    cut = min(3, whole_tiles)
    down_near = [
        [
            wire.start(down_half.at[at, span], down_full.at[at, span], neighbour)
            for at in blocks
        ]
        for span in (slice(0, cut * tile), slice(cut * tile, wide))
    ]

    def split(source, into_away, into_stay):
        for b in range(halfn):
            for ref, which in ((into_away, 1 - w.near), (into_stay, w.near)):
                at = pl.ds(pl.multiple_of((2 * b + which) * piece, piece), piece)
                ref[:, b * piece : (b + 1) * piece] = source[:, at]

    loads[0].wait()
    split(two, two_away, two_stay)
    loads[1].wait()

    def columns(start, size):
        return pl.ds(pl.multiple_of(start, LANES), size)

    def tile_parts(t):
        lo = t * tile
        return ((send_down, got_down, lo), (send_gu, got_gu, lo), (send_gu, got_gu, wide + lo))

    def move(t, size, j):
        ref, into, start = tile_parts(t)[j]
        at = columns(start, size)
        return tiled.make(ref.at[:, :, at], into.at[:, :, at], neighbour, 3 * t + j)

    def forward(t, size):
        lo = t * tile
        here = columns(lo, size)
        there = columns(wide + lo, size)

        @pl.loop(0, both // 256)
        def _(r):
            at = pl.ds(pl.multiple_of(r * 256, 256), 256)
            left = two[at, :]
            gate = jnp.dot(left, gu_full[:, here], preferred_element_type=f32)
            up = jnp.dot(left, gu_full[:, there], preferred_element_type=f32)
            hidden[at, here] = (gate / (1.0 + jnp.exp(-gate)) * up).astype(bf16)
            grad_gu[at, here] = gate.astype(bf16)
            grad_gu[at, there] = up.astype(bf16)

    def store_away(ref, left, right, at):
        value = dot_rows(left[...], right[:, at]).astype(bf16)
        for b in range(halfn):
            ref[b, :, at] = value[b * piece : (b + 1) * piece]

    def away_down(t, size):
        store_away(send_down, grad_away, hidden, columns(t * tile, size))
        move(t, size, 0).start()

    def backward(t, size):
        lo = t * tile
        here = columns(lo, size)
        there = columns(wide + lo, size)

        @pl.loop(0, both // 256)
        def _(r):
            at = pl.ds(pl.multiple_of(r * 256, 256), 256)
            gate = grad_gu[at, here].astype(f32)
            up = grad_gu[at, there].astype(f32)
            back = jnp.dot(grad[at, :], down_full[:, here], preferred_element_type=f32)
            sigma = 1.0 / (1.0 + jnp.exp(-gate))
            grad_gu[at, here] = (back * up * (sigma * (1.0 + gate * (1.0 - sigma)))).astype(bf16)
            grad_gu[at, there] = (back * (gate * sigma)).astype(bf16)

        store_away(send_gu, two_away, grad_gu, here)
        store_away(send_gu, two_away, grad_gu, there)
        move(t, size, 1).start()

    rest = wide - whole_tiles * tile

    def some(step_of, lo, hi):
        top = min(hi, whole_tiles)
        if top > lo:

            @pl.loop(lo, top)
            def _(t):
                step_of(t, tile)

        if hi > whole_tiles and rest:
            step_of(whole_tiles, rest)

    def every(step_of):
        @pl.loop(0, whole_tiles)
        def _(t):
            step_of(t, tile)

        if rest:
            step_of(whole_tiles, rest)

    every(forward)

    @pl.when(crossing)
    def _():
        cross.wait_recv()

    @pl.when(jnp.logical_not(crossing))
    def _():
        stay.wait()

    grad_pair = wire.start(grad.at[:rows, :], grad.at[rows:, :], w.along_stream(1))
    grad_pair.wait_recv()
    split(grad, grad_away, grad_stay)
    every(away_down)
    for copy in down_own:
        copy.wait()
    for copy in down_near[0]:
        copy.wait_recv()
    some(backward, 0, cut)
    for copy in down_near[1]:
        copy.wait_recv()
    some(backward, cut, tiles)

    landed = (landed_down, landed_gate)

    def landing(t, size, j, k):
        ref, _, start = tile_parts(t)[j]
        mask = w.masks[k]
        at = columns(start, size)
        return tiled.make(
            ref.at[flip(w.at, mask // 2), :, at],
            landed[j].at[mask // 2 - 1, :, columns(t * tile, size)],
            w.along_frames(mask),
            3 * tiles + (3 * t + j) * len(w.masks) + k,
        )

    lefts = (grad_stay, two_stay, two_stay)
    rights = (hidden, grad_gu, grad_gu)

    def reduce_part(t, size, j):
        ref, into, start = tile_parts(t)[j]
        at = columns(start, size)
        move(t, size, j).wait()
        value = dot_rows(lefts[j][...], rights[j][:, at])
        for b in range(halfn):
            total = value[b * piece : (b + 1) * piece] + into[b, :, at].astype(f32)
            ref[b, :, at] = total.astype(bf16)
        for k in range(len(w.masks)):
            landing(t, size, j, k).start()

    def reduce_down(t, size):
        reduce_part(t, size, 0)

    def reduce_gu(t, size):
        reduce_part(t, size, 1)

    def stay_up(t, size):
        at = columns(wide + t * tile, size)
        store_away(got_gu, two_stay, grad_gu, at)

    def rows_of(position):
        quarter = both // 4
        return pl.ds(pl.multiple_of(position * quarter, quarter), quarter)

    def partial(left, right, t):
        at = pl.ds(pl.multiple_of(t * 256, 256), 256)
        return dot_columns(left[at, :], right[...])

    @pl.loop(0, rows // 256)
    def _(t):
        to = pl.ds(pl.multiple_of(t * 256, 256), 256)
        away[to, :] = partial(grad_gu, gu_full, rows // 256 + t).astype(bf16)

    first = wire.start(away, got, w.along_stream(1))

    @pl.loop(0, rows // 256)
    def _(t):
        to = pl.ds(pl.multiple_of(t * 256, 256), 256)
        out_mid[to, :] = partial(grad_gu, gu_full, t)

    some(reduce_down, 0, min(2, whole_tiles))

    late[0].wait()
    first.wait_recv()
    gain = gains[1:2, :]
    out_gain[...] = jnp.zeros_like(out_gain)

    @pl.loop(0, rows // step)
    def _(t):
        at = pl.ds(pl.multiple_of(t * step, step), step)
        grad_normed = out_mid[at, :] + got[at, :].astype(f32)
        values = values_mid[at, :]
        scale = lax.rsqrt(jnp.mean(values * values, axis=-1, keepdims=True) + norm_eps)
        weighted = grad_normed * gain
        inner = jnp.mean(weighted * values, axis=-1, keepdims=True)
        total = grad[at, :].astype(f32) + scale * weighted
        total = total - values * (scale * scale * scale * inner)
        out_mid[at, :] = total
        two[at, :] = total.astype(bf16)
        out_gain[...] += jnp.sum(grad_normed * values * scale, axis=0, keepdims=True)

    second = wire.start(two.at[:rows, :], two.at[rows:, :], w.along_stream(1))
    late[1].wait()

    def back_rows(lo, hi):
        @pl.loop(lo, hi)
        def _(t):
            at = pl.ds(pl.multiple_of(t * 256, 256), 256)
            value = jnp.dot(two[at, :], out_full[...], preferred_element_type=f32)
            grad_rows[at, :] = value.astype(bf16)

    back_rows(0, rows // 256)
    second.wait_recv()
    back_rows(rows // 256, both // 256)
    mixing = {}
    for mask in (3, 1, 2):
        mixing[mask] = wire.start(
            grad_rows.at[rows_of(flip(w.position, mask)), :],
            grad_mixed.at[w.position],
            w.with_position(mask),
        )
    own = local.start(grad_rows.at[rows_of(w.position), :], grad_mixed.at[w.position])
    store_pair = local.start(two, out_pair)

    some(reduce_down, min(2, whole_tiles), tiles)
    own.wait()
    late[2].wait()
    late[3].wait()
    for mask in (2, 1, 3):
        mixing[mask].wait_recv()
    fold_held, spread_held = fold[...], spread[...]

    @pl.loop(0, both // 4 // step)
    def _(t):
        at = pl.ds(pl.multiple_of(t * step, step), step)
        attention_backward_rows(
            at, qkv_mixed, probs, grad_mixed, fold_held, spread_held, grad_qkv
        )

    returning = {}
    for mask in (3, 1, 2):
        returning[mask] = wire.start(
            grad_qkv.at[flip(w.position, mask)],
            out_qkv.at[rows_of(w.position), :],
            w.with_position(mask),
        )
    own_back = local.start(grad_qkv.at[w.position], out_qkv.at[rows_of(w.position), :])
    early = min(2, whole_tiles)
    some(reduce_gu, 0, early)
    some(stay_up, 0, tiles)

    wire.sent(first)

    @pl.loop(0, rows // 256)
    def _(t):
        to = pl.ds(pl.multiple_of(t * 256, 256), 256)
        away[to, :] = partial(hidden, down_full, rows // 256 + t).astype(bf16)

    third = wire.start(away, got, w.along_stream(1))

    @pl.loop(0, rows // 256)
    def _(t):
        to = pl.ds(pl.multiple_of(t * 256, 256), 256)
        values_mid[to, :] = values_mid[to, :] + partial(hidden, down_full, t)

    third.wait_recv()

    @pl.loop(0, rows // step)
    def _(t):
        at = pl.ds(pl.multiple_of(t * step, step), step)
        out_rows[at, :] = (values_mid[at, :] + got[at, :].astype(f32)).astype(bf16)

    some(reduce_gu, early, tiles)
    kept = [
        local.start(send_down.at[w.at], out_down),
        local.start(send_gu.at[w.at, :, :wide], out_gate),
        local.start(send_gu.at[:, :, wide:], out_up),
        local.start(got_gu.at[:, :, wide:], out_up_stay),
    ]
    own_back.wait()
    store_pair.wait()
    for mask in (2, 1, 3):
        returning[mask].wait_recv()
    for t in range(tiles):
        for j in range(2):
            for k in range(len(w.masks)):
                landing(t, tile if t < whole_tiles else rest, j, k).wait()
    for copy in kept:
        copy.wait()

    @pl.when(crossing)
    def _():
        cross.wait_send()

    wire.finish()


def back_scratch(n, rows, depth, wide, head_width):
    both, halfn, piece = 2 * rows, n // 2, depth // n
    pairs = len(PAIRS)
    quarter = both // 4
    shapes = [
        ((both, depth), bf16),
        ((both, depth), bf16),
        ((depth, 2 * wide), bf16),
        ((depth, wide), bf16),
        ((depth, head_width), bf16),
        ((both, depth // 2), bf16),
        ((both, depth // 2), bf16),
        ((both, depth // 2), bf16),
        ((both, depth // 2), bf16),
        ((both, wide), bf16),
        ((both, 2 * wide), bf16),
        ((halfn, piece, wide), bf16),
        ((halfn, piece, 2 * wide), bf16),
        ((halfn, piece, wide), bf16),
        ((halfn, piece, 2 * wide), bf16),
        ((rows, depth), f32),
        ((rows, depth), bf16),
        ((rows, depth), bf16),
        ((both, head_width), bf16),
        ((4, quarter, head_width), bf16),
        ((4, quarter, 3 * head_width), bf16),
        ((pairs, quarter, LANES), f32),
        ((4, quarter, 3 * head_width), bf16),
    ]
    outs = [((rows, depth), f32), ((rows, depth), bf16)]
    return shapes, sum(math.prod(dims) * jnp.dtype(kind).itemsize for dims, kind in shapes + outs)


def back(
    n, pair_two, home_grad, resid, gu_full, down_half, out_full, qkv_mixed, probs, gains
):
    rows, depth = resid.shape
    wide, head_width = down_half.shape[1], out_full.shape[1]
    shapes, _ = back_scratch(n, rows, depth, wide, head_width)
    tiles = -(-wide // (2 * LANES))
    fold, spread = fold_matrices(head_width)
    shape = jax.ShapeDtypeStruct
    moves = 3 * tiles * (1 + n // 2 - 1)
    return pl.pallas_call(
        functools.partial(back_body, n),
        in_specs=[ANY] * 8 + [VMEM] * 3,
        out_specs=[ANY, ANY, ANY, ANY, ANY, ANY, VMEM, VMEM, ANY, VMEM, ANY],
        out_shape=[
            shape((depth // n, wide), bf16),
            shape((depth // n, wide), bf16),
            shape((n // 2, depth // n, wide), bf16),
            shape((n // 2, depth // n, wide), bf16),
            shape((n // 2 - 1, depth // n, wide), bf16),
            shape((n // 2 - 1, depth // n, wide), bf16),
            shape((rows, depth), f32),
            shape((1, depth), f32),
            shape((2 * rows, depth), bf16),
            shape((rows, depth), bf16),
            shape((2 * rows, 3 * head_width), bf16),
        ],
        scratch_shapes=[pltpu.VMEM(dims, kind) for dims, kind in shapes]
        + [
            pltpu.SemaphoreType.DMA((16 + 2 * n,)),
            pltpu.SemaphoreType.DMA((16 + 2 * n,)),
            pltpu.SemaphoreType.DMA((moves,)),
            pltpu.SemaphoreType.DMA((moves,)),
            pltpu.SemaphoreType.DMA((16 + n,)),
        ],
        compiler_params=pltpu.CompilerParams(
            collective_id=4, has_side_effects=True, vmem_limit_bytes=67_000_000
        ),
        name="back",
    )(
        pair_two, home_grad, resid, gu_full, down_half, out_full, qkv_mixed, probs,
        gains, fold, spread,
    )


def shards(
    inputs,
    context,
    cotangent,
    live_frames,
    ctx_weight,
    norm_gains,
    qkv_weight,
    out_weight,
    gate_up_weight,
    down_weight,
):
    n = lax.axis_size("frames")
    stream_index = lax.axis_index("stream")
    frame_index = lax.axis_index("frames")
    half_index = stream_index % 2
    place = (frame_index // 2) % 2
    position = (stream_index // 2) * 2 + place
    frame_count = inputs.shape[0]
    width_model = inputs.shape[2]
    offsets = lax.broadcasted_iota(jnp.int32, (frame_count,), 0)
    valid_mask = (offsets % SLOT < jnp.repeat(live_frames, SLOT)).astype(f32)[:, None]
    gain_one = norm_gains[0]
    gain_two = norm_gains[1]

    (
        qkv_full,
        out_full,
        gate_up_full,
        down_half,
        ctx_pieces,
        resid_in,
        resid_mid,
        paired_one,
        paired_two,
        grad_rows,
        qkv_mixed,
        probs,
        mixed,
    ) = front(
        n,
        context,
        ctx_weight,
        inputs[:, 0],
        cotangent,
        valid_mask,
        norm_gains,
        qkv_weight[0],
        out_weight[0],
        gate_up_weight[0],
        down_weight[0],
    )
    near = frame_index % 2

    def paired(mine):
        return jnp.concatenate([mine, swap_stream(mine, 1)], axis=0)

    def own_sum(partial_value):
        return partial_value[:frame_count] + swap_stream(
            partial_value[frame_count:].astype(bf16), 1
        ).astype(f32)

    def rows_times(left, right):
        return jnp.dot(left, right, preferred_element_type=f32)

    def rows_back(left, right):
        return lax.dot_general(left, right, (((1,), (1,)), ((), ())), preferred_element_type=f32)

    def returned(value):
        _, quarter, width = value.shape
        out = jnp.zeros((4, quarter, width), value.dtype)
        own = lax.dynamic_index_in_dim(value, position, 0, keepdims=False)
        out = lax.dynamic_update_index_in_dim(out, own, position, 0)
        for mask in (2, 1, 3):
            there = position ^ mask
            got = peer(lax.dynamic_index_in_dim(value, there, 0, keepdims=False), mask)
            out = lax.dynamic_update_index_in_dim(out, got, there, 0)
        return out.reshape(4 * quarter, width)

    head_width = out_full.shape[1]
    _, needed = back_scratch(n, frame_count, width_model, down_weight.shape[3], head_width)
    if needed <= 66_000_000 and (width_model // n) % LANES == 0:
        (
            own_down,
            own_gate,
            up_send,
            up_stay,
            landed_down,
            landed_gate,
            grad_mid,
            grad_gain_two,
            paired_grad_attn,
            result_rows,
            grad_qkv_low,
        ) = back(
            n,
            paired_two,
            grad_rows,
            resid_mid,
            gate_up_full,
            down_half,
            out_full,
            qkv_mixed,
            probs,
            norm_gains,
        )
    else:
        paired_grad_ffn = paired(transposed(grad_rows))
        blocks = down_half.reshape(n // 2, 2, -1, down_half.shape[1])
        blocks = lax.dynamic_index_in_dim(blocks, near, 1, keepdims=False)
        others = swap_frames(blocks, 1)
        even, odd = jnp.where(near == 0, blocks, others), jnp.where(near == 0, others, blocks)
        down_full = jnp.stack([even, odd], axis=1).reshape(down_half.shape)
        scale_two = norm_scale(resid_mid)
        gate_up = rows_times(paired_two, gate_up_full)
        ffn_half = down_full.shape[1]
        gate_part = gate_up[:, :ffn_half]
        up_part = gate_up[:, ffn_half:]
        sigmoid_gate = jax.nn.sigmoid(gate_part)
        activated = gate_part * sigmoid_gate
        hidden = (activated * up_part).astype(bf16)

        grad_res = paired_grad_ffn[:frame_count]
        sum_down = scattered(halves(paired_grad_ffn, near), hidden, frame_index, place)
        grad_hidden = rows_times(paired_grad_ffn, down_full)
        grad_gate = grad_hidden * up_part * (sigmoid_gate * (1.0 + gate_part * (1.0 - sigmoid_gate)))
        grad_up = grad_hidden * activated
        grad_gu_low = jnp.concatenate([grad_gate, grad_up], axis=-1).astype(bf16)
        grad_normed_two = own_sum(rows_back(grad_gu_low, gate_up_full))
        sum_gate_up = scattered(halves(paired_two, near), grad_gu_low, frame_index, place)
        back_two, grad_gain_two = norm_back(resid_mid, scale_two, gain_two, grad_normed_two)
        grad_mid = grad_res.astype(f32) + back_two
        paired_grad_attn = paired(grad_mid.astype(bf16))
        grad_mixed = rows_times(paired_grad_attn, out_full).astype(bf16)
        grad_qkv_mixed = attention_backward(qkv_mixed, probs, exchange_rows(grad_mixed, position))
        grad_qkv_low = returned(grad_qkv_mixed)
        result_rows = (resid_mid + own_sum(rows_back(hidden, down_full))).astype(bf16)
        grad_gain_two = grad_gain_two[None]

    wide_q = qkv_full.shape[1]
    count = ctx_pieces.shape[1]
    _, needed = ending_scratch(
        n, frame_count, width_model, context.shape, count, wide_q, head_width, down_half.shape[1]
    )
    if needed <= 66_000_000 and (width_model // n) % LANES == 0:
        (
            own_qkv,
            own_out,
            own_up,
            landed_qkv,
            landed_out,
            landed_up,
            grad_home,
            result,
            sum_context,
            sum_ctx,
            sum_gains,
        ) = ending(
            n,
            resid_in,
            grad_mid,
            norm_gains,
            grad_gain_two,
            result_rows,
            paired_one,
            paired_grad_attn,
            mixed,
            grad_qkv_low,
            qkv_full,
            context,
            ctx_pieces,
            up_send,
            up_stay,
        )
        sum_ctx, sum_gains = sum_ctx.T, sum_gains[:, :2].T
        sum_qkv, sum_out, sum_gate_up, sum_down, grad_home, result = finish(
            (own_qkv, own_out, own_gate, own_up, own_down),
            (landed_qkv, landed_out, landed_gate, landed_up, landed_down),
            grad_home,
            result,
            valid_mask,
        )
    else:

        def parts(left, right):
            away, stay = halves(left, near)
            block = width_model // n
            return [
                dot_rows(part, right).astype(bf16).reshape(n // 2, block, right.shape[1])
                for part in (away, stay)
            ]

        part_away = rows_back(grad_qkv_low[frame_count:], qkv_full).astype(bf16)
        part_stay = rows_back(grad_qkv_low[:frame_count], qkv_full)
        sum_qkv, sum_out, grad_home, result, sum_context, ctx_total = tail(
            n,
            part_away,
            part_stay,
            resid_in,
            grad_mid,
            norm_gains,
            grad_gain_two,
            result_rows,
            *parts(paired_one, grad_qkv_low),
            *parts(paired_grad_attn, mixed),
            context,
            ctx_pieces.transpose(1, 0, 2).reshape(-1, width_model),
        )
        result = (result.astype(f32) * valid_mask)[:, None]
        grad_home = grad_home[:, None]
        ctx_total = ctx_total.T
        sum_ctx = ctx_total[: ctx_weight.shape[0]]
        sum_gains = ctx_total[ctx_weight.shape[0] : ctx_weight.shape[0] + 2]

    return (
        result,
        grad_home,
        sum_context,
        sum_ctx,
        sum_gains,
        sum_qkv[None],
        sum_out[None],
        sum_gate_up[None],
        sum_down[None],
    )


def solution(mesh):
    placed = (
        P("frames", "stream", None),
        P("frames", None),
        P("frames", "stream", None),
        P("frames"),
        P(None, "frames"),
        P(),
        P("stream", None, "frames", None),
        P("stream", None, "frames", None),
        P("stream", None, "frames", None),
        P("stream", None, "frames", None),
    )
    return jax.shard_map(
        shards,
        mesh=mesh,
        in_specs=placed,
        out_specs=(
            P("frames", "stream", None),
            P("frames", "stream", None),
            P("frames", "stream"),
            P(None, ("stream", "frames")),
            P(None, ("stream", "frames")),
            P("stream", None, "frames", None),
            P("stream", None, "frames", None),
            P("stream", None, "frames", None),
            P("stream", None, "frames", None),
        ),
        check_vma=False,
    )
```
